32 devices in a mesh: seq: 4 (over y, x), dp: 8 (over z, core).
Axes of the slice: x: 2, y: 2, z: 4, core: 2. Of those that a mesh axis runs over, the one named last changes fastest.
Arguments:
- hidden_in: bfloat16 [8, 1024, 1536], P('dp', 'seq'), may hold values from -6 to 6
- lengths: int32 [8], P('dp'), may hold values from 256 to 1024, as said below
- routes: int32 [8, 1024, 4], P('dp', 'seq'), may hold values from 0 to 31, all different within a row
- gates: float32 [8, 1024, 4], P('dp', 'seq'), may hold values from 0.1 to 0.4
- priority: int32 [8, 4, 1024], P('dp', 'seq'), may hold values from 0 to 1023, each once within a row
- attn_gain: bfloat16 [1536], P(('seq', 'dp')), may hold values from 0.5 to 1.5
- mlp_gain: bfloat16 [1536], P(('seq', 'dp')), may hold values from 0.5 to 1.5
- w_query: bfloat16 [1536, 1536], P(('seq', 'dp')), may hold values from -0.15625 to 0.15625
- key_projection: bfloat16 [1536, 256], P(('seq', 'dp')), may hold values from -0.15625 to 0.15625
- value_projection: bfloat16 [1536, 256], P(('seq', 'dp')), may hold values from -0.15625 to 0.15625
- w_out: bfloat16 [1536, 1536], P(('seq', 'dp')), may hold values from -2 to 2
- w_gate: bfloat16 [32, 1536, 768], P('dp', 'seq'), may hold values from -0.15625 to 0.15625
- w_up: bfloat16 [32, 1536, 768], P('dp', 'seq'), may hold values from -0.15625 to 0.15625
- w_down: bfloat16 [32, 768, 1536], P('dp', 'seq'), may hold values from -0.21875 to 0.21875
- cotangent: bfloat16 [8, 1024, 1536], P('dp', 'seq'), may hold values from -6 to 6
Outputs:
- layer_out: float32 [8, 1024, 1536], P('dp', 'seq')
- input_grad: float32 [8, 1024, 1536], P('dp', 'seq')
- attn_gain_grad: float32 [1536], P(('seq', 'dp'))
- mlp_gain_grad: float32 [1536], P(('seq', 'dp'))
- query_weight_grad: float32 [1536, 1536], P(('seq', 'dp'))
- key_weight_grad: float32 [1536, 256], P(('seq', 'dp'))
- value_weight_grad: float32 [1536, 256], P(('seq', 'dp'))
- out_weight_grad: float32 [1536, 1536], P(('seq', 'dp'))
- gate_weight_grad: float32 [32, 1536, 768], P('dp', 'seq')
- up_weight_grad: float32 [32, 1536, 768], P('dp', 'seq')
- down_weight_grad: float32 [32, 768, 1536], P('dp', 'seq')
The draws below stay inside these ranges and needn't reach their ends.
Inputs may be any that keep to these rules, and one draw needn't show every extreme that they name: Positions below lengths[s] of slot s are valid, the rest padding; in every draw some slot is full. `routes`: each token names 4 different experts. `priority`: for each slot and block index, the 1024 entries are a permutation; entry t_local * 4 + k is the claiming rank of the pair of the block's token t_local and its k-th route.
All inputs are finite; a program needn't handle non-finite values.
Results may differ from the reference program's by a relative error of at most 0.015.
Values may be sent and summed in bfloat16 or wider, within the bound.
A program may use at most 256 MiB of HBM per device.

```python
import math
import jax
import jax.numpy as jnp
from jax import lax

MODEL_DIM = 1536
QUERY_HEADS = 12
KEY_VALUE_HEADS = 2
HEAD_DIM = 128
EXPERTS = 32
FF = 768
TOP = 4
STRETCH = 256
LEN = 1024
SLOTS = 8
CAP = 40
N_SEQ = 4


def draw_lengths(key, part):
    drawn = jax.random.randint(key, (SLOTS,), LEN // 4, LEN + 1, dtype=jnp.int32)
    chosen = jax.random.randint(jax.random.fold_in(key, 7), (), 0, SLOTS, dtype=jnp.int32)
    return jnp.where(jnp.arange(SLOTS, dtype=jnp.int32) == chosen, LEN, drawn).astype(jnp.int32)


def steps_of(key, extent, shards, least, top_value):
    level = 1.0
    for dim, parts in shards:
        draws = jax.random.uniform(jax.random.fold_in(jax.random.fold_in(key, 6), dim), (parts,), jnp.float32, least / len(shards), top_value / len(shards))
        level = level * jnp.repeat(jnp.exp(draws), extent[dim] // parts).reshape((-1,) + (1,) * (len(extent) - 1 - dim))
    return level


def distinct(key, rows, amount, top, lift):
    ranking = jax.random.permutation(jax.random.fold_in(key, 1), amount)
    favour = ranking
    for power in range(3):
        favour = favour * favour // amount
    favour = favour * lift // amount
    lots = jax.random.randint(jax.random.fold_in(key, 2), (rows, amount), 0, 4096) + favour
    fixed_rows = jax.random.permutation(jax.random.fold_in(key, 3), rows)[jnp.arange(amount) % rows]
    lots = jnp.where(jnp.arange(rows)[:, None] == fixed_rows[None, :], 1 << 14, lots)
    merit = lots * amount + jnp.arange(amount)
    return lax.top_k(merit.astype(jnp.int32), top)[1].astype(jnp.int32)


def centred(stream_key, dims, width, bound, cuts=(), kind=jnp.bfloat16):
    loudness = steps_of(stream_key, dims, cuts, -0.22, 0.18) if cuts else 1.0
    result = jax.random.normal(stream_key, dims, jnp.float32) * width * loudness
    return jnp.minimum(jnp.maximum(result, -bound), bound).astype(kind)


def setup_inputs(seed: int = 0) -> dict:
    arg_keys = jax.random.split(jax.random.key(seed), 16)
    hidden_in = centred(arg_keys[0], (SLOTS, LEN, MODEL_DIM), 1.0, 6.0, ((0, 8), (1, 4)))
    lengths = draw_lengths(jax.random.fold_in(arg_keys[15], 71), 0)
    routes = distinct(arg_keys[2], SLOTS * LEN, EXPERTS, TOP, 0).reshape((SLOTS, LEN, TOP))
    gates = jnp.clip(jnp.exp(math.log(0.4) - 1.3862944 * jax.random.uniform(arg_keys[3], (SLOTS, LEN, TOP), jnp.float32) ** steps_of(arg_keys[3], (SLOTS, LEN, TOP), ((0, 8), (1, 4)), -0.2, 0.2)), 0.1, 0.4)
    priority = jax.vmap(lambda own: jax.random.permutation(own, STRETCH * TOP))(jax.random.split(arg_keys[4], SLOTS * N_SEQ)).reshape((SLOTS, N_SEQ, STRETCH * TOP)).astype(jnp.int32)
    attn_gain = jnp.clip(1.0 + 0.1 * jax.random.normal(arg_keys[5], (MODEL_DIM,), jnp.float32), 0.5, 1.5).astype(jnp.bfloat16)
    mlp_gain = jnp.clip(1.0 + 0.1 * jax.random.normal(arg_keys[6], (MODEL_DIM,), jnp.float32), 0.5, 1.5).astype(jnp.bfloat16)
    w_query = centred(arg_keys[7], (MODEL_DIM, QUERY_HEADS * HEAD_DIM), MODEL_DIM ** -0.5, 0.15625, ((0, 32),))
    key_projection = centred(arg_keys[8], (MODEL_DIM, KEY_VALUE_HEADS * HEAD_DIM), MODEL_DIM ** -0.5, 0.15625, ((0, 32),))
    value_projection = centred(arg_keys[9], (MODEL_DIM, KEY_VALUE_HEADS * HEAD_DIM), MODEL_DIM ** -0.5, 0.15625, ((0, 32),))
    w_out = centred(arg_keys[10], (QUERY_HEADS * HEAD_DIM, MODEL_DIM), (max(QUERY_HEADS * HEAD_DIM // 256, 8)) ** -0.5, 2.0, ((0, 32),))
    w_gate = centred(arg_keys[11], (EXPERTS, MODEL_DIM, FF), MODEL_DIM ** -0.5, 0.15625, ((0, 8), (1, 4)))
    w_up = centred(arg_keys[12], (EXPERTS, MODEL_DIM, FF), MODEL_DIM ** -0.5, 0.15625, ((0, 8), (1, 4)))
    w_down = centred(arg_keys[13], (EXPERTS, FF, MODEL_DIM), FF ** -0.5, 0.21875, ((0, 8), (1, 4)))
    cotangent = centred(arg_keys[14], (SLOTS, LEN, MODEL_DIM), 1.0, 6.0, ((0, 8), (1, 4)))
    return {"hidden_in": hidden_in, "lengths": lengths, "routes": routes, "gates": gates, "priority": priority, "attn_gain": attn_gain, "mlp_gain": mlp_gain, "w_query": w_query, "key_projection": key_projection, "value_projection": value_projection, "w_out": w_out, "w_gate": w_gate, "w_up": w_up, "w_down": w_down, "cotangent": cotangent}


EPSILON = 1e-06
ROPE_BASE = 10000.0
NEG_FILL = -1e+30

@jax.custom_vjp
def low(v):
    return lax.optimization_barrier(v.astype(jnp.bfloat16)).astype(jnp.float32)

@jax.custom_vjp
def low_back(v):
    return v

def low_keep(v):
    return (low(v), None)

def low_pass(kept, grad):
    return (grad,)

def back_keep(v):
    return (v, None)

def back_low(kept, grad):
    return (low(grad),)
low.defvjp(low_keep, low_pass)
low_back.defvjp(back_keep, back_low)

def exact_dot(left, right):
    return jnp.dot(left, right, precision=lax.Precision.HIGHEST, preferred_element_type=jnp.float32)

def row_scale(values):
    return lax.rsqrt(lax.optimization_barrier(jnp.mean(values * values, axis=-1, keepdims=True)) + EPSILON)

def rope_angles(positions, head_size):
    half_dim = head_size // 2
    frequency = ROPE_BASE ** (-(2.0 * jnp.arange(half_dim, dtype=jnp.float32)) / head_size)
    angles = positions.astype(jnp.float32)[:, None] * frequency[None, :]
    return (jnp.cos(angles)[:, None, :], jnp.sin(angles)[:, None, :])

def apply_rotary(values, cosine_lookup, sine_lookup):
    half_dim = values.shape[-1] // 2
    lower_half = values[..., :half_dim]
    upper_half = values[..., half_dim:]
    return jnp.concatenate([lower_half * cosine_lookup - upper_half * sine_lookup, upper_half * cosine_lookup + lower_half * sine_lookup], axis=-1)

def route_slots(route_rows, order_rank, valid_rows, experts, capacity):
    pair_routes = route_rows.reshape(-1).astype(jnp.int32)
    pair_count = pair_routes.shape[0]
    is_live = jnp.repeat(valid_rows, route_rows.shape[1])
    onehot = ((pair_routes[:, None] == jnp.arange(experts, dtype=jnp.int32)[None, :]) & is_live[:, None]).astype(jnp.int32)
    by_rank = jnp.argsort(order_rank).astype(jnp.int32)
    sorted_hot = onehot[by_rank]
    before = (jnp.cumsum(sorted_hot, axis=0).astype(jnp.int32) - sorted_hot).astype(jnp.int32)
    rank_sorted = lax.optimization_barrier(jnp.sum(before * sorted_hot, axis=1)).astype(jnp.int32)
    claim_rank = rank_sorted[order_rank]
    is_kept = is_live & (claim_rank < capacity)
    target = jnp.where(is_kept, pair_routes * capacity + claim_rank, experts * capacity).astype(jnp.int32)
    source_pair = jnp.full((experts * capacity + 1,), pair_count, jnp.int32)
    source_pair = source_pair.at[target].set(jnp.arange(pair_count, dtype=jnp.int32))
    return (source_pair[:experts * capacity], target)

def attend_block(query_block, key_all, value_all, row_start, length):
    rows = query_block.shape[0]
    query_pos = row_start + jnp.arange(rows, dtype=jnp.int32)
    key_pos = jnp.arange(key_all.shape[0], dtype=jnp.int32)
    scores = jnp.einsum('qhgd,khd->hgqk', query_block, key_all, precision=lax.Precision.HIGHEST) / math.sqrt(HEAD_DIM)
    scores = low_back(scores)
    key_mask = (key_pos[None, :] <= query_pos[:, None]) & (key_pos[None, :] < length)
    scores = jnp.where(key_mask, scores, NEG_FILL)
    attn_probs = low(jax.nn.softmax(scores, axis=-1))
    return jnp.einsum('hgqk,khd->qhgd', attn_probs, value_all, precision=lax.Precision.HIGHEST)

def slot_attention(query_slot, key_slot, value_slot, length):
    sequence_extent = query_slot.shape[0]
    block_rows = min(512, sequence_extent)
    block_count = sequence_extent // block_rows
    pieces = query_slot.reshape((block_count, block_rows) + query_slot.shape[1:])
    starts = jnp.arange(block_count, dtype=jnp.int32) * block_rows
    produced = lax.map(lambda operands: jax.checkpoint(attend_block)(operands[0], key_slot, value_slot, operands[1], length), (pieces, starts))
    return produced.reshape(query_slot.shape)

def expert_apply(slot_rows, gate_one, up_one, down_one):
    gate_pre = low_back(exact_dot(slot_rows, gate_one))
    up_pre = low_back(exact_dot(slot_rows, up_one))
    expert_hidden = low(jax.nn.silu(gate_pre) * up_pre)
    return low_back(low(exact_dot(expert_hidden, down_one)))

def forward(inputs, gain_one, gain_two, query_w, key_w, value_w, out_w, gate_w, up_w, down_w, lengths, gate_rows, token_of, target):
    slot_total_count, sequence_extent, model_width = inputs.shape
    normed = low(inputs * row_scale(inputs) * gain_one)
    normed_rows = normed.reshape(-1, model_width)
    query_rows = low_back(exact_dot(normed_rows, query_w))
    key_matrix_rows = low_back(exact_dot(normed_rows, key_w))
    value_matrix_rows = low_back(low(exact_dot(normed_rows, value_w)))
    positions = jnp.arange(sequence_extent, dtype=jnp.int32)
    cosine_lookup, sine_lookup = rope_angles(positions, HEAD_DIM)
    query_rotated = low(apply_rotary(query_rows.reshape(slot_total_count, sequence_extent, QUERY_HEADS, HEAD_DIM), cosine_lookup, sine_lookup))
    key_rotated = low(apply_rotary(key_matrix_rows.reshape(slot_total_count, sequence_extent, KEY_VALUE_HEADS, HEAD_DIM), cosine_lookup, sine_lookup))
    value_head_split = value_matrix_rows.reshape(slot_total_count, sequence_extent, KEY_VALUE_HEADS, HEAD_DIM)
    query_head_groups = query_rotated.reshape(slot_total_count, sequence_extent, KEY_VALUE_HEADS, QUERY_HEADS // KEY_VALUE_HEADS, HEAD_DIM)
    attended = lax.map(lambda operands: slot_attention(operands[0], operands[1], operands[2], operands[3]), (query_head_groups, key_rotated, value_head_split, lengths))
    attended = low_back(low(attended.reshape(slot_total_count * sequence_extent, QUERY_HEADS * HEAD_DIM)))
    branch = low_back(exact_dot(attended, out_w)).reshape(slot_total_count, sequence_extent, model_width)
    middle = inputs + branch
    moe_input = low(middle * row_scale(middle) * gain_two)
    block_total = slot_total_count * N_SEQ
    local_rows = sequence_extent // N_SEQ
    moe_blocks = moe_input.reshape(block_total, local_rows, model_width)
    padded = jnp.concatenate([moe_blocks, jnp.zeros((block_total, 1, model_width), jnp.float32)], axis=1)
    slot_rows = low_back(jax.vmap(lambda source_table, index_rows: source_table[index_rows])(padded, token_of))
    by_expert = slot_rows.reshape(block_total, EXPERTS, CAP, model_width).transpose(1, 0, 2, 3)
    by_expert = by_expert.reshape(EXPERTS, block_total * CAP, model_width)
    produced = lax.map(lambda operands: jax.checkpoint(expert_apply)(operands[0], operands[1], operands[2], operands[3]), (by_expert, gate_w, up_w, down_w))
    produced = produced.reshape(EXPERTS, block_total, CAP, model_width).transpose(1, 0, 2, 3)
    produced = produced.reshape(block_total, EXPERTS * CAP, model_width)
    produced = jnp.concatenate([produced, jnp.zeros((block_total, 1, model_width), jnp.float32)], axis=1)
    pair_rows = jax.vmap(lambda source_table, index_rows: source_table[index_rows])(produced, target)
    pair_rows = pair_rows.reshape(block_total, local_rows, TOP, model_width)
    weights = gate_rows.reshape(block_total, local_rows, TOP, 1)
    expert_sum = lax.optimization_barrier(jnp.sum(weights * pair_rows, axis=2)).reshape(slot_total_count, sequence_extent, model_width)
    return middle + expert_sum

def reference(hidden_in, lengths, routes, gates, priority, attn_gain, mlp_gain, w_query, key_projection, value_projection, w_out, w_gate, w_up, w_down, cotangent):
    positions = jnp.arange(LEN, dtype=jnp.int32)
    valid = positions[None, :] < lengths[:, None].astype(jnp.int32)
    valid_blocks = valid.reshape(SLOTS * N_SEQ, STRETCH)
    source_pair, target = jax.vmap(lambda route_rows, order_rank, valid_rows: route_slots(route_rows, order_rank, valid_rows, EXPERTS, CAP))(routes.reshape(SLOTS * N_SEQ, STRETCH, TOP).astype(jnp.int32), priority.reshape(SLOTS * N_SEQ, STRETCH * TOP).astype(jnp.int32), valid_blocks)
    token_of = jnp.where(source_pair < STRETCH * TOP, source_pair // TOP, STRETCH).astype(jnp.int32)
    gate_rows = gates.astype(jnp.float32)

    def layer(inputs, gain_one, gain_two, query_w, key_w, value_w, out_w, gate_w, up_w, down_w):
        return forward(inputs, gain_one, gain_two, query_w, key_w, value_w, out_w, gate_w, up_w, down_w, lengths.astype(jnp.int32), gate_rows, token_of, target)
    layer_out, pullback = jax.vjp(layer, hidden_in.astype(jnp.float32), attn_gain.astype(jnp.float32), mlp_gain.astype(jnp.float32), w_query.astype(jnp.float32), key_projection.astype(jnp.float32), value_projection.astype(jnp.float32), w_out.astype(jnp.float32), w_gate.astype(jnp.float32), w_up.astype(jnp.float32), w_down.astype(jnp.float32))
    out_grad = cotangent.astype(jnp.float32) * valid[:, :, None].astype(jnp.float32)
    grads = pullback(out_grad)
    return (layer_out, grads[0], grads[1], grads[2], grads[3], grads[4], grads[5], grads[6], grads[7], grads[8], grads[9])
```

```python
import math

import jax
import jax.numpy as jnp
from jax import lax
from jax.sharding import PartitionSpec as P

HEAD_DIM = 128
EXPERTS = 32
TOP = 4
CAP = 40

EPSILON = 1e-06
ROPE_BASE = 10000.0
NEG_FILL = -1e30
LANES = 128
BOTH = ("seq", "dp")
BF16 = jnp.bfloat16
F32 = jnp.float32


def rope_angles(positions, head_size):
    half_dim = head_size // 2
    frequency = ROPE_BASE ** (-(2.0 * jnp.arange(half_dim, dtype=F32)) / head_size)
    angles = positions.astype(F32)[:, None] * frequency[None, :]
    return (jnp.cos(angles)[:, None, :], jnp.sin(angles)[:, None, :])


def apply_rotary(values, cosine_lookup, sine_lookup):
    half_dim = values.shape[-1] // 2
    lower_half = values[..., :half_dim]
    upper_half = values[..., half_dim:]
    return jnp.concatenate(
        [
            lower_half * cosine_lookup - upper_half * sine_lookup,
            upper_half * cosine_lookup + lower_half * sine_lookup,
        ],
        axis=-1,
    )


def dot(left, right, contract):
    return lax.dot_general(left, right, (contract, ((), ())), preferred_element_type=F32)


def nn(left, right):
    return dot(left, right, ((1,), (0,)))


def nt(left, right):
    return dot(left, right, ((1,), (1,)))


def tn(left, right):
    return dot(left, right, ((0,), (0,)))


def claim_places(routes, priority, is_valid):
    pair_routes = routes.reshape(-1)
    live = jnp.repeat(is_valid, TOP)
    key = jnp.where(live, pair_routes, -1)
    earlier = (key[None, :] == pair_routes[:, None]) & (priority[None, :] < priority[:, None])
    place = jnp.sum(earlier.astype(F32), axis=1).astype(jnp.int32)
    return pair_routes, place, live & (place < CAP)


def masked_scores(query_group, key_head, query_pos, key_pos, length, score_scale):
    scores = (
        jnp.einsum("qgd,kd->gqk", query_group, key_head, preferred_element_type=F32) * score_scale
    )
    key_mask = (key_pos[None, :] <= query_pos[:, None]) & (key_pos[None, :] < length)
    return jnp.where(key_mask[None], scores, NEG_FILL)


def head_forward(query_group, key_head, value_head, query_pos, key_pos, length, score_scale):
    scores = masked_scores(query_group, key_head, query_pos, key_pos, length, score_scale)
    row_max = jnp.max(scores, axis=-1, keepdims=True)
    exp_scores = jnp.exp(scores - row_max)
    exp_total = jnp.sum(exp_scores, axis=-1, keepdims=True)
    attn_probs = (exp_scores / exp_total).astype(BF16)
    head_out = jnp.einsum("gqk,kd->qgd", attn_probs, value_head, preferred_element_type=F32)
    return (head_out, (row_max + jnp.log(exp_total))[..., 0])


def head_backward(
    query_group, key_head, value_head, head_grad, log_total, query_pos, key_pos, length, score_scale
):
    scores = masked_scores(query_group, key_head, query_pos, key_pos, length, score_scale)
    attn_probs = jnp.exp(scores - log_total[..., None])
    prob_grad = jnp.einsum("qgd,kd->gqk", head_grad, value_head, preferred_element_type=F32)
    row_delta = jnp.sum(attn_probs * prob_grad, axis=-1, keepdims=True)
    score_grad = (attn_probs * (prob_grad - row_delta)).astype(BF16)
    query_part = (
        jnp.einsum("gqk,kd->qgd", score_grad, key_head, preferred_element_type=F32) * score_scale
    )
    key_part = (
        jnp.einsum("gqk,qgd->kd", score_grad, query_group, preferred_element_type=F32) * score_scale
    )
    value_part = jnp.einsum(
        "gqk,qgd->kd", attn_probs.astype(BF16), head_grad, preferred_element_type=F32
    )
    return (query_part, key_part, value_part)


def norm_back(values, scale_rows, gain_vec, incoming):
    weighted = incoming * gain_vec
    inner_mean = jnp.mean(weighted * values, axis=-1, keepdims=True)
    values_grad = scale_rows * weighted - values * scale_rows * scale_rows * scale_rows * inner_mean
    return (values_grad, jnp.sum(incoming * values * scale_rows, axis=0))


def split_heads(gathered, kv_heads):
    return gathered.reshape(gathered.shape[0], kv_heads, HEAD_DIM).transpose(1, 0, 2)


def swap(blocks, axes):
    return lax.all_to_all(blocks, axes, split_axis=0, concat_axis=0, tiled=True)


def on_device(
    hidden_in,
    lengths,
    routes,
    gates,
    priority,
    attn_gain,
    mlp_gain,
    w_query,
    key_projection,
    value_projection,
    w_out,
    w_gate,
    w_up,
    w_down,
    cotangent,
):
    rows = hidden_in.shape[1]
    width = hidden_in.shape[2]
    dp_count = lax.axis_size("dp")
    seq_count = lax.axis_size("seq")
    devices = dp_count * seq_count
    own_experts = w_gate.shape[0]
    sharers = seq_count // own_experts
    hidden_units = w_gate.shape[2]
    my_seq = lax.axis_index("seq")
    extent = rows * seq_count
    query_pos = my_seq * rows + jnp.arange(rows, dtype=jnp.int32)
    key_pos = jnp.arange(extent, dtype=jnp.int32)
    length = lengths[0]
    is_valid = query_pos < length
    score_scale = 1.0 / math.sqrt(HEAD_DIM)
    q_width = w_query.shape[1]
    kv_width = key_projection.shape[1]
    q_heads = q_width // HEAD_DIM
    kv_heads = kv_width // HEAD_DIM
    group_size = q_heads // kv_heads
    cosine_lookup, sine_lookup = rope_angles(query_pos, HEAD_DIM)

    gain_block = jnp.concatenate(
        [attn_gain[:, None], mlp_gain[:, None], jnp.zeros((attn_gain.shape[0], LANES - 2), BF16)],
        axis=1,
    )
    packed = jnp.concatenate([w_query, key_projection, value_projection, gain_block], axis=1)
    packed_full = lax.all_gather(packed, BOTH, axis=0, tiled=True)
    out_full = lax.all_gather(w_out, BOTH, axis=0, tiled=True)
    query_full = packed_full[:, :q_width]
    key_full = packed_full[:, q_width : q_width + kv_width]
    value_full = packed_full[:, q_width + kv_width : q_width + 2 * kv_width]
    gain_one = packed_full[:, q_width + 2 * kv_width].astype(F32)
    gain_two = packed_full[:, q_width + 2 * kv_width + 1].astype(F32)

    gate_full = swap(jnp.repeat(w_gate, sharers, axis=0), "seq").reshape(width, hidden_units)
    up_full = swap(jnp.repeat(w_up, sharers, axis=0), "seq").reshape(width, hidden_units)
    down_full = swap(jnp.repeat(w_down, sharers, axis=0), "seq").reshape(hidden_units, width)

    pair_routes, place, kept = claim_places(routes[0], priority[0, 0], is_valid)
    holder = (pair_routes // own_experts) * seq_count + (pair_routes % own_experts) * sharers
    holder = holder + my_seq * sharers // seq_count
    slots = devices * CAP
    target = jnp.where(kept, holder * CAP + place, slots).reshape(rows, TOP)
    slot_ids = jnp.arange(slots, dtype=jnp.int32)
    hits = target[:, :, None] == slot_ids[None, None, :]
    gate_rows = gates[0]
    token_hot = jnp.any(hits, axis=1).astype(BF16)
    slot_gate = jnp.sum(jnp.where(hits, gate_rows[:, :, None], 0.0), axis=(0, 1))

    live_cotangent = jnp.where(is_valid[:, None], cotangent[0], jnp.zeros((), BF16))
    out_grad = live_cotangent.astype(F32)
    grad_send = (tn(token_hot, live_cotangent) * slot_gate[:, None]).astype(BF16)
    grad_rows = swap(grad_send.reshape(devices, CAP, width), ("dp", "seq")).reshape(slots, width)

    inputs = hidden_in[0].astype(F32)
    scale_one = lax.rsqrt(jnp.mean(inputs * inputs, axis=-1, keepdims=True) + EPSILON)
    normed = (inputs * scale_one * gain_one).astype(BF16)
    query_rows = nn(normed, query_full)
    key_matrix_rows = nn(normed, key_full)
    value_matrix_rows = nn(normed, value_full).astype(BF16)
    query_rotated = apply_rotary(
        query_rows.reshape(rows, q_heads, HEAD_DIM), cosine_lookup, sine_lookup
    ).astype(BF16)
    key_rotated = apply_rotary(
        key_matrix_rows.reshape(rows, kv_heads, HEAD_DIM), cosine_lookup, sine_lookup
    ).astype(BF16)
    key_rotated = key_rotated.reshape(rows, kv_width)
    kv_mine = jnp.concatenate([key_rotated, value_matrix_rows], axis=1)
    kv_all = swap(jnp.broadcast_to(kv_mine[None], (seq_count, rows, 2 * kv_width)), "seq")
    kv_all = kv_all.reshape(extent, 2 * kv_width)
    key_all, value_all = kv_all[:, :kv_width], kv_all[:, kv_width:]
    query_head_groups = query_rotated.reshape(rows, kv_heads, group_size, HEAD_DIM).transpose(
        1, 0, 2, 3
    )
    key_heads, value_heads = split_heads(key_all, kv_heads), split_heads(value_all, kv_heads)
    attended, log_total = lax.map(
        lambda operands: head_forward(
            operands[0], operands[1], operands[2], query_pos, key_pos, length, score_scale
        ),
        (query_head_groups, key_heads, value_heads),
    )
    attended = attended.transpose(1, 0, 2, 3).reshape(rows, q_width).astype(BF16)
    middle = inputs + nn(attended, out_full)
    scale_two = lax.rsqrt(jnp.mean(middle * middle, axis=-1, keepdims=True) + EPSILON)
    moe_input = (middle * scale_two * gain_two).astype(BF16)

    send_rows = tn(token_hot, moe_input).astype(BF16).reshape(devices, CAP, width)
    slot_rows = swap(send_rows, ("dp", "seq")).reshape(slots, width)
    gate_pre = nn(slot_rows, gate_full)
    up_pre = nn(slot_rows, up_full)
    gate_sigmoid = jax.nn.sigmoid(gate_pre)
    gate_act = gate_pre * gate_sigmoid
    gate_slope = gate_sigmoid * (1.0 + gate_pre * (1.0 - gate_sigmoid))
    expert_hidden = (gate_act * up_pre).astype(BF16)
    hidden_grad = nt(grad_rows, down_full)
    gate_pre_grad = (hidden_grad * up_pre * gate_slope).astype(BF16)
    up_pre_grad = (hidden_grad * gate_act).astype(BF16)
    row_grad = (nt(gate_pre_grad, gate_full) + nt(up_pre_grad, up_full)).astype(BF16)
    row_back = swap(row_grad.reshape(devices, CAP, width), ("dp", "seq")).reshape(slots, width)

    gate_grad = tn(slot_rows, gate_pre_grad).astype(BF16)
    up_grad = tn(slot_rows, up_pre_grad).astype(BF16)
    down_grad = tn(expert_hidden, grad_rows).astype(BF16)

    def to_owners(grad):
        pieces = swap(grad.reshape(seq_count, -1, grad.shape[1]), "seq")
        pieces = pieces.reshape((own_experts, sharers) + pieces.shape[1:])
        return jnp.sum(pieces.astype(F32), axis=1)

    expert_grads = (to_owners(gate_grad), to_owners(up_grad), to_owners(down_grad))

    expert_out = nn(expert_hidden, down_full).astype(BF16)
    returned = swap(expert_out.reshape(devices, CAP, width), ("dp", "seq")).reshape(slots, width)
    gate_high = gate_rows.astype(BF16)
    gate_low = (gate_rows - gate_high.astype(F32)).astype(BF16)

    def gate_hot(weights):
        return jnp.sum(
            jnp.where(hits, weights.astype(F32)[:, :, None], 0.0), axis=1
        ).astype(BF16)

    layer_out = middle + nn(gate_hot(gate_high), returned) + nn(gate_hot(gate_low), returned)

    moe_input_grad = nn(token_hot, row_back)
    middle_norm_grad, gain_two_grad = norm_back(middle, scale_two, gain_two, moe_input_grad)
    middle_grad = out_grad + middle_norm_grad
    branch_grad = middle_grad.astype(BF16)
    out_weight_grad = tn(attended, branch_grad)
    attended_grad = nt(branch_grad, out_full).astype(BF16)
    attended_grad = attended_grad.reshape(rows, kv_heads, group_size, HEAD_DIM).transpose(
        1, 0, 2, 3
    )
    query_part, key_part, value_part = lax.map(
        lambda operands: head_backward(
            operands[0],
            operands[1],
            operands[2],
            operands[3],
            operands[4],
            query_pos,
            key_pos,
            length,
            score_scale,
        ),
        (query_head_groups, key_heads, value_heads, attended_grad, log_total),
    )
    kv_terms = jnp.concatenate(
        [
            key_part.transpose(1, 0, 2).reshape(extent, kv_width),
            value_part.transpose(1, 0, 2).reshape(extent, kv_width),
        ],
        axis=1,
    ).astype(BF16)
    kv_back = swap(kv_terms.reshape(seq_count, rows, 2 * kv_width), "seq")
    kv_sum = jnp.sum(kv_back.astype(F32), axis=0)
    key_grad = apply_rotary(
        kv_sum[:, :kv_width].reshape(rows, kv_heads, HEAD_DIM), cosine_lookup, -sine_lookup
    )
    key_grad = key_grad.reshape(rows, kv_width).astype(BF16)
    value_grad = kv_sum[:, kv_width:].astype(BF16)
    query_grad = apply_rotary(
        query_part.transpose(1, 0, 2, 3).reshape(rows, q_heads, HEAD_DIM),
        cosine_lookup,
        -sine_lookup,
    )
    query_grad = query_grad.reshape(rows, q_width).astype(BF16)
    normed_grad = nt(query_grad, query_full) + nt(key_grad, key_full) + nt(value_grad, value_full)
    input_norm_grad, gain_one_grad = norm_back(inputs, scale_one, gain_one, normed_grad)
    input_grad = middle_grad + input_norm_grad

    def with_gain(parts, gain_grad):
        column = jnp.pad(gain_grad[:, None].astype(BF16), ((0, 0), (0, LANES - 1)))
        return jnp.concatenate([p.astype(BF16) for p in parts] + [column], axis=1)

    out_terms = with_gain([out_weight_grad], gain_two_grad)
    out_owned = lax.psum_scatter(out_terms, BOTH, scatter_dimension=0, tiled=True).astype(F32)
    query_terms = with_gain(
        [tn(normed, query_grad), tn(normed, key_grad), tn(normed, value_grad)], gain_one_grad
    )
    owned = lax.psum_scatter(query_terms, BOTH, scatter_dimension=0, tiled=True).astype(F32)
    return (
        layer_out[None],
        input_grad[None],
        owned[:, q_width + 2 * kv_width],
        out_owned[:, width],
        owned[:, :q_width],
        owned[:, q_width : q_width + kv_width],
        owned[:, q_width + kv_width : q_width + 2 * kv_width],
        out_owned[:, :width],
        *expert_grads,
    )


def solution(mesh):
    part = P("dp", "seq", None)
    both = P(BOTH)
    both_rows = P(BOTH, None)
    return jax.shard_map(
        on_device,
        mesh=mesh,
        in_specs=(part, P("dp"), part, part, part, both, both)
        + (both_rows,) * 4
        + (part,) * 4,
        out_specs=(part, part, both, both) + (both_rows,) * 4 + (part,) * 3,
        check_vma=False,
    )
```

```python
import functools
import math

import jax
import jax.numpy as jnp
from jax import lax
from jax.experimental import pallas as pl
from jax.experimental.pallas import tpu as pltpu
from jax.sharding import PartitionSpec as P

HEAD_DIM = 128
EXPERTS = 32
TOP = 4
CAP = 40

EPSILON = 1e-06
ROPE_BASE = 10000.0
NEG_FILL = -1e30
LANES = 128
BOTH = ("seq", "dp")
BF16 = jnp.bfloat16
F32 = jnp.float32


def rope_angles(positions, head_size):
    half_dim = head_size // 2
    frequency = ROPE_BASE ** (-(2.0 * jnp.arange(half_dim, dtype=F32)) / head_size)
    angles = positions.astype(F32)[:, None] * frequency[None, :]
    return (jnp.cos(angles)[:, None, :], jnp.sin(angles)[:, None, :])


def apply_rotary(values, cosine_lookup, sine_lookup):
    half_dim = values.shape[-1] // 2
    lower_half = values[..., :half_dim]
    upper_half = values[..., half_dim:]
    return jnp.concatenate(
        [
            lower_half * cosine_lookup - upper_half * sine_lookup,
            upper_half * cosine_lookup + lower_half * sine_lookup,
        ],
        axis=-1,
    )


def dot(left, right, contract):
    return lax.dot_general(left, right, (contract, ((), ())), preferred_element_type=F32)


def nn(left, right):
    return dot(left, right, ((1,), (0,)))


def nt(left, right):
    return dot(left, right, ((1,), (1,)))


def tn(left, right):
    return dot(left, right, ((0,), (0,)))


def claim_places(routes, priority, is_valid):
    pair_routes = routes.reshape(-1)
    live = jnp.repeat(is_valid, TOP)
    key = jnp.where(live, pair_routes, -1)
    earlier = (key[None, :] == pair_routes[:, None]) & (priority[None, :] < priority[:, None])
    place = jnp.sum(earlier.astype(F32), axis=1).astype(jnp.int32)
    return pair_routes, place, live & (place < CAP)


def masked_scores(query_group, key_head, query_pos, key_pos, length, score_scale):
    scores = (
        jnp.einsum("qgd,kd->gqk", query_group, key_head, preferred_element_type=F32) * score_scale
    )
    key_mask = (key_pos[None, :] <= query_pos[:, None]) & (key_pos[None, :] < length)
    return jnp.where(key_mask[None], scores, NEG_FILL)


def head_forward(query_group, key_head, value_head, query_pos, key_pos, length, score_scale):
    scores = masked_scores(query_group, key_head, query_pos, key_pos, length, score_scale)
    row_max = jnp.max(scores, axis=-1, keepdims=True)
    exp_scores = jnp.exp(scores - row_max)
    exp_total = jnp.sum(exp_scores, axis=-1, keepdims=True)
    attn_probs = (exp_scores / exp_total).astype(BF16)
    head_out = jnp.einsum("gqk,kd->qgd", attn_probs, value_head, preferred_element_type=F32)
    return (head_out, (row_max + jnp.log(exp_total))[..., 0])


def head_backward(
    query_group, key_head, value_head, head_grad, log_total, query_pos, key_pos, length, score_scale
):
    scores = masked_scores(query_group, key_head, query_pos, key_pos, length, score_scale)
    attn_probs = jnp.exp(scores - log_total[..., None])
    prob_grad = jnp.einsum("qgd,kd->gqk", head_grad, value_head, preferred_element_type=F32)
    row_delta = jnp.sum(attn_probs * prob_grad, axis=-1, keepdims=True)
    score_grad = (attn_probs * (prob_grad - row_delta)).astype(BF16)
    query_part = (
        jnp.einsum("gqk,kd->qgd", score_grad, key_head, preferred_element_type=F32) * score_scale
    )
    key_part = (
        jnp.einsum("gqk,qgd->kd", score_grad, query_group, preferred_element_type=F32) * score_scale
    )
    value_part = jnp.einsum(
        "gqk,qgd->kd", attn_probs.astype(BF16), head_grad, preferred_element_type=F32
    )
    return (query_part, key_part, value_part)


def norm_back(values, scale_rows, gain_vec, incoming):
    weighted = incoming * gain_vec
    inner_mean = jnp.mean(weighted * values, axis=-1, keepdims=True)
    values_grad = scale_rows * weighted - values * scale_rows * scale_rows * scale_rows * inner_mean
    return (values_grad, jnp.sum(incoming * values * scale_rows, axis=0))


def split_heads(gathered, kv_heads):
    return gathered.reshape(gathered.shape[0], kv_heads, HEAD_DIM).transpose(1, 0, 2)


def swap(blocks, axes):
    return lax.all_to_all(blocks, axes, split_axis=0, concat_axis=0, tiled=True)


MESH_IDS = pl.DeviceIdType.MESH


def exchange_kernel(count, n, block_of, *refs):
    sources, targets = refs[:n], refs[n : 2 * n]
    send_sems, recv_sems, local_sems = refs[2 * n :]
    me = lax.axis_index("seq")
    barrier = pltpu.get_barrier_semaphore()
    for step in range(1, count):
        peer = lax.rem(me + step, count)
        pl.semaphore_signal(barrier, inc=1, device_id={"seq": peer}, device_id_type=MESH_IDS)
    pl.semaphore_wait(barrier, count - 1)
    copies = []
    for i in range(n):
        for step in range(1, count):
            peer = lax.rem(me + step, count)
            copy = pltpu.make_async_remote_copy(
                src_ref=block_of(sources[i], peer),
                dst_ref=targets[i].at[me],
                send_sem=send_sems.at[i, step - 1],
                recv_sem=recv_sems.at[i, step - 1],
                device_id={"seq": peer},
                device_id_type=MESH_IDS,
            )
            copy.start()
            copies.append(copy)
        copy = pltpu.make_async_copy(
            block_of(sources[i], me), targets[i].at[me], local_sems.at[i]
        )
        copy.start()
        copies.append(copy)
    for copy in copies:
        copy.wait()


def seq_exchange(arrays, collective_id, block_of, block_shapes, name):
    count, n = lax.axis_size("seq"), len(arrays)
    sent = sum(math.prod(shape) for shape in block_shapes) * (count - 1) * 2
    return pl.pallas_call(
        functools.partial(exchange_kernel, count, n, block_of),
        out_shape=[jax.ShapeDtypeStruct((count,) + shape, BF16) for shape in block_shapes],
        in_specs=[pl.BlockSpec(memory_space=pl.ANY)] * n,
        out_specs=[pl.BlockSpec(memory_space=pl.ANY)] * n,
        scratch_shapes=[
            pltpu.SemaphoreType.DMA((n, count - 1)),
            pltpu.SemaphoreType.DMA((n, count - 1)),
            pltpu.SemaphoreType.DMA((n,)),
        ],
        compiler_params=pltpu.CompilerParams(
            collective_id=collective_id, vmem_limit_bytes=4 << 20
        ),
        cost_estimate=pl.CostEstimate(flops=0, bytes_accessed=20 * sent, transcendentals=0),
        name=name,
    )(*arrays)


def on_device(
    hidden_in,
    lengths,
    routes,
    gates,
    priority,
    attn_gain,
    mlp_gain,
    w_query,
    key_projection,
    value_projection,
    w_out,
    w_gate,
    w_up,
    w_down,
    cotangent,
):
    rows = hidden_in.shape[1]
    width = hidden_in.shape[2]
    dp_count = lax.axis_size("dp")
    seq_count = lax.axis_size("seq")
    devices = dp_count * seq_count
    own_experts = w_gate.shape[0]
    sharers = seq_count // own_experts
    hidden_units = w_gate.shape[2]
    my_seq = lax.axis_index("seq")
    extent = rows * seq_count
    query_pos = my_seq * rows + jnp.arange(rows, dtype=jnp.int32)
    key_pos = jnp.arange(extent, dtype=jnp.int32)
    length = lengths[0]
    is_valid = query_pos < length
    score_scale = 1.0 / math.sqrt(HEAD_DIM)
    q_width = w_query.shape[1]
    kv_width = key_projection.shape[1]
    q_heads = q_width // HEAD_DIM
    kv_heads = kv_width // HEAD_DIM
    group_size = q_heads // kv_heads
    cosine_lookup, sine_lookup = rope_angles(query_pos, HEAD_DIM)

    gain_block = jnp.concatenate(
        [attn_gain[:, None], mlp_gain[:, None], jnp.zeros((attn_gain.shape[0], LANES - 2), BF16)],
        axis=1,
    )
    packed = jnp.concatenate([w_query, key_projection, value_projection, gain_block], axis=1)
    pair_routes, place, kept = claim_places(routes[0], priority[0, 0], is_valid)
    holder = (pair_routes // own_experts) * seq_count + (pair_routes % own_experts) * sharers
    holder = holder + my_seq * sharers // seq_count
    slots = devices * CAP
    target = jnp.where(kept, holder * CAP + place, slots).reshape(rows, TOP)
    slot_ids = jnp.arange(slots, dtype=jnp.int32)
    hits = target[:, :, None] == slot_ids[None, None, :]
    gate_rows = gates[0]
    token_hot = jnp.any(hits, axis=1).astype(BF16)
    slot_gate = jnp.sum(jnp.where(hits, gate_rows[:, :, None], 0.0), axis=(0, 1))

    live_cotangent = jnp.where(is_valid[:, None], cotangent[0], jnp.zeros((), BF16))
    out_grad = live_cotangent.astype(F32)
    grad_send = (tn(token_hot, live_cotangent) * slot_gate[:, None]).astype(BF16)
    grad_send, hidden_in, packed, w_out = lax.optimization_barrier(
        (grad_send, hidden_in, packed, w_out)
    )
    grad_rows = swap(grad_send.reshape(devices, CAP, width), ("dp", "seq")).reshape(slots, width)

    packed_full = lax.all_gather(packed, BOTH, axis=0, tiled=True)
    out_full = lax.all_gather(w_out, BOTH, axis=0, tiled=True)
    query_full = packed_full[:, :q_width]
    key_full = packed_full[:, q_width : q_width + kv_width]
    value_full = packed_full[:, q_width + kv_width : q_width + 2 * kv_width]
    gain_one = packed_full[:, q_width + 2 * kv_width].astype(F32)
    gain_two = packed_full[:, q_width + 2 * kv_width + 1].astype(F32)

    inputs = hidden_in[0].astype(F32)
    scale_one = lax.rsqrt(jnp.mean(inputs * inputs, axis=-1, keepdims=True) + EPSILON)
    normed = (inputs * scale_one * gain_one).astype(BF16)
    query_rows = nn(normed, query_full)
    key_matrix_rows = nn(normed, key_full)
    value_matrix_rows = nn(normed, value_full).astype(BF16)
    query_rotated = apply_rotary(
        query_rows.reshape(rows, q_heads, HEAD_DIM), cosine_lookup, sine_lookup
    ).astype(BF16)
    key_rotated = apply_rotary(
        key_matrix_rows.reshape(rows, kv_heads, HEAD_DIM), cosine_lookup, sine_lookup
    ).astype(BF16)
    key_rotated = key_rotated.reshape(rows, kv_width)
    kv_mine = jnp.concatenate([key_rotated, value_matrix_rows], axis=1)
    (kv_all,) = seq_exchange(
        [kv_mine], 1, lambda ref, peer: ref, [(rows, 2 * kv_width)], "gather_keys"
    )
    kv_all = kv_all.reshape(extent, 2 * kv_width)
    key_all, value_all = kv_all[:, :kv_width], kv_all[:, kv_width:]
    query_head_groups = query_rotated.reshape(rows, kv_heads, group_size, HEAD_DIM).transpose(
        1, 0, 2, 3
    )
    key_heads, value_heads = split_heads(key_all, kv_heads), split_heads(value_all, kv_heads)
    attended, log_total = lax.map(
        lambda operands: head_forward(
            operands[0], operands[1], operands[2], query_pos, key_pos, length, score_scale
        ),
        (query_head_groups, key_heads, value_heads),
    )
    attended = attended.transpose(1, 0, 2, 3).reshape(rows, q_width).astype(BF16)
    middle = inputs + nn(attended, out_full)
    scale_two = lax.rsqrt(jnp.mean(middle * middle, axis=-1, keepdims=True) + EPSILON)
    moe_input = (middle * scale_two * gain_two).astype(BF16)

    send_rows = tn(token_hot, moe_input).astype(BF16).reshape(devices, CAP, width)
    send_rows, grad_rows, w_gate, w_up, w_down = lax.optimization_barrier(
        (send_rows, grad_rows, w_gate, w_up, w_down)
    )
    slot_rows = swap(send_rows, ("dp", "seq")).reshape(slots, width)
    gate_full, up_full, down_full = seq_exchange(
        [w_gate, w_up, w_down],
        2,
        lambda ref, peer: ref.at[peer // sharers],
        [w_gate.shape[1:], w_up.shape[1:], w_down.shape[1:]],
        "gather_expert",
    )
    gate_full = gate_full.reshape(width, hidden_units)
    up_full = up_full.reshape(width, hidden_units)
    down_full = down_full.reshape(hidden_units, width)
    gate_pre = nn(slot_rows, gate_full)
    up_pre = nn(slot_rows, up_full)
    gate_sigmoid = jax.nn.sigmoid(gate_pre)
    gate_act = gate_pre * gate_sigmoid
    gate_slope = gate_sigmoid * (1.0 + gate_pre * (1.0 - gate_sigmoid))
    expert_hidden = (gate_act * up_pre).astype(BF16)
    hidden_grad = nt(grad_rows, down_full)
    gate_pre_grad = (hidden_grad * up_pre * gate_slope).astype(BF16)
    up_pre_grad = (hidden_grad * gate_act).astype(BF16)
    row_grad = (nt(gate_pre_grad, gate_full) + nt(up_pre_grad, up_full)).astype(BF16)
    row_back = swap(row_grad.reshape(devices, CAP, width), ("dp", "seq")).reshape(slots, width)

    gate_grad = tn(slot_rows, gate_pre_grad).astype(BF16)
    up_grad = tn(slot_rows, up_pre_grad).astype(BF16)
    down_grad = tn(expert_hidden, grad_rows).astype(BF16)

    pieces = seq_exchange(
        [g.reshape(seq_count, -1, g.shape[1]) for g in (gate_grad, up_grad, down_grad)],
        3,
        lambda ref, peer: ref.at[peer],
        [w_gate.shape[1:], w_up.shape[1:], w_down.shape[1:]],
        "return_expert_grads",
    )

    row_back, *pieces = lax.optimization_barrier((row_back, *pieces))

    def owned_sum(piece):
        piece = piece.reshape((own_experts, sharers) + piece.shape[1:])
        return jnp.sum(piece.astype(F32), axis=1)

    expert_grads = [owned_sum(piece) for piece in pieces]

    expert_out = nn(expert_hidden, down_full).astype(BF16)
    expert_out, row_back = lax.optimization_barrier((expert_out, row_back))
    returned = swap(expert_out.reshape(devices, CAP, width), ("dp", "seq")).reshape(slots, width)
    moe_input_grad = nn(token_hot, row_back)
    middle_norm_grad, gain_two_grad = norm_back(middle, scale_two, gain_two, moe_input_grad)
    middle_grad = out_grad + middle_norm_grad
    branch_grad = middle_grad.astype(BF16)
    out_weight_grad = tn(attended, branch_grad)
    attended_grad = nt(branch_grad, out_full).astype(BF16)
    attended_grad = attended_grad.reshape(rows, kv_heads, group_size, HEAD_DIM).transpose(
        1, 0, 2, 3
    )
    query_part, key_part, value_part = lax.map(
        lambda operands: head_backward(
            operands[0],
            operands[1],
            operands[2],
            operands[3],
            operands[4],
            query_pos,
            key_pos,
            length,
            score_scale,
        ),
        (query_head_groups, key_heads, value_heads, attended_grad, log_total),
    )
    kv_terms = jnp.concatenate(
        [
            key_part.transpose(1, 0, 2).reshape(extent, kv_width),
            value_part.transpose(1, 0, 2).reshape(extent, kv_width),
        ],
        axis=1,
    ).astype(BF16)
    (kv_back,) = seq_exchange(
        [kv_terms.reshape(seq_count, rows, 2 * kv_width)],
        4,
        lambda ref, peer: ref.at[peer],
        [(rows, 2 * kv_width)],
        "return_key_grads",
    )
    kv_sum = jnp.sum(kv_back.astype(F32), axis=0)
    key_grad = apply_rotary(
        kv_sum[:, :kv_width].reshape(rows, kv_heads, HEAD_DIM), cosine_lookup, -sine_lookup
    )
    key_grad = key_grad.reshape(rows, kv_width).astype(BF16)
    value_grad = kv_sum[:, kv_width:].astype(BF16)
    query_grad = apply_rotary(
        query_part.transpose(1, 0, 2, 3).reshape(rows, q_heads, HEAD_DIM),
        cosine_lookup,
        -sine_lookup,
    )
    query_grad = query_grad.reshape(rows, q_width).astype(BF16)
    normed_grad = nt(query_grad, query_full) + nt(key_grad, key_full) + nt(value_grad, value_full)
    input_norm_grad, gain_one_grad = norm_back(inputs, scale_one, gain_one, normed_grad)
    input_grad = middle_grad + input_norm_grad

    def with_gain(parts, gain_grad):
        column = jnp.pad(gain_grad[:, None].astype(BF16), ((0, 0), (0, LANES - 1)))
        return jnp.concatenate([p.astype(BF16) for p in parts] + [column], axis=1)

    out_terms = with_gain([out_weight_grad], gain_two_grad)
    out_owned = lax.psum_scatter(out_terms, BOTH, scatter_dimension=0, tiled=True).astype(F32)
    query_terms = with_gain(
        [tn(normed, query_grad), tn(normed, key_grad), tn(normed, value_grad)], gain_one_grad
    )
    returned, query_terms = lax.optimization_barrier((returned, query_terms))
    owned = lax.psum_scatter(query_terms, BOTH, scatter_dimension=0, tiled=True).astype(F32)
    gate_high = gate_rows.astype(BF16)
    gate_low = (gate_rows - gate_high.astype(F32)).astype(BF16)

    def gate_hot(weights):
        return jnp.sum(
            jnp.where(hits, weights.astype(F32)[:, :, None], 0.0), axis=1
        ).astype(BF16)

    layer_out = middle + nn(gate_hot(gate_high), returned) + nn(gate_hot(gate_low), returned)

    return (
        layer_out[None],
        input_grad[None],
        owned[:, q_width + 2 * kv_width],
        out_owned[:, width],
        owned[:, :q_width],
        owned[:, q_width : q_width + kv_width],
        owned[:, q_width + kv_width : q_width + 2 * kv_width],
        out_owned[:, :width],
        *expert_grads,
    )


def solution(mesh):
    part = P("dp", "seq", None)
    both = P(BOTH)
    both_rows = P(BOTH, None)
    return jax.shard_map(
        on_device,
        mesh=mesh,
        in_specs=(part, P("dp"), part, part, part, both, both)
        + (both_rows,) * 4
        + (part,) * 4,
        out_specs=(part, part, both, both) + (both_rows,) * 4 + (part,) * 3,
        check_vma=False,
    )
```

```python
import functools
import math

import jax
import jax.numpy as jnp
from jax import lax
from jax.experimental import pallas as pl
from jax.experimental.pallas import tpu as pltpu
from jax.sharding import PartitionSpec as P

HEAD_DIM = 128
EXPERTS = 32
TOP = 4
CAP = 40

EPSILON = 1e-06
ROPE_BASE = 10000.0
NEG_FILL = -1e30
LANES = 128
BOTH = ("seq", "dp")
BF16 = jnp.bfloat16
F32 = jnp.float32


def rope_angles(positions, head_size):
    half_dim = head_size // 2
    frequency = ROPE_BASE ** (-(2.0 * jnp.arange(half_dim, dtype=F32)) / head_size)
    angles = positions.astype(F32)[:, None] * frequency[None, :]
    return (jnp.cos(angles)[:, None, :], jnp.sin(angles)[:, None, :])


def apply_rotary(values, cosine_lookup, sine_lookup):
    half_dim = values.shape[-1] // 2
    lower_half = values[..., :half_dim]
    upper_half = values[..., half_dim:]
    return jnp.concatenate(
        [
            lower_half * cosine_lookup - upper_half * sine_lookup,
            upper_half * cosine_lookup + lower_half * sine_lookup,
        ],
        axis=-1,
    )


def dot(left, right, contract):
    return lax.dot_general(left, right, (contract, ((), ())), preferred_element_type=F32)


def nn(left, right):
    return dot(left, right, ((1,), (0,)))


def nt(left, right):
    return dot(left, right, ((1,), (1,)))


def tn(left, right):
    return dot(left, right, ((0,), (0,)))


def claim_places(routes, priority, is_valid):
    pair_routes = routes.reshape(-1)
    live = jnp.repeat(is_valid, TOP)
    key = jnp.where(live, pair_routes, -1)
    earlier = (key[None, :] == pair_routes[:, None]) & (priority[None, :] < priority[:, None])
    place = jnp.sum(earlier.astype(F32), axis=1).astype(jnp.int32)
    return pair_routes, place, live & (place < CAP)


def masked_scores(query_group, key_head, query_pos, key_pos, length, score_scale):
    scores = (
        jnp.einsum("qgd,kd->gqk", query_group, key_head, preferred_element_type=F32) * score_scale
    )
    key_mask = (key_pos[None, :] <= query_pos[:, None]) & (key_pos[None, :] < length)
    return jnp.where(key_mask[None], scores, NEG_FILL)


def head_forward(query_group, key_head, value_head, query_pos, key_pos, length, score_scale):
    scores = masked_scores(query_group, key_head, query_pos, key_pos, length, score_scale)
    row_max = jnp.max(scores, axis=-1, keepdims=True)
    exp_scores = jnp.exp(scores - row_max)
    exp_total = jnp.sum(exp_scores, axis=-1, keepdims=True)
    attn_probs = (exp_scores / exp_total).astype(BF16)
    head_out = jnp.einsum("gqk,kd->qgd", attn_probs, value_head, preferred_element_type=F32)
    return (head_out, (row_max + jnp.log(exp_total))[..., 0])


def head_backward(
    query_group, key_head, value_head, head_grad, log_total, query_pos, key_pos, length, score_scale
):
    scores = masked_scores(query_group, key_head, query_pos, key_pos, length, score_scale)
    attn_probs = jnp.exp(scores - log_total[..., None])
    prob_grad = jnp.einsum("qgd,kd->gqk", head_grad, value_head, preferred_element_type=F32)
    row_delta = jnp.sum(attn_probs * prob_grad, axis=-1, keepdims=True)
    score_grad = (attn_probs * (prob_grad - row_delta)).astype(BF16)
    query_part = (
        jnp.einsum("gqk,kd->qgd", score_grad, key_head, preferred_element_type=F32) * score_scale
    )
    key_part = (
        jnp.einsum("gqk,qgd->kd", score_grad, query_group, preferred_element_type=F32) * score_scale
    )
    value_part = jnp.einsum(
        "gqk,qgd->kd", attn_probs.astype(BF16), head_grad, preferred_element_type=F32
    )
    return (query_part, key_part, value_part)


def norm_back(values, scale_rows, gain_vec, incoming):
    weighted = incoming * gain_vec
    inner_mean = jnp.mean(weighted * values, axis=-1, keepdims=True)
    values_grad = scale_rows * weighted - values * scale_rows * scale_rows * scale_rows * inner_mean
    return (values_grad, jnp.sum(incoming * values * scale_rows, axis=0))


def split_heads(gathered, kv_heads):
    return gathered.reshape(gathered.shape[0], kv_heads, HEAD_DIM).transpose(1, 0, 2)


def swap(blocks, axes):
    return lax.all_to_all(blocks, axes, split_axis=0, concat_axis=0, tiled=True)


MESH_IDS = pl.DeviceIdType.MESH


def exchange_kernel(count, n, block_of, *refs):
    sources, targets = refs[:n], refs[n : 2 * n]
    send_sems, recv_sems, local_sems = refs[2 * n :]
    me = lax.axis_index("seq")
    barrier = pltpu.get_barrier_semaphore()
    for step in range(1, count):
        peer = lax.rem(me + step, count)
        pl.semaphore_signal(barrier, inc=1, device_id={"seq": peer}, device_id_type=MESH_IDS)
    pl.semaphore_wait(barrier, count - 1)
    copies = []
    for i in range(n):
        for step in range(1, count):
            peer = lax.rem(me + step, count)
            copy = pltpu.make_async_remote_copy(
                src_ref=block_of(sources[i], peer),
                dst_ref=targets[i].at[me],
                send_sem=send_sems.at[i, step - 1],
                recv_sem=recv_sems.at[i, step - 1],
                device_id={"seq": peer},
                device_id_type=MESH_IDS,
            )
            copy.start()
            copies.append(copy)
        copy = pltpu.make_async_copy(
            block_of(sources[i], me), targets[i].at[me], local_sems.at[i]
        )
        copy.start()
        copies.append(copy)
    for copy in copies:
        copy.wait()


def seq_exchange(arrays, collective_id, block_of, block_shapes, name):
    count, n = lax.axis_size("seq"), len(arrays)
    sent = sum(math.prod(shape) for shape in block_shapes) * (count - 1) * 2
    return pl.pallas_call(
        functools.partial(exchange_kernel, count, n, block_of),
        out_shape=[jax.ShapeDtypeStruct((count,) + shape, BF16) for shape in block_shapes],
        in_specs=[pl.BlockSpec(memory_space=pl.ANY)] * n,
        out_specs=[pl.BlockSpec(memory_space=pl.ANY)] * n,
        scratch_shapes=[
            pltpu.SemaphoreType.DMA((n, count - 1)),
            pltpu.SemaphoreType.DMA((n, count - 1)),
            pltpu.SemaphoreType.DMA((n,)),
        ],
        compiler_params=pltpu.CompilerParams(
            collective_id=collective_id, vmem_limit_bytes=4 << 20
        ),
        cost_estimate=pl.CostEstimate(flops=0, bytes_accessed=20 * sent, transcendentals=0),
        name=name,
    )(*arrays)


def on_device(
    hidden_in,
    lengths,
    routes,
    gates,
    priority,
    attn_gain,
    mlp_gain,
    w_query,
    key_projection,
    value_projection,
    w_out,
    w_gate,
    w_up,
    w_down,
    cotangent,
):
    rows = hidden_in.shape[1]
    width = hidden_in.shape[2]
    dp_count = lax.axis_size("dp")
    seq_count = lax.axis_size("seq")
    devices = dp_count * seq_count
    own_experts = w_gate.shape[0]
    sharers = seq_count // own_experts
    hidden_units = w_gate.shape[2]
    my_seq = lax.axis_index("seq")
    extent = rows * seq_count
    query_pos = my_seq * rows + jnp.arange(rows, dtype=jnp.int32)
    key_pos = jnp.arange(extent, dtype=jnp.int32)
    length = lengths[0]
    is_valid = query_pos < length
    score_scale = 1.0 / math.sqrt(HEAD_DIM)
    q_width = w_query.shape[1]
    kv_width = key_projection.shape[1]
    q_heads = q_width // HEAD_DIM
    kv_heads = kv_width // HEAD_DIM
    group_size = q_heads // kv_heads
    cosine_lookup, sine_lookup = rope_angles(query_pos, HEAD_DIM)

    gain_block = jnp.concatenate(
        [attn_gain[:, None], mlp_gain[:, None], jnp.zeros((attn_gain.shape[0], LANES - 2), BF16)],
        axis=1,
    )
    packed = jnp.concatenate([w_query, key_projection, value_projection, gain_block], axis=1)
    packed_full = lax.all_gather(packed, BOTH, axis=0, tiled=True)
    out_full = lax.all_gather(w_out, BOTH, axis=0, tiled=True)
    gate_full, up_full = seq_exchange(
        [w_gate, w_up],
        2,
        lambda ref, peer: ref.at[peer // sharers],
        [w_gate.shape[1:], w_up.shape[1:]],
        "gather_gate_up",
    )

    pair_routes, place, kept = claim_places(routes[0], priority[0, 0], is_valid)
    holder = (pair_routes // own_experts) * seq_count + (pair_routes % own_experts) * sharers
    holder = holder + my_seq * sharers // seq_count
    slots = devices * CAP
    target = jnp.where(kept, holder * CAP + place, slots).reshape(rows, TOP)
    slot_ids = jnp.arange(slots, dtype=jnp.int32)
    hits = target[:, :, None] == slot_ids[None, None, :]
    gate_rows = gates[0]
    token_hot = jnp.any(hits, axis=1).astype(BF16)
    slot_gate = jnp.sum(jnp.where(hits, gate_rows[:, :, None], 0.0), axis=(0, 1))

    live_cotangent = jnp.where(is_valid[:, None], cotangent[0], jnp.zeros((), BF16))
    out_grad = live_cotangent.astype(F32)
    grad_send = (tn(token_hot, live_cotangent) * slot_gate[:, None]).astype(BF16)
    packed_full, gate_full, up_full, grad_send = lax.optimization_barrier(
        (packed_full, gate_full, up_full, grad_send)
    )
    gain_one = packed_full[:, q_width + 2 * kv_width].astype(F32)
    gain_two = packed_full[:, q_width + 2 * kv_width + 1].astype(F32)
    grad_rows = swap(grad_send.reshape(devices, CAP, width), ("dp", "seq")).reshape(slots, width)

    inputs = hidden_in[0].astype(F32)
    scale_one = lax.rsqrt(jnp.mean(inputs * inputs, axis=-1, keepdims=True) + EPSILON)
    normed = (inputs * scale_one * gain_one).astype(BF16)
    projected = nn(normed, packed_full)
    query_rows = projected[:, :q_width]
    key_matrix_rows = projected[:, q_width : q_width + kv_width]
    value_matrix_rows = projected[:, q_width + kv_width : q_width + 2 * kv_width].astype(BF16)
    query_rotated = apply_rotary(
        query_rows.reshape(rows, q_heads, HEAD_DIM), cosine_lookup, sine_lookup
    ).astype(BF16)
    key_rotated = apply_rotary(
        key_matrix_rows.reshape(rows, kv_heads, HEAD_DIM), cosine_lookup, sine_lookup
    ).astype(BF16)
    key_rotated = key_rotated.reshape(rows, kv_width)
    kv_mine = jnp.concatenate([key_rotated, value_matrix_rows], axis=1)
    (kv_all,) = seq_exchange(
        [kv_mine], 1, lambda ref, peer: ref, [(rows, 2 * kv_width)], "gather_keys"
    )
    kv_all = kv_all.reshape(extent, 2 * kv_width)
    key_all, value_all = kv_all[:, :kv_width], kv_all[:, kv_width:]
    query_head_groups = query_rotated.reshape(rows, kv_heads, group_size, HEAD_DIM).transpose(
        1, 0, 2, 3
    )
    key_heads, value_heads = split_heads(key_all, kv_heads), split_heads(value_all, kv_heads)
    attended, log_total = lax.map(
        lambda operands: head_forward(
            operands[0], operands[1], operands[2], query_pos, key_pos, length, score_scale
        ),
        (query_head_groups, key_heads, value_heads),
    )
    attended = attended.transpose(1, 0, 2, 3).reshape(rows, q_width).astype(BF16)
    middle = inputs + nn(attended, out_full)
    scale_two = lax.rsqrt(jnp.mean(middle * middle, axis=-1, keepdims=True) + EPSILON)
    moe_input = (middle * scale_two * gain_two).astype(BF16)

    send_rows = tn(token_hot, moe_input).astype(BF16).reshape(devices, CAP, width)
    send_rows, grad_rows, w_down = lax.optimization_barrier((send_rows, grad_rows, w_down))
    slot_rows = swap(send_rows, ("dp", "seq")).reshape(slots, width)
    (down_full,) = seq_exchange(
        [w_down], 5, lambda ref, peer: ref.at[peer // sharers], [w_down.shape[1:]], "gather_down"
    )
    slot_rows, down_full = lax.optimization_barrier((slot_rows, down_full))
    gate_full = gate_full.reshape(width, hidden_units)
    up_full = up_full.reshape(width, hidden_units)
    down_full = down_full.reshape(hidden_units, width)
    gate_pre = nn(slot_rows, gate_full)
    up_pre = nn(slot_rows, up_full)
    gate_sigmoid = jax.nn.sigmoid(gate_pre)
    gate_act = gate_pre * gate_sigmoid
    gate_slope = gate_sigmoid * (1.0 + gate_pre * (1.0 - gate_sigmoid))
    expert_hidden = (gate_act * up_pre).astype(BF16)
    hidden_grad = nt(grad_rows, down_full)
    gate_pre_grad = (hidden_grad * up_pre * gate_slope).astype(BF16)
    up_pre_grad = (hidden_grad * gate_act).astype(BF16)
    row_grad = (nt(gate_pre_grad, gate_full) + nt(up_pre_grad, up_full)).astype(BF16)
    row_back = swap(row_grad.reshape(devices, CAP, width), ("dp", "seq")).reshape(slots, width)

    gate_grad = tn(slot_rows, gate_pre_grad).astype(BF16)
    up_grad = tn(slot_rows, up_pre_grad).astype(BF16)
    down_grad = tn(expert_hidden, grad_rows).astype(BF16)

    def to_owners(grads, collective_id, name):
        return seq_exchange(
            [g.reshape(seq_count, -1, g.shape[1]) for g in grads],
            collective_id,
            lambda ref, peer: ref.at[peer],
            [(g.shape[0] // seq_count, g.shape[1]) for g in grads],
            name,
        )

    (gate_pieces,) = to_owners([gate_grad], 3, "return_gate_grad")
    row_back, gate_pieces, up_grad, down_grad = lax.optimization_barrier(
        (row_back, gate_pieces, up_grad, down_grad)
    )

    def owned_sum(piece):
        piece = piece.reshape((own_experts, sharers) + piece.shape[1:])
        return jnp.sum(piece.astype(F32), axis=1)

    expert_out = nn(expert_hidden, down_full).astype(BF16)
    expert_out, row_back = lax.optimization_barrier((expert_out, row_back))
    returned = swap(expert_out.reshape(devices, CAP, width), ("dp", "seq")).reshape(slots, width)
    moe_input_grad = nn(token_hot, row_back)
    middle_norm_grad, gain_two_grad = norm_back(middle, scale_two, gain_two, moe_input_grad)
    middle_grad = out_grad + middle_norm_grad
    branch_grad = middle_grad.astype(BF16)
    no_grad = jnp.zeros((rows, LANES), BF16)

    def with_gain(terms, gain_grad):
        column = jnp.zeros((width, LANES), BF16).at[:, 0].set(gain_grad.astype(BF16))
        return lax.dynamic_update_slice(terms, column, (0, terms.shape[1] - LANES))

    out_terms = with_gain(
        tn(attended, jnp.concatenate([branch_grad, no_grad], axis=1)).astype(BF16), gain_two_grad
    )
    attended_grad = nt(branch_grad, out_full).astype(BF16)
    attended_grad, out_terms = lax.optimization_barrier((attended_grad, out_terms))
    attended_grad = attended_grad.reshape(rows, kv_heads, group_size, HEAD_DIM).transpose(
        1, 0, 2, 3
    )
    query_part, key_part, value_part = lax.map(
        lambda operands: head_backward(
            operands[0],
            operands[1],
            operands[2],
            operands[3],
            operands[4],
            query_pos,
            key_pos,
            length,
            score_scale,
        ),
        (query_head_groups, key_heads, value_heads, attended_grad, log_total),
    )
    kv_terms = jnp.concatenate(
        [
            key_part.transpose(1, 0, 2).reshape(extent, kv_width),
            value_part.transpose(1, 0, 2).reshape(extent, kv_width),
        ],
        axis=1,
    ).astype(BF16)
    (kv_back,) = seq_exchange(
        [kv_terms.reshape(seq_count, rows, 2 * kv_width)],
        4,
        lambda ref, peer: ref.at[peer],
        [(rows, 2 * kv_width)],
        "return_key_grads",
    )
    kv_sum = jnp.sum(kv_back.astype(F32), axis=0)
    key_grad = apply_rotary(
        kv_sum[:, :kv_width].reshape(rows, kv_heads, HEAD_DIM), cosine_lookup, -sine_lookup
    )
    key_grad = key_grad.reshape(rows, kv_width).astype(BF16)
    value_grad = kv_sum[:, kv_width:].astype(BF16)
    query_grad = apply_rotary(
        query_part.transpose(1, 0, 2, 3).reshape(rows, q_heads, HEAD_DIM),
        cosine_lookup,
        -sine_lookup,
    )
    query_grad = query_grad.reshape(rows, q_width).astype(BF16)
    projected_grad = jnp.concatenate([query_grad, key_grad, value_grad, no_grad], axis=1)
    returned, projected_grad = lax.optimization_barrier((returned, projected_grad))
    normed_grad = nt(projected_grad, packed_full)
    input_norm_grad, gain_one_grad = norm_back(inputs, scale_one, gain_one, normed_grad)
    input_grad = middle_grad + input_norm_grad

    out_owned = lax.psum_scatter(out_terms, BOTH, scatter_dimension=0, tiled=True)
    query_terms = with_gain(tn(normed, projected_grad).astype(BF16), gain_one_grad)
    query_terms, up_grad, down_grad = lax.optimization_barrier((query_terms, up_grad, down_grad))
    owned = lax.psum_scatter(query_terms, BOTH, scatter_dimension=0, tiled=True).astype(F32)
    pieces = to_owners([up_grad, down_grad], 6, "return_up_down_grads")
    out_owned, *pieces = lax.optimization_barrier((out_owned, *pieces))
    out_owned = out_owned.astype(F32)
    expert_grads = [owned_sum(piece) for piece in (gate_pieces, *pieces)]
    gate_high = gate_rows.astype(BF16)
    gate_low = (gate_rows - gate_high.astype(F32)).astype(BF16)

    def gate_hot(weights):
        return jnp.sum(
            jnp.where(hits, weights.astype(F32)[:, :, None], 0.0), axis=1
        ).astype(BF16)

    layer_out = middle + nn(gate_hot(gate_high), returned) + nn(gate_hot(gate_low), returned)

    return (
        layer_out[None],
        input_grad[None],
        owned[:, q_width + 2 * kv_width],
        out_owned[:, width],
        owned[:, :q_width],
        owned[:, q_width : q_width + kv_width],
        owned[:, q_width + kv_width : q_width + 2 * kv_width],
        out_owned[:, :width],
        *expert_grads,
    )


def solution(mesh):
    part = P("dp", "seq", None)
    both = P(BOTH)
    both_rows = P(BOTH, None)
    return jax.shard_map(
        on_device,
        mesh=mesh,
        in_specs=(part, P("dp"), part, part, part, both, both)
        + (both_rows,) * 4
        + (part,) * 4,
        out_specs=(part, part, both, both) + (both_rows,) * 4 + (part,) * 3,
        check_vma=False,
    )
```

```python
import functools
import math

import jax
import jax.numpy as jnp
from jax import lax
from jax.experimental import pallas as pl
from jax.experimental.pallas import tpu as pltpu
from jax.sharding import PartitionSpec as P

HEAD_DIM = 128
EXPERTS = 32
TOP = 4
CAP = 40

EPSILON = 1e-06
ROPE_BASE = 10000.0
NEG_FILL = -1e30
LANES = 128
BOTH = ("seq", "dp")
BF16 = jnp.bfloat16
F32 = jnp.float32


def rope_angles(positions, head_size):
    half_dim = head_size // 2
    frequency = ROPE_BASE ** (-(2.0 * jnp.arange(half_dim, dtype=F32)) / head_size)
    angles = positions.astype(F32)[:, None] * frequency[None, :]
    return (jnp.cos(angles)[:, None, :], jnp.sin(angles)[:, None, :])


def apply_rotary(values, cosine_lookup, sine_lookup):
    half_dim = values.shape[-1] // 2
    lower_half = values[..., :half_dim]
    upper_half = values[..., half_dim:]
    return jnp.concatenate(
        [
            lower_half * cosine_lookup - upper_half * sine_lookup,
            upper_half * cosine_lookup + lower_half * sine_lookup,
        ],
        axis=-1,
    )


def dot(left, right, contract):
    return lax.dot_general(left, right, (contract, ((), ())), preferred_element_type=F32)


def nn(left, right):
    return dot(left, right, ((1,), (0,)))


def nt(left, right):
    return dot(left, right, ((1,), (1,)))


def tn(left, right):
    return dot(left, right, ((0,), (0,)))


def claim_places(routes, priority, is_valid):
    pair_routes = routes.reshape(-1)
    live = jnp.repeat(is_valid, TOP)
    key = jnp.where(live, pair_routes, -1)
    earlier = (key[None, :] == pair_routes[:, None]) & (priority[None, :] < priority[:, None])
    place = jnp.sum(earlier.astype(F32), axis=1).astype(jnp.int32)
    return pair_routes, place, live & (place < CAP)


def masked_scores(query_group, key_head, query_pos, key_pos, length, score_scale):
    scores = (
        jnp.einsum("qgd,kd->gqk", query_group, key_head, preferred_element_type=F32) * score_scale
    )
    key_mask = (key_pos[None, :] <= query_pos[:, None]) & (key_pos[None, :] < length)
    return jnp.where(key_mask[None], scores, NEG_FILL)


def head_forward(query_group, key_head, value_head, query_pos, key_pos, length, score_scale):
    scores = masked_scores(query_group, key_head, query_pos, key_pos, length, score_scale)
    row_max = jnp.max(scores, axis=-1, keepdims=True)
    exp_scores = jnp.exp(scores - row_max)
    exp_total = jnp.sum(exp_scores, axis=-1, keepdims=True)
    attn_probs = (exp_scores / exp_total).astype(BF16)
    head_out = jnp.einsum("gqk,kd->qgd", attn_probs, value_head, preferred_element_type=F32)
    return (head_out, (row_max + jnp.log(exp_total))[..., 0])


def head_backward(
    query_group, key_head, value_head, head_grad, log_total, query_pos, key_pos, length, score_scale
):
    scores = masked_scores(query_group, key_head, query_pos, key_pos, length, score_scale)
    attn_probs = jnp.exp(scores - log_total[..., None])
    prob_grad = jnp.einsum("qgd,kd->gqk", head_grad, value_head, preferred_element_type=F32)
    row_delta = jnp.sum(attn_probs * prob_grad, axis=-1, keepdims=True)
    score_grad = (attn_probs * (prob_grad - row_delta)).astype(BF16)
    query_part = (
        jnp.einsum("gqk,kd->qgd", score_grad, key_head, preferred_element_type=F32) * score_scale
    )
    key_part = (
        jnp.einsum("gqk,qgd->kd", score_grad, query_group, preferred_element_type=F32) * score_scale
    )
    value_part = jnp.einsum(
        "gqk,qgd->kd", attn_probs.astype(BF16), head_grad, preferred_element_type=F32
    )
    return (query_part, key_part, value_part)


def norm_back(values, scale_rows, gain_vec, incoming):
    weighted = incoming * gain_vec
    inner_mean = jnp.mean(weighted * values, axis=-1, keepdims=True)
    values_grad = scale_rows * weighted - values * scale_rows * scale_rows * scale_rows * inner_mean
    return (values_grad, jnp.sum(incoming * values * scale_rows, axis=0))


def split_heads(gathered, kv_heads):
    return gathered.reshape(gathered.shape[0], kv_heads, HEAD_DIM).transpose(1, 0, 2)


def swap(blocks, axes):
    return lax.all_to_all(blocks, axes, split_axis=0, concat_axis=0, tiled=True)


MESH_IDS = pl.DeviceIdType.MESH


def torus_place():
    seq, dp = lax.axis_index("seq"), lax.axis_index("dp")
    return seq // 2, seq % 2, dp // 2, dp % 2


def torus_id(a, b, z, c):
    return {"seq": 2 * a + b, "dp": 2 * z + c}


def torus_peers(line):
    a, b, z, c = torus_place()
    peers = [torus_id(a, b, z, 1 - c), torus_id(a, 1 - b, z, c), torus_id(1 - a, b, z, c)]
    peers.append(torus_id(1 - a, 1 - b, z, c))
    return peers + [torus_id(a, b, lax.rem(z + k, line), c) for k in range(1, line)]


def greet(peers):
    barrier = pltpu.get_barrier_semaphore()
    for peer in peers:
        pl.semaphore_signal(barrier, inc=1, device_id=peer, device_id_type=MESH_IDS)
    pl.semaphore_wait(barrier, len(peers))


def column_chunks(widths, limit):
    chunks = []
    for k, whole in enumerate(widths):
        start = 0
        while start < whole:
            size = limit if whole - start >= 2 * limit else whole - start
            chunks.append((k, start, size))
            start += size
    return chunks


def remote(src, dst, sems, i, j, device_id):
    send, recv = sems
    return pltpu.make_async_remote_copy(
        src_ref=src,
        dst_ref=dst,
        send_sem=send.at[i, j],
        recv_sem=recv.at[i, j],
        device_id=device_id,
        device_id_type=MESH_IDS,
    )


def start_exchange(count, sources, targets, block_of, sems):
    send_sems, recv_sems, local_sems = sems
    me = lax.axis_index("seq")
    copies = []
    for i, source in enumerate(sources):
        for step in range(1, count):
            peer = lax.rem(me + step, count)
            copies.append(
                pltpu.make_async_remote_copy(
                    src_ref=block_of(source, peer),
                    dst_ref=targets[i].at[me],
                    send_sem=send_sems.at[i, step - 1],
                    recv_sem=recv_sems.at[i, step - 1],
                    device_id={"seq": peer},
                    device_id_type=MESH_IDS,
                )
            )
        copies.append(
            pltpu.make_async_copy(block_of(source, me), targets[i].at[me], local_sems.at[i])
        )
    for copy in copies:
        copy.start()
    return copies


def exchange_sems(n, count):
    return [
        pltpu.SemaphoreType.DMA((n, count - 1)),
        pltpu.SemaphoreType.DMA((n, count - 1)),
        pltpu.SemaphoreType.DMA((n,)),
    ]


def gather_kernel(line, chunks, n, extras, block_of, *refs):
    sources, more_sources = refs[:n], refs[n : n + extras]
    refs = refs[n + extras :]
    targets, more_targets = refs[:n], refs[n : n + extras]
    send, recv, local, *more_sems = refs[n + extras :]
    sems = (send, recv)
    a, b, z, c = torus_place()
    greet(torus_peers(line))
    more = start_exchange(4, more_sources, more_targets, block_of, more_sems) if extras else []
    sent = []

    def start(copy):
        copy.start()
        sent.append(copy)
        return copy

    arriving = []
    for i, (k, first, size) in enumerate(chunks):
        cols = pl.ds(first, size)
        own = targets[k].at[a, b, z, c, :, cols]
        keep = pltpu.make_async_copy(sources[k].at[:, cols], own, local.at[i])
        keep.start()
        waits = []
        for step in range(1, line):
            peer = torus_id(a, b, lax.rem(z + step, line), c)
            waits.append(start(remote(sources[k].at[:, cols], own, sems, i, 2 + step, peer)))
        arriving.append((keep, waits))
    pending = []
    for i, (k, first, size) in enumerate(chunks):
        keep, waits = arriving[i]
        keep.wait()
        for copy in waits:
            copy.wait_recv()
        block = targets[k].at[a, b, :, c, :, pl.ds(first, size)]
        peer = torus_id(a, 1 - b, z, c) if i % 2 == 0 else torus_id(1 - a, b, z, c)
        pending.append(start(remote(block, block, sems, i, 1, peer)))
    second = []
    for i, (k, first, size) in enumerate(chunks):
        pending[i].wait_recv()
        cols = pl.ds(first, size)
        if i % 2 == 0:
            block, peer = targets[k].at[a, :, :, c, :, cols], torus_id(1 - a, b, z, c)
        else:
            block, peer = targets[k].at[:, b, :, c, :, cols], torus_id(a, 1 - b, z, c)
        second.append(start(remote(block, block, sems, i, 2, peer)))
    third = []
    for i, (k, first, size) in enumerate(chunks):
        second[i].wait_recv()
        block = targets[k].at[:, :, :, c, :, pl.ds(first, size)]
        third.append(start(remote(block, block, sems, i, 0, torus_id(a, b, z, 1 - c))))
    for copy in third:
        copy.wait_recv()
    for copy in sent:
        copy.wait_send()
    for copy in more:
        copy.wait()


def staged_gather(arrays, extras, block_of, collective_id, name):
    seq_count, line = lax.axis_size("seq"), lax.axis_size("dp") // 2
    rows, n = arrays[0].shape[0], len(arrays)
    chunks = column_chunks([x.shape[1] for x in arrays], 512)
    m = len(chunks)
    shape = (seq_count // 2, 2, line, 2, rows)
    size = sum(x.shape[1] for x in arrays) * rows * 64
    count = n + len(extras)
    outs = pl.pallas_call(
        functools.partial(gather_kernel, line, chunks, n, len(extras), block_of),
        out_shape=[jax.ShapeDtypeStruct(shape + (x.shape[1],), BF16) for x in arrays]
        + [jax.ShapeDtypeStruct((seq_count,) + x.shape[1:], BF16) for x in extras],
        in_specs=[pl.BlockSpec(memory_space=pl.ANY)] * count,
        out_specs=[pl.BlockSpec(memory_space=pl.ANY)] * count,
        scratch_shapes=[
            pltpu.SemaphoreType.DMA((m, 2 + line)),
            pltpu.SemaphoreType.DMA((m, 2 + line)),
            pltpu.SemaphoreType.DMA((m,)),
        ]
        + (exchange_sems(len(extras), seq_count) if extras else []),
        compiler_params=pltpu.CompilerParams(
            collective_id=collective_id, vmem_limit_bytes=4 << 20
        ),
        cost_estimate=pl.CostEstimate(flops=0, bytes_accessed=10 * size, transcendentals=0),
        name=name,
    )(*arrays, *extras)
    return [o.reshape(-1, o.shape[-1]) for o in outs]


def scatter_kernel(line, chunks, n, extras, block_of, *refs):
    m = len(chunks)
    sources, more_sources = refs[:n], refs[n : n + extras]
    refs = refs[n + extras :]
    targets, more_targets = refs[:n], refs[n : n + extras]
    scratch = refs[n + extras :]
    owns, ins1, accs2, ins2, accs3, ins3, ins4 = (scratch[m * s : m * (s + 1)] for s in range(7))
    send, recv, local, *more_sems = scratch[7 * m :]
    sems = (send, recv)
    a, b, z, c = torus_place()
    greet(torus_peers(line))
    sent = []

    def start(copy):
        copy.start()
        sent.append(copy)
        return copy

    def add_lines(target, left, right):
        def one(j, carry):
            target[j] = (left[j].astype(F32) + right[j].astype(F32)).astype(BF16)
            return carry

        lax.fori_loop(0, line, one, 0)

    first_stage = []
    for i, (k, first, size) in enumerate(chunks):
        cols = pl.ds(first, size)
        keep = pltpu.make_async_copy(sources[k].at[:, :, :, c, :, cols], owns[i], local.at[i])
        keep.start()
        swap_core = remote(
            sources[k].at[:, :, :, 1 - c, :, cols], ins1[i], sems, i, 0, torus_id(a, b, z, 1 - c)
        )
        first_stage.append((keep, start(swap_core)))
    more = start_exchange(4, more_sources, more_targets, block_of, more_sems) if extras else []
    second_stage = []
    for i in range(m):
        keep, copy = first_stage[i]
        keep.wait()
        copy.wait_recv()
        for p in range(2):
            for q in range(2):
                add_lines(owns[i].at[p, q], owns[i].at[p, q], ins1[i].at[p, q])
        if i % 2 == 0:
            block, peer = owns[i].at[:, 1 - b], torus_id(a, 1 - b, z, c)
        else:
            block, peer = owns[i].at[1 - a], torus_id(1 - a, b, z, c)
        second_stage.append(start(remote(block, ins2[i], sems, i, 1, peer)))
    third_stage = []
    for i in range(m):
        second_stage[i].wait_recv()
        for p in range(2):
            mine = owns[i].at[p, b] if i % 2 == 0 else owns[i].at[a, p]
            add_lines(accs2[i].at[p], mine, ins2[i].at[p])
        if i % 2 == 0:
            block, peer = accs2[i].at[1 - a], torus_id(1 - a, b, z, c)
        else:
            block, peer = accs2[i].at[1 - b], torus_id(a, 1 - b, z, c)
        third_stage.append(start(remote(block, ins3[i], sems, i, 2, peer)))
    last_stage = []
    for i in range(m):
        third_stage[i].wait_recv()
        add_lines(accs3[i], accs2[i].at[a if i % 2 == 0 else b], ins3[i])
        copies = []
        for step in range(1, line):
            to = lax.rem(z + step, line)
            copies.append(
                start(
                    remote(
                        accs3[i].at[to], ins4[i].at[z], sems, i, 2 + step, torus_id(a, b, to, c)
                    )
                )
            )
        last_stage.append(copies)
    for i, (k, first, size) in enumerate(chunks):
        total = accs3[i][z].astype(F32)
        for step in range(1, line):
            last_stage[i][step - 1].wait_recv()
            total = total + ins4[i][lax.rem(z + line - step, line)].astype(F32)
        targets[k][:, first : first + size] = total
    for copy in sent:
        copy.wait_send()
    for copy in more:
        copy.wait()


def staged_scatter(arrays, extras, block_of, collective_id, name):
    seq_count, line = lax.axis_size("seq"), lax.axis_size("dp") // 2
    rows, n = arrays[0].shape[0] // (2 * line * seq_count), len(arrays)
    chunks = column_chunks([x.shape[1] for x in arrays], 512)
    m = len(chunks)
    leads = [(2, 2, line), (2, 2, line), (2, line), (2, line), (line,), (line,), (line,)]
    size = sum(x.shape[1] for x in arrays) * rows * 64
    anywhere = pl.BlockSpec(memory_space=pl.ANY)
    return pl.pallas_call(
        functools.partial(scatter_kernel, line, chunks, n, len(extras), block_of),
        out_shape=[jax.ShapeDtypeStruct((rows, x.shape[1]), F32) for x in arrays]
        + [jax.ShapeDtypeStruct((seq_count,) + x.shape[1:], BF16) for x in extras],
        in_specs=[anywhere] * (n + len(extras)),
        out_specs=[pl.BlockSpec(memory_space=pltpu.VMEM)] * n + [anywhere] * len(extras),
        scratch_shapes=[
            pltpu.VMEM(lead + (rows, width), BF16) for lead in leads for _, _, width in chunks
        ]
        + [
            pltpu.SemaphoreType.DMA((m, 2 + line)),
            pltpu.SemaphoreType.DMA((m, 2 + line)),
            pltpu.SemaphoreType.DMA((m,)),
        ]
        + (exchange_sems(len(extras), seq_count) if extras else []),
        compiler_params=pltpu.CompilerParams(
            collective_id=collective_id, vmem_limit_bytes=36 << 20
        ),
        cost_estimate=pl.CostEstimate(flops=0, bytes_accessed=size, transcendentals=0),
        name=name,
    )(*[x.reshape(2, 2, line, 2, rows, x.shape[1]) for x in arrays], *extras)


def exchange_kernel(count, n, block_of, *refs):
    me = lax.axis_index("seq")
    greet([{"seq": lax.rem(me + step, count)} for step in range(1, count)])
    for copy in start_exchange(count, refs[:n], refs[n : 2 * n], block_of, refs[2 * n :]):
        copy.wait()


def seq_exchange(arrays, collective_id, block_of, block_shapes, name):
    count, n = lax.axis_size("seq"), len(arrays)
    sent = sum(math.prod(shape) for shape in block_shapes) * (count - 1) * 2
    return pl.pallas_call(
        functools.partial(exchange_kernel, count, n, block_of),
        out_shape=[jax.ShapeDtypeStruct((count,) + shape, BF16) for shape in block_shapes],
        in_specs=[pl.BlockSpec(memory_space=pl.ANY)] * n,
        out_specs=[pl.BlockSpec(memory_space=pl.ANY)] * n,
        scratch_shapes=exchange_sems(n, count),
        compiler_params=pltpu.CompilerParams(
            collective_id=collective_id, vmem_limit_bytes=4 << 20
        ),
        cost_estimate=pl.CostEstimate(flops=0, bytes_accessed=20 * sent, transcendentals=0),
        name=name,
    )(*arrays)


def on_device(
    hidden_in,
    lengths,
    routes,
    gates,
    priority,
    attn_gain,
    mlp_gain,
    w_query,
    key_projection,
    value_projection,
    w_out,
    w_gate,
    w_up,
    w_down,
    cotangent,
):
    rows = hidden_in.shape[1]
    width = hidden_in.shape[2]
    dp_count = lax.axis_size("dp")
    seq_count = lax.axis_size("seq")
    devices = dp_count * seq_count
    own_experts = w_gate.shape[0]
    sharers = seq_count // own_experts
    hidden_units = w_gate.shape[2]
    my_seq = lax.axis_index("seq")
    extent = rows * seq_count
    query_pos = my_seq * rows + jnp.arange(rows, dtype=jnp.int32)
    key_pos = jnp.arange(extent, dtype=jnp.int32)
    length = lengths[0]
    is_valid = query_pos < length
    score_scale = 1.0 / math.sqrt(HEAD_DIM)
    q_width = w_query.shape[1]
    kv_width = key_projection.shape[1]
    q_heads = q_width // HEAD_DIM
    kv_heads = kv_width // HEAD_DIM
    group_size = q_heads // kv_heads
    cosine_lookup, sine_lookup = rope_angles(query_pos, HEAD_DIM)

    gain_block = jnp.concatenate(
        [attn_gain[:, None], mlp_gain[:, None], jnp.zeros((attn_gain.shape[0], LANES - 2), BF16)],
        axis=1,
    )
    packed = jnp.concatenate([w_query, key_projection, value_projection, gain_block], axis=1)
    staged = seq_count == 4 and w_query.shape[0] % 16 == 0
    owner_block = lambda ref, peer: ref.at[peer // sharers]
    piece_block = lambda ref, peer: ref.at[peer]

    if staged:
        packed_full, out_full, gate_full = staged_gather(
            [packed, w_out], [w_gate], owner_block, 2, "gather_attention_weights"
        )
    else:
        packed_full = lax.all_gather(packed, BOTH, axis=0, tiled=True)
        out_full = lax.all_gather(w_out, BOTH, axis=0, tiled=True)
        (gate_full,) = seq_exchange([w_gate], 2, owner_block, [w_gate.shape[1:]], "gather_gate")

    pair_routes, place, kept = claim_places(routes[0], priority[0, 0], is_valid)
    holder = (pair_routes // own_experts) * seq_count + (pair_routes % own_experts) * sharers
    holder = holder + my_seq * sharers // seq_count
    slots = devices * CAP
    target = jnp.where(kept, holder * CAP + place, slots).reshape(rows, TOP)
    slot_ids = jnp.arange(slots, dtype=jnp.int32)
    hits = target[:, :, None] == slot_ids[None, None, :]
    gate_rows = gates[0]
    token_hot = jnp.any(hits, axis=1).astype(BF16)
    slot_gate = jnp.sum(jnp.where(hits, gate_rows[:, :, None], 0.0), axis=(0, 1))

    live_cotangent = jnp.where(is_valid[:, None], cotangent[0], jnp.zeros((), BF16))
    out_grad = live_cotangent.astype(F32)
    grad_send = (tn(token_hot, live_cotangent) * slot_gate[:, None]).astype(BF16)
    packed_full, out_full, gate_full, grad_send = lax.optimization_barrier(
        (packed_full, out_full, gate_full, grad_send)
    )
    gain_one = packed_full[:, q_width + 2 * kv_width].astype(F32)
    gain_two = packed_full[:, q_width + 2 * kv_width + 1].astype(F32)
    grad_rows = swap(grad_send.reshape(devices, CAP, width), ("dp", "seq")).reshape(slots, width)

    inputs = hidden_in[0].astype(F32)
    scale_one = lax.rsqrt(jnp.mean(inputs * inputs, axis=-1, keepdims=True) + EPSILON)
    normed = (inputs * scale_one * gain_one).astype(BF16)
    projected = nn(normed, packed_full)
    query_rows = projected[:, :q_width]
    key_matrix_rows = projected[:, q_width : q_width + kv_width]
    value_matrix_rows = projected[:, q_width + kv_width : q_width + 2 * kv_width].astype(BF16)
    query_rotated = apply_rotary(
        query_rows.reshape(rows, q_heads, HEAD_DIM), cosine_lookup, sine_lookup
    ).astype(BF16)
    key_rotated = apply_rotary(
        key_matrix_rows.reshape(rows, kv_heads, HEAD_DIM), cosine_lookup, sine_lookup
    ).astype(BF16)
    key_rotated = key_rotated.reshape(rows, kv_width)
    kv_mine = jnp.concatenate([key_rotated, value_matrix_rows], axis=1)
    (kv_all,) = seq_exchange(
        [kv_mine], 1, lambda ref, peer: ref, [(rows, 2 * kv_width)], "gather_keys"
    )
    kv_all = kv_all.reshape(extent, 2 * kv_width)
    key_all, value_all = kv_all[:, :kv_width], kv_all[:, kv_width:]
    query_head_groups = query_rotated.reshape(rows, kv_heads, group_size, HEAD_DIM).transpose(
        1, 0, 2, 3
    )
    key_heads, value_heads = split_heads(key_all, kv_heads), split_heads(value_all, kv_heads)
    attended, log_total = lax.map(
        lambda operands: head_forward(
            operands[0], operands[1], operands[2], query_pos, key_pos, length, score_scale
        ),
        (query_head_groups, key_heads, value_heads),
    )
    attended = attended.transpose(1, 0, 2, 3).reshape(rows, q_width).astype(BF16)
    middle = inputs + nn(attended, out_full)
    scale_two = lax.rsqrt(jnp.mean(middle * middle, axis=-1, keepdims=True) + EPSILON)
    moe_input = (middle * scale_two * gain_two).astype(BF16)

    send_rows = tn(token_hot, moe_input).astype(BF16).reshape(devices, CAP, width)
    send_rows, grad_rows, w_up, w_down = lax.optimization_barrier(
        (send_rows, grad_rows, w_up, w_down)
    )
    slot_rows = swap(send_rows, ("dp", "seq")).reshape(slots, width)
    up_full, down_full = seq_exchange(
        [w_up, w_down], 5, owner_block, [w_up.shape[1:], w_down.shape[1:]], "gather_up_down"
    )
    slot_rows, up_full, down_full = lax.optimization_barrier((slot_rows, up_full, down_full))
    gate_full = gate_full.reshape(width, hidden_units)
    up_full = up_full.reshape(width, hidden_units)
    down_full = down_full.reshape(hidden_units, width)
    gate_pre = nn(slot_rows, gate_full)
    up_pre = nn(slot_rows, up_full)
    gate_sigmoid = jax.nn.sigmoid(gate_pre)
    gate_act = gate_pre * gate_sigmoid
    gate_slope = gate_sigmoid * (1.0 + gate_pre * (1.0 - gate_sigmoid))
    expert_hidden = (gate_act * up_pre).astype(BF16)
    hidden_grad = nt(grad_rows, down_full)
    gate_pre_grad = (hidden_grad * up_pre * gate_slope).astype(BF16)
    up_pre_grad = (hidden_grad * gate_act).astype(BF16)
    row_grad = (nt(gate_pre_grad, gate_full) + nt(up_pre_grad, up_full)).astype(BF16)
    row_back = swap(row_grad.reshape(devices, CAP, width), ("dp", "seq")).reshape(slots, width)

    gate_grad = tn(slot_rows, gate_pre_grad).astype(BF16)
    up_grad = tn(slot_rows, up_pre_grad).astype(BF16)
    down_grad = tn(expert_hidden, grad_rows).astype(BF16)

    def pieces_of(grad):
        return grad.reshape(seq_count, -1, grad.shape[1])

    gate_pieces, up_pieces = seq_exchange(
        [pieces_of(gate_grad), pieces_of(up_grad)],
        3,
        piece_block,
        [w_gate.shape[1:], w_up.shape[1:]],
        "return_gate_up_grads",
    )
    row_back, gate_pieces, up_pieces, down_grad = lax.optimization_barrier(
        (row_back, gate_pieces, up_pieces, down_grad)
    )

    def owned_sum(piece):
        piece = piece.reshape((own_experts, sharers) + piece.shape[1:])
        return jnp.sum(piece.astype(F32), axis=1)

    expert_out = nn(expert_hidden, down_full).astype(BF16)
    expert_out, row_back = lax.optimization_barrier((expert_out, row_back))
    returned = swap(expert_out.reshape(devices, CAP, width), ("dp", "seq")).reshape(slots, width)
    moe_input_grad = nn(token_hot, row_back)
    middle_norm_grad, gain_two_grad = norm_back(middle, scale_two, gain_two, moe_input_grad)
    middle_grad = out_grad + middle_norm_grad
    branch_grad = middle_grad.astype(BF16)
    no_grad = jnp.zeros((rows, LANES), BF16)

    out_terms = tn(attended, branch_grad).astype(BF16)
    attended_grad = nt(branch_grad, out_full).astype(BF16)
    attended_grad, out_terms = lax.optimization_barrier((attended_grad, out_terms))
    attended_grad = attended_grad.reshape(rows, kv_heads, group_size, HEAD_DIM).transpose(
        1, 0, 2, 3
    )
    query_part, key_part, value_part = lax.map(
        lambda operands: head_backward(
            operands[0],
            operands[1],
            operands[2],
            operands[3],
            operands[4],
            query_pos,
            key_pos,
            length,
            score_scale,
        ),
        (query_head_groups, key_heads, value_heads, attended_grad, log_total),
    )
    kv_terms = jnp.concatenate(
        [
            key_part.transpose(1, 0, 2).reshape(extent, kv_width),
            value_part.transpose(1, 0, 2).reshape(extent, kv_width),
        ],
        axis=1,
    ).astype(BF16)
    (kv_back,) = seq_exchange(
        [kv_terms.reshape(seq_count, rows, 2 * kv_width)],
        4,
        lambda ref, peer: ref.at[peer],
        [(rows, 2 * kv_width)],
        "return_key_grads",
    )
    kv_sum = jnp.sum(kv_back.astype(F32), axis=0)
    key_grad = apply_rotary(
        kv_sum[:, :kv_width].reshape(rows, kv_heads, HEAD_DIM), cosine_lookup, -sine_lookup
    )
    key_grad = key_grad.reshape(rows, kv_width).astype(BF16)
    value_grad = kv_sum[:, kv_width:].astype(BF16)
    query_grad = apply_rotary(
        query_part.transpose(1, 0, 2, 3).reshape(rows, q_heads, HEAD_DIM),
        cosine_lookup,
        -sine_lookup,
    )
    query_grad = query_grad.reshape(rows, q_width).astype(BF16)
    projected_grad = jnp.concatenate([query_grad, key_grad, value_grad, no_grad], axis=1)
    normed_grad = nt(projected_grad, packed_full)
    input_norm_grad, gain_one_grad = norm_back(inputs, scale_one, gain_one, normed_grad)
    input_grad = middle_grad + input_norm_grad

    gain_columns = jnp.zeros((width, LANES), BF16)
    gain_columns = gain_columns.at[:, 0].set(gain_one_grad.astype(BF16))
    gain_columns = gain_columns.at[:, 1].set(gain_two_grad.astype(BF16))
    query_terms = lax.dynamic_update_slice(
        tn(normed, projected_grad).astype(BF16), gain_columns, (0, projected_grad.shape[1] - LANES)
    )
    down_pieces = pieces_of(down_grad)
    if staged:
        out_owned, owned, down_pieces = staged_scatter(
            [out_terms, query_terms], [down_pieces], piece_block, 6, "scatter_attention_grads"
        )
    else:
        terms = jnp.concatenate([out_terms, query_terms], axis=1)
        terms = lax.psum_scatter(terms, BOTH, scatter_dimension=0, tiled=True).astype(F32)
        out_owned, owned = terms[:, :width], terms[:, width:]
        (down_pieces,) = seq_exchange(
            [down_pieces], 6, piece_block, [w_down.shape[1:]], "return_down_grads"
        )
    returned, owned = lax.optimization_barrier((returned, owned))
    expert_grads = [owned_sum(piece) for piece in (gate_pieces, up_pieces, down_pieces)]

    gate_high = gate_rows.astype(BF16)
    gate_low = (gate_rows - gate_high.astype(F32)).astype(BF16)

    def gate_hot(weights):
        return jnp.sum(
            jnp.where(hits, weights.astype(F32)[:, :, None], 0.0), axis=1
        ).astype(BF16)

    layer_out = middle + nn(gate_hot(gate_high), returned) + nn(gate_hot(gate_low), returned)

    return (
        layer_out[None],
        input_grad[None],
        owned[:, q_width + 2 * kv_width],
        owned[:, q_width + 2 * kv_width + 1],
        owned[:, :q_width],
        owned[:, q_width : q_width + kv_width],
        owned[:, q_width + kv_width : q_width + 2 * kv_width],
        out_owned,
        *expert_grads,
    )


def solution(mesh):
    part = P("dp", "seq", None)
    both = P(BOTH)
    both_rows = P(BOTH, None)
    return jax.shard_map(
        on_device,
        mesh=mesh,
        in_specs=(part, P("dp"), part, part, part, both, both)
        + (both_rows,) * 4
        + (part,) * 4,
        out_specs=(part, part, both, both) + (both_rows,) * 4 + (part,) * 3,
        check_vma=False,
    )
```

```python
import functools
import math

import jax
import jax.numpy as jnp
from jax import lax
from jax.experimental import pallas as pl
from jax.experimental.pallas import tpu as pltpu
from jax.sharding import PartitionSpec as P

HEAD_DIM = 128
EXPERTS = 32
TOP = 4
CAP = 40

EPSILON = 1e-06
ROPE_BASE = 10000.0
NEG_FILL = -1e30
LANES = 128
BOTH = ("seq", "dp")
BF16 = jnp.bfloat16
F32 = jnp.float32


def rope_angles(positions, head_size):
    half_dim = head_size // 2
    frequency = ROPE_BASE ** (-(2.0 * jnp.arange(half_dim, dtype=F32)) / head_size)
    angles = positions.astype(F32)[:, None] * frequency[None, :]
    return (jnp.cos(angles)[:, None, :], jnp.sin(angles)[:, None, :])


def apply_rotary(values, cosine_lookup, sine_lookup):
    half_dim = values.shape[-1] // 2
    lower_half = values[..., :half_dim]
    upper_half = values[..., half_dim:]
    return jnp.concatenate(
        [
            lower_half * cosine_lookup - upper_half * sine_lookup,
            upper_half * cosine_lookup + lower_half * sine_lookup,
        ],
        axis=-1,
    )


def dot(left, right, contract):
    return lax.dot_general(left, right, (contract, ((), ())), preferred_element_type=F32)


def nn(left, right):
    return dot(left, right, ((1,), (0,)))


def nt(left, right):
    return dot(left, right, ((1,), (1,)))


def tn(left, right):
    return dot(left, right, ((0,), (0,)))


def claim_places(routes, priority, is_valid):
    pair_routes = routes.reshape(-1)
    live = jnp.repeat(is_valid, TOP)
    key = jnp.where(live, pair_routes, -1)
    earlier = (key[None, :] == pair_routes[:, None]) & (priority[None, :] < priority[:, None])
    place = jnp.sum(earlier.astype(F32), axis=1).astype(jnp.int32)
    return pair_routes, place, live & (place < CAP)


def masked_scores(query_group, key_head, query_pos, key_pos, length, score_scale):
    scores = (
        jnp.einsum("qgd,kd->gqk", query_group, key_head, preferred_element_type=F32) * score_scale
    )
    key_mask = (key_pos[None, :] <= query_pos[:, None]) & (key_pos[None, :] < length)
    return jnp.where(key_mask[None], scores, NEG_FILL)


def head_forward(query_group, key_head, value_head, query_pos, key_pos, length, score_scale):
    scores = masked_scores(query_group, key_head, query_pos, key_pos, length, score_scale)
    row_max = jnp.max(scores, axis=-1, keepdims=True)
    exp_scores = jnp.exp(scores - row_max)
    exp_total = jnp.sum(exp_scores, axis=-1, keepdims=True)
    attn_probs = (exp_scores / exp_total).astype(BF16)
    head_out = jnp.einsum("gqk,kd->qgd", attn_probs, value_head, preferred_element_type=F32)
    return (head_out, (row_max + jnp.log(exp_total))[..., 0])


def head_backward(
    query_group, key_head, value_head, head_grad, log_total, query_pos, key_pos, length, score_scale
):
    scores = masked_scores(query_group, key_head, query_pos, key_pos, length, score_scale)
    attn_probs = jnp.exp(scores - log_total[..., None])
    prob_grad = jnp.einsum("qgd,kd->gqk", head_grad, value_head, preferred_element_type=F32)
    row_delta = jnp.sum(attn_probs * prob_grad, axis=-1, keepdims=True)
    score_grad = (attn_probs * (prob_grad - row_delta)).astype(BF16)
    query_part = (
        jnp.einsum("gqk,kd->qgd", score_grad, key_head, preferred_element_type=F32) * score_scale
    )
    key_part = (
        jnp.einsum("gqk,qgd->kd", score_grad, query_group, preferred_element_type=F32) * score_scale
    )
    value_part = jnp.einsum(
        "gqk,qgd->kd", attn_probs.astype(BF16), head_grad, preferred_element_type=F32
    )
    return (query_part, key_part, value_part)


def norm_back(values, scale_rows, gain_vec, incoming):
    weighted = incoming * gain_vec
    inner_mean = jnp.mean(weighted * values, axis=-1, keepdims=True)
    values_grad = scale_rows * weighted - values * scale_rows * scale_rows * scale_rows * inner_mean
    return (values_grad, jnp.sum(incoming * values * scale_rows, axis=0))


def split_heads(gathered, kv_heads):
    return gathered.reshape(gathered.shape[0], kv_heads, HEAD_DIM).transpose(1, 0, 2)


def swap(blocks, axes):
    return lax.all_to_all(blocks, axes, split_axis=0, concat_axis=0, tiled=True)


MESH_IDS = pl.DeviceIdType.MESH


def torus_place():
    seq, dp = lax.axis_index("seq"), lax.axis_index("dp")
    return seq // 2, seq % 2, dp // 2, dp % 2


def torus_id(a, b, z, c):
    return {"seq": 2 * a + b, "dp": 2 * z + c}


def torus_peers(line):
    a, b, z, c = torus_place()
    peers = [torus_id(a, b, z, 1 - c), torus_id(a, 1 - b, z, c), torus_id(1 - a, b, z, c)]
    peers.append(torus_id(1 - a, 1 - b, z, c))
    return peers + [torus_id(a, b, lax.rem(z + k, line), c) for k in range(1, line)]


def greet(peers):
    barrier = pltpu.get_barrier_semaphore()
    for peer in peers:
        pl.semaphore_signal(barrier, inc=1, device_id=peer, device_id_type=MESH_IDS)
    pl.semaphore_wait(barrier, len(peers))


def column_chunks(widths, parts):
    chunks = []
    for part in range(parts):
        for k, whole in enumerate(widths):
            tiles = whole // LANES
            first, end = tiles * part // parts, tiles * (part + 1) // parts
            chunks.append((k, first * LANES, (end - first) * LANES))
    return chunks


def remote(src, dst, sems, i, j, device_id):
    send, recv = sems
    return pltpu.make_async_remote_copy(
        src_ref=src,
        dst_ref=dst,
        send_sem=send.at[i, j],
        recv_sem=recv.at[i, j],
        device_id=device_id,
        device_id_type=MESH_IDS,
    )


def start_exchange(count, sources, targets, block_of, sems):
    send_sems, recv_sems, local_sems = sems
    me = lax.axis_index("seq")
    copies = []
    for i, source in enumerate(sources):
        for step in range(1, count):
            peer = lax.rem(me + step, count)
            copies.append(
                pltpu.make_async_remote_copy(
                    src_ref=block_of(source, peer),
                    dst_ref=targets[i].at[me],
                    send_sem=send_sems.at[i, step - 1],
                    recv_sem=recv_sems.at[i, step - 1],
                    device_id={"seq": peer},
                    device_id_type=MESH_IDS,
                )
            )
        copies.append(
            pltpu.make_async_copy(block_of(source, me), targets[i].at[me], local_sems.at[i])
        )
    for copy in copies:
        copy.start()
    return copies


def exchange_sems(n, count):
    return [
        pltpu.SemaphoreType.DMA((n, count - 1)),
        pltpu.SemaphoreType.DMA((n, count - 1)),
        pltpu.SemaphoreType.DMA((n,)),
    ]


def in_steps(count, stages):
    for step in range((count + 1) // 2 + len(stages) - 1):
        for behind, stage in enumerate(stages):
            for i in (2 * (step - behind), 2 * (step - behind) + 1):
                if 0 <= i < count:
                    stage(i)


def gather_kernel(line, chunks, n, extras, block_of, *refs):
    sources, more_sources = refs[:n], refs[n : n + extras]
    refs = refs[n + extras :]
    targets, more_targets = refs[:n], refs[n : n + extras]
    send, recv, local, *more_sems = refs[n + extras :]
    sems = (send, recv)
    a, b, z, c = torus_place()
    greet(torus_peers(line))
    more = start_exchange(4, more_sources, more_targets, block_of, more_sems) if extras else []
    sent = []

    def start(copy):
        copy.start()
        sent.append(copy)
        return copy

    along_line, first_hop, second_hop, third_hop = {}, {}, {}, {}

    def send_line(i):
        k, first, size = chunks[i]
        cols = pl.ds(first, size)
        own = targets[k].at[a, b, z, c, :, cols]
        keep = pltpu.make_async_copy(sources[k].at[:, cols], own, local.at[i])
        keep.start()
        along_line[i] = [
            start(
                remote(
                    sources[k].at[:, cols],
                    own,
                    sems,
                    i,
                    2 + step,
                    torus_id(a, b, lax.rem(z + step, line), c),
                )
            )
            for step in range(1, line)
        ]
        along_line[i].append(keep)

    def send_first(i):
        k, first, size = chunks[i]
        *copies, keep = along_line[i]
        keep.wait()
        for copy in copies:
            copy.wait_recv()
        block = targets[k].at[a, b, :, c, :, pl.ds(first, size)]
        peer = torus_id(a, 1 - b, z, c) if i % 2 == 0 else torus_id(1 - a, b, z, c)
        first_hop[i] = start(remote(block, block, sems, i, 1, peer))

    def send_second(i):
        k, first, size = chunks[i]
        first_hop[i].wait_recv()
        cols = pl.ds(first, size)
        if i % 2 == 0:
            block, peer = targets[k].at[a, :, :, c, :, cols], torus_id(1 - a, b, z, c)
        else:
            block, peer = targets[k].at[:, b, :, c, :, cols], torus_id(a, 1 - b, z, c)
        second_hop[i] = start(remote(block, block, sems, i, 2, peer))

    def send_third(i):
        k, first, size = chunks[i]
        second_hop[i].wait_recv()
        block = targets[k].at[:, :, :, c, :, pl.ds(first, size)]
        third_hop[i] = start(remote(block, block, sems, i, 0, torus_id(a, b, z, 1 - c)))

    in_steps(len(chunks), [send_line, send_first, send_second, send_third])
    for copy in third_hop.values():
        copy.wait_recv()
    for copy in sent:
        copy.wait_send()
    for copy in more:
        copy.wait()


def staged_gather(arrays, extras, block_of, collective_id, name, parts=6):
    seq_count, line = lax.axis_size("seq"), lax.axis_size("dp") // 2
    rows, n = arrays[0].shape[0], len(arrays)
    chunks = column_chunks([x.shape[1] for x in arrays], parts)
    m = len(chunks)
    shape = (seq_count // 2, 2, line, 2, rows)
    size = sum(x.shape[1] for x in arrays) * rows * 64
    count = n + len(extras)
    outs = pl.pallas_call(
        functools.partial(gather_kernel, line, chunks, n, len(extras), block_of),
        out_shape=[jax.ShapeDtypeStruct(shape + (x.shape[1],), BF16) for x in arrays]
        + [jax.ShapeDtypeStruct((seq_count,) + x.shape[1:], BF16) for x in extras],
        in_specs=[pl.BlockSpec(memory_space=pl.ANY)] * count,
        out_specs=[pl.BlockSpec(memory_space=pl.ANY)] * count,
        scratch_shapes=[
            pltpu.SemaphoreType.DMA((m, 2 + line)),
            pltpu.SemaphoreType.DMA((m, 2 + line)),
            pltpu.SemaphoreType.DMA((m,)),
        ]
        + (exchange_sems(len(extras), seq_count) if extras else []),
        compiler_params=pltpu.CompilerParams(
            collective_id=collective_id, vmem_limit_bytes=4 << 20
        ),
        cost_estimate=pl.CostEstimate(flops=0, bytes_accessed=10 * size, transcendentals=0),
        name=name,
    )(*arrays, *extras)
    return [o.reshape(-1, o.shape[-1]) for o in outs]


def scatter_kernel(line, chunks, n, extras, block_of, *refs):
    m = len(chunks)
    sources, more_sources = refs[:n], refs[n : n + extras]
    refs = refs[n + extras :]
    targets, more_targets = refs[:n], refs[n : n + extras]
    scratch = refs[n + extras :]
    owns, ins1, accs2, ins2, accs3, ins3, ins4 = (scratch[m * s : m * (s + 1)] for s in range(7))
    send, recv, local, *more_sems = scratch[7 * m :]
    sems = (send, recv)
    a, b, z, c = torus_place()
    greet(torus_peers(line))
    sent = []

    def start(copy):
        copy.start()
        sent.append(copy)
        return copy

    def add_lines(target, left, right):
        def one(j, carry):
            target[j] = (left[j].astype(F32) + right[j].astype(F32)).astype(BF16)
            return carry

        lax.fori_loop(0, line, one, 0)

    between_cores, first_hop, second_hop, along_line = {}, {}, {}, {}

    def send_core(i):
        k, first, size = chunks[i]
        cols = pl.ds(first, size)
        keep = pltpu.make_async_copy(sources[k].at[:, :, :, c, :, cols], owns[i], local.at[i])
        keep.start()
        swap_core = remote(
            sources[k].at[:, :, :, 1 - c, :, cols], ins1[i], sems, i, 0, torus_id(a, b, z, 1 - c)
        )
        between_cores[i] = (keep, start(swap_core))

    def send_first(i):
        keep, copy = between_cores[i]
        keep.wait()
        copy.wait_recv()
        for p in range(2):
            for q in range(2):
                add_lines(owns[i].at[p, q], owns[i].at[p, q], ins1[i].at[p, q])
        if i % 2 == 0:
            block, peer = owns[i].at[:, 1 - b], torus_id(a, 1 - b, z, c)
        else:
            block, peer = owns[i].at[1 - a], torus_id(1 - a, b, z, c)
        first_hop[i] = start(remote(block, ins2[i], sems, i, 1, peer))

    def send_second(i):
        first_hop[i].wait_recv()
        for p in range(2):
            mine = owns[i].at[p, b] if i % 2 == 0 else owns[i].at[a, p]
            add_lines(accs2[i].at[p], mine, ins2[i].at[p])
        if i % 2 == 0:
            block, peer = accs2[i].at[1 - a], torus_id(1 - a, b, z, c)
        else:
            block, peer = accs2[i].at[1 - b], torus_id(a, 1 - b, z, c)
        second_hop[i] = start(remote(block, ins3[i], sems, i, 2, peer))

    def send_line(i):
        second_hop[i].wait_recv()
        add_lines(accs3[i], accs2[i].at[a if i % 2 == 0 else b], ins3[i])
        copies = []
        for step in range(1, line):
            to = lax.rem(z + step, line)
            peer = torus_id(a, b, to, c)
            copies.append(start(remote(accs3[i].at[to], ins4[i].at[z], sems, i, 2 + step, peer)))
        along_line[i] = copies

    def finish(i):
        k, first, size = chunks[i]
        total = accs3[i][z].astype(F32)
        for step in range(1, line):
            along_line[i][step - 1].wait_recv()
            total = total + ins4[i][lax.rem(z + line - step, line)].astype(F32)
        targets[k][:, first : first + size] = total

    more = start_exchange(4, more_sources, more_targets, block_of, more_sems) if extras else []
    in_steps(m, [send_core, send_first, send_second, send_line, finish])
    for copy in sent:
        copy.wait_send()
    for copy in more:
        copy.wait()


def staged_scatter(arrays, extras, block_of, collective_id, name, parts=6):
    seq_count, line = lax.axis_size("seq"), lax.axis_size("dp") // 2
    rows, n = arrays[0].shape[0] // (2 * line * seq_count), len(arrays)
    chunks = column_chunks([x.shape[1] for x in arrays], parts)
    m = len(chunks)
    leads = [(2, 2, line), (2, 2, line), (2, line), (2, line), (line,), (line,), (line,)]
    size = sum(x.shape[1] for x in arrays) * rows * 64
    anywhere = pl.BlockSpec(memory_space=pl.ANY)
    return pl.pallas_call(
        functools.partial(scatter_kernel, line, chunks, n, len(extras), block_of),
        out_shape=[jax.ShapeDtypeStruct((rows, x.shape[1]), F32) for x in arrays]
        + [jax.ShapeDtypeStruct((seq_count,) + x.shape[1:], BF16) for x in extras],
        in_specs=[anywhere] * (n + len(extras)),
        out_specs=[pl.BlockSpec(memory_space=pltpu.VMEM)] * n + [anywhere] * len(extras),
        scratch_shapes=[
            pltpu.VMEM(lead + (rows, width), BF16) for lead in leads for _, _, width in chunks
        ]
        + [
            pltpu.SemaphoreType.DMA((m, 2 + line)),
            pltpu.SemaphoreType.DMA((m, 2 + line)),
            pltpu.SemaphoreType.DMA((m,)),
        ]
        + (exchange_sems(len(extras), seq_count) if extras else []),
        compiler_params=pltpu.CompilerParams(
            collective_id=collective_id, vmem_limit_bytes=36 << 20
        ),
        cost_estimate=pl.CostEstimate(flops=0, bytes_accessed=10 * size, transcendentals=0),
        name=name,
    )(*[x.reshape(2, 2, line, 2, rows, x.shape[1]) for x in arrays], *extras)


def exchange_kernel(count, n, block_of, *refs):
    me = lax.axis_index("seq")
    greet([{"seq": lax.rem(me + step, count)} for step in range(1, count)])
    for copy in start_exchange(count, refs[:n], refs[n : 2 * n], block_of, refs[2 * n :]):
        copy.wait()


def seq_exchange(arrays, collective_id, block_of, block_shapes, name):
    count, n = lax.axis_size("seq"), len(arrays)
    sent = sum(math.prod(shape) for shape in block_shapes) * (count - 1) * 2
    return pl.pallas_call(
        functools.partial(exchange_kernel, count, n, block_of),
        out_shape=[jax.ShapeDtypeStruct((count,) + shape, BF16) for shape in block_shapes],
        in_specs=[pl.BlockSpec(memory_space=pl.ANY)] * n,
        out_specs=[pl.BlockSpec(memory_space=pl.ANY)] * n,
        scratch_shapes=exchange_sems(n, count),
        compiler_params=pltpu.CompilerParams(
            collective_id=collective_id, vmem_limit_bytes=4 << 20
        ),
        cost_estimate=pl.CostEstimate(flops=0, bytes_accessed=20 * sent, transcendentals=0),
        name=name,
    )(*arrays)


def seq_permutes(block_for):
    count, me = lax.axis_size("seq"), lax.axis_index("seq")
    pieces = [block_for(me)]
    for step in range(1, count):
        ring = [(i, (i + step) % count) for i in range(count)]
        pieces.append(lax.ppermute(block_for(lax.rem(me + step, count)), "seq", ring))
    return pieces


def in_seq_order(pieces, dtype):
    count, me = len(pieces), lax.axis_index("seq")
    whole = jnp.zeros((count,) + pieces[0].shape, dtype)
    for step, piece in enumerate(pieces):
        place = lax.rem(me + count - step, count)
        whole = lax.dynamic_update_index_in_dim(whole, piece.astype(dtype), place, 0)
    return whole


def on_device(
    hidden_in,
    lengths,
    routes,
    gates,
    priority,
    attn_gain,
    mlp_gain,
    w_query,
    key_projection,
    value_projection,
    w_out,
    w_gate,
    w_up,
    w_down,
    cotangent,
):
    rows = hidden_in.shape[1]
    width = hidden_in.shape[2]
    dp_count = lax.axis_size("dp")
    seq_count = lax.axis_size("seq")
    devices = dp_count * seq_count
    own_experts = w_gate.shape[0]
    sharers = seq_count // own_experts
    hidden_units = w_gate.shape[2]
    my_seq = lax.axis_index("seq")
    extent = rows * seq_count
    query_pos = my_seq * rows + jnp.arange(rows, dtype=jnp.int32)
    key_pos = jnp.arange(extent, dtype=jnp.int32)
    length = lengths[0]
    is_valid = query_pos < length
    score_scale = 1.0 / math.sqrt(HEAD_DIM)
    q_width = w_query.shape[1]
    kv_width = key_projection.shape[1]
    q_heads = q_width // HEAD_DIM
    kv_heads = kv_width // HEAD_DIM
    group_size = q_heads // kv_heads
    cosine_lookup, sine_lookup = rope_angles(query_pos, HEAD_DIM)

    gain_block = jnp.concatenate(
        [attn_gain[:, None], mlp_gain[:, None], jnp.zeros((attn_gain.shape[0], LANES - 2), BF16)],
        axis=1,
    )
    packed = jnp.concatenate([w_query, key_projection, value_projection, gain_block], axis=1)
    staged = seq_count == 4 and w_query.shape[0] % 16 == 0

    def expert_pieces(weights):
        def block_for(peer):
            return lax.dynamic_index_in_dim(weights, peer // sharers, 0, keepdims=False)

        return seq_permutes(block_for)

    gate_parts = expert_pieces(w_gate)
    if staged:
        packed_full, out_full = staged_gather(
            [packed, w_out], [], None, 2, "gather_attention_weights"
        )
    else:
        packed_full = lax.all_gather(packed, BOTH, axis=0, tiled=True)
        out_full = lax.all_gather(w_out, BOTH, axis=0, tiled=True)

    pair_routes, place, kept = claim_places(routes[0], priority[0, 0], is_valid)
    holder = (pair_routes // own_experts) * seq_count + (pair_routes % own_experts) * sharers
    holder = holder + my_seq * sharers // seq_count
    slots = devices * CAP
    target = jnp.where(kept, holder * CAP + place, slots).reshape(rows, TOP)
    slot_ids = jnp.arange(slots, dtype=jnp.int32)
    hits = target[:, :, None] == slot_ids[None, None, :]
    gate_rows = gates[0]
    token_hot = jnp.any(hits, axis=1).astype(BF16)
    slot_gate = jnp.sum(jnp.where(hits, gate_rows[:, :, None], 0.0), axis=(0, 1))

    live_cotangent = jnp.where(is_valid[:, None], cotangent[0], jnp.zeros((), BF16))
    out_grad = live_cotangent.astype(F32)
    grad_send = (tn(token_hot, live_cotangent) * slot_gate[:, None]).astype(BF16)
    packed_full, out_full, gate_parts, grad_send, w_up, w_down = lax.optimization_barrier(
        (packed_full, out_full, gate_parts, grad_send, w_up, w_down)
    )
    up_parts, down_parts = expert_pieces(w_up), expert_pieces(w_down)
    gain_one = packed_full[:, q_width + 2 * kv_width].astype(F32)
    gain_two = packed_full[:, q_width + 2 * kv_width + 1].astype(F32)
    grad_rows = swap(grad_send.reshape(devices, CAP, width), ("dp", "seq")).reshape(slots, width)

    inputs = hidden_in[0].astype(F32)
    scale_one = lax.rsqrt(jnp.mean(inputs * inputs, axis=-1, keepdims=True) + EPSILON)
    normed = (inputs * scale_one * gain_one).astype(BF16)
    projected = nn(normed, packed_full)
    query_rows = projected[:, :q_width]
    key_matrix_rows = projected[:, q_width : q_width + kv_width]
    value_matrix_rows = projected[:, q_width + kv_width : q_width + 2 * kv_width].astype(BF16)
    query_rotated = apply_rotary(
        query_rows.reshape(rows, q_heads, HEAD_DIM), cosine_lookup, sine_lookup
    ).astype(BF16)
    key_rotated = apply_rotary(
        key_matrix_rows.reshape(rows, kv_heads, HEAD_DIM), cosine_lookup, sine_lookup
    ).astype(BF16)
    key_rotated = key_rotated.reshape(rows, kv_width)
    kv_mine = jnp.concatenate([key_rotated, value_matrix_rows], axis=1)
    (kv_all,) = seq_exchange(
        [kv_mine], 1, lambda ref, peer: ref, [(rows, 2 * kv_width)], "gather_keys"
    )
    kv_all = kv_all.reshape(extent, 2 * kv_width)
    key_all, value_all = kv_all[:, :kv_width], kv_all[:, kv_width:]
    query_head_groups = query_rotated.reshape(rows, kv_heads, group_size, HEAD_DIM).transpose(
        1, 0, 2, 3
    )
    key_heads, value_heads = split_heads(key_all, kv_heads), split_heads(value_all, kv_heads)
    attended, log_total = lax.map(
        lambda operands: head_forward(
            operands[0], operands[1], operands[2], query_pos, key_pos, length, score_scale
        ),
        (query_head_groups, key_heads, value_heads),
    )
    attended = attended.transpose(1, 0, 2, 3).reshape(rows, q_width).astype(BF16)
    middle = inputs + nn(attended, out_full)
    scale_two = lax.rsqrt(jnp.mean(middle * middle, axis=-1, keepdims=True) + EPSILON)
    moe_input = (middle * scale_two * gain_two).astype(BF16)

    send_rows = tn(token_hot, moe_input).astype(BF16).reshape(devices, CAP, width)
    send_rows, grad_rows, up_parts = lax.optimization_barrier((send_rows, grad_rows, up_parts))
    slot_rows = swap(send_rows, ("dp", "seq")).reshape(slots, width)
    gate_full = in_seq_order(gate_parts, BF16).reshape(width, hidden_units)
    up_full = in_seq_order(up_parts, BF16).reshape(width, hidden_units)
    down_full = in_seq_order(down_parts, BF16).reshape(hidden_units, width)
    slot_rows, gate_full, up_full, down_full = lax.optimization_barrier(
        (slot_rows, gate_full, up_full, down_full)
    )
    gate_pre = nn(slot_rows, gate_full)
    up_pre = nn(slot_rows, up_full)
    gate_sigmoid = jax.nn.sigmoid(gate_pre)
    gate_act = gate_pre * gate_sigmoid
    gate_slope = gate_sigmoid * (1.0 + gate_pre * (1.0 - gate_sigmoid))
    expert_hidden = (gate_act * up_pre).astype(BF16)
    hidden_grad = nt(grad_rows, down_full)
    gate_pre_grad = (hidden_grad * up_pre * gate_slope).astype(BF16)
    up_pre_grad = (hidden_grad * gate_act).astype(BF16)
    row_grad = (nt(gate_pre_grad, gate_full) + nt(up_pre_grad, up_full)).astype(BF16)
    row_back = swap(row_grad.reshape(devices, CAP, width), ("dp", "seq")).reshape(slots, width)

    gate_grad = tn(slot_rows, gate_pre_grad).astype(BF16)
    up_grad = tn(slot_rows, up_pre_grad).astype(BF16)
    down_grad = tn(expert_hidden, grad_rows).astype(BF16)

    def to_owners(grad):
        grad = grad.reshape(seq_count, -1, grad.shape[1])

        def block_for(peer):
            return lax.dynamic_index_in_dim(grad, peer, 0, keepdims=False)

        return seq_permutes(block_for)

    def owned_sum(pieces):
        whole = in_seq_order(pieces, F32)
        return jnp.sum(whole.reshape((own_experts, sharers) + whole.shape[1:]), axis=1)

    gate_grad_parts, up_grad_parts = to_owners(gate_grad), to_owners(up_grad)
    row_back, down_grad = lax.optimization_barrier((row_back, down_grad))
    down_grad_parts = to_owners(down_grad)
    expert_out = nn(expert_hidden, down_full).astype(BF16)
    expert_out, row_back = lax.optimization_barrier((expert_out, row_back))
    returned = swap(expert_out.reshape(devices, CAP, width), ("dp", "seq")).reshape(slots, width)
    moe_input_grad = nn(token_hot, row_back)
    middle_norm_grad, gain_two_grad = norm_back(middle, scale_two, gain_two, moe_input_grad)
    middle_grad = out_grad + middle_norm_grad
    branch_grad = middle_grad.astype(BF16)
    no_grad = jnp.zeros((rows, LANES), BF16)

    out_terms = tn(attended, branch_grad).astype(BF16)
    attended_grad = nt(branch_grad, out_full).astype(BF16)
    attended_grad, out_terms = lax.optimization_barrier((attended_grad, out_terms))
    attended_grad = attended_grad.reshape(rows, kv_heads, group_size, HEAD_DIM).transpose(
        1, 0, 2, 3
    )
    query_part, key_part, value_part = lax.map(
        lambda operands: head_backward(
            operands[0],
            operands[1],
            operands[2],
            operands[3],
            operands[4],
            query_pos,
            key_pos,
            length,
            score_scale,
        ),
        (query_head_groups, key_heads, value_heads, attended_grad, log_total),
    )
    kv_terms = jnp.concatenate(
        [
            key_part.transpose(1, 0, 2).reshape(extent, kv_width),
            value_part.transpose(1, 0, 2).reshape(extent, kv_width),
        ],
        axis=1,
    ).astype(BF16)
    (kv_back,) = seq_exchange(
        [kv_terms.reshape(seq_count, rows, 2 * kv_width)],
        4,
        lambda ref, peer: ref.at[peer],
        [(rows, 2 * kv_width)],
        "return_key_grads",
    )
    kv_sum = jnp.sum(kv_back.astype(F32), axis=0)
    key_grad = apply_rotary(
        kv_sum[:, :kv_width].reshape(rows, kv_heads, HEAD_DIM), cosine_lookup, -sine_lookup
    )
    key_grad = key_grad.reshape(rows, kv_width).astype(BF16)
    value_grad = kv_sum[:, kv_width:].astype(BF16)
    query_grad = apply_rotary(
        query_part.transpose(1, 0, 2, 3).reshape(rows, q_heads, HEAD_DIM),
        cosine_lookup,
        -sine_lookup,
    )
    query_grad = query_grad.reshape(rows, q_width).astype(BF16)
    projected_grad = jnp.concatenate([query_grad, key_grad, value_grad, no_grad], axis=1)
    normed_grad = nt(projected_grad, packed_full)
    input_norm_grad, gain_one_grad = norm_back(inputs, scale_one, gain_one, normed_grad)
    input_grad = middle_grad + input_norm_grad

    gain_columns = jnp.zeros((width, LANES), BF16)
    gain_columns = gain_columns.at[:, 0].set(gain_one_grad.astype(BF16))
    gain_columns = gain_columns.at[:, 1].set(gain_two_grad.astype(BF16))
    query_terms = lax.dynamic_update_slice(
        tn(normed, projected_grad).astype(BF16), gain_columns, (0, projected_grad.shape[1] - LANES)
    )
    query_terms, down_grad_parts = lax.optimization_barrier((query_terms, down_grad_parts))
    grad_parts = [gate_grad_parts, up_grad_parts, down_grad_parts]
    if staged:
        out_owned, owned = staged_scatter(
            [out_terms, query_terms], [], None, 6, "scatter_attention_grads"
        )
    else:
        terms = jnp.concatenate([out_terms, query_terms], axis=1)
        terms = lax.psum_scatter(terms, BOTH, scatter_dimension=0, tiled=True).astype(F32)
        out_owned, owned = terms[:, :width], terms[:, width:]
    returned, owned = lax.optimization_barrier((returned, owned))
    expert_grads = [owned_sum(parts) for parts in grad_parts]

    gate_high = gate_rows.astype(BF16)
    gate_low = (gate_rows - gate_high.astype(F32)).astype(BF16)

    def gate_hot(weights):
        return jnp.sum(
            jnp.where(hits, weights.astype(F32)[:, :, None], 0.0), axis=1
        ).astype(BF16)

    layer_out = middle + nn(gate_hot(gate_high), returned) + nn(gate_hot(gate_low), returned)

    return (
        layer_out[None],
        input_grad[None],
        owned[:, q_width + 2 * kv_width],
        owned[:, q_width + 2 * kv_width + 1],
        owned[:, :q_width],
        owned[:, q_width : q_width + kv_width],
        owned[:, q_width + kv_width : q_width + 2 * kv_width],
        out_owned,
        *expert_grads,
    )


def solution(mesh):
    part = P("dp", "seq", None)
    both = P(BOTH)
    both_rows = P(BOTH, None)
    return jax.shard_map(
        on_device,
        mesh=mesh,
        in_specs=(part, P("dp"), part, part, part, both, both)
        + (both_rows,) * 4
        + (part,) * 4,
        out_specs=(part, part, both, both) + (both_rows,) * 4 + (part,) * 3,
        check_vma=False,
    )
```

```python
import functools
import math

import jax
import jax.numpy as jnp
from jax import lax
from jax.experimental import pallas as pl
from jax.experimental.pallas import tpu as pltpu
from jax.sharding import PartitionSpec as P

HEAD_DIM = 128
EXPERTS = 32
TOP = 4
CAP = 40

EPSILON = 1e-06
ROPE_BASE = 10000.0
NEG_FILL = -1e30
LANES = 128
BOTH = ("seq", "dp")
BF16 = jnp.bfloat16
F32 = jnp.float32


def rope_angles(positions, head_size):
    half_dim = head_size // 2
    frequency = ROPE_BASE ** (-(2.0 * jnp.arange(half_dim, dtype=F32)) / head_size)
    angles = positions.astype(F32)[:, None] * frequency[None, :]
    return (jnp.cos(angles)[:, None, :], jnp.sin(angles)[:, None, :])


def apply_rotary(values, cosine_lookup, sine_lookup):
    half_dim = values.shape[-1] // 2
    lower_half = values[..., :half_dim]
    upper_half = values[..., half_dim:]
    return jnp.concatenate(
        [
            lower_half * cosine_lookup - upper_half * sine_lookup,
            upper_half * cosine_lookup + lower_half * sine_lookup,
        ],
        axis=-1,
    )


def dot(left, right, contract):
    return lax.dot_general(left, right, (contract, ((), ())), preferred_element_type=F32)


def nn(left, right):
    return dot(left, right, ((1,), (0,)))


def nt(left, right):
    return dot(left, right, ((1,), (1,)))


def tn(left, right):
    return dot(left, right, ((0,), (0,)))


def claim_places(routes, priority, is_valid):
    pair_routes = routes.reshape(-1)
    live = jnp.repeat(is_valid, TOP)
    key = jnp.where(live, pair_routes, -1)
    earlier = (key[None, :] == pair_routes[:, None]) & (priority[None, :] < priority[:, None])
    place = jnp.sum(earlier.astype(F32), axis=1).astype(jnp.int32)
    return pair_routes, place, live & (place < CAP)


def masked_scores(query_group, key_head, query_pos, key_pos, length, score_scale):
    scores = (
        jnp.einsum("qgd,kd->gqk", query_group, key_head, preferred_element_type=F32) * score_scale
    )
    key_mask = (key_pos[None, :] <= query_pos[:, None]) & (key_pos[None, :] < length)
    return jnp.where(key_mask[None], scores, NEG_FILL)


def head_forward(query_group, key_head, value_head, query_pos, key_pos, length, score_scale):
    scores = masked_scores(query_group, key_head, query_pos, key_pos, length, score_scale)
    row_max = jnp.max(scores, axis=-1, keepdims=True)
    exp_scores = jnp.exp(scores - row_max)
    exp_total = jnp.sum(exp_scores, axis=-1, keepdims=True)
    attn_probs = (exp_scores / exp_total).astype(BF16)
    head_out = jnp.einsum("gqk,kd->qgd", attn_probs, value_head, preferred_element_type=F32)
    return (head_out, (row_max + jnp.log(exp_total))[..., 0])


def head_backward(
    query_group, key_head, value_head, head_grad, log_total, query_pos, key_pos, length, score_scale
):
    scores = masked_scores(query_group, key_head, query_pos, key_pos, length, score_scale)
    attn_probs = jnp.exp(scores - log_total[..., None])
    prob_grad = jnp.einsum("qgd,kd->gqk", head_grad, value_head, preferred_element_type=F32)
    row_delta = jnp.sum(attn_probs * prob_grad, axis=-1, keepdims=True)
    score_grad = (attn_probs * (prob_grad - row_delta)).astype(BF16)
    query_part = (
        jnp.einsum("gqk,kd->qgd", score_grad, key_head, preferred_element_type=F32) * score_scale
    )
    key_part = (
        jnp.einsum("gqk,qgd->kd", score_grad, query_group, preferred_element_type=F32) * score_scale
    )
    value_part = jnp.einsum(
        "gqk,qgd->kd", attn_probs.astype(BF16), head_grad, preferred_element_type=F32
    )
    return (query_part, key_part, value_part)


def norm_back(values, scale_rows, gain_vec, incoming):
    weighted = incoming * gain_vec
    inner_mean = jnp.mean(weighted * values, axis=-1, keepdims=True)
    values_grad = scale_rows * weighted - values * scale_rows * scale_rows * scale_rows * inner_mean
    return (values_grad, jnp.sum(incoming * values * scale_rows, axis=0))


def split_heads(gathered, kv_heads):
    return gathered.reshape(gathered.shape[0], kv_heads, HEAD_DIM).transpose(1, 0, 2)


def swap(blocks, axes):
    return lax.all_to_all(blocks, axes, split_axis=0, concat_axis=0, tiled=True)


MESH_IDS = pl.DeviceIdType.MESH


def torus_place():
    seq, dp = lax.axis_index("seq"), lax.axis_index("dp")
    return seq // 2, seq % 2, dp // 2, dp % 2


def torus_id(a, b, z, c):
    return {"seq": 2 * a + b, "dp": 2 * z + c}


def torus_peers(line):
    a, b, z, c = torus_place()
    peers = [torus_id(a, b, z, 1 - c), torus_id(a, 1 - b, z, c), torus_id(1 - a, b, z, c)]
    peers.append(torus_id(1 - a, 1 - b, z, c))
    return peers + [torus_id(a, b, lax.rem(z + k, line), c) for k in range(1, line)]


def greet(peers):
    barrier = pltpu.get_barrier_semaphore()
    for peer in peers:
        pl.semaphore_signal(barrier, inc=1, device_id=peer, device_id_type=MESH_IDS)
    pl.semaphore_wait(barrier, len(peers))


def column_chunks(widths, parts):
    chunks = []
    for part in range(parts):
        for k, whole in enumerate(widths):
            tiles = whole // LANES
            first, end = tiles * part // parts, tiles * (part + 1) // parts
            if end > first:
                chunks.append((k, first * LANES, (end - first) * LANES))
    return chunks


def remote(src, dst, sems, i, j, device_id):
    send, recv = sems
    return pltpu.make_async_remote_copy(
        src_ref=src,
        dst_ref=dst,
        send_sem=send.at[i, j],
        recv_sem=recv.at[i, j],
        device_id=device_id,
        device_id_type=MESH_IDS,
    )


def start_exchange(count, sources, targets, block_of, sems):
    send_sems, recv_sems, local_sems = sems
    me = lax.axis_index("seq")
    copies = []
    for i, source in enumerate(sources):
        for step in range(1, count):
            peer = lax.rem(me + step, count)
            copies.append(
                pltpu.make_async_remote_copy(
                    src_ref=block_of(source, peer),
                    dst_ref=targets[i].at[me],
                    send_sem=send_sems.at[i, step - 1],
                    recv_sem=recv_sems.at[i, step - 1],
                    device_id={"seq": peer},
                    device_id_type=MESH_IDS,
                )
            )
        copies.append(
            pltpu.make_async_copy(block_of(source, me), targets[i].at[me], local_sems.at[i])
        )
    for copy in copies:
        copy.start()
    return copies


def exchange_sems(n, count):
    return [
        pltpu.SemaphoreType.DMA((n, count - 1)),
        pltpu.SemaphoreType.DMA((n, count - 1)),
        pltpu.SemaphoreType.DMA((n,)),
    ]


def in_steps(count, stages):
    for step in range((count + 1) // 2 + len(stages) - 1):
        for behind, stage in enumerate(stages):
            for i in (2 * (step - behind), 2 * (step - behind) + 1):
                if 0 <= i < count:
                    stage(i)


def gather_kernel(line, chunks, n, extras, block_of, *refs):
    sources, more_sources = refs[:n], refs[n : n + extras]
    refs = refs[n + extras :]
    targets, more_targets = refs[:n], refs[n : n + extras]
    send, recv, local, *more_sems = refs[n + extras :]
    sems = (send, recv)
    a, b, z, c = torus_place()
    greet(torus_peers(line))
    more = start_exchange(4, more_sources, more_targets, block_of, more_sems) if extras else []
    sent = []

    def start(copy):
        copy.start()
        sent.append(copy)
        return copy

    along_line, first_hop, second_hop, third_hop = {}, {}, {}, {}

    def send_line(i):
        k, first, size = chunks[i]
        cols = pl.ds(first, size)
        own = targets[k].at[a, b, z, c, :, cols]
        keep = pltpu.make_async_copy(sources[k].at[:, cols], own, local.at[i])
        keep.start()
        along_line[i] = [
            start(
                remote(
                    sources[k].at[:, cols],
                    own,
                    sems,
                    i,
                    2 + step,
                    torus_id(a, b, lax.rem(z + step, line), c),
                )
            )
            for step in range(1, line)
        ]
        along_line[i].append(keep)

    def send_first(i):
        k, first, size = chunks[i]
        *copies, keep = along_line[i]
        keep.wait()
        for copy in copies:
            copy.wait_recv()
        block = targets[k].at[a, b, :, c, :, pl.ds(first, size)]
        peer = torus_id(a, 1 - b, z, c) if i % 2 == 0 else torus_id(1 - a, b, z, c)
        first_hop[i] = start(remote(block, block, sems, i, 1, peer))

    def send_second(i):
        k, first, size = chunks[i]
        first_hop[i].wait_recv()
        cols = pl.ds(first, size)
        if i % 2 == 0:
            block, peer = targets[k].at[a, :, :, c, :, cols], torus_id(1 - a, b, z, c)
        else:
            block, peer = targets[k].at[:, b, :, c, :, cols], torus_id(a, 1 - b, z, c)
        second_hop[i] = start(remote(block, block, sems, i, 2, peer))

    def send_third(i):
        k, first, size = chunks[i]
        second_hop[i].wait_recv()
        block = targets[k].at[:, :, :, c, :, pl.ds(first, size)]
        third_hop[i] = start(remote(block, block, sems, i, 0, torus_id(a, b, z, 1 - c)))

    in_steps(len(chunks), [send_line, send_first, send_second, send_third])
    for copy in third_hop.values():
        copy.wait_recv()
    for copy in sent:
        copy.wait_send()
    for copy in more:
        copy.wait()


def staged_gather(arrays, extras, block_of, collective_id, name, parts=6):
    seq_count, line = lax.axis_size("seq"), lax.axis_size("dp") // 2
    rows, n = arrays[0].shape[0], len(arrays)
    chunks = column_chunks([x.shape[1] for x in arrays], parts)
    m = len(chunks)
    shape = (seq_count // 2, 2, line, 2, rows)
    size = sum(x.shape[1] for x in arrays) * rows * 64
    count = n + len(extras)
    outs = pl.pallas_call(
        functools.partial(gather_kernel, line, chunks, n, len(extras), block_of),
        out_shape=[jax.ShapeDtypeStruct(shape + (x.shape[1],), BF16) for x in arrays]
        + [jax.ShapeDtypeStruct((seq_count,) + x.shape[1:], BF16) for x in extras],
        in_specs=[pl.BlockSpec(memory_space=pl.ANY)] * count,
        out_specs=[pl.BlockSpec(memory_space=pl.ANY)] * count,
        scratch_shapes=[
            pltpu.SemaphoreType.DMA((m, 2 + line)),
            pltpu.SemaphoreType.DMA((m, 2 + line)),
            pltpu.SemaphoreType.DMA((m,)),
        ]
        + (exchange_sems(len(extras), seq_count) if extras else []),
        compiler_params=pltpu.CompilerParams(
            collective_id=collective_id, vmem_limit_bytes=4 << 20
        ),
        cost_estimate=pl.CostEstimate(flops=0, bytes_accessed=size, transcendentals=0),
        name=name,
    )(*arrays, *extras)
    return [o.reshape(-1, o.shape[-1]) for o in outs]


def scatter_kernel(line, chunks, n, extras, block_of, *refs):
    m = len(chunks)
    sources, more_sources = refs[:n], refs[n : n + extras]
    refs = refs[n + extras :]
    targets, more_targets = refs[:n], refs[n : n + extras]
    scratch = refs[n + extras :]
    owns, ins1, accs2, ins2, accs3, ins3, ins4 = (scratch[m * s : m * (s + 1)] for s in range(7))
    send, recv, local, *more_sems = scratch[7 * m :]
    sems = (send, recv)
    a, b, z, c = torus_place()
    greet(torus_peers(line))
    sent = []

    def start(copy):
        copy.start()
        sent.append(copy)
        return copy

    def add_lines(target, left, right):
        def one(j, carry):
            target[j] = (left[j].astype(F32) + right[j].astype(F32)).astype(BF16)
            return carry

        lax.fori_loop(0, line, one, 0)

    between_cores, first_hop, second_hop, along_line = {}, {}, {}, {}

    def send_core(i):
        k, first, size = chunks[i]
        cols = pl.ds(first, size)
        keep = pltpu.make_async_copy(sources[k].at[:, :, :, c, :, cols], owns[i], local.at[i])
        keep.start()
        swap_core = remote(
            sources[k].at[:, :, :, 1 - c, :, cols], ins1[i], sems, i, 0, torus_id(a, b, z, 1 - c)
        )
        between_cores[i] = (keep, start(swap_core))

    def send_first(i):
        keep, copy = between_cores[i]
        keep.wait()
        copy.wait_recv()
        for p in range(2):
            for q in range(2):
                add_lines(owns[i].at[p, q], owns[i].at[p, q], ins1[i].at[p, q])
        if i % 2 == 0:
            block, peer = owns[i].at[:, 1 - b], torus_id(a, 1 - b, z, c)
        else:
            block, peer = owns[i].at[1 - a], torus_id(1 - a, b, z, c)
        first_hop[i] = start(remote(block, ins2[i], sems, i, 1, peer))

    def send_second(i):
        first_hop[i].wait_recv()
        for p in range(2):
            mine = owns[i].at[p, b] if i % 2 == 0 else owns[i].at[a, p]
            add_lines(accs2[i].at[p], mine, ins2[i].at[p])
        if i % 2 == 0:
            block, peer = accs2[i].at[1 - a], torus_id(1 - a, b, z, c)
        else:
            block, peer = accs2[i].at[1 - b], torus_id(a, 1 - b, z, c)
        second_hop[i] = start(remote(block, ins3[i], sems, i, 2, peer))

    def send_line(i):
        second_hop[i].wait_recv()
        add_lines(accs3[i], accs2[i].at[a if i % 2 == 0 else b], ins3[i])
        copies = []
        for step in range(1, line):
            to = lax.rem(z + step, line)
            peer = torus_id(a, b, to, c)
            copies.append(start(remote(accs3[i].at[to], ins4[i].at[z], sems, i, 2 + step, peer)))
        along_line[i] = copies

    def finish(i):
        k, first, size = chunks[i]
        total = accs3[i][z].astype(F32)
        for step in range(1, line):
            along_line[i][step - 1].wait_recv()
            total = total + ins4[i][lax.rem(z + line - step, line)].astype(F32)
        targets[k][:, first : first + size] = total

    more = start_exchange(4, more_sources, more_targets, block_of, more_sems) if extras else []
    in_steps(m, [send_core, send_first, send_second, send_line, finish])
    for copy in sent:
        copy.wait_send()
    for copy in more:
        copy.wait()


def staged_scatter(arrays, extras, block_of, collective_id, name, parts=6):
    seq_count, line = lax.axis_size("seq"), lax.axis_size("dp") // 2
    rows, n = arrays[0].shape[0] // (2 * line * seq_count), len(arrays)
    chunks = column_chunks([x.shape[1] for x in arrays], parts)
    m = len(chunks)
    leads = [(2, 2, line), (2, 2, line), (2, line), (2, line), (line,), (line,), (line,)]
    size = sum(x.shape[1] for x in arrays) * rows * 64
    anywhere = pl.BlockSpec(memory_space=pl.ANY)
    return pl.pallas_call(
        functools.partial(scatter_kernel, line, chunks, n, len(extras), block_of),
        out_shape=[jax.ShapeDtypeStruct((rows, x.shape[1]), F32) for x in arrays]
        + [jax.ShapeDtypeStruct((seq_count,) + x.shape[1:], BF16) for x in extras],
        in_specs=[anywhere] * (n + len(extras)),
        out_specs=[pl.BlockSpec(memory_space=pltpu.VMEM)] * n + [anywhere] * len(extras),
        scratch_shapes=[
            pltpu.VMEM(lead + (rows, width), BF16) for lead in leads for _, _, width in chunks
        ]
        + [
            pltpu.SemaphoreType.DMA((m, 2 + line)),
            pltpu.SemaphoreType.DMA((m, 2 + line)),
            pltpu.SemaphoreType.DMA((m,)),
        ]
        + (exchange_sems(len(extras), seq_count) if extras else []),
        compiler_params=pltpu.CompilerParams(
            collective_id=collective_id, vmem_limit_bytes=36 << 20
        ),
        cost_estimate=pl.CostEstimate(flops=0, bytes_accessed=size, transcendentals=0),
        name=name,
    )(*[x.reshape(2, 2, line, 2, rows, x.shape[1]) for x in arrays], *extras)


def exchange_kernel(count, n, block_of, *refs):
    me = lax.axis_index("seq")
    greet([{"seq": lax.rem(me + step, count)} for step in range(1, count)])
    for copy in start_exchange(count, refs[:n], refs[n : 2 * n], block_of, refs[2 * n :]):
        copy.wait()


def seq_exchange(arrays, collective_id, block_of, block_shapes, name):
    count, n = lax.axis_size("seq"), len(arrays)
    sent = sum(math.prod(shape) for shape in block_shapes) * (count - 1) * 2
    return pl.pallas_call(
        functools.partial(exchange_kernel, count, n, block_of),
        out_shape=[jax.ShapeDtypeStruct((count,) + shape, BF16) for shape in block_shapes],
        in_specs=[pl.BlockSpec(memory_space=pl.ANY)] * n,
        out_specs=[pl.BlockSpec(memory_space=pl.ANY)] * n,
        scratch_shapes=exchange_sems(n, count),
        compiler_params=pltpu.CompilerParams(
            collective_id=collective_id, vmem_limit_bytes=4 << 20
        ),
        cost_estimate=pl.CostEstimate(flops=0, bytes_accessed=sent, transcendentals=0),
        name=name,
    )(*arrays)


def seq_permutes(block_for):
    count, me = lax.axis_size("seq"), lax.axis_index("seq")
    pieces = [block_for(me)]
    for step in range(1, count):
        ring = [(i, (i + step) % count) for i in range(count)]
        pieces.append(lax.ppermute(block_for(lax.rem(me + step, count)), "seq", ring))
    return pieces


def in_seq_order(pieces, dtype):
    count, me = len(pieces), lax.axis_index("seq")
    whole = jnp.zeros((count,) + pieces[0].shape, dtype)
    for step, piece in enumerate(pieces):
        place = lax.rem(me + count - step, count)
        whole = lax.dynamic_update_index_in_dim(whole, piece.astype(dtype), place, 0)
    return whole


def on_device(
    hidden_in,
    lengths,
    routes,
    gates,
    priority,
    attn_gain,
    mlp_gain,
    w_query,
    key_projection,
    value_projection,
    w_out,
    w_gate,
    w_up,
    w_down,
    cotangent,
):
    rows = hidden_in.shape[1]
    width = hidden_in.shape[2]
    dp_count = lax.axis_size("dp")
    seq_count = lax.axis_size("seq")
    devices = dp_count * seq_count
    own_experts = w_gate.shape[0]
    sharers = seq_count // own_experts
    hidden_units = w_gate.shape[2]
    my_seq = lax.axis_index("seq")
    extent = rows * seq_count
    query_pos = my_seq * rows + jnp.arange(rows, dtype=jnp.int32)
    key_pos = jnp.arange(extent, dtype=jnp.int32)
    length = lengths[0]
    is_valid = query_pos < length
    score_scale = 1.0 / math.sqrt(HEAD_DIM)
    q_width = w_query.shape[1]
    kv_width = key_projection.shape[1]
    q_heads = q_width // HEAD_DIM
    kv_heads = kv_width // HEAD_DIM
    group_size = q_heads // kv_heads
    cosine_lookup, sine_lookup = rope_angles(query_pos, HEAD_DIM)

    gain_block = jnp.concatenate(
        [attn_gain[:, None], mlp_gain[:, None], jnp.zeros((attn_gain.shape[0], LANES - 2), BF16)],
        axis=1,
    )
    packed = jnp.concatenate([w_query, key_projection, value_projection], axis=1)
    staged = seq_count == 4 and w_query.shape[0] % 16 == 0

    def expert_pieces(weights):
        def block_for(peer):
            return lax.dynamic_index_in_dim(weights, peer // sharers, 0, keepdims=False)

        return seq_permutes(block_for)

    if staged:
        packed_full, gains_full, out_full, gate_full = staged_gather(
            [packed, gain_block, w_out],
            [w_gate],
            lambda ref, peer: ref.at[peer // sharers],
            2,
            "gather_attention_weights",
        )
        gate_full = gate_full.reshape(width, hidden_units)
    else:
        packed_full = lax.all_gather(packed, BOTH, axis=0, tiled=True)
        gains_full = lax.all_gather(gain_block, BOTH, axis=0, tiled=True)
        out_full = lax.all_gather(w_out, BOTH, axis=0, tiled=True)
        gate_full = in_seq_order(expert_pieces(w_gate), BF16).reshape(width, hidden_units)

    pair_routes, place, kept = claim_places(routes[0], priority[0, 0], is_valid)
    holder = (pair_routes // own_experts) * seq_count + (pair_routes % own_experts) * sharers
    holder = holder + my_seq * sharers // seq_count
    slots = devices * CAP
    target = jnp.where(kept, holder * CAP + place, slots).reshape(rows, TOP)
    slot_ids = jnp.arange(slots, dtype=jnp.int32)
    hits = target[:, :, None] == slot_ids[None, None, :]
    gate_rows = gates[0]
    token_hot = jnp.any(hits, axis=1).astype(BF16)
    slot_gate = jnp.sum(jnp.where(hits, gate_rows[:, :, None], 0.0), axis=(0, 1))

    live_cotangent = jnp.where(is_valid[:, None], cotangent[0], jnp.zeros((), BF16))
    out_grad = live_cotangent.astype(F32)
    grad_send = (tn(token_hot, live_cotangent) * slot_gate[:, None]).astype(BF16)
    packed_full, gains_full, out_full, gate_full, grad_send, w_up, w_down = (
        lax.optimization_barrier(
            (packed_full, gains_full, out_full, gate_full, grad_send, w_up, w_down)
        )
    )
    up_parts, down_parts = expert_pieces(w_up), expert_pieces(w_down)
    gain_one, gain_two = gains_full[:, 0].astype(F32), gains_full[:, 1].astype(F32)
    grad_rows = swap(grad_send.reshape(devices, CAP, width), ("dp", "seq")).reshape(slots, width)

    inputs = hidden_in[0].astype(F32)
    scale_one = lax.rsqrt(jnp.mean(inputs * inputs, axis=-1, keepdims=True) + EPSILON)
    normed = (inputs * scale_one * gain_one).astype(BF16)
    projected = nn(normed, packed_full)
    query_rows = projected[:, :q_width]
    key_matrix_rows = projected[:, q_width : q_width + kv_width]
    value_matrix_rows = projected[:, q_width + kv_width : q_width + 2 * kv_width].astype(BF16)
    query_rotated = apply_rotary(
        query_rows.reshape(rows, q_heads, HEAD_DIM), cosine_lookup, sine_lookup
    ).astype(BF16)
    key_rotated = apply_rotary(
        key_matrix_rows.reshape(rows, kv_heads, HEAD_DIM), cosine_lookup, sine_lookup
    ).astype(BF16)
    key_rotated = key_rotated.reshape(rows, kv_width)
    kv_mine = jnp.concatenate([key_rotated, value_matrix_rows], axis=1)
    (kv_all,) = seq_exchange(
        [kv_mine], 1, lambda ref, peer: ref, [(rows, 2 * kv_width)], "gather_keys"
    )
    kv_all = kv_all.reshape(extent, 2 * kv_width)
    key_all, value_all = kv_all[:, :kv_width], kv_all[:, kv_width:]
    query_head_groups = query_rotated.reshape(rows, kv_heads, group_size, HEAD_DIM).transpose(
        1, 0, 2, 3
    )
    key_heads, value_heads = split_heads(key_all, kv_heads), split_heads(value_all, kv_heads)
    attended, log_total = lax.map(
        lambda operands: head_forward(
            operands[0], operands[1], operands[2], query_pos, key_pos, length, score_scale
        ),
        (query_head_groups, key_heads, value_heads),
    )
    attended = attended.transpose(1, 0, 2, 3).reshape(rows, q_width).astype(BF16)
    middle = inputs + nn(attended, out_full)
    scale_two = lax.rsqrt(jnp.mean(middle * middle, axis=-1, keepdims=True) + EPSILON)
    moe_input = (middle * scale_two * gain_two).astype(BF16)

    send_rows = tn(token_hot, moe_input).astype(BF16).reshape(devices, CAP, width)
    send_rows, grad_rows, up_parts = lax.optimization_barrier((send_rows, grad_rows, up_parts))
    slot_rows = swap(send_rows, ("dp", "seq")).reshape(slots, width)
    up_full = in_seq_order(up_parts, BF16).reshape(width, hidden_units)
    down_full = in_seq_order(down_parts, BF16).reshape(hidden_units, width)
    slot_rows, gate_full, up_full, down_full = lax.optimization_barrier(
        (slot_rows, gate_full, up_full, down_full)
    )
    gate_pre = nn(slot_rows, gate_full)
    up_pre = nn(slot_rows, up_full)
    gate_sigmoid = jax.nn.sigmoid(gate_pre)
    gate_act = gate_pre * gate_sigmoid
    gate_slope = gate_sigmoid * (1.0 + gate_pre * (1.0 - gate_sigmoid))
    expert_hidden = (gate_act * up_pre).astype(BF16)
    hidden_grad = nt(grad_rows, down_full)
    gate_pre_grad = (hidden_grad * up_pre * gate_slope).astype(BF16)
    up_pre_grad = (hidden_grad * gate_act).astype(BF16)
    row_grad = (nt(gate_pre_grad, gate_full) + nt(up_pre_grad, up_full)).astype(BF16)
    row_back = swap(row_grad.reshape(devices, CAP, width), ("dp", "seq")).reshape(slots, width)

    gate_grad = tn(slot_rows, gate_pre_grad).astype(BF16)
    up_grad = tn(slot_rows, up_pre_grad).astype(BF16)
    down_grad = tn(expert_hidden, grad_rows).astype(BF16)

    def to_owners(grad):
        grad = grad.reshape(seq_count, -1, grad.shape[1])

        def block_for(peer):
            return lax.dynamic_index_in_dim(grad, peer, 0, keepdims=False)

        return seq_permutes(block_for)

    def owned_sum(pieces):
        whole = in_seq_order(pieces, F32)
        return jnp.sum(whole.reshape((own_experts, sharers) + whole.shape[1:]), axis=1)

    gate_grad_parts, up_grad_parts = to_owners(gate_grad), to_owners(up_grad)
    row_back, down_grad = lax.optimization_barrier((row_back, down_grad))
    down_grad_parts = to_owners(down_grad)
    expert_out = nn(expert_hidden, down_full).astype(BF16)
    expert_out, row_back = lax.optimization_barrier((expert_out, row_back))
    returned = swap(expert_out.reshape(devices, CAP, width), ("dp", "seq")).reshape(slots, width)
    moe_input_grad = nn(token_hot, row_back)
    middle_norm_grad, gain_two_grad = norm_back(middle, scale_two, gain_two, moe_input_grad)
    middle_grad = out_grad + middle_norm_grad
    branch_grad = middle_grad.astype(BF16)
    out_terms = tn(attended, branch_grad).astype(BF16)
    attended_grad = nt(branch_grad, out_full).astype(BF16)
    attended_grad, out_terms = lax.optimization_barrier((attended_grad, out_terms))
    attended_grad = attended_grad.reshape(rows, kv_heads, group_size, HEAD_DIM).transpose(
        1, 0, 2, 3
    )
    query_part, key_part, value_part = lax.map(
        lambda operands: head_backward(
            operands[0],
            operands[1],
            operands[2],
            operands[3],
            operands[4],
            query_pos,
            key_pos,
            length,
            score_scale,
        ),
        (query_head_groups, key_heads, value_heads, attended_grad, log_total),
    )
    kv_terms = jnp.concatenate(
        [
            key_part.transpose(1, 0, 2).reshape(extent, kv_width),
            value_part.transpose(1, 0, 2).reshape(extent, kv_width),
        ],
        axis=1,
    ).astype(BF16)
    kv_terms, down_grad_parts = lax.optimization_barrier((kv_terms, down_grad_parts))
    (kv_back,) = seq_exchange(
        [kv_terms.reshape(seq_count, rows, 2 * kv_width)],
        4,
        lambda ref, peer: ref.at[peer],
        [(rows, 2 * kv_width)],
        "return_key_grads",
    )
    kv_sum = jnp.sum(kv_back.astype(F32), axis=0)
    key_grad = apply_rotary(
        kv_sum[:, :kv_width].reshape(rows, kv_heads, HEAD_DIM), cosine_lookup, -sine_lookup
    )
    key_grad = key_grad.reshape(rows, kv_width).astype(BF16)
    value_grad = kv_sum[:, kv_width:].astype(BF16)
    query_grad = apply_rotary(
        query_part.transpose(1, 0, 2, 3).reshape(rows, q_heads, HEAD_DIM),
        cosine_lookup,
        -sine_lookup,
    )
    query_grad = query_grad.reshape(rows, q_width).astype(BF16)
    projected_grad = jnp.concatenate([query_grad, key_grad, value_grad], axis=1)
    normed_grad = nt(projected_grad, packed_full)
    input_norm_grad, gain_one_grad = norm_back(inputs, scale_one, gain_one, normed_grad)
    input_grad = middle_grad + input_norm_grad

    lane = lax.broadcasted_iota(jnp.int32, (width, LANES), 1)
    gain_terms = jnp.where(lane == 0, gain_one_grad[:, None], gain_two_grad[:, None])
    gain_terms = jnp.where(lane < 2, gain_terms, 0.0).astype(BF16)
    query_terms = tn(normed, projected_grad).astype(BF16)
    grad_parts = [gate_grad_parts, up_grad_parts, down_grad_parts]
    if staged:
        out_owned, gains_owned, owned = staged_scatter(
            [out_terms, gain_terms, query_terms], [], None, 6, "scatter_attention_grads"
        )
    else:
        terms = jnp.concatenate([out_terms, gain_terms, query_terms], axis=1)
        terms = lax.psum_scatter(terms, BOTH, scatter_dimension=0, tiled=True).astype(F32)
        out_owned, gains_owned = terms[:, :width], terms[:, width : width + LANES]
        owned = terms[:, width + LANES :]
    returned, owned = lax.optimization_barrier((returned, owned))
    expert_grads = [owned_sum(parts) for parts in grad_parts]

    gate_hot = jnp.sum(jnp.where(hits, gate_rows[:, :, None], 0.0), axis=1).astype(BF16)
    layer_out = middle + nn(gate_hot, returned)
    return (
        layer_out[None],
        input_grad[None],
        gains_owned[:, 0],
        gains_owned[:, 1],
        owned[:, :q_width],
        owned[:, q_width : q_width + kv_width],
        owned[:, q_width + kv_width : q_width + 2 * kv_width],
        out_owned,
        *expert_grads,
    )


def solution(mesh):
    part = P("dp", "seq", None)
    both = P(BOTH)
    both_rows = P(BOTH, None)
    return jax.shard_map(
        on_device,
        mesh=mesh,
        in_specs=(part, P("dp"), part, part, part, both, both)
        + (both_rows,) * 4
        + (part,) * 4,
        out_specs=(part, part, both, both) + (both_rows,) * 4 + (part,) * 3,
        check_vma=False,
    )
```

```python
import functools
import math

import jax
import jax.numpy as jnp
from jax import lax
from jax.experimental import pallas as pl
from jax.experimental.pallas import tpu as pltpu
from jax.sharding import PartitionSpec as P

HEAD_DIM = 128
EXPERTS = 32
TOP = 4
CAP = 40

EPSILON = 1e-06
ROPE_BASE = 10000.0
NEG_FILL = -1e30
LANES = 128
BOTH = ("seq", "dp")
BF16 = jnp.bfloat16
F32 = jnp.float32


def rope_angles(positions, head_size):
    half_dim = head_size // 2
    frequency = ROPE_BASE ** (-(2.0 * jnp.arange(half_dim, dtype=F32)) / head_size)
    angles = positions.astype(F32)[:, None] * frequency[None, :]
    return (jnp.cos(angles)[:, None, :], jnp.sin(angles)[:, None, :])


def apply_rotary(values, cosine_lookup, sine_lookup):
    half_dim = values.shape[-1] // 2
    lower_half = values[..., :half_dim]
    upper_half = values[..., half_dim:]
    return jnp.concatenate(
        [
            lower_half * cosine_lookup - upper_half * sine_lookup,
            upper_half * cosine_lookup + lower_half * sine_lookup,
        ],
        axis=-1,
    )


def dot(left, right, contract):
    return lax.dot_general(left, right, (contract, ((), ())), preferred_element_type=F32)


def nn(left, right):
    return dot(left, right, ((1,), (0,)))


def nt(left, right):
    return dot(left, right, ((1,), (1,)))


def tn(left, right):
    return dot(left, right, ((0,), (0,)))


def claim_places(routes, priority, is_valid):
    pair_routes = routes.reshape(-1)
    live = jnp.repeat(is_valid, TOP)
    key = jnp.where(live, pair_routes, -1)
    earlier = (key[None, :] == pair_routes[:, None]) & (priority[None, :] < priority[:, None])
    place = jnp.sum(earlier.astype(F32), axis=1).astype(jnp.int32)
    return pair_routes, place, live & (place < CAP)


def masked_scores(query_group, key_head, query_pos, key_pos, length, score_scale):
    scores = (
        jnp.einsum("qgd,kd->gqk", query_group, key_head, preferred_element_type=F32) * score_scale
    )
    key_mask = (key_pos[None, :] <= query_pos[:, None]) & (key_pos[None, :] < length)
    return jnp.where(key_mask[None], scores, NEG_FILL)


def head_forward(query_group, key_head, value_head, query_pos, key_pos, length, score_scale):
    scores = masked_scores(query_group, key_head, query_pos, key_pos, length, score_scale)
    row_max = jnp.max(scores, axis=-1, keepdims=True)
    exp_scores = jnp.exp(scores - row_max)
    exp_total = jnp.sum(exp_scores, axis=-1, keepdims=True)
    attn_probs = (exp_scores / exp_total).astype(BF16)
    head_out = jnp.einsum("gqk,kd->qgd", attn_probs, value_head, preferred_element_type=F32)
    return (head_out, (row_max + jnp.log(exp_total))[..., 0])


def norm_back(values, scale_rows, gain_vec, incoming):
    weighted = incoming * gain_vec
    inner_mean = jnp.mean(weighted * values, axis=-1, keepdims=True)
    values_grad = scale_rows * weighted - values * scale_rows * scale_rows * scale_rows * inner_mean
    return (values_grad, jnp.sum(incoming * values * scale_rows, axis=0))


def split_heads(gathered, kv_heads):
    return gathered.reshape(gathered.shape[0], kv_heads, HEAD_DIM).transpose(1, 0, 2)


def swap(blocks, axes):
    return lax.all_to_all(blocks, axes, split_axis=0, concat_axis=0, tiled=True)


MESH_IDS = pl.DeviceIdType.MESH


def torus_place():
    seq, dp = lax.axis_index("seq"), lax.axis_index("dp")
    return seq // 2, seq % 2, dp // 2, dp % 2


def torus_id(a, b, z, c):
    return {"seq": 2 * a + b, "dp": 2 * z + c}


def torus_peers(line):
    a, b, z, c = torus_place()
    peers = [torus_id(a, b, z, 1 - c), torus_id(a, 1 - b, z, c), torus_id(1 - a, b, z, c)]
    peers.append(torus_id(1 - a, 1 - b, z, c))
    return peers + [torus_id(a, b, lax.rem(z + k, line), c) for k in range(1, line)]


def greet(peers):
    barrier = pltpu.get_barrier_semaphore()
    for peer in peers:
        pl.semaphore_signal(barrier, inc=1, device_id=peer, device_id_type=MESH_IDS)
    pl.semaphore_wait(barrier, len(peers))


def column_chunks(widths, parts):
    chunks = []
    for part in range(parts):
        for k, whole in enumerate(widths):
            tiles = whole // LANES
            first, end = tiles * part // parts, tiles * (part + 1) // parts
            if end > first:
                chunks.append((k, first * LANES, (end - first) * LANES))
    return chunks


def remote(src, dst, sems, i, j, device_id):
    send, recv = sems
    return pltpu.make_async_remote_copy(
        src_ref=src,
        dst_ref=dst,
        send_sem=send.at[i, j],
        recv_sem=recv.at[i, j],
        device_id=device_id,
        device_id_type=MESH_IDS,
    )


def start_exchange(count, sources, targets, block_of, sems):
    send_sems, recv_sems, local_sems = sems
    me = lax.axis_index("seq")
    copies = []
    for i, source in enumerate(sources):
        for step in range(1, count):
            peer = lax.rem(me + step, count)
            copies.append(
                pltpu.make_async_remote_copy(
                    src_ref=block_of(source, peer),
                    dst_ref=targets[i].at[me],
                    send_sem=send_sems.at[i, step - 1],
                    recv_sem=recv_sems.at[i, step - 1],
                    device_id={"seq": peer},
                    device_id_type=MESH_IDS,
                )
            )
        copies.append(
            pltpu.make_async_copy(block_of(source, me), targets[i].at[me], local_sems.at[i])
        )
    for copy in copies:
        copy.start()
    return copies


def exchange_sems(n, count):
    return [
        pltpu.SemaphoreType.DMA((n, count - 1)),
        pltpu.SemaphoreType.DMA((n, count - 1)),
        pltpu.SemaphoreType.DMA((n,)),
    ]


def in_steps(count, stages):
    for step in range((count + 1) // 2 + len(stages) - 1):
        for behind, stage in enumerate(stages):
            for i in (2 * (step - behind), 2 * (step - behind) + 1):
                if 0 <= i < count:
                    stage(i)


def gather_kernel(line, chunks, n, extras, block_of, *refs):
    sources, more_sources = refs[:n], refs[n : n + extras]
    refs = refs[n + extras :]
    targets, more_targets = refs[:n], refs[n : n + extras]
    send, recv, local, *more_sems = refs[n + extras :]
    sems = (send, recv)
    a, b, z, c = torus_place()
    greet(torus_peers(line))
    more = start_exchange(4, more_sources, more_targets, block_of, more_sems) if extras else []
    sent = []

    def start(copy):
        copy.start()
        sent.append(copy)
        return copy

    along_line, first_hop, second_hop, third_hop = {}, {}, {}, {}

    def send_line(i):
        k, first, size = chunks[i]
        cols = pl.ds(first, size)
        own = targets[k].at[a, b, z, c, :, cols]
        keep = pltpu.make_async_copy(sources[k].at[:, cols], own, local.at[i])
        keep.start()
        along_line[i] = [
            start(
                remote(
                    sources[k].at[:, cols],
                    own,
                    sems,
                    i,
                    2 + step,
                    torus_id(a, b, lax.rem(z + step, line), c),
                )
            )
            for step in range(1, line)
        ]
        along_line[i].append(keep)

    def send_first(i):
        k, first, size = chunks[i]
        *copies, keep = along_line[i]
        keep.wait()
        for copy in copies:
            copy.wait_recv()
        block = targets[k].at[a, b, :, c, :, pl.ds(first, size)]
        peer = torus_id(a, 1 - b, z, c) if i % 2 == 0 else torus_id(1 - a, b, z, c)
        first_hop[i] = start(remote(block, block, sems, i, 1, peer))

    def send_second(i):
        k, first, size = chunks[i]
        first_hop[i].wait_recv()
        cols = pl.ds(first, size)
        if i % 2 == 0:
            block, peer = targets[k].at[a, :, :, c, :, cols], torus_id(1 - a, b, z, c)
        else:
            block, peer = targets[k].at[:, b, :, c, :, cols], torus_id(a, 1 - b, z, c)
        second_hop[i] = start(remote(block, block, sems, i, 2, peer))

    def send_third(i):
        k, first, size = chunks[i]
        second_hop[i].wait_recv()
        block = targets[k].at[:, :, :, c, :, pl.ds(first, size)]
        third_hop[i] = start(remote(block, block, sems, i, 0, torus_id(a, b, z, 1 - c)))

    in_steps(len(chunks), [send_line, send_first, send_second, send_third])
    for copy in third_hop.values():
        copy.wait_recv()
    for copy in sent:
        copy.wait_send()
    for copy in more:
        copy.wait()


def staged_gather(arrays, extras, block_of, collective_id, name, parts=6):
    seq_count, line = lax.axis_size("seq"), lax.axis_size("dp") // 2
    rows, n = arrays[0].shape[0], len(arrays)
    chunks = column_chunks([x.shape[1] for x in arrays], parts)
    m = len(chunks)
    shape = (seq_count // 2, 2, line, 2, rows)
    size = sum(x.shape[1] for x in arrays) * rows * 64
    count = n + len(extras)
    outs = pl.pallas_call(
        functools.partial(gather_kernel, line, chunks, n, len(extras), block_of),
        out_shape=[jax.ShapeDtypeStruct(shape + (x.shape[1],), BF16) for x in arrays]
        + [jax.ShapeDtypeStruct((seq_count,) + x.shape[1:], BF16) for x in extras],
        in_specs=[pl.BlockSpec(memory_space=pl.ANY)] * count,
        out_specs=[pl.BlockSpec(memory_space=pl.ANY)] * count,
        scratch_shapes=[
            pltpu.SemaphoreType.DMA((m, 2 + line)),
            pltpu.SemaphoreType.DMA((m, 2 + line)),
            pltpu.SemaphoreType.DMA((m,)),
        ]
        + (exchange_sems(len(extras), seq_count) if extras else []),
        compiler_params=pltpu.CompilerParams(
            collective_id=collective_id, vmem_limit_bytes=4 << 20
        ),
        cost_estimate=pl.CostEstimate(flops=0, bytes_accessed=size, transcendentals=0),
        name=name,
    )(*arrays, *extras)
    return [o.reshape(-1, o.shape[-1]) for o in outs]


def scatter_kernel(line, chunks, n, extras, block_of, *refs):
    m = len(chunks)
    sources, more_sources = refs[:n], refs[n : n + extras]
    refs = refs[n + extras :]
    targets, more_targets = refs[:n], refs[n : n + extras]
    scratch = refs[n + extras :]
    owns, ins1, accs2, ins2, accs3, ins3, ins4 = (scratch[m * s : m * (s + 1)] for s in range(7))
    send, recv, local, *more_sems = scratch[7 * m :]
    sems = (send, recv)
    a, b, z, c = torus_place()
    greet(torus_peers(line))
    sent = []

    def start(copy):
        copy.start()
        sent.append(copy)
        return copy

    def add_lines(target, left, right):
        def one(j, carry):
            target[j] = (left[j].astype(F32) + right[j].astype(F32)).astype(BF16)
            return carry

        lax.fori_loop(0, line, one, 0)

    between_cores, first_hop, second_hop, along_line = {}, {}, {}, {}

    def send_core(i):
        k, first, size = chunks[i]
        cols = pl.ds(first, size)
        keep = pltpu.make_async_copy(sources[k].at[:, :, :, c, :, cols], owns[i], local.at[i])
        keep.start()
        swap_core = remote(
            sources[k].at[:, :, :, 1 - c, :, cols], ins1[i], sems, i, 0, torus_id(a, b, z, 1 - c)
        )
        between_cores[i] = (keep, start(swap_core))

    def send_first(i):
        keep, copy = between_cores[i]
        keep.wait()
        copy.wait_recv()
        for p in range(2):
            for q in range(2):
                add_lines(owns[i].at[p, q], owns[i].at[p, q], ins1[i].at[p, q])
        if i % 2 == 0:
            block, peer = owns[i].at[:, 1 - b], torus_id(a, 1 - b, z, c)
        else:
            block, peer = owns[i].at[1 - a], torus_id(1 - a, b, z, c)
        first_hop[i] = start(remote(block, ins2[i], sems, i, 1, peer))

    def send_second(i):
        first_hop[i].wait_recv()
        for p in range(2):
            mine = owns[i].at[p, b] if i % 2 == 0 else owns[i].at[a, p]
            add_lines(accs2[i].at[p], mine, ins2[i].at[p])
        if i % 2 == 0:
            block, peer = accs2[i].at[1 - a], torus_id(1 - a, b, z, c)
        else:
            block, peer = accs2[i].at[1 - b], torus_id(a, 1 - b, z, c)
        second_hop[i] = start(remote(block, ins3[i], sems, i, 2, peer))

    def send_line(i):
        second_hop[i].wait_recv()
        add_lines(accs3[i], accs2[i].at[a if i % 2 == 0 else b], ins3[i])
        copies = []
        for step in range(1, line):
            to = lax.rem(z + step, line)
            peer = torus_id(a, b, to, c)
            copies.append(start(remote(accs3[i].at[to], ins4[i].at[z], sems, i, 2 + step, peer)))
        along_line[i] = copies

    def finish(i):
        k, first, size = chunks[i]
        total = accs3[i][z].astype(F32)
        for step in range(1, line):
            along_line[i][step - 1].wait_recv()
            total = total + ins4[i][lax.rem(z + line - step, line)].astype(F32)
        targets[k][:, first : first + size] = total

    more = start_exchange(4, more_sources, more_targets, block_of, more_sems) if extras else []
    in_steps(m, [send_core, send_first, send_second, send_line, finish])
    for copy in sent:
        copy.wait_send()
    for copy in more:
        copy.wait()


def staged_scatter(arrays, extras, block_of, collective_id, name, parts=6):
    seq_count, line = lax.axis_size("seq"), lax.axis_size("dp") // 2
    rows, n = arrays[0].shape[0] // (2 * line * seq_count), len(arrays)
    chunks = column_chunks([x.shape[1] for x in arrays], parts)
    m = len(chunks)
    leads = [(2, 2, line), (2, 2, line), (2, line), (2, line), (line,), (line,), (line,)]
    size = sum(x.shape[1] for x in arrays) * rows * 64
    anywhere = pl.BlockSpec(memory_space=pl.ANY)
    return pl.pallas_call(
        functools.partial(scatter_kernel, line, chunks, n, len(extras), block_of),
        out_shape=[jax.ShapeDtypeStruct((rows, x.shape[1]), F32) for x in arrays]
        + [jax.ShapeDtypeStruct((seq_count,) + x.shape[1:], BF16) for x in extras],
        in_specs=[anywhere] * (n + len(extras)),
        out_specs=[pl.BlockSpec(memory_space=pltpu.VMEM)] * n + [anywhere] * len(extras),
        scratch_shapes=[
            pltpu.VMEM(lead + (rows, width), BF16) for lead in leads for _, _, width in chunks
        ]
        + [
            pltpu.SemaphoreType.DMA((m, 2 + line)),
            pltpu.SemaphoreType.DMA((m, 2 + line)),
            pltpu.SemaphoreType.DMA((m,)),
        ]
        + (exchange_sems(len(extras), seq_count) if extras else []),
        compiler_params=pltpu.CompilerParams(
            collective_id=collective_id, vmem_limit_bytes=36 << 20
        ),
        cost_estimate=pl.CostEstimate(flops=0, bytes_accessed=size, transcendentals=0),
        name=name,
    )(*[x.reshape(2, 2, line, 2, rows, x.shape[1]) for x in arrays], *extras)


def spread_kernel(count, parts, source, target, *sems):
    me = lax.axis_index("seq")
    greet([{"seq": lax.rem(me + step, count)} for step in range(1, count)])
    size = source.shape[0] // parts
    pieces = [pl.ds(part * size, size) for part in range(parts)]
    sources = [source.at[piece] for piece in pieces]
    targets = [target.at[:, piece] for piece in pieces]
    for copy in start_exchange(count, sources, targets, lambda ref, peer: ref, sems):
        copy.wait()


def seq_spread(array, parts, collective_id, name):
    count = lax.axis_size("seq")
    return pl.pallas_call(
        functools.partial(spread_kernel, count, parts),
        out_shape=jax.ShapeDtypeStruct((count,) + array.shape, BF16),
        in_specs=[pl.BlockSpec(memory_space=pl.ANY)],
        out_specs=pl.BlockSpec(memory_space=pl.ANY),
        scratch_shapes=exchange_sems(parts, count),
        compiler_params=pltpu.CompilerParams(
            collective_id=collective_id, vmem_limit_bytes=4 << 20
        ),
        cost_estimate=pl.CostEstimate(
            flops=0, bytes_accessed=2 * count * array.size, transcendentals=0
        ),
        name=name,
    )(array)


def rotate(values, cosines, sines):
    return values * cosines + pltpu.roll(values, HEAD_DIM // 2, 1) * sines


def attention_back_kernel(count, heads, kv_heads, *refs):
    length_ref, q_ref, kv_ref, grad_ref, lse_ref, delta_ref, cos_ref, sin_ref, out_ref = refs[:9]
    dq_ref, part_ref, leaving, arriving, send, recv = refs[9:]
    me = lax.axis_index("seq")
    rows, kv_width = q_ref.shape[0], kv_heads * HEAD_DIM
    group, scale = heads // kv_heads, 1.0 / math.sqrt(HEAD_DIM)
    greet([{"seq": lax.rem(me + step, count)} for step in range(1, count)])
    length = length_ref[0]
    query_pos = me * rows + lax.broadcasted_iota(jnp.int32, (rows, rows), 1)
    key_local = lax.broadcasted_iota(jnp.int32, (rows, rows), 0)
    dq_ref[...] = jnp.zeros_like(dq_ref)

    def key_block(j):
        key_pos = j * rows + key_local
        mask = (key_pos <= query_pos) & (key_pos < length)
        part_ref[...] = jnp.zeros_like(part_ref)
        key_rows = pl.ds(pl.multiple_of(j * rows, rows), rows)
        for g in range(kv_heads):
            key_cols = slice(g * HEAD_DIM, (g + 1) * HEAD_DIM)
            value_cols = slice(kv_width + g * HEAD_DIM, kv_width + (g + 1) * HEAD_DIM)

            def one_head(i, carry):
                h = g * group + i
                cols = pl.ds(pl.multiple_of(h * HEAD_DIM, HEAD_DIM), HEAD_DIM)
                keys, values = kv_ref[key_rows, key_cols], kv_ref[key_rows, value_cols]
                queries, grads = q_ref[:, cols], grad_ref[:, cols]
                scores = nt(keys, queries) * scale
                probs = jnp.where(mask, jnp.exp(scores - lse_ref[pl.ds(h, 1), :]), 0.0)
                prob_grad = nt(values, grads)
                score_grad = (probs * (prob_grad - delta_ref[pl.ds(h, 1), :])).astype(BF16)
                part_ref[:, key_cols] += nn(score_grad, queries)
                part_ref[:, value_cols] += nn(probs.astype(BF16), grads)
                dq_ref[:, cols] += tn(score_grad, keys)
                return carry

            lax.fori_loop(0, group, one_head, 0)
        part_ref[:, :kv_width] = part_ref[:, :kv_width] * scale

    def to_owner(j):
        return pltpu.make_async_remote_copy(
            src_ref=leaving.at[j],
            dst_ref=arriving.at[me],
            send_sem=send.at[j],
            recv_sem=recv.at[me],
            device_id={"seq": j},
            device_id_type=MESH_IDS,
        )

    def other_block(j, carry):
        key_block(j)
        leaving[j] = part_ref[...].astype(BF16)
        to_owner(j).start()
        return carry

    lax.fori_loop(0, me, other_block, 0)
    key_block(me)
    part_ref[...] = part_ref[...].astype(BF16).astype(F32)
    cosines, sines = cos_ref[...], -sin_ref[...]

    def one_query(h, carry):
        cols = pl.ds(pl.multiple_of(h * HEAD_DIM, HEAD_DIM), HEAD_DIM)
        out_ref[:, cols] = rotate(dq_ref[:, cols] * scale, cosines, sines).astype(BF16)
        return carry

    lax.fori_loop(0, heads, one_query, 0)

    def add_arrived(m, carry):
        pltpu.make_async_remote_copy(
            src_ref=leaving.at[m],
            dst_ref=arriving.at[m],
            send_sem=send.at[m],
            recv_sem=recv.at[m],
            device_id={"seq": m},
            device_id_type=MESH_IDS,
        ).wait_recv()
        part_ref[...] += arriving[m].astype(F32)
        return carry

    lax.fori_loop(me + 1, count, add_arrived, 0)
    first = heads * HEAD_DIM
    for g in range(kv_heads):
        cols = slice(g * HEAD_DIM, (g + 1) * HEAD_DIM)
        out_ref[:, first + g * HEAD_DIM : first + (g + 1) * HEAD_DIM] = rotate(
            part_ref[:, cols], cosines, sines
        ).astype(BF16)
    out_ref[:, first + kv_width :] = part_ref[:, kv_width:].astype(BF16)

    def sent(j, carry):
        to_owner(j).wait_send()
        return carry

    lax.fori_loop(0, me, sent, 0)


def attention_back(length, queries, kv_all, grads, lse, delta, cosines, sines, collective_id):
    count = lax.axis_size("seq")
    rows, q_width = queries.shape
    kv_width = kv_all.shape[1] // 2
    heads, kv_heads = q_width // HEAD_DIM, kv_width // HEAD_DIM
    vmem = pl.BlockSpec(memory_space=pltpu.VMEM)
    return pl.pallas_call(
        functools.partial(attention_back_kernel, count, heads, kv_heads),
        out_shape=jax.ShapeDtypeStruct((rows, q_width + 2 * kv_width), BF16),
        in_specs=[pl.BlockSpec(memory_space=pltpu.SMEM)] + [vmem] * 7,
        out_specs=vmem,
        scratch_shapes=[
            pltpu.VMEM((rows, q_width), F32),
            pltpu.VMEM((rows, 2 * kv_width), F32),
            pltpu.VMEM((count, rows, 2 * kv_width), BF16),
            pltpu.VMEM((count, rows, 2 * kv_width), BF16),
            pltpu.SemaphoreType.DMA((count,)),
            pltpu.SemaphoreType.DMA((count,)),
        ],
        compiler_params=pltpu.CompilerParams(
            collective_id=collective_id, vmem_limit_bytes=30 << 20
        ),
        cost_estimate=pl.CostEstimate(
            flops=10 * count * rows * rows * q_width, bytes_accessed=1 << 20, transcendentals=0
        ),
        name="attention_backward",
    )(length, queries, kv_all, grads, lse, delta, cosines, sines)


def seq_permutes(block_for):
    count, me = lax.axis_size("seq"), lax.axis_index("seq")
    pieces = [block_for(me)]
    for step in range(1, count):
        ring = [(i, (i + step) % count) for i in range(count)]
        pieces.append(lax.ppermute(block_for(lax.rem(me + step, count)), "seq", ring))
    return pieces


def in_seq_order(pieces, dtype):
    count, me = len(pieces), lax.axis_index("seq")
    whole = jnp.zeros((count,) + pieces[0].shape, dtype)
    for step, piece in enumerate(pieces):
        place = lax.rem(me + count - step, count)
        whole = lax.dynamic_update_index_in_dim(whole, piece.astype(dtype), place, 0)
    return whole


def on_device(
    hidden_in,
    lengths,
    routes,
    gates,
    priority,
    attn_gain,
    mlp_gain,
    w_query,
    key_projection,
    value_projection,
    w_out,
    w_gate,
    w_up,
    w_down,
    cotangent,
):
    rows = hidden_in.shape[1]
    width = hidden_in.shape[2]
    dp_count = lax.axis_size("dp")
    seq_count = lax.axis_size("seq")
    devices = dp_count * seq_count
    own_experts = w_gate.shape[0]
    sharers = seq_count // own_experts
    hidden_units = w_gate.shape[2]
    my_seq = lax.axis_index("seq")
    extent = rows * seq_count
    query_pos = my_seq * rows + jnp.arange(rows, dtype=jnp.int32)
    key_pos = jnp.arange(extent, dtype=jnp.int32)
    length = lengths[0]
    is_valid = query_pos < length
    score_scale = 1.0 / math.sqrt(HEAD_DIM)
    q_width = w_query.shape[1]
    kv_width = key_projection.shape[1]
    q_heads = q_width // HEAD_DIM
    kv_heads = kv_width // HEAD_DIM
    group_size = q_heads // kv_heads
    cosine_lookup, sine_lookup = rope_angles(query_pos, HEAD_DIM)

    gain_block = jnp.concatenate(
        [attn_gain[:, None], mlp_gain[:, None], jnp.zeros((attn_gain.shape[0], LANES - 2), BF16)],
        axis=1,
    )
    packed = jnp.concatenate([w_query, key_projection, value_projection], axis=1)
    staged = seq_count == 4 and w_query.shape[0] % 16 == 0

    def expert_pieces(weights):
        def block_for(peer):
            return lax.dynamic_index_in_dim(weights, peer // sharers, 0, keepdims=False)

        return seq_permutes(block_for)

    gate_parts = expert_pieces(w_gate)
    if staged:
        packed_full, gains_full, out_full = staged_gather(
            [packed, gain_block, w_out], [], None, 2, "gather_attention_weights"
        )
    else:
        packed_full = lax.all_gather(packed, BOTH, axis=0, tiled=True)
        gains_full = lax.all_gather(gain_block, BOTH, axis=0, tiled=True)
        out_full = lax.all_gather(w_out, BOTH, axis=0, tiled=True)

    pair_routes, place, kept = claim_places(routes[0], priority[0, 0], is_valid)
    holder = (pair_routes // own_experts) * seq_count + (pair_routes % own_experts) * sharers
    holder = holder + my_seq * sharers // seq_count
    slots = devices * CAP
    target = jnp.where(kept, holder * CAP + place, slots).reshape(rows, TOP)
    slot_ids = jnp.arange(slots, dtype=jnp.int32)
    hits = target[:, :, None] == slot_ids[None, None, :]
    gate_rows = gates[0]
    token_hot = jnp.any(hits, axis=1).astype(BF16)
    slot_gate = jnp.sum(jnp.where(hits, gate_rows[:, :, None], 0.0), axis=(0, 1))

    live_cotangent = jnp.where(is_valid[:, None], cotangent[0], jnp.zeros((), BF16))
    out_grad = live_cotangent.astype(F32)
    grad_send = (tn(token_hot, live_cotangent) * slot_gate[:, None]).astype(BF16)
    packed_full, gains_full, out_full, gate_parts, grad_send = lax.optimization_barrier(
        (packed_full, gains_full, out_full, gate_parts, grad_send)
    )
    gain_one, gain_two = gains_full[:, 0].astype(F32), gains_full[:, 1].astype(F32)
    grad_rows = swap(grad_send.reshape(devices, CAP, width), ("dp", "seq")).reshape(slots, width)

    inputs = hidden_in[0].astype(F32)
    scale_one = lax.rsqrt(jnp.mean(inputs * inputs, axis=-1, keepdims=True) + EPSILON)
    normed = (inputs * scale_one * gain_one).astype(BF16)
    projected = nn(normed, packed_full)
    query_rows = projected[:, :q_width]
    key_matrix_rows = projected[:, q_width : q_width + kv_width]
    value_matrix_rows = projected[:, q_width + kv_width : q_width + 2 * kv_width].astype(BF16)
    query_rotated = apply_rotary(
        query_rows.reshape(rows, q_heads, HEAD_DIM), cosine_lookup, sine_lookup
    ).astype(BF16)
    key_rotated = apply_rotary(
        key_matrix_rows.reshape(rows, kv_heads, HEAD_DIM), cosine_lookup, sine_lookup
    ).astype(BF16)
    key_rotated = key_rotated.reshape(rows, kv_width)
    kv_mine = jnp.concatenate([key_rotated, value_matrix_rows], axis=1)
    kv_all = seq_spread(kv_mine, 8, 1, "gather_keys").reshape(extent, 2 * kv_width)
    kv_all, w_up, w_down = lax.optimization_barrier((kv_all, w_up, w_down))
    up_parts, down_parts = expert_pieces(w_up), expert_pieces(w_down)
    key_all, value_all = kv_all[:, :kv_width], kv_all[:, kv_width:]
    query_head_groups = query_rotated.reshape(rows, kv_heads, group_size, HEAD_DIM).transpose(
        1, 0, 2, 3
    )
    key_heads, value_heads = split_heads(key_all, kv_heads), split_heads(value_all, kv_heads)
    attended, log_total = lax.map(
        lambda operands: head_forward(
            operands[0], operands[1], operands[2], query_pos, key_pos, length, score_scale
        ),
        (query_head_groups, key_heads, value_heads),
    )
    attended = attended.transpose(1, 0, 2, 3).reshape(rows, q_width).astype(BF16)
    middle = inputs + nn(attended, out_full)
    scale_two = lax.rsqrt(jnp.mean(middle * middle, axis=-1, keepdims=True) + EPSILON)
    moe_input = (middle * scale_two * gain_two).astype(BF16)

    send_rows = tn(token_hot, moe_input).astype(BF16).reshape(devices, CAP, width)
    send_rows, grad_rows, up_parts = lax.optimization_barrier((send_rows, grad_rows, up_parts))
    slot_rows = swap(send_rows, ("dp", "seq")).reshape(slots, width)
    gate_full = in_seq_order(gate_parts, BF16).reshape(width, hidden_units)
    up_full = in_seq_order(up_parts, BF16).reshape(width, hidden_units)
    down_full = in_seq_order(down_parts, BF16).reshape(hidden_units, width)
    slot_rows, gate_full, up_full, down_full = lax.optimization_barrier(
        (slot_rows, gate_full, up_full, down_full)
    )
    gate_pre = nn(slot_rows, gate_full)
    up_pre = nn(slot_rows, up_full)
    gate_sigmoid = jax.nn.sigmoid(gate_pre)
    gate_act = gate_pre * gate_sigmoid
    gate_slope = gate_sigmoid * (1.0 + gate_pre * (1.0 - gate_sigmoid))
    expert_hidden = (gate_act * up_pre).astype(BF16)
    hidden_grad = nt(grad_rows, down_full)
    gate_pre_grad = (hidden_grad * up_pre * gate_slope).astype(BF16)
    up_pre_grad = (hidden_grad * gate_act).astype(BF16)
    row_grad = (nt(gate_pre_grad, gate_full) + nt(up_pre_grad, up_full)).astype(BF16)
    row_back = swap(row_grad.reshape(devices, CAP, width), ("dp", "seq")).reshape(slots, width)

    gate_grad = tn(slot_rows, gate_pre_grad).astype(BF16)
    up_grad = tn(slot_rows, up_pre_grad).astype(BF16)
    down_grad = tn(expert_hidden, grad_rows).astype(BF16)

    def to_owners(grad):
        grad = grad.reshape(seq_count, -1, grad.shape[1])

        def block_for(peer):
            return lax.dynamic_index_in_dim(grad, peer, 0, keepdims=False)

        return seq_permutes(block_for)

    def owned_sum(pieces):
        whole = in_seq_order(pieces, F32)
        return jnp.sum(whole.reshape((own_experts, sharers) + whole.shape[1:]), axis=1)

    gate_grad_parts, up_grad_parts = to_owners(gate_grad), to_owners(up_grad)
    row_back, down_grad = lax.optimization_barrier((row_back, down_grad))
    down_grad_parts = to_owners(down_grad)
    expert_out = nn(expert_hidden, down_full).astype(BF16)
    expert_out, row_back = lax.optimization_barrier((expert_out, row_back))
    returned = swap(expert_out.reshape(devices, CAP, width), ("dp", "seq")).reshape(slots, width)
    moe_input_grad = nn(token_hot, row_back)
    middle_norm_grad, gain_two_grad = norm_back(middle, scale_two, gain_two, moe_input_grad)
    middle_grad = out_grad + middle_norm_grad
    branch_grad = middle_grad.astype(BF16)
    out_terms = tn(attended, branch_grad).astype(BF16)
    attended_grad = nt(branch_grad, out_full).astype(BF16)
    attended_grad, out_terms = lax.optimization_barrier((attended_grad, out_terms))
    delta = attended_grad.astype(F32) * attended.astype(F32)
    delta = jnp.sum(delta.reshape(rows, q_heads, HEAD_DIM), axis=-1).T
    cosines, sines = cosine_lookup[:, 0], sine_lookup[:, 0]
    projected_grad = attention_back(
        lengths,
        query_rotated.reshape(rows, q_width),
        kv_all,
        attended_grad,
        log_total.reshape(q_heads, rows),
        delta,
        jnp.concatenate([cosines, cosines], axis=1),
        jnp.concatenate([-sines, sines], axis=1),
        4,
    )
    normed_grad = nt(projected_grad, packed_full)
    input_norm_grad, gain_one_grad = norm_back(inputs, scale_one, gain_one, normed_grad)
    input_grad = middle_grad + input_norm_grad

    lane = lax.broadcasted_iota(jnp.int32, (width, LANES), 1)
    gain_terms = jnp.where(lane == 0, gain_one_grad[:, None], gain_two_grad[:, None])
    gain_terms = jnp.where(lane < 2, gain_terms, 0.0).astype(BF16)
    projected_grad, down_grad_parts = lax.optimization_barrier((projected_grad, down_grad_parts))
    query_terms = tn(normed, projected_grad).astype(BF16)
    grad_parts = [gate_grad_parts, up_grad_parts, down_grad_parts]
    if staged:
        out_owned, gains_owned, owned = staged_scatter(
            [out_terms, gain_terms, query_terms], [], None, 6, "scatter_attention_grads"
        )
    else:
        terms = jnp.concatenate([out_terms, gain_terms, query_terms], axis=1)
        terms = lax.psum_scatter(terms, BOTH, scatter_dimension=0, tiled=True).astype(F32)
        out_owned, gains_owned = terms[:, :width], terms[:, width : width + LANES]
        owned = terms[:, width + LANES :]
    returned, owned = lax.optimization_barrier((returned, owned))
    expert_grads = [owned_sum(parts) for parts in grad_parts]

    gate_hot = jnp.sum(jnp.where(hits, gate_rows[:, :, None], 0.0), axis=1).astype(BF16)
    layer_out = middle + nn(gate_hot, returned)
    return (
        layer_out[None],
        input_grad[None],
        gains_owned[:, 0],
        gains_owned[:, 1],
        owned[:, :q_width],
        owned[:, q_width : q_width + kv_width],
        owned[:, q_width + kv_width : q_width + 2 * kv_width],
        out_owned,
        *expert_grads,
    )


def solution(mesh):
    part = P("dp", "seq", None)
    both = P(BOTH)
    both_rows = P(BOTH, None)
    return jax.shard_map(
        on_device,
        mesh=mesh,
        in_specs=(part, P("dp"), part, part, part, both, both)
        + (both_rows,) * 4
        + (part,) * 4,
        out_specs=(part, part, both, both) + (both_rows,) * 4 + (part,) * 3,
        check_vma=False,
    )
```

```python
import functools
import math

import jax
import jax.numpy as jnp
from jax import lax
from jax.experimental import pallas as pl
from jax.experimental.pallas import tpu as pltpu
from jax.sharding import PartitionSpec as P

HEAD_DIM = 128
EXPERTS = 32
TOP = 4
CAP = 40
EARLY = 16

EPSILON = 1e-06
ROPE_BASE = 10000.0
NEG_FILL = -1e30
LANES = 128
BOTH = ("seq", "dp")
BF16 = jnp.bfloat16
F32 = jnp.float32


def rope_angles(positions, head_size):
    half_dim = head_size // 2
    frequency = ROPE_BASE ** (-(2.0 * jnp.arange(half_dim, dtype=F32)) / head_size)
    angles = positions.astype(F32)[:, None] * frequency[None, :]
    return (jnp.cos(angles)[:, None, :], jnp.sin(angles)[:, None, :])


def apply_rotary(values, cosine_lookup, sine_lookup):
    half_dim = values.shape[-1] // 2
    lower_half = values[..., :half_dim]
    upper_half = values[..., half_dim:]
    return jnp.concatenate(
        [
            lower_half * cosine_lookup - upper_half * sine_lookup,
            upper_half * cosine_lookup + lower_half * sine_lookup,
        ],
        axis=-1,
    )


def dot(left, right, contract):
    return lax.dot_general(left, right, (contract, ((), ())), preferred_element_type=F32)


def nn(left, right):
    return dot(left, right, ((1,), (0,)))


def nt(left, right):
    return dot(left, right, ((1,), (1,)))


def tn(left, right):
    return dot(left, right, ((0,), (0,)))


def claim_places(routes, priority, is_valid):
    pair_routes = routes.reshape(-1)
    live = jnp.repeat(is_valid, TOP)
    key = jnp.where(live, pair_routes, -1)
    earlier = (key[None, :] == pair_routes[:, None]) & (priority[None, :] < priority[:, None])
    place = jnp.sum(earlier.astype(F32), axis=1).astype(jnp.int32)
    return pair_routes, place, live & (place < CAP)


def masked_scores(query_group, key_head, query_pos, key_pos, length, score_scale):
    scores = (
        jnp.einsum("qgd,kd->gqk", query_group, key_head, preferred_element_type=F32) * score_scale
    )
    key_mask = (key_pos[None, :] <= query_pos[:, None]) & (key_pos[None, :] < length)
    return jnp.where(key_mask[None], scores, NEG_FILL)


def head_forward(query_group, key_head, value_head, query_pos, key_pos, length, score_scale):
    scores = masked_scores(query_group, key_head, query_pos, key_pos, length, score_scale)
    row_max = jnp.max(scores, axis=-1, keepdims=True)
    exp_scores = jnp.exp(scores - row_max)
    exp_total = jnp.sum(exp_scores, axis=-1, keepdims=True)
    attn_probs = (exp_scores / exp_total).astype(BF16)
    head_out = jnp.einsum("gqk,kd->qgd", attn_probs, value_head, preferred_element_type=F32)
    return (head_out, (row_max + jnp.log(exp_total))[..., 0])


def norm_back(values, scale_rows, gain_vec, incoming):
    weighted = incoming * gain_vec
    inner_mean = jnp.mean(weighted * values, axis=-1, keepdims=True)
    values_grad = scale_rows * weighted - values * scale_rows * scale_rows * scale_rows * inner_mean
    return (values_grad, jnp.sum(incoming * values * scale_rows, axis=0))


def split_heads(gathered, kv_heads):
    return gathered.reshape(gathered.shape[0], kv_heads, HEAD_DIM).transpose(1, 0, 2)


def swap(blocks, axes):
    return lax.all_to_all(blocks, axes, split_axis=0, concat_axis=0, tiled=True)


MESH_IDS = pl.DeviceIdType.MESH


def torus_place():
    seq, dp = lax.axis_index("seq"), lax.axis_index("dp")
    return seq // 2, seq % 2, dp // 2, dp % 2


def torus_id(a, b, z, c):
    return {"seq": 2 * a + b, "dp": 2 * z + c}


def torus_peers(line):
    a, b, z, c = torus_place()
    peers = [torus_id(a, b, z, 1 - c), torus_id(a, 1 - b, z, c), torus_id(1 - a, b, z, c)]
    peers.append(torus_id(1 - a, 1 - b, z, c))
    return peers + [torus_id(a, b, lax.rem(z + k, line), c) for k in range(1, line)]


def greet(peers):
    barrier = pltpu.get_barrier_semaphore()
    for peer in peers:
        pl.semaphore_signal(barrier, inc=1, device_id=peer, device_id_type=MESH_IDS)
    pl.semaphore_wait(barrier, len(peers))


def column_chunks(widths, parts):
    chunks = []
    for part in range(parts):
        for k, whole in enumerate(widths):
            tiles = whole // LANES
            first, end = tiles * part // parts, tiles * (part + 1) // parts
            if end > first:
                chunks.append((k, first * LANES, (end - first) * LANES))
    return chunks


def remote(src, dst, sems, i, j, device_id):
    send, recv = sems
    return pltpu.make_async_remote_copy(
        src_ref=src,
        dst_ref=dst,
        send_sem=send.at[i, j],
        recv_sem=recv.at[i, j],
        device_id=device_id,
        device_id_type=MESH_IDS,
    )


def start_exchange(count, sources, targets, block_of, sems):
    send_sems, recv_sems, local_sems = sems
    me = lax.axis_index("seq")
    copies = []
    for i, source in enumerate(sources):
        for step in range(1, count):
            peer = lax.rem(me + step, count)
            copies.append(
                pltpu.make_async_remote_copy(
                    src_ref=block_of(source, peer),
                    dst_ref=targets[i].at[me],
                    send_sem=send_sems.at[i, step - 1],
                    recv_sem=recv_sems.at[i, step - 1],
                    device_id={"seq": peer},
                    device_id_type=MESH_IDS,
                )
            )
        copies.append(
            pltpu.make_async_copy(block_of(source, me), targets[i].at[me], local_sems.at[i])
        )
    for copy in copies:
        copy.start()
    return copies


def exchange_sems(n, count):
    return [
        pltpu.SemaphoreType.DMA((n, count - 1)),
        pltpu.SemaphoreType.DMA((n, count - 1)),
        pltpu.SemaphoreType.DMA((n,)),
    ]


def in_steps(count, stages, after=None):
    for step in range((count + 1) // 2 + len(stages) - 1):
        if after is not None and step == (count + 1) // 2 + 1:
            after()
        for behind, stage in enumerate(stages):
            for i in (2 * (step - behind), 2 * (step - behind) + 1):
                if 0 <= i < count:
                    stage(i)


def gather_kernel(line, chunks, n, extras, block_of, *refs):
    sources, more_sources = refs[:n], refs[n : n + extras]
    refs = refs[n + extras :]
    targets, more_targets = refs[:n], refs[n : n + extras]
    send, recv, local, *more_sems = refs[n + extras :]
    sems = (send, recv)
    a, b, z, c = torus_place()
    greet(torus_peers(line))
    more = start_exchange(4, more_sources, more_targets, block_of, more_sems) if extras else []
    sent = []

    def start(copy):
        copy.start()
        sent.append(copy)
        return copy

    along_line, first_hop, second_hop, third_hop = {}, {}, {}, {}

    def send_line(i):
        k, first, size = chunks[i]
        cols = pl.ds(first, size)
        own = targets[k].at[a, b, z, c, :, cols]
        keep = pltpu.make_async_copy(sources[k].at[:, cols], own, local.at[i])
        keep.start()
        along_line[i] = [
            start(
                remote(
                    sources[k].at[:, cols],
                    own,
                    sems,
                    i,
                    2 + step,
                    torus_id(a, b, lax.rem(z + step, line), c),
                )
            )
            for step in range(1, line)
        ]
        along_line[i].append(keep)

    def send_first(i):
        k, first, size = chunks[i]
        *copies, keep = along_line[i]
        keep.wait()
        for copy in copies:
            copy.wait_recv()
        block = targets[k].at[a, b, :, c, :, pl.ds(first, size)]
        peer = torus_id(a, 1 - b, z, c) if i % 2 == 0 else torus_id(1 - a, b, z, c)
        first_hop[i] = start(remote(block, block, sems, i, 1, peer))

    def send_second(i):
        k, first, size = chunks[i]
        first_hop[i].wait_recv()
        cols = pl.ds(first, size)
        if i % 2 == 0:
            block, peer = targets[k].at[a, :, :, c, :, cols], torus_id(1 - a, b, z, c)
        else:
            block, peer = targets[k].at[:, b, :, c, :, cols], torus_id(a, 1 - b, z, c)
        second_hop[i] = start(remote(block, block, sems, i, 2, peer))

    def send_third(i):
        k, first, size = chunks[i]
        second_hop[i].wait_recv()
        block = targets[k].at[:, :, :, c, :, pl.ds(first, size)]
        third_hop[i] = start(remote(block, block, sems, i, 0, torus_id(a, b, z, 1 - c)))

    in_steps(len(chunks), [send_line, send_first, send_second, send_third])
    for copy in third_hop.values():
        copy.wait_recv()
    for copy in sent:
        copy.wait_send()
    for copy in more:
        copy.wait()


def staged_gather(arrays, extras, block_of, collective_id, name, parts=6):
    seq_count, line = lax.axis_size("seq"), lax.axis_size("dp") // 2
    rows, n = arrays[0].shape[0], len(arrays)
    chunks = column_chunks([x.shape[1] for x in arrays], parts)
    m = len(chunks)
    shape = (seq_count // 2, 2, line, 2, rows)
    size = sum(x.shape[1] for x in arrays) * rows * 64
    count = n + len(extras)
    outs = pl.pallas_call(
        functools.partial(gather_kernel, line, chunks, n, len(extras), block_of),
        out_shape=[jax.ShapeDtypeStruct(shape + (x.shape[1],), BF16) for x in arrays]
        + [jax.ShapeDtypeStruct((seq_count,) + x.shape[1:], BF16) for x in extras],
        in_specs=[pl.BlockSpec(memory_space=pl.ANY)] * count,
        out_specs=[pl.BlockSpec(memory_space=pl.ANY)] * count,
        scratch_shapes=[
            pltpu.SemaphoreType.DMA((m, 2 + line)),
            pltpu.SemaphoreType.DMA((m, 2 + line)),
            pltpu.SemaphoreType.DMA((m,)),
        ]
        + (exchange_sems(len(extras), seq_count) if extras else []),
        compiler_params=pltpu.CompilerParams(
            collective_id=collective_id, vmem_limit_bytes=4 << 20
        ),
        cost_estimate=pl.CostEstimate(flops=0, bytes_accessed=size, transcendentals=0),
        name=name,
    )(*arrays, *extras)
    return [o.reshape(-1, o.shape[-1]) for o in outs]


def scatter_kernel(line, chunks, n, extras, block_of, *refs):
    m = len(chunks)
    sources, more_sources = refs[:n], refs[n : n + extras]
    refs = refs[n + extras :]
    targets, more_targets = refs[:n], refs[n : n + extras]
    scratch = refs[n + extras :]
    owns, ins1, accs2, ins2, accs3, ins3, ins4 = (scratch[m * s : m * (s + 1)] for s in range(7))
    send, recv, local, *more_sems = scratch[7 * m :]
    sems = (send, recv)
    a, b, z, c = torus_place()
    greet(torus_peers(line))
    sent = []

    def start(copy):
        copy.start()
        sent.append(copy)
        return copy

    def add_lines(target, left, right):
        def one(j, carry):
            target[j] = (left[j].astype(F32) + right[j].astype(F32)).astype(BF16)
            return carry

        lax.fori_loop(0, line, one, 0)

    between_cores, first_hop, second_hop, along_line = {}, {}, {}, {}

    def send_core(i):
        k, first, size = chunks[i]
        cols = pl.ds(first, size)
        keep = pltpu.make_async_copy(sources[k].at[:, :, :, c, :, cols], owns[i], local.at[i])
        keep.start()
        swap_core = remote(
            sources[k].at[:, :, :, 1 - c, :, cols], ins1[i], sems, i, 0, torus_id(a, b, z, 1 - c)
        )
        between_cores[i] = (keep, start(swap_core))

    def send_first(i):
        keep, copy = between_cores[i]
        keep.wait()
        copy.wait_recv()
        for p in range(2):
            for q in range(2):
                add_lines(owns[i].at[p, q], owns[i].at[p, q], ins1[i].at[p, q])
        if i % 2 == 0:
            block, peer = owns[i].at[:, 1 - b], torus_id(a, 1 - b, z, c)
        else:
            block, peer = owns[i].at[1 - a], torus_id(1 - a, b, z, c)
        first_hop[i] = start(remote(block, ins2[i], sems, i, 1, peer))

    def send_second(i):
        first_hop[i].wait_recv()
        for p in range(2):
            mine = owns[i].at[p, b] if i % 2 == 0 else owns[i].at[a, p]
            add_lines(accs2[i].at[p], mine, ins2[i].at[p])
        if i % 2 == 0:
            block, peer = accs2[i].at[1 - a], torus_id(1 - a, b, z, c)
        else:
            block, peer = accs2[i].at[1 - b], torus_id(a, 1 - b, z, c)
        second_hop[i] = start(remote(block, ins3[i], sems, i, 2, peer))

    def send_line(i):
        second_hop[i].wait_recv()
        add_lines(accs3[i], accs2[i].at[a if i % 2 == 0 else b], ins3[i])
        copies = []
        for step in range(1, line):
            to = lax.rem(z + step, line)
            peer = torus_id(a, b, to, c)
            copies.append(start(remote(accs3[i].at[to], ins4[i].at[z], sems, i, 2 + step, peer)))
        along_line[i] = copies

    def finish(i):
        k, first, size = chunks[i]
        total = accs3[i][z].astype(F32)
        for step in range(1, line):
            along_line[i][step - 1].wait_recv()
            total = total + ins4[i][lax.rem(z + line - step, line)].astype(F32)
        targets[k][:, first : first + size] = total

    more = []

    def send_more():
        if extras:
            more.extend(start_exchange(4, more_sources, more_targets, block_of, more_sems))

    in_steps(m, [send_core, send_first, send_second, send_line, finish], send_more)
    for copy in sent:
        copy.wait_send()
    for copy in more:
        copy.wait()


def staged_scatter(arrays, extras, block_of, collective_id, name, parts=6):
    seq_count, line = lax.axis_size("seq"), lax.axis_size("dp") // 2
    rows, n = arrays[0].shape[0] // (2 * line * seq_count), len(arrays)
    chunks = column_chunks([x.shape[1] for x in arrays], parts)
    m = len(chunks)
    leads = [(2, 2, line), (2, 2, line), (2, line), (2, line), (line,), (line,), (line,)]
    size = sum(x.shape[1] for x in arrays) * rows * 64
    anywhere = pl.BlockSpec(memory_space=pl.ANY)
    return pl.pallas_call(
        functools.partial(scatter_kernel, line, chunks, n, len(extras), block_of),
        out_shape=[jax.ShapeDtypeStruct((rows, x.shape[1]), F32) for x in arrays]
        + [jax.ShapeDtypeStruct((seq_count,) + x.shape[1:], BF16) for x in extras],
        in_specs=[anywhere] * (n + len(extras)),
        out_specs=[pl.BlockSpec(memory_space=pltpu.VMEM)] * n + [anywhere] * len(extras),
        scratch_shapes=[
            pltpu.VMEM(lead + (rows, width), BF16) for lead in leads for _, _, width in chunks
        ]
        + [
            pltpu.SemaphoreType.DMA((m, 2 + line)),
            pltpu.SemaphoreType.DMA((m, 2 + line)),
            pltpu.SemaphoreType.DMA((m,)),
        ]
        + (exchange_sems(len(extras), seq_count) if extras else []),
        compiler_params=pltpu.CompilerParams(
            collective_id=collective_id, vmem_limit_bytes=36 << 20
        ),
        cost_estimate=pl.CostEstimate(flops=0, bytes_accessed=size, transcendentals=0),
        name=name,
    )(*[x.reshape(2, 2, line, 2, rows, x.shape[1]) for x in arrays], *extras)


def spread_kernel(count, parts, source, target, *sems):
    me = lax.axis_index("seq")
    greet([{"seq": lax.rem(me + step, count)} for step in range(1, count)])
    size = source.shape[0] // parts
    pieces = [pl.ds(part * size, size) for part in range(parts)]
    sources = [source.at[piece] for piece in pieces]
    targets = [target.at[:, piece] for piece in pieces]
    for copy in start_exchange(count, sources, targets, lambda ref, peer: ref, sems):
        copy.wait()


def seq_spread(array, parts, collective_id, name):
    count = lax.axis_size("seq")
    return pl.pallas_call(
        functools.partial(spread_kernel, count, parts),
        out_shape=jax.ShapeDtypeStruct((count,) + array.shape, BF16),
        in_specs=[pl.BlockSpec(memory_space=pl.ANY)],
        out_specs=pl.BlockSpec(memory_space=pl.ANY),
        scratch_shapes=exchange_sems(parts, count),
        compiler_params=pltpu.CompilerParams(
            collective_id=collective_id, vmem_limit_bytes=4 << 20
        ),
        cost_estimate=pl.CostEstimate(
            flops=0, bytes_accessed=2 * count * array.size, transcendentals=0
        ),
        name=name,
    )(array)


def rotate(values, cosines, sines):
    return values * cosines + pltpu.roll(values, HEAD_DIM // 2, 1) * sines


def attention_back_kernel(count, heads, kv_heads, *refs):
    length_ref, q_ref, kv_ref, grad_ref, lse_ref, delta_ref, cos_ref, sin_ref, out_ref = refs[:9]
    dq_ref, part_ref, leaving, arriving, send, recv = refs[9:]
    me = lax.axis_index("seq")
    rows, kv_width = q_ref.shape[0], kv_heads * HEAD_DIM
    group, scale = heads // kv_heads, 1.0 / math.sqrt(HEAD_DIM)
    greet([{"seq": lax.rem(me + step, count)} for step in range(1, count)])
    length = length_ref[0]
    query_pos = me * rows + lax.broadcasted_iota(jnp.int32, (rows, rows), 1)
    key_local = lax.broadcasted_iota(jnp.int32, (rows, rows), 0)
    dq_ref[...] = jnp.zeros_like(dq_ref)

    def key_block(j):
        key_pos = j * rows + key_local
        mask = (key_pos <= query_pos) & (key_pos < length)
        part_ref[...] = jnp.zeros_like(part_ref)
        key_rows = pl.ds(pl.multiple_of(j * rows, rows), rows)
        for g in range(kv_heads):
            key_cols = slice(g * HEAD_DIM, (g + 1) * HEAD_DIM)
            value_cols = slice(kv_width + g * HEAD_DIM, kv_width + (g + 1) * HEAD_DIM)

            def one_head(i, carry):
                h = g * group + i
                cols = pl.ds(pl.multiple_of(h * HEAD_DIM, HEAD_DIM), HEAD_DIM)
                keys, values = kv_ref[key_rows, key_cols], kv_ref[key_rows, value_cols]
                queries, grads = q_ref[:, cols], grad_ref[:, cols]
                scores = nt(keys, queries) * scale
                probs = jnp.where(mask, jnp.exp(scores - lse_ref[pl.ds(h, 1), :]), 0.0)
                prob_grad = nt(values, grads)
                score_grad = (probs * (prob_grad - delta_ref[pl.ds(h, 1), :])).astype(BF16)
                part_ref[:, key_cols] += nn(score_grad, queries)
                part_ref[:, value_cols] += nn(probs.astype(BF16), grads)
                dq_ref[:, cols] += tn(score_grad, keys)
                return carry

            lax.fori_loop(0, group, one_head, 0, unroll=3)
        part_ref[:, :kv_width] = part_ref[:, :kv_width] * scale

    def to_owner(j):
        return pltpu.make_async_remote_copy(
            src_ref=leaving.at[j],
            dst_ref=arriving.at[me],
            send_sem=send.at[j],
            recv_sem=recv.at[me],
            device_id={"seq": j},
            device_id_type=MESH_IDS,
        )

    def other_block(j, carry):
        key_block(j)
        leaving[j] = part_ref[...].astype(BF16)
        to_owner(j).start()
        return carry

    lax.fori_loop(0, me, other_block, 0)
    key_block(me)
    part_ref[...] = part_ref[...].astype(BF16).astype(F32)
    cosines, sines = cos_ref[...], -sin_ref[...]

    def one_query(h, carry):
        cols = pl.ds(pl.multiple_of(h * HEAD_DIM, HEAD_DIM), HEAD_DIM)
        out_ref[:, cols] = rotate(dq_ref[:, cols] * scale, cosines, sines).astype(BF16)
        return carry

    lax.fori_loop(0, heads, one_query, 0)

    def add_arrived(m, carry):
        pltpu.make_async_remote_copy(
            src_ref=leaving.at[m],
            dst_ref=arriving.at[m],
            send_sem=send.at[m],
            recv_sem=recv.at[m],
            device_id={"seq": m},
            device_id_type=MESH_IDS,
        ).wait_recv()
        part_ref[...] += arriving[m].astype(F32)
        return carry

    lax.fori_loop(me + 1, count, add_arrived, 0)
    first = heads * HEAD_DIM
    for g in range(kv_heads):
        cols = slice(g * HEAD_DIM, (g + 1) * HEAD_DIM)
        out_ref[:, first + g * HEAD_DIM : first + (g + 1) * HEAD_DIM] = rotate(
            part_ref[:, cols], cosines, sines
        ).astype(BF16)
    out_ref[:, first + kv_width :] = part_ref[:, kv_width:].astype(BF16)

    def sent(j, carry):
        to_owner(j).wait_send()
        return carry

    lax.fori_loop(0, me, sent, 0)


def attention_back(length, queries, kv_all, grads, lse, delta, cosines, sines, collective_id):
    count = lax.axis_size("seq")
    rows, q_width = queries.shape
    kv_width = kv_all.shape[1] // 2
    heads, kv_heads = q_width // HEAD_DIM, kv_width // HEAD_DIM
    vmem = pl.BlockSpec(memory_space=pltpu.VMEM)
    return pl.pallas_call(
        functools.partial(attention_back_kernel, count, heads, kv_heads),
        out_shape=jax.ShapeDtypeStruct((rows, q_width + 2 * kv_width), BF16),
        in_specs=[pl.BlockSpec(memory_space=pltpu.SMEM)] + [vmem] * 7,
        out_specs=vmem,
        scratch_shapes=[
            pltpu.VMEM((rows, q_width), F32),
            pltpu.VMEM((rows, 2 * kv_width), F32),
            pltpu.VMEM((count, rows, 2 * kv_width), BF16),
            pltpu.VMEM((count, rows, 2 * kv_width), BF16),
            pltpu.SemaphoreType.DMA((count,)),
            pltpu.SemaphoreType.DMA((count,)),
        ],
        compiler_params=pltpu.CompilerParams(
            collective_id=collective_id, vmem_limit_bytes=30 << 20
        ),
        cost_estimate=pl.CostEstimate(
            flops=10 * count * rows * rows * q_width, bytes_accessed=1 << 20, transcendentals=0
        ),
        name="attention_backward",
    )(length, queries, kv_all, grads, lse, delta, cosines, sines)


def seq_permutes(block_for):
    count, me = lax.axis_size("seq"), lax.axis_index("seq")
    pieces = [block_for(me)]
    for step in range(1, count):
        ring = [(i, (i + step) % count) for i in range(count)]
        pieces.append(lax.ppermute(block_for(lax.rem(me + step, count)), "seq", ring))
    return pieces


def in_seq_order(pieces, dtype):
    count, me = len(pieces), lax.axis_index("seq")
    whole = jnp.zeros((count,) + pieces[0].shape, dtype)
    for step, piece in enumerate(pieces):
        place = lax.rem(me + count - step, count)
        whole = lax.dynamic_update_index_in_dim(whole, piece.astype(dtype), place, 0)
    return whole


def on_device(
    hidden_in,
    lengths,
    routes,
    gates,
    priority,
    attn_gain,
    mlp_gain,
    w_query,
    key_projection,
    value_projection,
    w_out,
    w_gate,
    w_up,
    w_down,
    cotangent,
):
    rows = hidden_in.shape[1]
    width = hidden_in.shape[2]
    dp_count = lax.axis_size("dp")
    seq_count = lax.axis_size("seq")
    devices = dp_count * seq_count
    own_experts = w_gate.shape[0]
    sharers = seq_count // own_experts
    hidden_units = w_gate.shape[2]
    my_seq = lax.axis_index("seq")
    extent = rows * seq_count
    query_pos = my_seq * rows + jnp.arange(rows, dtype=jnp.int32)
    key_pos = jnp.arange(extent, dtype=jnp.int32)
    length = lengths[0]
    is_valid = query_pos < length
    score_scale = 1.0 / math.sqrt(HEAD_DIM)
    q_width = w_query.shape[1]
    kv_width = key_projection.shape[1]
    q_heads = q_width // HEAD_DIM
    kv_heads = kv_width // HEAD_DIM
    group_size = q_heads // kv_heads
    cosine_lookup, sine_lookup = rope_angles(query_pos, HEAD_DIM)

    gain_block = jnp.concatenate(
        [attn_gain[:, None], mlp_gain[:, None], jnp.zeros((attn_gain.shape[0], LANES - 2), BF16)],
        axis=1,
    )
    packed = jnp.concatenate([w_query, key_projection, value_projection], axis=1)
    staged = seq_count == 4 and w_query.shape[0] % 16 == 0

    def expert_pieces(weights):
        def block_for(peer):
            return lax.dynamic_index_in_dim(weights, peer // sharers, 0, keepdims=False)

        return seq_permutes(block_for)

    gate_parts = expert_pieces(w_gate)
    if staged:
        packed_full, gains_full, out_full = staged_gather(
            [packed, gain_block, w_out], [], None, 2, "gather_attention_weights"
        )
    else:
        packed_full = lax.all_gather(packed, BOTH, axis=0, tiled=True)
        gains_full = lax.all_gather(gain_block, BOTH, axis=0, tiled=True)
        out_full = lax.all_gather(w_out, BOTH, axis=0, tiled=True)

    pair_routes, place, kept = claim_places(routes[0], priority[0, 0], is_valid)
    holder = (pair_routes // own_experts) * seq_count + (pair_routes % own_experts) * sharers
    holder = holder + my_seq * sharers // seq_count
    slots = devices * CAP
    target = jnp.where(kept, holder * CAP + place, slots).reshape(rows, TOP)
    slot_ids = jnp.arange(slots, dtype=jnp.int32)
    hits = target[:, :, None] == slot_ids[None, None, :]
    gate_rows = gates[0]
    token_hot = jnp.any(hits, axis=1).astype(BF16)

    def hot_of(first, size):
        mine = kept & (place >= first) & (place < first + size)
        spot = jnp.where(mine, holder * size + place - first, slots).reshape(rows, TOP)
        ids = jnp.arange(devices * size, dtype=jnp.int32)
        return jnp.any(spot[:, :, None] == ids[None, None, :], axis=1).astype(BF16)

    early_hot, late_hot = hot_of(0, EARLY), hot_of(EARLY, CAP - EARLY)
    slot_gate = jnp.sum(jnp.where(hits, gate_rows[:, :, None], 0.0), axis=(0, 1))

    live_cotangent = jnp.where(is_valid[:, None], cotangent[0], jnp.zeros((), BF16))
    out_grad = live_cotangent.astype(F32)
    grad_send = (tn(token_hot, live_cotangent) * slot_gate[:, None]).astype(BF16)
    packed_full, gains_full, out_full, gate_parts, grad_send = lax.optimization_barrier(
        (packed_full, gains_full, out_full, gate_parts, grad_send)
    )
    gain_one, gain_two = gains_full[:, 0].astype(F32), gains_full[:, 1].astype(F32)
    grad_rows = swap(grad_send.reshape(devices, CAP, width), ("dp", "seq"))

    inputs = hidden_in[0].astype(F32)
    scale_one = lax.rsqrt(jnp.mean(inputs * inputs, axis=-1, keepdims=True) + EPSILON)
    normed = (inputs * scale_one * gain_one).astype(BF16)
    projected = nn(normed, packed_full)
    query_rows = projected[:, :q_width]
    key_matrix_rows = projected[:, q_width : q_width + kv_width]
    value_matrix_rows = projected[:, q_width + kv_width : q_width + 2 * kv_width].astype(BF16)
    query_rotated = apply_rotary(
        query_rows.reshape(rows, q_heads, HEAD_DIM), cosine_lookup, sine_lookup
    ).astype(BF16)
    key_rotated = apply_rotary(
        key_matrix_rows.reshape(rows, kv_heads, HEAD_DIM), cosine_lookup, sine_lookup
    ).astype(BF16)
    key_rotated = key_rotated.reshape(rows, kv_width)
    kv_mine = jnp.concatenate([key_rotated, value_matrix_rows], axis=1)
    kv_all = seq_spread(kv_mine, 8, 1, "gather_keys").reshape(extent, 2 * kv_width)
    kv_all, w_up, w_down = lax.optimization_barrier((kv_all, w_up, w_down))
    up_parts, down_parts = expert_pieces(w_up), expert_pieces(w_down)
    key_all, value_all = kv_all[:, :kv_width], kv_all[:, kv_width:]
    query_head_groups = query_rotated.reshape(rows, kv_heads, group_size, HEAD_DIM).transpose(
        1, 0, 2, 3
    )
    key_heads, value_heads = split_heads(key_all, kv_heads), split_heads(value_all, kv_heads)
    attended, log_total = lax.map(
        lambda operands: head_forward(
            operands[0], operands[1], operands[2], query_pos, key_pos, length, score_scale
        ),
        (query_head_groups, key_heads, value_heads),
    )
    attended = attended.transpose(1, 0, 2, 3).reshape(rows, q_width).astype(BF16)
    middle = inputs + nn(attended, out_full)
    scale_two = lax.rsqrt(jnp.mean(middle * middle, axis=-1, keepdims=True) + EPSILON)
    moe_input = (middle * scale_two * gain_two).astype(BF16)

    def to_experts(hot):
        return tn(hot, moe_input).astype(BF16).reshape(devices, -1, width)

    early_send, late_send = to_experts(early_hot), to_experts(late_hot)
    query_flat = query_rotated.reshape(rows, q_width)
    early_send, late_send, grad_rows, up_parts, query_flat, attended = lax.optimization_barrier(
        (early_send, late_send, grad_rows, up_parts, query_flat, attended)
    )
    early_rows = swap(early_send, ("dp", "seq"))
    early_rows, late_send = lax.optimization_barrier((early_rows, late_send))
    late_rows = swap(late_send, ("dp", "seq"))
    gate_full = in_seq_order(gate_parts, BF16).reshape(width, hidden_units)
    up_full = in_seq_order(up_parts, BF16).reshape(width, hidden_units)
    down_full = in_seq_order(down_parts, BF16).reshape(hidden_units, width)
    early_grads, late_grads = grad_rows[:, :EARLY], grad_rows[:, EARLY:]
    early_rows, gate_full, up_full, down_full, early_grads, late_grads = (
        lax.optimization_barrier(
            (early_rows, gate_full, up_full, down_full, early_grads, late_grads)
        )
    )

    def run_expert(slot_rows, grads):
        blocks = slot_rows.shape[:2]
        slot_rows, grads = slot_rows.reshape(-1, width), grads.reshape(-1, width)
        gate_pre = nn(slot_rows, gate_full)
        up_pre = nn(slot_rows, up_full)
        gate_sigmoid = jax.nn.sigmoid(gate_pre)
        gate_act = gate_pre * gate_sigmoid
        gate_slope = gate_sigmoid * (1.0 + gate_pre * (1.0 - gate_sigmoid))
        hidden = (gate_act * up_pre).astype(BF16)
        hidden_grad = nt(grads, down_full)
        gate_pre_grad = (hidden_grad * up_pre * gate_slope).astype(BF16)
        up_pre_grad = (hidden_grad * gate_act).astype(BF16)
        row_grad = (nt(gate_pre_grad, gate_full) + nt(up_pre_grad, up_full)).astype(BF16)
        return [x.reshape(blocks + (-1,)) for x in (hidden, gate_pre_grad, up_pre_grad, row_grad)]

    *early_terms, early_row_grad = run_expert(early_rows, early_grads)
    late_rows, early_row_grad = lax.optimization_barrier((late_rows, early_row_grad))
    early_back = swap(early_row_grad, ("dp", "seq"))
    *late_terms, late_row_grad = run_expert(late_rows, late_grads)
    slot_rows, expert_hidden, gate_pre_grad, up_pre_grad = (
        jnp.concatenate(both, axis=1).reshape(slots, -1)
        for both in zip([early_rows, *early_terms], [late_rows, *late_terms], strict=True)
    )
    gate_grad = tn(slot_rows, gate_pre_grad).astype(BF16)
    up_grad = tn(slot_rows, up_pre_grad).astype(BF16)
    early_back, late_row_grad, gate_grad, up_grad = lax.optimization_barrier(
        (early_back, late_row_grad, gate_grad, up_grad)
    )
    late_back = swap(late_row_grad, ("dp", "seq"))
    down_grad = tn(expert_hidden, grad_rows.reshape(slots, width)).astype(BF16)

    def to_owners(grad):
        grad = grad.reshape(seq_count, -1, grad.shape[1])

        def block_for(peer):
            return lax.dynamic_index_in_dim(grad, peer, 0, keepdims=False)

        return seq_permutes(block_for)

    def owned_sum(pieces):
        whole = in_seq_order(pieces, F32)
        return jnp.sum(whole.reshape((own_experts, sharers) + whole.shape[1:]), axis=1)

    gate_owned, up_owned = owned_sum(to_owners(gate_grad)), owned_sum(to_owners(up_grad))
    expert_out = nn(expert_hidden, down_full).astype(BF16)
    expert_out, late_back, gate_owned, up_owned, down_grad = lax.optimization_barrier(
        (expert_out, late_back, gate_owned, up_owned, down_grad)
    )
    returned = swap(expert_out.reshape(devices, CAP, width), ("dp", "seq")).reshape(slots, width)
    early_back, late_back = early_back.reshape(-1, width), late_back.reshape(-1, width)
    moe_input_grad = nn(early_hot, early_back) + nn(late_hot, late_back)
    middle_norm_grad, gain_two_grad = norm_back(middle, scale_two, gain_two, moe_input_grad)
    middle_grad = out_grad + middle_norm_grad
    branch_grad = middle_grad.astype(BF16)
    out_terms = tn(attended, branch_grad).astype(BF16)
    attended_grad = nt(branch_grad, out_full).astype(BF16)
    attended_grad, out_terms = lax.optimization_barrier((attended_grad, out_terms))
    delta = attended_grad.astype(F32) * attended.astype(F32)
    delta = jnp.sum(delta.reshape(rows, q_heads, HEAD_DIM), axis=-1).T
    cosines, sines = cosine_lookup[:, 0], sine_lookup[:, 0]
    projected_grad = attention_back(
        lengths,
        query_flat,
        kv_all,
        attended_grad,
        log_total.reshape(q_heads, rows),
        delta,
        jnp.concatenate([cosines, cosines], axis=1),
        jnp.concatenate([-sines, sines], axis=1),
        4,
    )
    normed_grad = nt(projected_grad, packed_full)
    input_norm_grad, gain_one_grad = norm_back(inputs, scale_one, gain_one, normed_grad)
    input_grad = middle_grad + input_norm_grad

    lane = lax.broadcasted_iota(jnp.int32, (width, LANES), 1)
    gain_terms = jnp.where(lane == 0, gain_one_grad[:, None], gain_two_grad[:, None])
    gain_terms = jnp.where(lane < 2, gain_terms, 0.0).astype(BF16)
    query_terms = tn(normed, projected_grad).astype(BF16)
    if staged:
        out_owned, gains_owned, owned, down_owned = staged_scatter(
            [out_terms, gain_terms, query_terms],
            [down_grad.reshape(seq_count, -1, width)],
            lambda ref, peer: ref.at[peer],
            6,
            "scatter_attention_grads",
        )
        down_owned = down_owned.astype(F32)
    else:
        terms = jnp.concatenate([out_terms, gain_terms, query_terms], axis=1)
        terms = lax.psum_scatter(terms, BOTH, scatter_dimension=0, tiled=True).astype(F32)
        out_owned, gains_owned = terms[:, :width], terms[:, width : width + LANES]
        owned = terms[:, width + LANES :]
        down_owned = owned_sum(to_owners(down_grad))
    returned, owned = lax.optimization_barrier((returned, owned))
    expert_grads = [gate_owned, up_owned, down_owned]

    gate_hot = jnp.sum(jnp.where(hits, gate_rows[:, :, None], 0.0), axis=1).astype(BF16)
    layer_out = middle + nn(gate_hot, returned)
    return (
        layer_out[None],
        input_grad[None],
        gains_owned[:, 0],
        gains_owned[:, 1],
        owned[:, :q_width],
        owned[:, q_width : q_width + kv_width],
        owned[:, q_width + kv_width : q_width + 2 * kv_width],
        out_owned,
        *expert_grads,
    )


def solution(mesh):
    part = P("dp", "seq", None)
    both = P(BOTH)
    both_rows = P(BOTH, None)
    return jax.shard_map(
        on_device,
        mesh=mesh,
        in_specs=(part, P("dp"), part, part, part, both, both)
        + (both_rows,) * 4
        + (part,) * 4,
        out_specs=(part, part, both, both) + (both_rows,) * 4 + (part,) * 3,
        check_vma=False,
    )
```

```python
import functools
import math

import jax
import jax.numpy as jnp
from jax import lax
from jax.experimental import pallas as pl
from jax.experimental.pallas import tpu as pltpu
from jax.sharding import PartitionSpec as P

HEAD_DIM = 128
EXPERTS = 32
TOP = 4
CAP = 40
EARLY = 16

EPSILON = 1e-06
ROPE_BASE = 10000.0
NEG_FILL = -1e30
LANES = 128
BOTH = ("seq", "dp")
BF16 = jnp.bfloat16
F32 = jnp.float32


def rope_angles(positions, head_size):
    half_dim = head_size // 2
    frequency = ROPE_BASE ** (-(2.0 * jnp.arange(half_dim, dtype=F32)) / head_size)
    angles = positions.astype(F32)[:, None] * frequency[None, :]
    return (jnp.cos(angles)[:, None, :], jnp.sin(angles)[:, None, :])


def apply_rotary(values, cosine_lookup, sine_lookup):
    half_dim = values.shape[-1] // 2
    lower_half = values[..., :half_dim]
    upper_half = values[..., half_dim:]
    return jnp.concatenate(
        [
            lower_half * cosine_lookup - upper_half * sine_lookup,
            upper_half * cosine_lookup + lower_half * sine_lookup,
        ],
        axis=-1,
    )


def dot(left, right, contract):
    return lax.dot_general(left, right, (contract, ((), ())), preferred_element_type=F32)


def nn(left, right):
    return dot(left, right, ((1,), (0,)))


def nt(left, right):
    return dot(left, right, ((1,), (1,)))


def tn(left, right):
    return dot(left, right, ((0,), (0,)))


def claim_places(routes, priority, is_valid):
    pair_routes = routes.reshape(-1)
    live = jnp.repeat(is_valid, TOP)
    key = jnp.where(live, pair_routes, -1)
    earlier = (key[None, :] == pair_routes[:, None]) & (priority[None, :] < priority[:, None])
    place = jnp.sum(earlier.astype(F32), axis=1).astype(jnp.int32)
    return pair_routes, place, live & (place < CAP)


def masked_scores(query_group, key_head, query_pos, key_pos, length, score_scale):
    scores = (
        jnp.einsum("qgd,kd->gqk", query_group, key_head, preferred_element_type=F32) * score_scale
    )
    key_mask = (key_pos[None, :] <= query_pos[:, None]) & (key_pos[None, :] < length)
    return jnp.where(key_mask[None], scores, NEG_FILL)


def head_forward(query_group, key_head, value_head, query_pos, key_pos, length, score_scale):
    scores = masked_scores(query_group, key_head, query_pos, key_pos, length, score_scale)
    row_max = jnp.max(scores, axis=-1, keepdims=True)
    exp_scores = jnp.exp(scores - row_max)
    exp_total = jnp.sum(exp_scores, axis=-1, keepdims=True)
    attn_probs = (exp_scores / exp_total).astype(BF16)
    head_out = jnp.einsum("gqk,kd->qgd", attn_probs, value_head, preferred_element_type=F32)
    return (head_out, (row_max + jnp.log(exp_total))[..., 0])


def norm_back(values, scale_rows, gain_vec, incoming):
    weighted = incoming * gain_vec
    inner_mean = jnp.mean(weighted * values, axis=-1, keepdims=True)
    values_grad = scale_rows * weighted - values * scale_rows * scale_rows * scale_rows * inner_mean
    return (values_grad, jnp.sum(incoming * values * scale_rows, axis=0))


def split_heads(gathered, kv_heads):
    return gathered.reshape(gathered.shape[0], kv_heads, HEAD_DIM).transpose(1, 0, 2)


def swap(blocks, axes):
    return lax.all_to_all(blocks, axes, split_axis=0, concat_axis=0, tiled=True)


MESH_IDS = pl.DeviceIdType.MESH


def torus_place():
    seq, dp = lax.axis_index("seq"), lax.axis_index("dp")
    return seq // 2, seq % 2, dp // 2, dp % 2


def torus_id(a, b, z, c):
    return {"seq": 2 * a + b, "dp": 2 * z + c}


def torus_peers(line):
    a, b, z, c = torus_place()
    peers = [torus_id(a, b, z, 1 - c), torus_id(a, 1 - b, z, c), torus_id(1 - a, b, z, c)]
    peers.append(torus_id(1 - a, 1 - b, z, c))
    return peers + [torus_id(a, b, lax.rem(z + k, line), c) for k in range(1, line)]


def greet(peers):
    barrier = pltpu.get_barrier_semaphore()
    for peer in peers:
        pl.semaphore_signal(barrier, inc=1, device_id=peer, device_id_type=MESH_IDS)
    pl.semaphore_wait(barrier, len(peers))


def column_chunks(widths, parts):
    chunks = []
    for part in range(parts):
        for k, whole in enumerate(widths):
            tiles = whole // LANES
            first, end = tiles * part // parts, tiles * (part + 1) // parts
            if end > first:
                chunks.append((k, first * LANES, (end - first) * LANES))
    return chunks


def remote(src, dst, sems, i, j, device_id):
    send, recv = sems
    return pltpu.make_async_remote_copy(
        src_ref=src,
        dst_ref=dst,
        send_sem=send.at[i, j],
        recv_sem=recv.at[i, j],
        device_id=device_id,
        device_id_type=MESH_IDS,
    )


def start_exchange(count, sources, targets, block_of, sems):
    send_sems, recv_sems, local_sems = sems
    me = lax.axis_index("seq")
    copies = []
    for i, source in enumerate(sources):
        for step in range(1, count):
            peer = lax.rem(me + step, count)
            copies.append(
                pltpu.make_async_remote_copy(
                    src_ref=block_of(source, peer),
                    dst_ref=targets[i].at[me],
                    send_sem=send_sems.at[i, step - 1],
                    recv_sem=recv_sems.at[i, step - 1],
                    device_id={"seq": peer},
                    device_id_type=MESH_IDS,
                )
            )
        copies.append(
            pltpu.make_async_copy(block_of(source, me), targets[i].at[me], local_sems.at[i])
        )
    for copy in copies:
        copy.start()
    return copies


def exchange_sems(n, count):
    return [
        pltpu.SemaphoreType.DMA((n, count - 1)),
        pltpu.SemaphoreType.DMA((n, count - 1)),
        pltpu.SemaphoreType.DMA((n,)),
    ]


def in_steps(count, stages, after=None):
    for step in range((count + 1) // 2 + len(stages) - 1):
        if after is not None and step == (count + 1) // 2 + 1:
            after()
        for behind, stage in enumerate(stages):
            for i in (2 * (step - behind), 2 * (step - behind) + 1):
                if 0 <= i < count:
                    stage(i)


def gather_kernel(line, chunks, n, extras, block_of, *refs):
    sources, more_sources = refs[:n], refs[n : n + extras]
    refs = refs[n + extras :]
    targets, more_targets = refs[:n], refs[n : n + extras]
    send, recv, local, *more_sems = refs[n + extras :]
    sems = (send, recv)
    a, b, z, c = torus_place()
    greet(torus_peers(line))
    more = start_exchange(4, more_sources, more_targets, block_of, more_sems) if extras else []
    sent = []

    def start(copy):
        copy.start()
        sent.append(copy)
        return copy

    along_line, first_hop, second_hop, third_hop = {}, {}, {}, {}

    def send_line(i):
        k, first, size = chunks[i]
        cols = pl.ds(first, size)
        own = targets[k].at[a, b, z, c, :, cols]
        keep = pltpu.make_async_copy(sources[k].at[:, cols], own, local.at[i])
        keep.start()
        along_line[i] = [
            start(
                remote(
                    sources[k].at[:, cols],
                    own,
                    sems,
                    i,
                    2 + step,
                    torus_id(a, b, lax.rem(z + step, line), c),
                )
            )
            for step in range(1, line)
        ]
        along_line[i].append(keep)

    def send_first(i):
        k, first, size = chunks[i]
        *copies, keep = along_line[i]
        keep.wait()
        for copy in copies:
            copy.wait_recv()
        block = targets[k].at[a, b, :, c, :, pl.ds(first, size)]
        peer = torus_id(a, 1 - b, z, c) if i % 2 == 0 else torus_id(1 - a, b, z, c)
        first_hop[i] = start(remote(block, block, sems, i, 1, peer))

    def send_second(i):
        k, first, size = chunks[i]
        first_hop[i].wait_recv()
        cols = pl.ds(first, size)
        if i % 2 == 0:
            block, peer = targets[k].at[a, :, :, c, :, cols], torus_id(1 - a, b, z, c)
        else:
            block, peer = targets[k].at[:, b, :, c, :, cols], torus_id(a, 1 - b, z, c)
        second_hop[i] = start(remote(block, block, sems, i, 2, peer))

    def send_third(i):
        k, first, size = chunks[i]
        second_hop[i].wait_recv()
        block = targets[k].at[:, :, :, c, :, pl.ds(first, size)]
        third_hop[i] = start(remote(block, block, sems, i, 0, torus_id(a, b, z, 1 - c)))

    in_steps(len(chunks), [send_line, send_first, send_second, send_third])
    for copy in third_hop.values():
        copy.wait_recv()
    for copy in sent:
        copy.wait_send()
    for copy in more:
        copy.wait()


def staged_gather(arrays, extras, block_of, collective_id, name, parts=6):
    seq_count, line = lax.axis_size("seq"), lax.axis_size("dp") // 2
    rows, n = arrays[0].shape[0], len(arrays)
    chunks = column_chunks([x.shape[1] for x in arrays], parts)
    m = len(chunks)
    shape = (seq_count // 2, 2, line, 2, rows)
    size = sum(x.shape[1] for x in arrays) * rows * 64
    count = n + len(extras)
    outs = pl.pallas_call(
        functools.partial(gather_kernel, line, chunks, n, len(extras), block_of),
        out_shape=[jax.ShapeDtypeStruct(shape + (x.shape[1],), BF16) for x in arrays]
        + [jax.ShapeDtypeStruct((seq_count,) + x.shape[1:], BF16) for x in extras],
        in_specs=[pl.BlockSpec(memory_space=pl.ANY)] * count,
        out_specs=[pl.BlockSpec(memory_space=pl.ANY)] * count,
        scratch_shapes=[
            pltpu.SemaphoreType.DMA((m, 2 + line)),
            pltpu.SemaphoreType.DMA((m, 2 + line)),
            pltpu.SemaphoreType.DMA((m,)),
        ]
        + (exchange_sems(len(extras), seq_count) if extras else []),
        compiler_params=pltpu.CompilerParams(
            collective_id=collective_id, vmem_limit_bytes=4 << 20
        ),
        cost_estimate=pl.CostEstimate(flops=0, bytes_accessed=size, transcendentals=0),
        name=name,
    )(*arrays, *extras)
    return [o.reshape(-1, o.shape[-1]) for o in outs]


def scatter_kernel(line, chunks, n, extras, block_of, *refs):
    m = len(chunks)
    sources, more_sources = refs[:n], refs[n : n + extras]
    refs = refs[n + extras :]
    targets, more_targets = refs[:n], refs[n : n + extras]
    scratch = refs[n + extras :]
    owns, ins1, accs2, ins2, accs3, ins3, ins4 = (scratch[m * s : m * (s + 1)] for s in range(7))
    send, recv, local, *more_sems = scratch[7 * m :]
    sems = (send, recv)
    a, b, z, c = torus_place()
    greet(torus_peers(line))
    sent = []

    def start(copy):
        copy.start()
        sent.append(copy)
        return copy

    def add_lines(target, left, right):
        def one(j, carry):
            target[j] = (left[j].astype(F32) + right[j].astype(F32)).astype(BF16)
            return carry

        lax.fori_loop(0, line, one, 0)

    between_cores, first_hop, second_hop, along_line = {}, {}, {}, {}

    def send_core(i):
        k, first, size = chunks[i]
        cols = pl.ds(first, size)
        keep = pltpu.make_async_copy(sources[k].at[:, :, :, c, :, cols], owns[i], local.at[i])
        keep.start()
        swap_core = remote(
            sources[k].at[:, :, :, 1 - c, :, cols], ins1[i], sems, i, 0, torus_id(a, b, z, 1 - c)
        )
        between_cores[i] = (keep, start(swap_core))

    def send_first(i):
        keep, copy = between_cores[i]
        keep.wait()
        copy.wait_recv()
        for p in range(2):
            for q in range(2):
                add_lines(owns[i].at[p, q], owns[i].at[p, q], ins1[i].at[p, q])
        if i % 2 == 0:
            block, peer = owns[i].at[:, 1 - b], torus_id(a, 1 - b, z, c)
        else:
            block, peer = owns[i].at[1 - a], torus_id(1 - a, b, z, c)
        first_hop[i] = start(remote(block, ins2[i], sems, i, 1, peer))

    def send_second(i):
        first_hop[i].wait_recv()
        for p in range(2):
            mine = owns[i].at[p, b] if i % 2 == 0 else owns[i].at[a, p]
            add_lines(accs2[i].at[p], mine, ins2[i].at[p])
        if i % 2 == 0:
            block, peer = accs2[i].at[1 - a], torus_id(1 - a, b, z, c)
        else:
            block, peer = accs2[i].at[1 - b], torus_id(a, 1 - b, z, c)
        second_hop[i] = start(remote(block, ins3[i], sems, i, 2, peer))

    def send_line(i):
        second_hop[i].wait_recv()
        add_lines(accs3[i], accs2[i].at[a if i % 2 == 0 else b], ins3[i])
        copies = []
        for step in range(1, line):
            to = lax.rem(z + step, line)
            peer = torus_id(a, b, to, c)
            copies.append(start(remote(accs3[i].at[to], ins4[i].at[z], sems, i, 2 + step, peer)))
        along_line[i] = copies

    def finish(i):
        k, first, size = chunks[i]
        total = accs3[i][z].astype(F32)
        for step in range(1, line):
            along_line[i][step - 1].wait_recv()
            total = total + ins4[i][lax.rem(z + line - step, line)].astype(F32)
        targets[k][:, first : first + size] = total

    more = []

    def send_more():
        if extras:
            more.extend(start_exchange(4, more_sources, more_targets, block_of, more_sems))

    in_steps(m, [send_core, send_first, send_second, send_line, finish], send_more)
    for copy in sent:
        copy.wait_send()
    for copy in more:
        copy.wait()


def staged_scatter(arrays, extras, block_of, collective_id, name, parts=6):
    seq_count, line = lax.axis_size("seq"), lax.axis_size("dp") // 2
    rows, n = arrays[0].shape[0] // (2 * line * seq_count), len(arrays)
    chunks = column_chunks([x.shape[1] for x in arrays], parts)
    m = len(chunks)
    leads = [(2, 2, line), (2, 2, line), (2, line), (2, line), (line,), (line,), (line,)]
    size = sum(x.shape[1] for x in arrays) * rows * 64
    anywhere = pl.BlockSpec(memory_space=pl.ANY)
    return pl.pallas_call(
        functools.partial(scatter_kernel, line, chunks, n, len(extras), block_of),
        out_shape=[jax.ShapeDtypeStruct((rows, x.shape[1]), F32) for x in arrays]
        + [jax.ShapeDtypeStruct((seq_count,) + x.shape[1:], BF16) for x in extras],
        in_specs=[anywhere] * (n + len(extras)),
        out_specs=[pl.BlockSpec(memory_space=pltpu.VMEM)] * n + [anywhere] * len(extras),
        scratch_shapes=[
            pltpu.VMEM(lead + (rows, width), BF16) for lead in leads for _, _, width in chunks
        ]
        + [
            pltpu.SemaphoreType.DMA((m, 2 + line)),
            pltpu.SemaphoreType.DMA((m, 2 + line)),
            pltpu.SemaphoreType.DMA((m,)),
        ]
        + (exchange_sems(len(extras), seq_count) if extras else []),
        compiler_params=pltpu.CompilerParams(
            collective_id=collective_id, vmem_limit_bytes=36 << 20
        ),
        cost_estimate=pl.CostEstimate(flops=0, bytes_accessed=size, transcendentals=0),
        name=name,
    )(*[x.reshape(2, 2, line, 2, rows, x.shape[1]) for x in arrays], *extras)


def spread_kernel(count, parts, source, target, *sems):
    me = lax.axis_index("seq")
    greet([{"seq": lax.rem(me + step, count)} for step in range(1, count)])
    size = source.shape[0] // parts
    pieces = [pl.ds(part * size, size) for part in range(parts)]
    sources = [source.at[piece] for piece in pieces]
    targets = [target.at[:, piece] for piece in pieces]
    for copy in start_exchange(count, sources, targets, lambda ref, peer: ref, sems):
        copy.wait()


def seq_spread(array, parts, collective_id, name):
    count = lax.axis_size("seq")
    return pl.pallas_call(
        functools.partial(spread_kernel, count, parts),
        out_shape=jax.ShapeDtypeStruct((count,) + array.shape, BF16),
        in_specs=[pl.BlockSpec(memory_space=pl.ANY)],
        out_specs=pl.BlockSpec(memory_space=pl.ANY),
        scratch_shapes=exchange_sems(parts, count),
        compiler_params=pltpu.CompilerParams(
            collective_id=collective_id, vmem_limit_bytes=4 << 20
        ),
        cost_estimate=pl.CostEstimate(
            flops=0, bytes_accessed=2 * count * array.size, transcendentals=0
        ),
        name=name,
    )(array)


def rotate(values, cosines, sines):
    return values * cosines + pltpu.roll(values, HEAD_DIM // 2, 1) * sines


def attention_back_kernel(count, heads, kv_heads, *refs):
    length_ref, q_ref, kv_ref, grad_ref, lse_ref, delta_ref, cos_ref, sin_ref, out_ref = refs[:9]
    dq_ref, part_ref, leaving, arriving, send, recv = refs[9:]
    me = lax.axis_index("seq")
    rows, kv_width = q_ref.shape[0], kv_heads * HEAD_DIM
    group, scale = heads // kv_heads, 1.0 / math.sqrt(HEAD_DIM)
    greet([{"seq": lax.rem(me + step, count)} for step in range(1, count)])
    length = length_ref[0]
    query_pos = me * rows + lax.broadcasted_iota(jnp.int32, (rows, rows), 1)
    key_local = lax.broadcasted_iota(jnp.int32, (rows, rows), 0)
    dq_ref[...] = jnp.zeros_like(dq_ref)

    def key_block(j):
        key_pos = j * rows + key_local
        mask = (key_pos <= query_pos) & (key_pos < length)
        part_ref[...] = jnp.zeros_like(part_ref)
        key_rows = pl.ds(pl.multiple_of(j * rows, rows), rows)
        for g in range(kv_heads):
            key_cols = slice(g * HEAD_DIM, (g + 1) * HEAD_DIM)
            value_cols = slice(kv_width + g * HEAD_DIM, kv_width + (g + 1) * HEAD_DIM)

            def one_head(i, carry):
                h = g * group + i
                cols = pl.ds(pl.multiple_of(h * HEAD_DIM, HEAD_DIM), HEAD_DIM)
                keys, values = kv_ref[key_rows, key_cols], kv_ref[key_rows, value_cols]
                queries, grads = q_ref[:, cols], grad_ref[:, cols]
                scores = nt(keys, queries) * scale
                probs = jnp.where(mask, jnp.exp(scores - lse_ref[pl.ds(h, 1), :]), 0.0)
                prob_grad = nt(values, grads)
                score_grad = (probs * (prob_grad - delta_ref[pl.ds(h, 1), :])).astype(BF16)
                part_ref[:, key_cols] += nn(score_grad, queries)
                part_ref[:, value_cols] += nn(probs.astype(BF16), grads)
                dq_ref[:, cols] += tn(score_grad, keys)
                return carry

            lax.fori_loop(0, group, one_head, 0, unroll=3)
        part_ref[:, :kv_width] = part_ref[:, :kv_width] * scale

    def to_owner(j):
        return pltpu.make_async_remote_copy(
            src_ref=leaving.at[j],
            dst_ref=arriving.at[me],
            send_sem=send.at[j],
            recv_sem=recv.at[me],
            device_id={"seq": j},
            device_id_type=MESH_IDS,
        )

    def other_block(j, carry):
        key_block(j)
        leaving[j] = part_ref[...].astype(BF16)
        to_owner(j).start()
        return carry

    lax.fori_loop(0, me, other_block, 0)
    key_block(me)
    part_ref[...] = part_ref[...].astype(BF16).astype(F32)
    cosines, sines = cos_ref[...], -sin_ref[...]

    def one_query(h, carry):
        cols = pl.ds(pl.multiple_of(h * HEAD_DIM, HEAD_DIM), HEAD_DIM)
        out_ref[:, cols] = rotate(dq_ref[:, cols] * scale, cosines, sines).astype(BF16)
        return carry

    lax.fori_loop(0, heads, one_query, 0)

    def add_arrived(m, carry):
        pltpu.make_async_remote_copy(
            src_ref=leaving.at[m],
            dst_ref=arriving.at[m],
            send_sem=send.at[m],
            recv_sem=recv.at[m],
            device_id={"seq": m},
            device_id_type=MESH_IDS,
        ).wait_recv()
        part_ref[...] += arriving[m].astype(F32)
        return carry

    lax.fori_loop(me + 1, count, add_arrived, 0)
    first = heads * HEAD_DIM
    for g in range(kv_heads):
        cols = slice(g * HEAD_DIM, (g + 1) * HEAD_DIM)
        out_ref[:, first + g * HEAD_DIM : first + (g + 1) * HEAD_DIM] = rotate(
            part_ref[:, cols], cosines, sines
        ).astype(BF16)
    out_ref[:, first + kv_width :] = part_ref[:, kv_width:].astype(BF16)

    def sent(j, carry):
        to_owner(j).wait_send()
        return carry

    lax.fori_loop(0, me, sent, 0)


def attention_back(length, queries, kv_all, grads, lse, delta, cosines, sines, collective_id):
    count = lax.axis_size("seq")
    rows, q_width = queries.shape
    kv_width = kv_all.shape[1] // 2
    heads, kv_heads = q_width // HEAD_DIM, kv_width // HEAD_DIM
    vmem = pl.BlockSpec(memory_space=pltpu.VMEM)
    return pl.pallas_call(
        functools.partial(attention_back_kernel, count, heads, kv_heads),
        out_shape=jax.ShapeDtypeStruct((rows, q_width + 2 * kv_width), BF16),
        in_specs=[pl.BlockSpec(memory_space=pltpu.SMEM)] + [vmem] * 7,
        out_specs=vmem,
        scratch_shapes=[
            pltpu.VMEM((rows, q_width), F32),
            pltpu.VMEM((rows, 2 * kv_width), F32),
            pltpu.VMEM((count, rows, 2 * kv_width), BF16),
            pltpu.VMEM((count, rows, 2 * kv_width), BF16),
            pltpu.SemaphoreType.DMA((count,)),
            pltpu.SemaphoreType.DMA((count,)),
        ],
        compiler_params=pltpu.CompilerParams(
            collective_id=collective_id, vmem_limit_bytes=30 << 20
        ),
        cost_estimate=pl.CostEstimate(
            flops=10 * count * rows * rows * q_width, bytes_accessed=1 << 20, transcendentals=0
        ),
        name="attention_backward",
    )(length, queries, kv_all, grads, lse, delta, cosines, sines)


def seq_permutes(block_for):
    count, me = lax.axis_size("seq"), lax.axis_index("seq")
    pieces = [block_for(me)]
    for step in range(1, count):
        ring = [(i, (i + step) % count) for i in range(count)]
        pieces.append(lax.ppermute(block_for(lax.rem(me + step, count)), "seq", ring))
    return pieces


def in_seq_order(pieces, dtype):
    count, me = len(pieces), lax.axis_index("seq")
    whole = jnp.zeros((count,) + pieces[0].shape, dtype)
    for step, piece in enumerate(pieces):
        place = lax.rem(me + count - step, count)
        whole = lax.dynamic_update_index_in_dim(whole, piece.astype(dtype), place, 0)
    return whole


def on_device(
    hidden_in,
    lengths,
    routes,
    gates,
    priority,
    attn_gain,
    mlp_gain,
    w_query,
    key_projection,
    value_projection,
    w_out,
    w_gate,
    w_up,
    w_down,
    cotangent,
):
    rows = hidden_in.shape[1]
    width = hidden_in.shape[2]
    dp_count = lax.axis_size("dp")
    seq_count = lax.axis_size("seq")
    devices = dp_count * seq_count
    own_experts = w_gate.shape[0]
    sharers = seq_count // own_experts
    hidden_units = w_gate.shape[2]
    my_seq = lax.axis_index("seq")
    extent = rows * seq_count
    query_pos = my_seq * rows + jnp.arange(rows, dtype=jnp.int32)
    key_pos = jnp.arange(extent, dtype=jnp.int32)
    length = lengths[0]
    is_valid = query_pos < length
    score_scale = 1.0 / math.sqrt(HEAD_DIM)
    q_width = w_query.shape[1]
    kv_width = key_projection.shape[1]
    q_heads = q_width // HEAD_DIM
    kv_heads = kv_width // HEAD_DIM
    group_size = q_heads // kv_heads
    cosine_lookup, sine_lookup = rope_angles(query_pos, HEAD_DIM)

    gain_block = jnp.concatenate(
        [attn_gain[:, None], mlp_gain[:, None], jnp.zeros((attn_gain.shape[0], LANES - 2), BF16)],
        axis=1,
    )
    packed = jnp.concatenate([w_query, key_projection, value_projection], axis=1)
    staged = seq_count == 4 and w_query.shape[0] % 16 == 0

    def expert_pieces(weights):
        def block_for(peer):
            return lax.dynamic_index_in_dim(weights, peer // sharers, 0, keepdims=False)

        return seq_permutes(block_for)

    gate_parts = expert_pieces(w_gate)
    if staged:
        packed_full, gains_full, out_full = staged_gather(
            [packed, gain_block, w_out], [], None, 2, "gather_attention_weights"
        )
    else:
        packed_full = lax.all_gather(packed, BOTH, axis=0, tiled=True)
        gains_full = lax.all_gather(gain_block, BOTH, axis=0, tiled=True)
        out_full = lax.all_gather(w_out, BOTH, axis=0, tiled=True)

    pair_routes, place, kept = claim_places(routes[0], priority[0, 0], is_valid)
    holder = (pair_routes // own_experts) * seq_count + (pair_routes % own_experts) * sharers
    holder = holder + my_seq * sharers // seq_count
    slots = devices * CAP
    target = jnp.where(kept, holder * CAP + place, slots).reshape(rows, TOP)
    slot_ids = jnp.arange(slots, dtype=jnp.int32)
    hits = target[:, :, None] == slot_ids[None, None, :]
    gate_rows = gates[0]
    token_hot = jnp.any(hits, axis=1).astype(BF16)

    def hot_of(first, size):
        mine = kept & (place >= first) & (place < first + size)
        spot = jnp.where(mine, holder * size + place - first, slots).reshape(rows, TOP)
        ids = jnp.arange(devices * size, dtype=jnp.int32)
        return jnp.any(spot[:, :, None] == ids[None, None, :], axis=1).astype(BF16)

    early_hot, late_hot = hot_of(0, EARLY), hot_of(EARLY, CAP - EARLY)
    slot_gate = jnp.sum(jnp.where(hits, gate_rows[:, :, None], 0.0), axis=(0, 1))

    live_cotangent = jnp.where(is_valid[:, None], cotangent[0], jnp.zeros((), BF16))
    out_grad = live_cotangent.astype(F32)
    grad_send = (tn(token_hot, live_cotangent) * slot_gate[:, None]).astype(BF16)
    packed_full, gains_full, out_full, gate_parts, grad_send = lax.optimization_barrier(
        (packed_full, gains_full, out_full, gate_parts, grad_send)
    )
    gain_one, gain_two = gains_full[:, 0].astype(F32), gains_full[:, 1].astype(F32)
    grad_rows = swap(grad_send.reshape(devices, CAP, width), ("dp", "seq"))

    inputs = hidden_in[0].astype(F32)
    scale_one = lax.rsqrt(jnp.mean(inputs * inputs, axis=-1, keepdims=True) + EPSILON)
    normed = (inputs * scale_one * gain_one).astype(BF16)
    projected = nn(normed, packed_full)
    query_rows = projected[:, :q_width]
    key_matrix_rows = projected[:, q_width : q_width + kv_width]
    value_matrix_rows = projected[:, q_width + kv_width : q_width + 2 * kv_width].astype(BF16)
    query_rotated = apply_rotary(
        query_rows.reshape(rows, q_heads, HEAD_DIM), cosine_lookup, sine_lookup
    ).astype(BF16)
    key_rotated = apply_rotary(
        key_matrix_rows.reshape(rows, kv_heads, HEAD_DIM), cosine_lookup, sine_lookup
    ).astype(BF16)
    key_rotated = key_rotated.reshape(rows, kv_width)
    kv_mine = jnp.concatenate([key_rotated, value_matrix_rows], axis=1)
    kv_all = seq_spread(kv_mine, 8, 1, "gather_keys").reshape(extent, 2 * kv_width)
    key_all, value_all = kv_all[:, :kv_width], kv_all[:, kv_width:]
    query_head_groups = query_rotated.reshape(rows, kv_heads, group_size, HEAD_DIM).transpose(
        1, 0, 2, 3
    )
    key_heads, value_heads = split_heads(key_all, kv_heads), split_heads(value_all, kv_heads)
    attended, log_total = lax.map(
        lambda operands: head_forward(
            operands[0], operands[1], operands[2], query_pos, key_pos, length, score_scale
        ),
        (query_head_groups, key_heads, value_heads),
    )
    attended = attended.transpose(1, 0, 2, 3).reshape(rows, q_width).astype(BF16)
    middle = inputs + nn(attended, out_full)
    scale_two = lax.rsqrt(jnp.mean(middle * middle, axis=-1, keepdims=True) + EPSILON)
    moe_input = (middle * scale_two * gain_two).astype(BF16)

    def to_experts(hot):
        return tn(hot, moe_input).astype(BF16).reshape(devices, -1, width)

    early_send, late_send = to_experts(early_hot), to_experts(late_hot)
    query_flat = query_rotated.reshape(rows, q_width)
    early_send, late_send, grad_rows, query_flat, attended, w_up, w_down = (
        lax.optimization_barrier(
            (early_send, late_send, grad_rows, query_flat, attended, w_up, w_down)
        )
    )
    up_parts, down_parts = expert_pieces(w_up), expert_pieces(w_down)
    early_rows = swap(early_send, ("dp", "seq"))
    early_rows, late_send = lax.optimization_barrier((early_rows, late_send))
    late_rows = swap(late_send, ("dp", "seq"))
    gate_full = in_seq_order(gate_parts, BF16).reshape(width, hidden_units)
    up_full = in_seq_order(up_parts, BF16).reshape(width, hidden_units)
    down_full = in_seq_order(down_parts, BF16).reshape(hidden_units, width)
    early_grads, late_grads = grad_rows[:, :EARLY], grad_rows[:, EARLY:]
    early_rows, gate_full, up_full, down_full, early_grads, late_grads = (
        lax.optimization_barrier(
            (early_rows, gate_full, up_full, down_full, early_grads, late_grads)
        )
    )

    def run_expert(slot_rows, grads):
        blocks = slot_rows.shape[:2]
        slot_rows, grads = slot_rows.reshape(-1, width), grads.reshape(-1, width)
        gate_pre = nn(slot_rows, gate_full)
        up_pre = nn(slot_rows, up_full)
        gate_sigmoid = jax.nn.sigmoid(gate_pre)
        gate_act = gate_pre * gate_sigmoid
        gate_slope = gate_sigmoid * (1.0 + gate_pre * (1.0 - gate_sigmoid))
        hidden = (gate_act * up_pre).astype(BF16)
        hidden_grad = nt(grads, down_full)
        gate_pre_grad = (hidden_grad * up_pre * gate_slope).astype(BF16)
        up_pre_grad = (hidden_grad * gate_act).astype(BF16)
        return [x.reshape(blocks + (-1,)) for x in (hidden, gate_pre_grad, up_pre_grad)]

    def row_grads(gate_pre_grad, up_pre_grad):
        blocks = gate_pre_grad.shape[:2]
        gate_pre_grad = gate_pre_grad.reshape(-1, hidden_units)
        up_pre_grad = up_pre_grad.reshape(-1, hidden_units)
        row_grad = (nt(gate_pre_grad, gate_full) + nt(up_pre_grad, up_full)).astype(BF16)
        return row_grad.reshape(blocks + (width,))

    def both_parts(early, late):
        return jnp.concatenate([early, late], axis=1).reshape(slots, -1)

    def to_owners(grad):
        grad = grad.reshape(seq_count, -1, grad.shape[1])

        def block_for(peer):
            return lax.dynamic_index_in_dim(grad, peer, 0, keepdims=False)

        return seq_permutes(block_for)

    def owned_sum(pieces):
        whole = in_seq_order(pieces, F32)
        return jnp.sum(whole.reshape((own_experts, sharers) + whole.shape[1:]), axis=1)

    early_hidden, *early_pre_grads = run_expert(early_rows, early_grads)
    early_row_grad = row_grads(*early_pre_grads)
    late_rows, early_row_grad = lax.optimization_barrier((late_rows, early_row_grad))
    early_back = swap(early_row_grad, ("dp", "seq"))
    late_hidden, *late_pre_grads = run_expert(late_rows, late_grads)
    expert_hidden = both_parts(early_hidden, late_hidden)
    down_grad = tn(expert_hidden, grad_rows.reshape(slots, width)).astype(BF16)
    late_rows, late_pre_grads, down_grad = lax.optimization_barrier(
        (late_rows, late_pre_grads, down_grad)
    )
    down_grad_parts = to_owners(down_grad)
    late_row_grad = row_grads(*late_pre_grads)
    early_back, late_row_grad, down_grad_parts = lax.optimization_barrier(
        (early_back, late_row_grad, down_grad_parts)
    )
    late_back = swap(late_row_grad, ("dp", "seq"))
    slot_rows = both_parts(early_rows, late_rows)
    gate_pre_grad, up_pre_grad = map(both_parts, early_pre_grads, late_pre_grads)
    gate_grad = tn(slot_rows, gate_pre_grad).astype(BF16)
    up_grad = tn(slot_rows, up_pre_grad).astype(BF16)
    gate_owned, up_owned = owned_sum(to_owners(gate_grad)), owned_sum(to_owners(up_grad))
    down_owned = owned_sum(down_grad_parts)
    expert_out = nn(expert_hidden, down_full).astype(BF16)
    expert_out, late_back, gate_owned, up_owned, down_owned = lax.optimization_barrier(
        (expert_out, late_back, gate_owned, up_owned, down_owned)
    )
    returned = swap(expert_out.reshape(devices, CAP, width), ("dp", "seq")).reshape(slots, width)
    early_back, late_back = early_back.reshape(-1, width), late_back.reshape(-1, width)
    moe_input_grad = nn(early_hot, early_back) + nn(late_hot, late_back)
    middle_norm_grad, gain_two_grad = norm_back(middle, scale_two, gain_two, moe_input_grad)
    middle_grad = out_grad + middle_norm_grad
    branch_grad = middle_grad.astype(BF16)
    out_terms = tn(attended, branch_grad).astype(BF16)
    attended_grad = nt(branch_grad, out_full).astype(BF16)
    attended_grad, out_terms = lax.optimization_barrier((attended_grad, out_terms))
    delta = attended_grad.astype(F32) * attended.astype(F32)
    delta = jnp.sum(delta.reshape(rows, q_heads, HEAD_DIM), axis=-1).T
    cosines, sines = cosine_lookup[:, 0], sine_lookup[:, 0]
    projected_grad = attention_back(
        lengths,
        query_flat,
        kv_all,
        attended_grad,
        log_total.reshape(q_heads, rows),
        delta,
        jnp.concatenate([cosines, cosines], axis=1),
        jnp.concatenate([-sines, sines], axis=1),
        4,
    )
    normed_grad = nt(projected_grad, packed_full)
    input_norm_grad, gain_one_grad = norm_back(inputs, scale_one, gain_one, normed_grad)
    input_grad = middle_grad + input_norm_grad

    lane = lax.broadcasted_iota(jnp.int32, (width, LANES), 1)
    gain_terms = jnp.where(lane == 0, gain_one_grad[:, None], gain_two_grad[:, None])
    gain_terms = jnp.where(lane < 2, gain_terms, 0.0).astype(BF16)
    query_terms = tn(normed, projected_grad).astype(BF16)
    if staged:
        out_owned, gains_owned, owned = staged_scatter(
            [out_terms, gain_terms, query_terms], [], None, 6, "scatter_attention_grads"
        )
    else:
        terms = jnp.concatenate([out_terms, gain_terms, query_terms], axis=1)
        terms = lax.psum_scatter(terms, BOTH, scatter_dimension=0, tiled=True).astype(F32)
        out_owned, gains_owned = terms[:, :width], terms[:, width : width + LANES]
        owned = terms[:, width + LANES :]
    returned, owned = lax.optimization_barrier((returned, owned))
    expert_grads = [gate_owned, up_owned, down_owned]

    gate_hot = jnp.sum(jnp.where(hits, gate_rows[:, :, None], 0.0), axis=1).astype(BF16)
    layer_out = middle + nn(gate_hot, returned)
    return (
        layer_out[None],
        input_grad[None],
        gains_owned[:, 0],
        gains_owned[:, 1],
        owned[:, :q_width],
        owned[:, q_width : q_width + kv_width],
        owned[:, q_width + kv_width : q_width + 2 * kv_width],
        out_owned,
        *expert_grads,
    )


def solution(mesh):
    part = P("dp", "seq", None)
    both = P(BOTH)
    both_rows = P(BOTH, None)
    return jax.shard_map(
        on_device,
        mesh=mesh,
        in_specs=(part, P("dp"), part, part, part, both, both)
        + (both_rows,) * 4
        + (part,) * 4,
        out_specs=(part, part, both, both) + (both_rows,) * 4 + (part,) * 3,
        check_vma=False,
    )
```

```python
import functools
import math

import jax
import jax.numpy as jnp
from jax import lax
from jax.experimental import pallas as pl
from jax.experimental.pallas import tpu as pltpu
from jax.sharding import PartitionSpec as P

HEAD_DIM = 128
EXPERTS = 32
TOP = 4
CAP = 40
EARLY = 16

EPSILON = 1e-06
ROPE_BASE = 10000.0
NEG_FILL = -1e30
LANES = 128
BOTH = ("seq", "dp")
BF16 = jnp.bfloat16
F32 = jnp.float32


def rope_angles(positions, head_size):
    half_dim = head_size // 2
    frequency = ROPE_BASE ** (-(2.0 * jnp.arange(half_dim, dtype=F32)) / head_size)
    angles = positions.astype(F32)[:, None] * frequency[None, :]
    return (jnp.cos(angles)[:, None, :], jnp.sin(angles)[:, None, :])


def dot(left, right, contract):
    return lax.dot_general(left, right, (contract, ((), ())), preferred_element_type=F32)


def nn(left, right):
    return dot(left, right, ((1,), (0,)))


def nt(left, right):
    return dot(left, right, ((1,), (1,)))


def tn(left, right):
    return dot(left, right, ((0,), (0,)))


def claim_places(routes, priority, is_valid):
    pair_routes = routes.reshape(-1)
    live = jnp.repeat(is_valid, TOP)
    key = jnp.where(live, pair_routes, -1)
    earlier = (key[None, :] == pair_routes[:, None]) & (priority[None, :] < priority[:, None])
    place = jnp.sum(earlier.astype(F32), axis=1).astype(jnp.int32)
    return pair_routes, place, live & (place < CAP)


def norm_back(values, scale_rows, gain_vec, incoming):
    weighted = incoming * gain_vec
    inner_mean = jnp.mean(weighted * values, axis=-1, keepdims=True)
    values_grad = scale_rows * weighted - values * scale_rows * scale_rows * scale_rows * inner_mean
    return (values_grad, jnp.sum(incoming * values * scale_rows, axis=0))


def swap(blocks, axes):
    return lax.all_to_all(blocks, axes, split_axis=0, concat_axis=0, tiled=True)


MESH_IDS = pl.DeviceIdType.MESH


def torus_place():
    seq, dp = lax.axis_index("seq"), lax.axis_index("dp")
    return seq // 2, seq % 2, dp // 2, dp % 2


def torus_id(a, b, z, c):
    return {"seq": 2 * a + b, "dp": 2 * z + c}


def torus_peers(line):
    a, b, z, c = torus_place()
    peers = [torus_id(a, b, z, 1 - c), torus_id(a, 1 - b, z, c), torus_id(1 - a, b, z, c)]
    peers.append(torus_id(1 - a, 1 - b, z, c))
    return peers + [torus_id(a, b, lax.rem(z + k, line), c) for k in range(1, line)]


def greet(peers):
    barrier = pltpu.get_barrier_semaphore()
    for peer in peers:
        pl.semaphore_signal(barrier, inc=1, device_id=peer, device_id_type=MESH_IDS)
    pl.semaphore_wait(barrier, len(peers))


def column_chunks(widths, parts):
    chunks = []
    for part in range(parts):
        for k, whole in enumerate(widths):
            tiles = whole // LANES
            first, end = tiles * part // parts, tiles * (part + 1) // parts
            if end > first:
                chunks.append((k, first * LANES, (end - first) * LANES))
    return chunks


def remote(src, dst, sems, i, j, device_id):
    send, recv = sems
    return pltpu.make_async_remote_copy(
        src_ref=src,
        dst_ref=dst,
        send_sem=send.at[i, j],
        recv_sem=recv.at[i, j],
        device_id=device_id,
        device_id_type=MESH_IDS,
    )


def start_exchange(count, sources, targets, block_of, sems):
    send_sems, recv_sems, local_sems = sems
    me = lax.axis_index("seq")
    copies = []
    for i, source in enumerate(sources):
        for step in range(1, count):
            peer = lax.rem(me + step, count)
            copies.append(
                pltpu.make_async_remote_copy(
                    src_ref=block_of(source, peer),
                    dst_ref=targets[i].at[me],
                    send_sem=send_sems.at[i, step - 1],
                    recv_sem=recv_sems.at[i, step - 1],
                    device_id={"seq": peer},
                    device_id_type=MESH_IDS,
                )
            )
        copies.append(
            pltpu.make_async_copy(block_of(source, me), targets[i].at[me], local_sems.at[i])
        )
    for copy in copies:
        copy.start()
    return copies


def exchange_sems(n, count):
    return [
        pltpu.SemaphoreType.DMA((n, count - 1)),
        pltpu.SemaphoreType.DMA((n, count - 1)),
        pltpu.SemaphoreType.DMA((n,)),
    ]


def in_steps(count, stages, after=None):
    for step in range((count + 1) // 2 + len(stages) - 1):
        if after is not None and step == (count + 1) // 2 + 1:
            after()
        for behind, stage in enumerate(stages):
            for i in (2 * (step - behind), 2 * (step - behind) + 1):
                if 0 <= i < count:
                    stage(i)


def gather_kernel(line, chunks, n, extras, block_of, *refs):
    sources, more_sources = refs[:n], refs[n : n + extras]
    refs = refs[n + extras :]
    targets, more_targets = refs[:n], refs[n : n + extras]
    send, recv, local, *more_sems = refs[n + extras :]
    sems = (send, recv)
    a, b, z, c = torus_place()
    greet(torus_peers(line))
    more = start_exchange(4, more_sources, more_targets, block_of, more_sems) if extras else []
    sent = []

    def start(copy):
        copy.start()
        sent.append(copy)
        return copy

    along_line, first_hop, second_hop, third_hop = {}, {}, {}, {}

    def send_line(i):
        k, first, size = chunks[i]
        cols = pl.ds(first, size)
        own = targets[k].at[a, b, z, c, :, cols]
        keep = pltpu.make_async_copy(sources[k].at[:, cols], own, local.at[i])
        keep.start()
        along_line[i] = [
            start(
                remote(
                    sources[k].at[:, cols],
                    own,
                    sems,
                    i,
                    2 + step,
                    torus_id(a, b, lax.rem(z + step, line), c),
                )
            )
            for step in range(1, line)
        ]
        along_line[i].append(keep)

    def send_first(i):
        k, first, size = chunks[i]
        *copies, keep = along_line[i]
        keep.wait()
        for copy in copies:
            copy.wait_recv()
        block = targets[k].at[a, b, :, c, :, pl.ds(first, size)]
        peer = torus_id(a, 1 - b, z, c) if i % 2 == 0 else torus_id(1 - a, b, z, c)
        first_hop[i] = start(remote(block, block, sems, i, 1, peer))

    def send_second(i):
        k, first, size = chunks[i]
        first_hop[i].wait_recv()
        cols = pl.ds(first, size)
        if i % 2 == 0:
            block, peer = targets[k].at[a, :, :, c, :, cols], torus_id(1 - a, b, z, c)
        else:
            block, peer = targets[k].at[:, b, :, c, :, cols], torus_id(a, 1 - b, z, c)
        second_hop[i] = start(remote(block, block, sems, i, 2, peer))

    def send_third(i):
        k, first, size = chunks[i]
        second_hop[i].wait_recv()
        block = targets[k].at[:, :, :, c, :, pl.ds(first, size)]
        third_hop[i] = start(remote(block, block, sems, i, 0, torus_id(a, b, z, 1 - c)))

    in_steps(len(chunks), [send_line, send_first, send_second, send_third])
    for copy in third_hop.values():
        copy.wait_recv()
    for copy in sent:
        copy.wait_send()
    for copy in more:
        copy.wait()


def staged_gather(arrays, extras, block_of, collective_id, name, parts=6):
    seq_count, line = lax.axis_size("seq"), lax.axis_size("dp") // 2
    rows, n = arrays[0].shape[0], len(arrays)
    chunks = column_chunks([x.shape[1] for x in arrays], parts)
    m = len(chunks)
    shape = (seq_count // 2, 2, line, 2, rows)
    size = sum(x.shape[1] for x in arrays) * rows * 64
    count = n + len(extras)
    outs = pl.pallas_call(
        functools.partial(gather_kernel, line, chunks, n, len(extras), block_of),
        out_shape=[jax.ShapeDtypeStruct(shape + (x.shape[1],), BF16) for x in arrays]
        + [jax.ShapeDtypeStruct((seq_count,) + x.shape[1:], BF16) for x in extras],
        in_specs=[pl.BlockSpec(memory_space=pl.ANY)] * count,
        out_specs=[pl.BlockSpec(memory_space=pl.ANY)] * count,
        scratch_shapes=[
            pltpu.SemaphoreType.DMA((m, 2 + line)),
            pltpu.SemaphoreType.DMA((m, 2 + line)),
            pltpu.SemaphoreType.DMA((m,)),
        ]
        + (exchange_sems(len(extras), seq_count) if extras else []),
        compiler_params=pltpu.CompilerParams(
            collective_id=collective_id, vmem_limit_bytes=4 << 20
        ),
        cost_estimate=pl.CostEstimate(flops=0, bytes_accessed=size, transcendentals=0),
        name=name,
    )(*arrays, *extras)
    return [o.reshape(-1, o.shape[-1]) for o in outs]


def scatter_kernel(line, chunks, n, extras, block_of, *refs):
    m = len(chunks)
    sources, more_sources = refs[:n], refs[n : n + extras]
    refs = refs[n + extras :]
    targets, more_targets = refs[:n], refs[n : n + extras]
    scratch = refs[n + extras :]
    owns, ins1, accs2, ins2, accs3, ins3, ins4 = (scratch[m * s : m * (s + 1)] for s in range(7))
    send, recv, local, *more_sems = scratch[7 * m :]
    sems = (send, recv)
    a, b, z, c = torus_place()
    greet(torus_peers(line))
    sent = []

    def start(copy):
        copy.start()
        sent.append(copy)
        return copy

    def add_lines(target, left, right):
        def one(j, carry):
            target[j] = (left[j].astype(F32) + right[j].astype(F32)).astype(BF16)
            return carry

        lax.fori_loop(0, line, one, 0)

    between_cores, first_hop, second_hop, along_line = {}, {}, {}, {}

    def send_core(i):
        k, first, size = chunks[i]
        cols = pl.ds(first, size)
        keep = pltpu.make_async_copy(sources[k].at[:, :, :, c, :, cols], owns[i], local.at[i])
        keep.start()
        swap_core = remote(
            sources[k].at[:, :, :, 1 - c, :, cols], ins1[i], sems, i, 0, torus_id(a, b, z, 1 - c)
        )
        between_cores[i] = (keep, start(swap_core))

    def send_first(i):
        keep, copy = between_cores[i]
        keep.wait()
        copy.wait_recv()
        for p in range(2):
            for q in range(2):
                add_lines(owns[i].at[p, q], owns[i].at[p, q], ins1[i].at[p, q])
        if i % 2 == 0:
            block, peer = owns[i].at[:, 1 - b], torus_id(a, 1 - b, z, c)
        else:
            block, peer = owns[i].at[1 - a], torus_id(1 - a, b, z, c)
        first_hop[i] = start(remote(block, ins2[i], sems, i, 1, peer))

    def send_second(i):
        first_hop[i].wait_recv()
        for p in range(2):
            mine = owns[i].at[p, b] if i % 2 == 0 else owns[i].at[a, p]
            add_lines(accs2[i].at[p], mine, ins2[i].at[p])
        if i % 2 == 0:
            block, peer = accs2[i].at[1 - a], torus_id(1 - a, b, z, c)
        else:
            block, peer = accs2[i].at[1 - b], torus_id(a, 1 - b, z, c)
        second_hop[i] = start(remote(block, ins3[i], sems, i, 2, peer))

    def send_line(i):
        second_hop[i].wait_recv()
        add_lines(accs3[i], accs2[i].at[a if i % 2 == 0 else b], ins3[i])
        copies = []
        for step in range(1, line):
            to = lax.rem(z + step, line)
            peer = torus_id(a, b, to, c)
            copies.append(start(remote(accs3[i].at[to], ins4[i].at[z], sems, i, 2 + step, peer)))
        along_line[i] = copies

    def finish(i):
        k, first, size = chunks[i]
        total = accs3[i][z].astype(F32)
        for step in range(1, line):
            along_line[i][step - 1].wait_recv()
            total = total + ins4[i][lax.rem(z + line - step, line)].astype(F32)
        targets[k][:, first : first + size] = total

    more = []

    def send_more():
        if extras:
            more.extend(start_exchange(4, more_sources, more_targets, block_of, more_sems))

    in_steps(m, [send_core, send_first, send_second, send_line, finish], send_more)
    for copy in sent:
        copy.wait_send()
    for copy in more:
        copy.wait()


def staged_scatter(arrays, extras, block_of, collective_id, name, parts=6):
    seq_count, line = lax.axis_size("seq"), lax.axis_size("dp") // 2
    rows, n = arrays[0].shape[0] // (2 * line * seq_count), len(arrays)
    chunks = column_chunks([x.shape[1] for x in arrays], parts)
    m = len(chunks)
    leads = [(2, 2, line), (2, 2, line), (2, line), (2, line), (line,), (line,), (line,)]
    size = sum(x.shape[1] for x in arrays) * rows * 64
    anywhere = pl.BlockSpec(memory_space=pl.ANY)
    return pl.pallas_call(
        functools.partial(scatter_kernel, line, chunks, n, len(extras), block_of),
        out_shape=[jax.ShapeDtypeStruct((rows, x.shape[1]), F32) for x in arrays]
        + [jax.ShapeDtypeStruct((seq_count,) + x.shape[1:], BF16) for x in extras],
        in_specs=[anywhere] * (n + len(extras)),
        out_specs=[pl.BlockSpec(memory_space=pltpu.VMEM)] * n + [anywhere] * len(extras),
        scratch_shapes=[
            pltpu.VMEM(lead + (rows, width), BF16) for lead in leads for _, _, width in chunks
        ]
        + [
            pltpu.SemaphoreType.DMA((m, 2 + line)),
            pltpu.SemaphoreType.DMA((m, 2 + line)),
            pltpu.SemaphoreType.DMA((m,)),
        ]
        + (exchange_sems(len(extras), seq_count) if extras else []),
        compiler_params=pltpu.CompilerParams(
            collective_id=collective_id, vmem_limit_bytes=36 << 20
        ),
        cost_estimate=pl.CostEstimate(flops=0, bytes_accessed=size, transcendentals=0),
        name=name,
    )(*[x.reshape(2, 2, line, 2, rows, x.shape[1]) for x in arrays], *extras)


def rotate(values, cosines, sines):
    return values * cosines + pltpu.roll(values, HEAD_DIM // 2, 1) * sines


def attention_kernel(count, heads, kv_heads, *refs):
    length_ref, projected_ref, cos_ref, sin_ref = refs[:4]
    attended_ref, lse_ref, q_ref, kv_ref = refs[4:8]
    max_ref, sum_ref, acc_ref, send, recv = refs[8:]
    me = lax.axis_index("seq")
    rows, kv_width = q_ref.shape[0], kv_heads * HEAD_DIM
    q_width, group, scale = heads * HEAD_DIM, heads // kv_heads, 1.0 / math.sqrt(HEAD_DIM)
    greet([{"seq": lax.rem(me + step, count)} for step in range(1, count)])
    cosines, sines = cos_ref[...], sin_ref[...]
    for g in range(kv_heads):
        cols = slice(g * HEAD_DIM, (g + 1) * HEAD_DIM)
        keys = projected_ref[:, q_width + g * HEAD_DIM : q_width + (g + 1) * HEAD_DIM]
        kv_ref[me, :, cols] = rotate(keys, cosines, sines).astype(BF16)
    kv_ref[me, :, kv_width:] = projected_ref[:, q_width + kv_width :].astype(BF16)

    def to_later(peer):
        return pltpu.make_async_remote_copy(
            src_ref=kv_ref.at[me],
            dst_ref=kv_ref.at[me],
            send_sem=send.at[peer],
            recv_sem=recv.at[me],
            device_id={"seq": peer},
            device_id_type=MESH_IDS,
        )

    def start(peer, carry):
        to_later(peer).start()
        return carry

    lax.fori_loop(me + 1, count, start, 0)

    def one_query(h, carry):
        cols = pl.ds(pl.multiple_of(h * HEAD_DIM, HEAD_DIM), HEAD_DIM)
        q_ref[:, cols] = rotate(projected_ref[:, cols], cosines, sines).astype(BF16)
        return carry

    lax.fori_loop(0, heads, one_query, 0)
    max_ref[...] = jnp.full_like(max_ref, NEG_FILL)
    sum_ref[...] = jnp.zeros_like(sum_ref)
    acc_ref[...] = jnp.zeros_like(acc_ref)
    length = length_ref[0]
    query_pos = me * rows + lax.broadcasted_iota(jnp.int32, (rows, rows), 1)
    key_local = lax.broadcasted_iota(jnp.int32, (rows, rows), 0)

    def key_block(j):
        key_pos = j * rows + key_local
        mask = (key_pos <= query_pos) & (key_pos < length)
        for g in range(kv_heads):
            key_cols = slice(g * HEAD_DIM, (g + 1) * HEAD_DIM)
            value_cols = slice(kv_width + g * HEAD_DIM, kv_width + (g + 1) * HEAD_DIM)

            def one_head(i, carry):
                h = g * group + i
                cols = pl.ds(pl.multiple_of(h * HEAD_DIM, HEAD_DIM), HEAD_DIM)
                row = pl.ds(h, 1)
                keys, values = kv_ref[j, :, key_cols], kv_ref[j, :, value_cols]
                scores = jnp.where(mask, nt(keys, q_ref[:, cols]) * scale, NEG_FILL)
                before = max_ref[row, :]
                top = jnp.maximum(before, jnp.max(scores, axis=0, keepdims=True))
                shrink = jnp.exp(before - top)
                weights = jnp.exp(scores - top)
                max_ref[row, :] = top
                sum_ref[row, :] = sum_ref[row, :] * shrink + jnp.sum(weights, axis=0, keepdims=True)
                acc_ref[h] = acc_ref[h] * shrink + tn(values, weights.astype(BF16))
                return carry

            lax.fori_loop(0, group, one_head, 0, unroll=2)

    key_block(me)

    def earlier_block(j, carry):
        pltpu.make_async_remote_copy(
            src_ref=kv_ref.at[j],
            dst_ref=kv_ref.at[j],
            send_sem=send.at[j],
            recv_sem=recv.at[j],
            device_id={"seq": j},
            device_id_type=MESH_IDS,
        ).wait_recv()
        key_block(j)
        return carry

    lax.fori_loop(0, me, earlier_block, 0)
    lse_ref[...] = max_ref[...] + jnp.log(sum_ref[...])

    def finish(h, carry):
        cols = pl.ds(pl.multiple_of(h * HEAD_DIM, HEAD_DIM), HEAD_DIM)
        attended_ref[:, cols] = (acc_ref[h] / sum_ref[pl.ds(h, 1), :]).T.astype(BF16)
        return carry

    lax.fori_loop(0, heads, finish, 0)

    def sent(peer, carry):
        to_later(peer).wait_send()
        return carry

    lax.fori_loop(me + 1, count, sent, 0)


def attention(length, projected, cosines, sines, q_width, collective_id):
    count = lax.axis_size("seq")
    rows = projected.shape[0]
    kv_width = (projected.shape[1] - q_width) // 2
    heads, kv_heads = q_width // HEAD_DIM, kv_width // HEAD_DIM
    vmem = pl.BlockSpec(memory_space=pltpu.VMEM)
    return pl.pallas_call(
        functools.partial(attention_kernel, count, heads, kv_heads),
        out_shape=[
            jax.ShapeDtypeStruct((rows, q_width), BF16),
            jax.ShapeDtypeStruct((heads, rows), F32),
            jax.ShapeDtypeStruct((rows, q_width), BF16),
            jax.ShapeDtypeStruct((count, rows, 2 * kv_width), BF16),
        ],
        in_specs=[pl.BlockSpec(memory_space=pltpu.SMEM)] + [vmem] * 3,
        out_specs=[vmem] * 4,
        scratch_shapes=[
            pltpu.VMEM((heads, rows), F32),
            pltpu.VMEM((heads, rows), F32),
            pltpu.VMEM((heads, HEAD_DIM, rows), F32),
            pltpu.SemaphoreType.DMA((count,)),
            pltpu.SemaphoreType.DMA((count,)),
        ],
        compiler_params=pltpu.CompilerParams(
            collective_id=collective_id, vmem_limit_bytes=30 << 20
        ),
        cost_estimate=pl.CostEstimate(flops=0, bytes_accessed=1 << 20, transcendentals=0),
        name="attention_forward",
    )(length, projected, cosines, sines)


def attention_back_kernel(count, heads, kv_heads, *refs):
    length_ref, q_ref, kv_ref, grad_ref, lse_ref, attended_ref, cos_ref, sin_ref = refs[:8]
    out_ref, delta_ref, dq_ref, part_ref, leaving, arriving, send, recv = refs[8:]
    me = lax.axis_index("seq")
    rows, kv_width = q_ref.shape[0], kv_heads * HEAD_DIM
    group, scale = heads // kv_heads, 1.0 / math.sqrt(HEAD_DIM)
    greet([{"seq": lax.rem(me + step, count)} for step in range(1, count)])
    length = length_ref[0]
    query_pos = me * rows + lax.broadcasted_iota(jnp.int32, (rows, rows), 1)
    key_local = lax.broadcasted_iota(jnp.int32, (rows, rows), 0)
    dq_ref[...] = jnp.zeros_like(dq_ref)
    ones = jnp.ones((8, HEAD_DIM), BF16)
    for h in range(heads):
        cols = slice(h * HEAD_DIM, (h + 1) * HEAD_DIM)
        terms = grad_ref[:, cols].astype(F32) * attended_ref[:, cols].astype(F32)
        high = terms.astype(BF16)
        low = (terms - high.astype(F32)).astype(BF16)
        delta_ref[h : h + 1, :] = (nt(ones, high) + nt(ones, low))[:1]

    def key_block(j):
        key_pos = j * rows + key_local
        mask = (key_pos <= query_pos) & (key_pos < length)
        part_ref[...] = jnp.zeros_like(part_ref)
        key_rows = pl.ds(pl.multiple_of(j * rows, rows), rows)
        for g in range(kv_heads):
            key_cols = slice(g * HEAD_DIM, (g + 1) * HEAD_DIM)
            value_cols = slice(kv_width + g * HEAD_DIM, kv_width + (g + 1) * HEAD_DIM)

            def one_head(i, carry):
                h = g * group + i
                cols = pl.ds(pl.multiple_of(h * HEAD_DIM, HEAD_DIM), HEAD_DIM)
                keys, values = kv_ref[key_rows, key_cols], kv_ref[key_rows, value_cols]
                queries, grads = q_ref[:, cols], grad_ref[:, cols]
                scores = nt(keys, queries) * scale
                probs = jnp.where(mask, jnp.exp(scores - lse_ref[pl.ds(h, 1), :]), 0.0)
                prob_grad = nt(values, grads)
                score_grad = (probs * (prob_grad - delta_ref[pl.ds(h, 1), :])).astype(BF16)
                part_ref[:, key_cols] += nn(score_grad, queries)
                part_ref[:, value_cols] += nn(probs.astype(BF16), grads)
                dq_ref[:, cols] += tn(score_grad, keys)
                return carry

            lax.fori_loop(0, group, one_head, 0, unroll=3)
        part_ref[:, :kv_width] = part_ref[:, :kv_width] * scale

    def to_owner(j):
        return pltpu.make_async_remote_copy(
            src_ref=leaving.at[j],
            dst_ref=arriving.at[me],
            send_sem=send.at[j],
            recv_sem=recv.at[me],
            device_id={"seq": j},
            device_id_type=MESH_IDS,
        )

    def other_block(j, carry):
        key_block(j)
        leaving[j] = part_ref[...].astype(BF16)
        to_owner(j).start()
        return carry

    lax.fori_loop(0, me, other_block, 0)
    key_block(me)
    part_ref[...] = part_ref[...].astype(BF16).astype(F32)
    cosines, sines = cos_ref[...], -sin_ref[...]

    def one_query(h, carry):
        cols = pl.ds(pl.multiple_of(h * HEAD_DIM, HEAD_DIM), HEAD_DIM)
        out_ref[:, cols] = rotate(dq_ref[:, cols] * scale, cosines, sines).astype(BF16)
        return carry

    lax.fori_loop(0, heads, one_query, 0)

    def add_arrived(m, carry):
        pltpu.make_async_remote_copy(
            src_ref=leaving.at[m],
            dst_ref=arriving.at[m],
            send_sem=send.at[m],
            recv_sem=recv.at[m],
            device_id={"seq": m},
            device_id_type=MESH_IDS,
        ).wait_recv()
        part_ref[...] += arriving[m].astype(F32)
        return carry

    lax.fori_loop(me + 1, count, add_arrived, 0)
    first = heads * HEAD_DIM
    for g in range(kv_heads):
        cols = slice(g * HEAD_DIM, (g + 1) * HEAD_DIM)
        out_ref[:, first + g * HEAD_DIM : first + (g + 1) * HEAD_DIM] = rotate(
            part_ref[:, cols], cosines, sines
        ).astype(BF16)
    out_ref[:, first + kv_width :] = part_ref[:, kv_width:].astype(BF16)

    def sent(j, carry):
        to_owner(j).wait_send()
        return carry

    lax.fori_loop(0, me, sent, 0)


def attention_back(length, queries, kv_all, grads, lse, attended, cosines, sines, collective_id):
    count = lax.axis_size("seq")
    rows, q_width = queries.shape
    kv_width = kv_all.shape[1] // 2
    heads, kv_heads = q_width // HEAD_DIM, kv_width // HEAD_DIM
    vmem = pl.BlockSpec(memory_space=pltpu.VMEM)
    return pl.pallas_call(
        functools.partial(attention_back_kernel, count, heads, kv_heads),
        out_shape=jax.ShapeDtypeStruct((rows, q_width + 2 * kv_width), BF16),
        in_specs=[pl.BlockSpec(memory_space=pltpu.SMEM)] + [vmem] * 7,
        out_specs=vmem,
        scratch_shapes=[
            pltpu.VMEM((heads, rows), F32),
            pltpu.VMEM((rows, q_width), F32),
            pltpu.VMEM((rows, 2 * kv_width), F32),
            pltpu.VMEM((count, rows, 2 * kv_width), BF16),
            pltpu.VMEM((count, rows, 2 * kv_width), BF16),
            pltpu.SemaphoreType.DMA((count,)),
            pltpu.SemaphoreType.DMA((count,)),
        ],
        compiler_params=pltpu.CompilerParams(
            collective_id=collective_id, vmem_limit_bytes=30 << 20
        ),
        cost_estimate=pl.CostEstimate(
            flops=10 * count * rows * rows * q_width, bytes_accessed=1 << 20, transcendentals=0
        ),
        name="attention_backward",
    )(length, queries, kv_all, grads, lse, attended, cosines, sines)


def seq_permutes(block_for):
    count, me = lax.axis_size("seq"), lax.axis_index("seq")
    pieces = [block_for(me)]
    for step in range(1, count):
        ring = [(i, (i + step) % count) for i in range(count)]
        pieces.append(lax.ppermute(block_for(lax.rem(me + step, count)), "seq", ring))
    return pieces


def in_seq_order(pieces, dtype):
    count, me = len(pieces), lax.axis_index("seq")
    whole = jnp.zeros((count,) + pieces[0].shape, dtype)
    for step, piece in enumerate(pieces):
        place = lax.rem(me + count - step, count)
        whole = lax.dynamic_update_index_in_dim(whole, piece.astype(dtype), place, 0)
    return whole


def on_device(
    hidden_in,
    lengths,
    routes,
    gates,
    priority,
    attn_gain,
    mlp_gain,
    w_query,
    key_projection,
    value_projection,
    w_out,
    w_gate,
    w_up,
    w_down,
    cotangent,
):
    rows = hidden_in.shape[1]
    width = hidden_in.shape[2]
    dp_count = lax.axis_size("dp")
    seq_count = lax.axis_size("seq")
    devices = dp_count * seq_count
    own_experts = w_gate.shape[0]
    sharers = seq_count // own_experts
    hidden_units = w_gate.shape[2]
    my_seq = lax.axis_index("seq")
    extent = rows * seq_count
    query_pos = my_seq * rows + jnp.arange(rows, dtype=jnp.int32)
    length = lengths[0]
    is_valid = query_pos < length
    q_width = w_query.shape[1]
    kv_width = key_projection.shape[1]
    cosine_lookup, sine_lookup = rope_angles(query_pos, HEAD_DIM)

    gain_block = jnp.concatenate(
        [attn_gain[:, None], mlp_gain[:, None], jnp.zeros((attn_gain.shape[0], LANES - 2), BF16)],
        axis=1,
    )
    packed = jnp.concatenate([w_query, key_projection, value_projection], axis=1)
    staged = seq_count == 4 and w_query.shape[0] % 16 == 0

    def expert_pieces(weights):
        def block_for(peer):
            return lax.dynamic_index_in_dim(weights, peer // sharers, 0, keepdims=False)

        return seq_permutes(block_for)

    gate_parts = expert_pieces(w_gate)
    if staged:
        packed_full, gains_full, out_full = staged_gather(
            [packed, gain_block, w_out], [], None, 2, "gather_attention_weights"
        )
    else:
        packed_full = lax.all_gather(packed, BOTH, axis=0, tiled=True)
        gains_full = lax.all_gather(gain_block, BOTH, axis=0, tiled=True)
        out_full = lax.all_gather(w_out, BOTH, axis=0, tiled=True)

    pair_routes, place, kept = claim_places(routes[0], priority[0, 0], is_valid)
    holder = (pair_routes // own_experts) * seq_count + (pair_routes % own_experts) * sharers
    holder = holder + my_seq * sharers // seq_count
    slots = devices * CAP
    target = jnp.where(kept, holder * CAP + place, slots).reshape(rows, TOP)
    slot_ids = jnp.arange(slots, dtype=jnp.int32)
    hits = target[:, :, None] == slot_ids[None, None, :]
    gate_rows = gates[0]
    token_hot = jnp.any(hits, axis=1).astype(BF16)

    def hot_of(first, size):
        mine = kept & (place >= first) & (place < first + size)
        spot = jnp.where(mine, holder * size + place - first, slots).reshape(rows, TOP)
        ids = jnp.arange(devices * size, dtype=jnp.int32)
        return jnp.any(spot[:, :, None] == ids[None, None, :], axis=1).astype(BF16)

    early_hot, late_hot = hot_of(0, EARLY), hot_of(EARLY, CAP - EARLY)
    slot_gate = jnp.sum(jnp.where(hits, gate_rows[:, :, None], 0.0), axis=(0, 1))

    live_cotangent = jnp.where(is_valid[:, None], cotangent[0], jnp.zeros((), BF16))
    out_grad = live_cotangent.astype(F32)
    grad_send = (tn(token_hot, live_cotangent) * slot_gate[:, None]).astype(BF16)
    packed_full, gains_full, out_full, gate_parts, grad_send = lax.optimization_barrier(
        (packed_full, gains_full, out_full, gate_parts, grad_send)
    )
    gain_one, gain_two = gains_full[:, 0].astype(F32), gains_full[:, 1].astype(F32)
    grad_rows = swap(grad_send.reshape(devices, CAP, width), ("dp", "seq"))

    inputs = hidden_in[0].astype(F32)
    scale_one = lax.rsqrt(jnp.mean(inputs * inputs, axis=-1, keepdims=True) + EPSILON)
    normed = (inputs * scale_one * gain_one).astype(BF16)
    projected = nn(normed, packed_full)
    cosines, sines = cosine_lookup[:, 0], sine_lookup[:, 0]
    cosines = jnp.concatenate([cosines, cosines], axis=1)
    sines = jnp.concatenate([-sines, sines], axis=1)
    attended, log_total, query_flat, kv_all = attention(
        lengths, projected, cosines, sines, q_width, 1
    )
    kv_all = kv_all.reshape(extent, 2 * kv_width)
    attended, w_up = lax.optimization_barrier((attended, w_up))
    up_parts = expert_pieces(w_up)
    middle = inputs + nn(attended, out_full)
    scale_two = lax.rsqrt(jnp.mean(middle * middle, axis=-1, keepdims=True) + EPSILON)
    moe_input = (middle * scale_two * gain_two).astype(BF16)

    def to_experts(hot):
        return tn(hot, moe_input).astype(BF16).reshape(devices, -1, width)

    early_send, late_send = to_experts(early_hot), to_experts(late_hot)
    early_send, late_send, grad_rows, query_flat, attended, w_down = lax.optimization_barrier(
        (early_send, late_send, grad_rows, query_flat, attended, w_down)
    )
    down_parts = expert_pieces(w_down)
    early_rows = swap(early_send, ("dp", "seq"))
    early_rows, late_send = lax.optimization_barrier((early_rows, late_send))
    late_rows = swap(late_send, ("dp", "seq"))
    gate_full = in_seq_order(gate_parts, BF16).reshape(width, hidden_units)
    up_full = in_seq_order(up_parts, BF16).reshape(width, hidden_units)
    down_full = in_seq_order(down_parts, BF16).reshape(hidden_units, width)
    early_grads, late_grads = grad_rows[:, :EARLY], grad_rows[:, EARLY:]
    early_rows, gate_full, up_full, down_full, early_grads, late_grads = (
        lax.optimization_barrier(
            (early_rows, gate_full, up_full, down_full, early_grads, late_grads)
        )
    )

    def run_expert(slot_rows, grads):
        blocks = slot_rows.shape[:2]
        slot_rows, grads = slot_rows.reshape(-1, width), grads.reshape(-1, width)
        gate_pre = nn(slot_rows, gate_full)
        up_pre = nn(slot_rows, up_full)
        gate_sigmoid = jax.nn.sigmoid(gate_pre)
        gate_act = gate_pre * gate_sigmoid
        gate_slope = gate_sigmoid * (1.0 + gate_pre * (1.0 - gate_sigmoid))
        hidden = (gate_act * up_pre).astype(BF16)
        hidden_grad = nt(grads, down_full)
        gate_pre_grad = (hidden_grad * up_pre * gate_slope).astype(BF16)
        up_pre_grad = (hidden_grad * gate_act).astype(BF16)
        return [x.reshape(blocks + (-1,)) for x in (hidden, gate_pre_grad, up_pre_grad)]

    def row_grads(gate_pre_grad, up_pre_grad):
        blocks = gate_pre_grad.shape[:2]
        gate_pre_grad = gate_pre_grad.reshape(-1, hidden_units)
        up_pre_grad = up_pre_grad.reshape(-1, hidden_units)
        row_grad = (nt(gate_pre_grad, gate_full) + nt(up_pre_grad, up_full)).astype(BF16)
        return row_grad.reshape(blocks + (width,))

    def both_parts(early, late):
        return jnp.concatenate([early, late], axis=1).reshape(slots, -1)

    def to_owners(grad):
        grad = grad.reshape(seq_count, -1, grad.shape[1])

        def block_for(peer):
            return lax.dynamic_index_in_dim(grad, peer, 0, keepdims=False)

        return seq_permutes(block_for)

    def owned_sum(pieces):
        whole = in_seq_order(pieces, F32)
        return jnp.sum(whole.reshape((own_experts, sharers) + whole.shape[1:]), axis=1)

    early_hidden, *early_pre_grads = run_expert(early_rows, early_grads)
    early_row_grad = row_grads(*early_pre_grads)
    late_rows, early_row_grad = lax.optimization_barrier((late_rows, early_row_grad))
    early_back = swap(early_row_grad, ("dp", "seq"))
    late_hidden, *late_pre_grads = run_expert(late_rows, late_grads)
    expert_hidden = both_parts(early_hidden, late_hidden)
    down_grad = tn(expert_hidden, grad_rows.reshape(slots, width)).astype(BF16)
    late_rows, late_pre_grads, down_grad = lax.optimization_barrier(
        (late_rows, late_pre_grads, down_grad)
    )
    down_grad_parts = to_owners(down_grad)
    late_row_grad = row_grads(*late_pre_grads)
    late_hidden = expert_hidden
    early_back, late_row_grad, down_grad_parts, late_pre_grads, late_hidden = (
        lax.optimization_barrier(
            (early_back, late_row_grad, down_grad_parts, late_pre_grads, late_hidden)
        )
    )
    late_back = swap(late_row_grad, ("dp", "seq"))
    slot_rows = both_parts(early_rows, late_rows)
    gate_pre_grad, up_pre_grad = map(both_parts, early_pre_grads, late_pre_grads)
    gate_grad = tn(slot_rows, gate_pre_grad).astype(BF16)
    up_grad = tn(slot_rows, up_pre_grad).astype(BF16)
    gate_owned, up_grad_parts = owned_sum(to_owners(gate_grad)), to_owners(up_grad)
    down_owned = owned_sum(down_grad_parts)
    expert_out = nn(late_hidden, down_full).astype(BF16)
    expert_out, late_back, gate_owned, down_owned, up_grad = lax.optimization_barrier(
        (expert_out, late_back, gate_owned, down_owned, up_grad)
    )
    returned = swap(expert_out.reshape(devices, CAP, width), ("dp", "seq")).reshape(slots, width)
    early_back, late_back = early_back.reshape(-1, width), late_back.reshape(-1, width)
    moe_input_grad = nn(early_hot, early_back) + nn(late_hot, late_back)
    middle_norm_grad, gain_two_grad = norm_back(middle, scale_two, gain_two, moe_input_grad)
    middle_grad = out_grad + middle_norm_grad
    branch_grad = middle_grad.astype(BF16)
    out_terms = tn(attended, branch_grad).astype(BF16)
    attended_grad = nt(branch_grad, out_full).astype(BF16)
    attended_grad, up_grad_parts = lax.optimization_barrier((attended_grad, up_grad_parts))
    projected_grad = attention_back(
        lengths,
        query_flat,
        kv_all,
        attended_grad,
        log_total,
        attended,
        cosines,
        sines,
        4,
    )
    normed_grad = nt(projected_grad, packed_full)
    input_norm_grad, gain_one_grad = norm_back(inputs, scale_one, gain_one, normed_grad)
    input_grad = middle_grad + input_norm_grad

    lane = lax.broadcasted_iota(jnp.int32, (width, LANES), 1)
    gain_terms = jnp.where(lane == 0, gain_one_grad[:, None], gain_two_grad[:, None])
    gain_terms = jnp.where(lane < 2, gain_terms, 0.0).astype(BF16)
    query_terms = tn(normed, projected_grad).astype(BF16)
    if staged:
        out_owned, gains_owned, owned = staged_scatter(
            [out_terms, gain_terms, query_terms], [], None, 6, "scatter_attention_grads"
        )
    else:
        terms = jnp.concatenate([out_terms, gain_terms, query_terms], axis=1)
        terms = lax.psum_scatter(terms, BOTH, scatter_dimension=0, tiled=True).astype(F32)
        out_owned, gains_owned = terms[:, :width], terms[:, width : width + LANES]
        owned = terms[:, width + LANES :]
    returned, owned = lax.optimization_barrier((returned, owned))
    expert_grads = [gate_owned, owned_sum(up_grad_parts), down_owned]

    gate_hot = jnp.sum(jnp.where(hits, gate_rows[:, :, None], 0.0), axis=1).astype(BF16)
    layer_out = middle + nn(gate_hot, returned)
    return (
        layer_out[None],
        input_grad[None],
        gains_owned[:, 0],
        gains_owned[:, 1],
        owned[:, :q_width],
        owned[:, q_width : q_width + kv_width],
        owned[:, q_width + kv_width : q_width + 2 * kv_width],
        out_owned,
        *expert_grads,
    )


def solution(mesh):
    part = P("dp", "seq", None)
    both = P(BOTH)
    both_rows = P(BOTH, None)
    return jax.shard_map(
        on_device,
        mesh=mesh,
        in_specs=(part, P("dp"), part, part, part, both, both)
        + (both_rows,) * 4
        + (part,) * 4,
        out_specs=(part, part, both, both) + (both_rows,) * 4 + (part,) * 3,
        check_vma=False,
    )
```

```python
import functools
import math

import jax
import jax.numpy as jnp
from jax import lax
from jax.experimental import pallas as pl
from jax.experimental.pallas import tpu as pltpu
from jax.sharding import PartitionSpec as P

HEAD_DIM = 128
EXPERTS = 32
TOP = 4
CAP = 40
EARLY = 16

EPSILON = 1e-06
ROPE_BASE = 10000.0
NEG_FILL = -1e30
LANES = 128
BOTH = ("seq", "dp")
BF16 = jnp.bfloat16
F32 = jnp.float32


def rope_angles(positions, head_size):
    half_dim = head_size // 2
    frequency = ROPE_BASE ** (-(2.0 * jnp.arange(half_dim, dtype=F32)) / head_size)
    angles = positions.astype(F32)[:, None] * frequency[None, :]
    return (jnp.cos(angles)[:, None, :], jnp.sin(angles)[:, None, :])


def dot(left, right, contract):
    return lax.dot_general(left, right, (contract, ((), ())), preferred_element_type=F32)


def nn(left, right):
    return dot(left, right, ((1,), (0,)))


def nt(left, right):
    return dot(left, right, ((1,), (1,)))


def tn(left, right):
    return dot(left, right, ((0,), (0,)))


def claim_places(routes, priority, is_valid):
    pair_routes = routes.reshape(-1)
    live = jnp.repeat(is_valid, TOP)
    key = jnp.where(live, pair_routes, -1)
    earlier = (key[None, :] == pair_routes[:, None]) & (priority[None, :] < priority[:, None])
    place = jnp.sum(earlier.astype(F32), axis=1).astype(jnp.int32)
    return pair_routes, place, live & (place < CAP)


def norm_back(values, scale_rows, gain_vec, incoming):
    weighted = incoming * gain_vec
    inner_mean = jnp.mean(weighted * values, axis=-1, keepdims=True)
    values_grad = scale_rows * weighted - values * scale_rows * scale_rows * scale_rows * inner_mean
    return (values_grad, jnp.sum(incoming * values * scale_rows, axis=0))


def swap(blocks, axes):
    return lax.all_to_all(blocks, axes, split_axis=0, concat_axis=0, tiled=True)


MESH_IDS = pl.DeviceIdType.MESH


def torus_place():
    seq, dp = lax.axis_index("seq"), lax.axis_index("dp")
    return seq // 2, seq % 2, dp // 2, dp % 2


def torus_id(a, b, z, c):
    return {"seq": 2 * a + b, "dp": 2 * z + c}


def torus_peers(line):
    a, b, z, c = torus_place()
    peers = [torus_id(a, b, z, 1 - c), torus_id(a, 1 - b, z, c), torus_id(1 - a, b, z, c)]
    peers.append(torus_id(1 - a, 1 - b, z, c))
    return peers + [torus_id(a, b, lax.rem(z + k, line), c) for k in range(1, line)]


def greet(peers):
    barrier = pltpu.get_barrier_semaphore()
    for peer in peers:
        pl.semaphore_signal(barrier, inc=1, device_id=peer, device_id_type=MESH_IDS)
    pl.semaphore_wait(barrier, len(peers))


def column_chunks(widths, parts):
    chunks = []
    for part in range(parts):
        for k, whole in enumerate(widths):
            tiles = whole // LANES
            first, end = tiles * part // parts, tiles * (part + 1) // parts
            if end > first:
                chunks.append((k, first * LANES, (end - first) * LANES))
    return chunks


def remote(src, dst, sems, i, j, device_id):
    send, recv = sems
    return pltpu.make_async_remote_copy(
        src_ref=src,
        dst_ref=dst,
        send_sem=send.at[i, j],
        recv_sem=recv.at[i, j],
        device_id=device_id,
        device_id_type=MESH_IDS,
    )


def start_exchange(count, sources, targets, block_of, sems):
    send_sems, recv_sems, local_sems = sems
    me = lax.axis_index("seq")
    copies = []
    for i, source in enumerate(sources):
        for step in range(1, count):
            peer = lax.rem(me + step, count)
            copies.append(
                pltpu.make_async_remote_copy(
                    src_ref=block_of(source, peer),
                    dst_ref=targets[i].at[me],
                    send_sem=send_sems.at[i, step - 1],
                    recv_sem=recv_sems.at[i, step - 1],
                    device_id={"seq": peer},
                    device_id_type=MESH_IDS,
                )
            )
        copies.append(
            pltpu.make_async_copy(block_of(source, me), targets[i].at[me], local_sems.at[i])
        )
    for copy in copies:
        copy.start()
    return copies


def exchange_sems(n, count):
    return [
        pltpu.SemaphoreType.DMA((n, count - 1)),
        pltpu.SemaphoreType.DMA((n, count - 1)),
        pltpu.SemaphoreType.DMA((n,)),
    ]


def in_steps(count, stages, after=None):
    for step in range((count + 1) // 2 + len(stages) - 1):
        if after is not None and step == (count + 1) // 2 + 1:
            after()
        for behind, stage in enumerate(stages):
            for i in (2 * (step - behind), 2 * (step - behind) + 1):
                if 0 <= i < count:
                    stage(i)


def gather_kernel(line, chunks, n, extras, block_of, *refs):
    sources, more_sources = refs[:n], refs[n : n + extras]
    refs = refs[n + extras :]
    targets, more_targets = refs[:n], refs[n : n + extras]
    send, recv, local, *more_sems = refs[n + extras :]
    sems = (send, recv)
    a, b, z, c = torus_place()
    greet(torus_peers(line))
    more = start_exchange(4, more_sources, more_targets, block_of, more_sems) if extras else []
    sent = []

    def start(copy):
        copy.start()
        sent.append(copy)
        return copy

    along_line, first_hop, second_hop, third_hop = {}, {}, {}, {}

    def send_line(i):
        k, first, size = chunks[i]
        cols = pl.ds(first, size)
        own = targets[k].at[a, b, z, c, :, cols]
        keep = pltpu.make_async_copy(sources[k].at[:, cols], own, local.at[i])
        keep.start()
        along_line[i] = [
            start(
                remote(
                    sources[k].at[:, cols],
                    own,
                    sems,
                    i,
                    2 + step,
                    torus_id(a, b, lax.rem(z + step, line), c),
                )
            )
            for step in range(1, line)
        ]
        along_line[i].append(keep)

    def send_first(i):
        k, first, size = chunks[i]
        *copies, keep = along_line[i]
        keep.wait()
        for copy in copies:
            copy.wait_recv()
        block = targets[k].at[a, b, :, c, :, pl.ds(first, size)]
        peer = torus_id(a, 1 - b, z, c) if i % 2 == 0 else torus_id(1 - a, b, z, c)
        first_hop[i] = start(remote(block, block, sems, i, 1, peer))

    def send_second(i):
        k, first, size = chunks[i]
        first_hop[i].wait_recv()
        cols = pl.ds(first, size)
        if i % 2 == 0:
            block, peer = targets[k].at[a, :, :, c, :, cols], torus_id(1 - a, b, z, c)
        else:
            block, peer = targets[k].at[:, b, :, c, :, cols], torus_id(a, 1 - b, z, c)
        second_hop[i] = start(remote(block, block, sems, i, 2, peer))

    def send_third(i):
        k, first, size = chunks[i]
        second_hop[i].wait_recv()
        block = targets[k].at[:, :, :, c, :, pl.ds(first, size)]
        third_hop[i] = start(remote(block, block, sems, i, 0, torus_id(a, b, z, 1 - c)))

    in_steps(len(chunks), [send_line, send_first, send_second, send_third])
    for copy in third_hop.values():
        copy.wait_recv()
    for copy in sent:
        copy.wait_send()
    for copy in more:
        copy.wait()


def staged_gather(arrays, extras, block_of, collective_id, name, parts=6):
    seq_count, line = lax.axis_size("seq"), lax.axis_size("dp") // 2
    rows, n = arrays[0].shape[0], len(arrays)
    chunks = column_chunks([x.shape[1] for x in arrays], parts)
    m = len(chunks)
    shape = (seq_count // 2, 2, line, 2, rows)
    size = sum(x.shape[1] for x in arrays) * rows * 64
    count = n + len(extras)
    outs = pl.pallas_call(
        functools.partial(gather_kernel, line, chunks, n, len(extras), block_of),
        out_shape=[jax.ShapeDtypeStruct(shape + (x.shape[1],), BF16) for x in arrays]
        + [jax.ShapeDtypeStruct((seq_count,) + x.shape[1:], BF16) for x in extras],
        in_specs=[pl.BlockSpec(memory_space=pl.ANY)] * count,
        out_specs=[pl.BlockSpec(memory_space=pl.ANY)] * count,
        scratch_shapes=[
            pltpu.SemaphoreType.DMA((m, 2 + line)),
            pltpu.SemaphoreType.DMA((m, 2 + line)),
            pltpu.SemaphoreType.DMA((m,)),
        ]
        + (exchange_sems(len(extras), seq_count) if extras else []),
        compiler_params=pltpu.CompilerParams(
            collective_id=collective_id, vmem_limit_bytes=4 << 20
        ),
        cost_estimate=pl.CostEstimate(flops=0, bytes_accessed=size, transcendentals=0),
        name=name,
    )(*arrays, *extras)
    return [o.reshape(-1, o.shape[-1]) for o in outs]


def scatter_kernel(line, chunks, n, extras, block_of, *refs):
    m = len(chunks)
    sources, more_sources = refs[:n], refs[n : n + extras]
    refs = refs[n + extras :]
    targets, more_targets = refs[:n], refs[n : n + extras]
    scratch = refs[n + extras :]
    owns, ins1, accs2, ins2, accs3, ins3, ins4 = (scratch[m * s : m * (s + 1)] for s in range(7))
    send, recv, local, *more_sems = scratch[7 * m :]
    sems = (send, recv)
    a, b, z, c = torus_place()
    greet(torus_peers(line))
    sent = []

    def start(copy):
        copy.start()
        sent.append(copy)
        return copy

    def add_lines(target, left, right):
        def one(j, carry):
            target[j] = (left[j].astype(F32) + right[j].astype(F32)).astype(BF16)
            return carry

        lax.fori_loop(0, line, one, 0)

    between_cores, first_hop, second_hop, along_line = {}, {}, {}, {}

    def send_core(i):
        k, first, size = chunks[i]
        cols = pl.ds(first, size)
        keep = pltpu.make_async_copy(sources[k].at[:, :, :, c, :, cols], owns[i], local.at[i])
        keep.start()
        swap_core = remote(
            sources[k].at[:, :, :, 1 - c, :, cols], ins1[i], sems, i, 0, torus_id(a, b, z, 1 - c)
        )
        between_cores[i] = (keep, start(swap_core))

    def send_first(i):
        keep, copy = between_cores[i]
        keep.wait()
        copy.wait_recv()
        for p in range(2):
            for q in range(2):
                add_lines(owns[i].at[p, q], owns[i].at[p, q], ins1[i].at[p, q])
        if i % 2 == 0:
            block, peer = owns[i].at[:, 1 - b], torus_id(a, 1 - b, z, c)
        else:
            block, peer = owns[i].at[1 - a], torus_id(1 - a, b, z, c)
        first_hop[i] = start(remote(block, ins2[i], sems, i, 1, peer))

    def send_second(i):
        first_hop[i].wait_recv()
        for p in range(2):
            mine = owns[i].at[p, b] if i % 2 == 0 else owns[i].at[a, p]
            add_lines(accs2[i].at[p], mine, ins2[i].at[p])
        if i % 2 == 0:
            block, peer = accs2[i].at[1 - a], torus_id(1 - a, b, z, c)
        else:
            block, peer = accs2[i].at[1 - b], torus_id(a, 1 - b, z, c)
        second_hop[i] = start(remote(block, ins3[i], sems, i, 2, peer))

    def send_line(i):
        second_hop[i].wait_recv()
        add_lines(accs3[i], accs2[i].at[a if i % 2 == 0 else b], ins3[i])
        copies = []
        for step in range(1, line):
            to = lax.rem(z + step, line)
            peer = torus_id(a, b, to, c)
            copies.append(start(remote(accs3[i].at[to], ins4[i].at[z], sems, i, 2 + step, peer)))
        along_line[i] = copies

    def finish(i):
        k, first, size = chunks[i]
        total = accs3[i][z].astype(F32)
        for step in range(1, line):
            along_line[i][step - 1].wait_recv()
            total = total + ins4[i][lax.rem(z + line - step, line)].astype(F32)
        targets[k][:, first : first + size] = total

    more = []

    def send_more():
        if extras:
            more.extend(start_exchange(4, more_sources, more_targets, block_of, more_sems))

    in_steps(m, [send_core, send_first, send_second, send_line, finish], send_more)
    for copy in sent:
        copy.wait_send()
    for copy in more:
        copy.wait()


def staged_scatter(arrays, extras, block_of, collective_id, name, parts=6):
    seq_count, line = lax.axis_size("seq"), lax.axis_size("dp") // 2
    rows, n = arrays[0].shape[0] // (2 * line * seq_count), len(arrays)
    chunks = column_chunks([x.shape[1] for x in arrays], parts)
    m = len(chunks)
    leads = [(2, 2, line), (2, 2, line), (2, line), (2, line), (line,), (line,), (line,)]
    size = sum(x.shape[1] for x in arrays) * rows * 64
    anywhere = pl.BlockSpec(memory_space=pl.ANY)
    return pl.pallas_call(
        functools.partial(scatter_kernel, line, chunks, n, len(extras), block_of),
        out_shape=[jax.ShapeDtypeStruct((rows, x.shape[1]), F32) for x in arrays]
        + [jax.ShapeDtypeStruct((seq_count,) + x.shape[1:], BF16) for x in extras],
        in_specs=[anywhere] * (n + len(extras)),
        out_specs=[pl.BlockSpec(memory_space=pltpu.VMEM)] * n + [anywhere] * len(extras),
        scratch_shapes=[
            pltpu.VMEM(lead + (rows, width), BF16) for lead in leads for _, _, width in chunks
        ]
        + [
            pltpu.SemaphoreType.DMA((m, 2 + line)),
            pltpu.SemaphoreType.DMA((m, 2 + line)),
            pltpu.SemaphoreType.DMA((m,)),
        ]
        + (exchange_sems(len(extras), seq_count) if extras else []),
        compiler_params=pltpu.CompilerParams(
            collective_id=collective_id, vmem_limit_bytes=36 << 20
        ),
        cost_estimate=pl.CostEstimate(flops=0, bytes_accessed=size, transcendentals=0),
        name=name,
    )(*[x.reshape(2, 2, line, 2, rows, x.shape[1]) for x in arrays], *extras)


def rotate(values, cosines, sines):
    return values * cosines + pltpu.roll(values, HEAD_DIM // 2, 1) * sines


def attention_kernel(count, heads, kv_heads, *refs):
    length_ref, projected_ref, cos_ref, sin_ref = refs[:4]
    attended_ref, lse_ref, q_ref, kv_ref = refs[4:8]
    max_ref, sum_ref, acc_ref, send, recv = refs[8:]
    me = lax.axis_index("seq")
    rows, kv_width = q_ref.shape[0], kv_heads * HEAD_DIM
    q_width, group, scale = heads * HEAD_DIM, heads // kv_heads, 1.0 / math.sqrt(HEAD_DIM)
    greet([{"seq": lax.rem(me + step, count)} for step in range(1, count)])
    cosines, sines = cos_ref[...], sin_ref[...]
    for g in range(kv_heads):
        cols = slice(g * HEAD_DIM, (g + 1) * HEAD_DIM)
        keys = projected_ref[:, q_width + g * HEAD_DIM : q_width + (g + 1) * HEAD_DIM]
        kv_ref[me, :, cols] = rotate(keys, cosines, sines).astype(BF16)
    kv_ref[me, :, kv_width:] = projected_ref[:, q_width + kv_width :].astype(BF16)

    def to_later(peer):
        return pltpu.make_async_remote_copy(
            src_ref=kv_ref.at[me],
            dst_ref=kv_ref.at[me],
            send_sem=send.at[peer],
            recv_sem=recv.at[me],
            device_id={"seq": peer},
            device_id_type=MESH_IDS,
        )

    def start(peer, carry):
        to_later(peer).start()
        return carry

    lax.fori_loop(me + 1, count, start, 0)

    def one_query(h, carry):
        cols = pl.ds(pl.multiple_of(h * HEAD_DIM, HEAD_DIM), HEAD_DIM)
        q_ref[:, cols] = rotate(projected_ref[:, cols], cosines, sines).astype(BF16)
        return carry

    lax.fori_loop(0, heads, one_query, 0)
    max_ref[...] = jnp.full_like(max_ref, NEG_FILL)
    sum_ref[...] = jnp.zeros_like(sum_ref)
    acc_ref[...] = jnp.zeros_like(acc_ref)
    length = length_ref[0]
    query_pos = me * rows + lax.broadcasted_iota(jnp.int32, (rows, rows), 1)
    key_local = lax.broadcasted_iota(jnp.int32, (rows, rows), 0)

    def key_block(j):
        key_pos = j * rows + key_local
        mask = (key_pos <= query_pos) & (key_pos < length)
        for g in range(kv_heads):
            key_cols = slice(g * HEAD_DIM, (g + 1) * HEAD_DIM)
            value_cols = slice(kv_width + g * HEAD_DIM, kv_width + (g + 1) * HEAD_DIM)

            def one_head(i, carry):
                h = g * group + i
                cols = pl.ds(pl.multiple_of(h * HEAD_DIM, HEAD_DIM), HEAD_DIM)
                row = pl.ds(h, 1)
                keys, values = kv_ref[j, :, key_cols], kv_ref[j, :, value_cols]
                scores = jnp.where(mask, nt(keys, q_ref[:, cols]) * scale, NEG_FILL)
                before = max_ref[row, :]
                top = jnp.maximum(before, jnp.max(scores, axis=0, keepdims=True))
                shrink = jnp.exp(before - top)
                weights = jnp.exp(scores - top)
                max_ref[row, :] = top
                sum_ref[row, :] = sum_ref[row, :] * shrink + jnp.sum(weights, axis=0, keepdims=True)
                acc_ref[h] = acc_ref[h] * shrink + tn(values, weights.astype(BF16))
                return carry

            lax.fori_loop(0, group, one_head, 0, unroll=2)

    key_block(me)

    def earlier_block(j, carry):
        pltpu.make_async_remote_copy(
            src_ref=kv_ref.at[j],
            dst_ref=kv_ref.at[j],
            send_sem=send.at[j],
            recv_sem=recv.at[j],
            device_id={"seq": j},
            device_id_type=MESH_IDS,
        ).wait_recv()
        key_block(j)
        return carry

    lax.fori_loop(0, me, earlier_block, 0)
    lse_ref[...] = max_ref[...] + jnp.log(sum_ref[...])

    def finish(h, carry):
        cols = pl.ds(pl.multiple_of(h * HEAD_DIM, HEAD_DIM), HEAD_DIM)
        attended_ref[:, cols] = (acc_ref[h] / sum_ref[pl.ds(h, 1), :]).T.astype(BF16)
        return carry

    lax.fori_loop(0, heads, finish, 0)

    def sent(peer, carry):
        to_later(peer).wait_send()
        return carry

    lax.fori_loop(me + 1, count, sent, 0)


def attention(length, projected, cosines, sines, q_width, collective_id):
    count = lax.axis_size("seq")
    rows = projected.shape[0]
    kv_width = (projected.shape[1] - q_width) // 2
    heads, kv_heads = q_width // HEAD_DIM, kv_width // HEAD_DIM
    vmem = pl.BlockSpec(memory_space=pltpu.VMEM)
    return pl.pallas_call(
        functools.partial(attention_kernel, count, heads, kv_heads),
        out_shape=[
            jax.ShapeDtypeStruct((rows, q_width), BF16),
            jax.ShapeDtypeStruct((heads, rows), F32),
            jax.ShapeDtypeStruct((rows, q_width), BF16),
            jax.ShapeDtypeStruct((count, rows, 2 * kv_width), BF16),
        ],
        in_specs=[pl.BlockSpec(memory_space=pltpu.SMEM)] + [vmem] * 3,
        out_specs=[vmem] * 4,
        scratch_shapes=[
            pltpu.VMEM((heads, rows), F32),
            pltpu.VMEM((heads, rows), F32),
            pltpu.VMEM((heads, HEAD_DIM, rows), F32),
            pltpu.SemaphoreType.DMA((count,)),
            pltpu.SemaphoreType.DMA((count,)),
        ],
        compiler_params=pltpu.CompilerParams(
            collective_id=collective_id, vmem_limit_bytes=30 << 20
        ),
        cost_estimate=pl.CostEstimate(flops=0, bytes_accessed=1 << 20, transcendentals=0),
        name="attention_forward",
    )(length, projected, cosines, sines)


def attention_back_kernel(count, heads, kv_heads, *refs):
    length_ref, q_ref, kv_ref, grad_ref, lse_ref, attended_ref, cos_ref, sin_ref = refs[:8]
    out_ref, delta_ref, dq_ref, part_ref, leaving, arriving, send, recv = refs[8:]
    me = lax.axis_index("seq")
    rows, kv_width = q_ref.shape[0], kv_heads * HEAD_DIM
    group, scale = heads // kv_heads, 1.0 / math.sqrt(HEAD_DIM)
    greet([{"seq": lax.rem(me + step, count)} for step in range(1, count)])
    length = length_ref[0]
    query_pos = me * rows + lax.broadcasted_iota(jnp.int32, (rows, rows), 1)
    key_local = lax.broadcasted_iota(jnp.int32, (rows, rows), 0)
    dq_ref[...] = jnp.zeros_like(dq_ref)
    ones = jnp.ones((8, HEAD_DIM), BF16)
    for h in range(heads):
        cols = slice(h * HEAD_DIM, (h + 1) * HEAD_DIM)
        terms = grad_ref[:, cols].astype(F32) * attended_ref[:, cols].astype(F32)
        high = terms.astype(BF16)
        low = (terms - high.astype(F32)).astype(BF16)
        delta_ref[h : h + 1, :] = (nt(ones, high) + nt(ones, low))[:1]

    def key_block(j):
        key_pos = j * rows + key_local
        mask = (key_pos <= query_pos) & (key_pos < length)
        part_ref[...] = jnp.zeros_like(part_ref)
        key_rows = pl.ds(pl.multiple_of(j * rows, rows), rows)
        for g in range(kv_heads):
            key_cols = slice(g * HEAD_DIM, (g + 1) * HEAD_DIM)
            value_cols = slice(kv_width + g * HEAD_DIM, kv_width + (g + 1) * HEAD_DIM)

            def one_head(i, carry):
                h = g * group + i
                cols = pl.ds(pl.multiple_of(h * HEAD_DIM, HEAD_DIM), HEAD_DIM)
                keys, values = kv_ref[key_rows, key_cols], kv_ref[key_rows, value_cols]
                queries, grads = q_ref[:, cols], grad_ref[:, cols]
                scores = nt(keys, queries) * scale
                probs = jnp.where(mask, jnp.exp(scores - lse_ref[pl.ds(h, 1), :]), 0.0)
                prob_grad = nt(values, grads)
                score_grad = (probs * (prob_grad - delta_ref[pl.ds(h, 1), :])).astype(BF16)
                part_ref[:, key_cols] += nn(score_grad, queries)
                part_ref[:, value_cols] += nn(probs.astype(BF16), grads)
                dq_ref[:, cols] += tn(score_grad, keys)
                return carry

            lax.fori_loop(0, group, one_head, 0, unroll=3)
        part_ref[:, :kv_width] = part_ref[:, :kv_width] * scale

    def to_owner(j):
        return pltpu.make_async_remote_copy(
            src_ref=leaving.at[j],
            dst_ref=arriving.at[me],
            send_sem=send.at[j],
            recv_sem=recv.at[me],
            device_id={"seq": j},
            device_id_type=MESH_IDS,
        )

    def other_block(j, carry):
        key_block(j)
        leaving[j] = part_ref[...].astype(BF16)
        to_owner(j).start()
        return carry

    lax.fori_loop(0, me, other_block, 0)
    key_block(me)
    part_ref[...] = part_ref[...].astype(BF16).astype(F32)
    cosines, sines = cos_ref[...], -sin_ref[...]

    def one_query(h, carry):
        cols = pl.ds(pl.multiple_of(h * HEAD_DIM, HEAD_DIM), HEAD_DIM)
        out_ref[:, cols] = rotate(dq_ref[:, cols] * scale, cosines, sines).astype(BF16)
        return carry

    lax.fori_loop(0, heads, one_query, 0)

    def add_arrived(m, carry):
        pltpu.make_async_remote_copy(
            src_ref=leaving.at[m],
            dst_ref=arriving.at[m],
            send_sem=send.at[m],
            recv_sem=recv.at[m],
            device_id={"seq": m},
            device_id_type=MESH_IDS,
        ).wait_recv()
        part_ref[...] += arriving[m].astype(F32)
        return carry

    lax.fori_loop(me + 1, count, add_arrived, 0)
    first = heads * HEAD_DIM
    for g in range(kv_heads):
        cols = slice(g * HEAD_DIM, (g + 1) * HEAD_DIM)
        out_ref[:, first + g * HEAD_DIM : first + (g + 1) * HEAD_DIM] = rotate(
            part_ref[:, cols], cosines, sines
        ).astype(BF16)
    out_ref[:, first + kv_width :] = part_ref[:, kv_width:].astype(BF16)

    def sent(j, carry):
        to_owner(j).wait_send()
        return carry

    lax.fori_loop(0, me, sent, 0)


def attention_back(length, queries, kv_all, grads, lse, attended, cosines, sines, collective_id):
    count = lax.axis_size("seq")
    rows, q_width = queries.shape
    kv_width = kv_all.shape[1] // 2
    heads, kv_heads = q_width // HEAD_DIM, kv_width // HEAD_DIM
    vmem = pl.BlockSpec(memory_space=pltpu.VMEM)
    return pl.pallas_call(
        functools.partial(attention_back_kernel, count, heads, kv_heads),
        out_shape=jax.ShapeDtypeStruct((rows, q_width + 2 * kv_width), BF16),
        in_specs=[pl.BlockSpec(memory_space=pltpu.SMEM)] + [vmem] * 7,
        out_specs=vmem,
        scratch_shapes=[
            pltpu.VMEM((heads, rows), F32),
            pltpu.VMEM((rows, q_width), F32),
            pltpu.VMEM((rows, 2 * kv_width), F32),
            pltpu.VMEM((count, rows, 2 * kv_width), BF16),
            pltpu.VMEM((count, rows, 2 * kv_width), BF16),
            pltpu.SemaphoreType.DMA((count,)),
            pltpu.SemaphoreType.DMA((count,)),
        ],
        compiler_params=pltpu.CompilerParams(
            collective_id=collective_id, vmem_limit_bytes=30 << 20
        ),
        cost_estimate=pl.CostEstimate(
            flops=10 * count * rows * rows * q_width, bytes_accessed=1 << 20, transcendentals=0
        ),
        name="attention_backward",
    )(length, queries, kv_all, grads, lse, attended, cosines, sines)


def weight_grad_kernel(n, left_ref, *refs):
    for right_ref, out_ref in zip(refs[:n], refs[n:], strict=True):
        out_ref[...] = tn(left_ref[...], right_ref[...]).astype(BF16)


def weight_grads(left, rights, name):
    total, columns = left.shape
    tile = 256
    return pl.pallas_call(
        functools.partial(weight_grad_kernel, len(rights)),
        grid=(columns // tile,),
        out_shape=[jax.ShapeDtypeStruct((columns, r.shape[1]), BF16) for r in rights],
        in_specs=[pl.BlockSpec((total, tile), lambda i: (0, i))]
        + [
            pl.BlockSpec(r.shape, lambda i: (0, 0), pipeline_mode=pl.Buffered(1)) for r in rights
        ],
        out_specs=[pl.BlockSpec((tile, r.shape[1]), lambda i: (i, 0)) for r in rights],
        compiler_params=pltpu.CompilerParams(vmem_limit_bytes=48 << 20),
        cost_estimate=pl.CostEstimate(flops=0, bytes_accessed=1 << 20, transcendentals=0),
        name=name,
    )(left, *rights)


def seq_permutes(block_for):
    count, me = lax.axis_size("seq"), lax.axis_index("seq")
    pieces = [block_for(me)]
    for step in range(1, count):
        ring = [(i, (i + step) % count) for i in range(count)]
        pieces.append(lax.ppermute(block_for(lax.rem(me + step, count)), "seq", ring))
    return pieces


def in_seq_order(pieces, dtype):
    count, me = len(pieces), lax.axis_index("seq")
    whole = jnp.zeros((count,) + pieces[0].shape, dtype)
    for step, piece in enumerate(pieces):
        place = lax.rem(me + count - step, count)
        whole = lax.dynamic_update_index_in_dim(whole, piece.astype(dtype), place, 0)
    return whole


def on_device(
    hidden_in,
    lengths,
    routes,
    gates,
    priority,
    attn_gain,
    mlp_gain,
    w_query,
    key_projection,
    value_projection,
    w_out,
    w_gate,
    w_up,
    w_down,
    cotangent,
):
    rows = hidden_in.shape[1]
    width = hidden_in.shape[2]
    dp_count = lax.axis_size("dp")
    seq_count = lax.axis_size("seq")
    devices = dp_count * seq_count
    own_experts = w_gate.shape[0]
    sharers = seq_count // own_experts
    hidden_units = w_gate.shape[2]
    my_seq = lax.axis_index("seq")
    extent = rows * seq_count
    query_pos = my_seq * rows + jnp.arange(rows, dtype=jnp.int32)
    length = lengths[0]
    is_valid = query_pos < length
    q_width = w_query.shape[1]
    kv_width = key_projection.shape[1]
    cosine_lookup, sine_lookup = rope_angles(query_pos, HEAD_DIM)

    gain_block = jnp.concatenate(
        [attn_gain[:, None], mlp_gain[:, None], jnp.zeros((attn_gain.shape[0], LANES - 2), BF16)],
        axis=1,
    )
    packed = jnp.concatenate([w_query, key_projection, value_projection], axis=1)
    staged = seq_count == 4 and w_query.shape[0] % 16 == 0

    def expert_pieces(weights):
        def block_for(peer):
            return lax.dynamic_index_in_dim(weights, peer // sharers, 0, keepdims=False)

        return seq_permutes(block_for)

    gate_parts = expert_pieces(w_gate)
    if staged:
        packed_full, gains_full, out_full = staged_gather(
            [packed, gain_block, w_out], [], None, 2, "gather_attention_weights"
        )
    else:
        packed_full = lax.all_gather(packed, BOTH, axis=0, tiled=True)
        gains_full = lax.all_gather(gain_block, BOTH, axis=0, tiled=True)
        out_full = lax.all_gather(w_out, BOTH, axis=0, tiled=True)

    pair_routes, place, kept = claim_places(routes[0], priority[0, 0], is_valid)
    holder = (pair_routes // own_experts) * seq_count + (pair_routes % own_experts) * sharers
    holder = holder + my_seq * sharers // seq_count
    slots = devices * CAP
    target = jnp.where(kept, holder * CAP + place, slots).reshape(rows, TOP)
    slot_ids = jnp.arange(slots, dtype=jnp.int32)
    hits = target[:, :, None] == slot_ids[None, None, :]
    gate_rows = gates[0]
    token_hot = jnp.any(hits, axis=1).astype(BF16)

    def hot_of(first, size):
        mine = kept & (place >= first) & (place < first + size)
        spot = jnp.where(mine, holder * size + place - first, slots).reshape(rows, TOP)
        ids = jnp.arange(devices * size, dtype=jnp.int32)
        return jnp.any(spot[:, :, None] == ids[None, None, :], axis=1).astype(BF16)

    early_hot, late_hot = hot_of(0, EARLY), hot_of(EARLY, CAP - EARLY)
    slot_gate = jnp.sum(jnp.where(hits, gate_rows[:, :, None], 0.0), axis=(0, 1))

    live_cotangent = jnp.where(is_valid[:, None], cotangent[0], jnp.zeros((), BF16))
    out_grad = live_cotangent.astype(F32)
    grad_send = (tn(token_hot, live_cotangent) * slot_gate[:, None]).astype(BF16)
    packed_full, gains_full, out_full, gate_parts, grad_send = lax.optimization_barrier(
        (packed_full, gains_full, out_full, gate_parts, grad_send)
    )
    gain_one, gain_two = gains_full[:, 0].astype(F32), gains_full[:, 1].astype(F32)
    grad_rows = swap(grad_send.reshape(devices, CAP, width), ("dp", "seq"))

    inputs = hidden_in[0].astype(F32)
    scale_one = lax.rsqrt(jnp.mean(inputs * inputs, axis=-1, keepdims=True) + EPSILON)
    normed = (inputs * scale_one * gain_one).astype(BF16)
    projected = nn(normed, packed_full)
    cosines, sines = cosine_lookup[:, 0], sine_lookup[:, 0]
    cosines = jnp.concatenate([cosines, cosines], axis=1)
    sines = jnp.concatenate([-sines, sines], axis=1)
    attended, log_total, query_flat, kv_all = attention(
        lengths, projected, cosines, sines, q_width, 1
    )
    kv_all = kv_all.reshape(extent, 2 * kv_width)
    attended, w_up = lax.optimization_barrier((attended, w_up))
    up_parts = expert_pieces(w_up)
    middle = inputs + nn(attended, out_full)
    scale_two = lax.rsqrt(jnp.mean(middle * middle, axis=-1, keepdims=True) + EPSILON)
    moe_input = (middle * scale_two * gain_two).astype(BF16)

    def to_experts(hot):
        return tn(hot, moe_input).astype(BF16).reshape(devices, -1, width)

    early_send, late_send = to_experts(early_hot), to_experts(late_hot)
    early_send, late_send, grad_rows, up_parts, w_down = lax.optimization_barrier(
        (early_send, late_send, grad_rows, up_parts, w_down)
    )
    early_grads, late_grads, w_down = lax.optimization_barrier(
        (grad_rows[:, :EARLY], grad_rows[:, EARLY:], w_down)
    )
    down_parts = expert_pieces(w_down)
    early_rows = swap(early_send, ("dp", "seq"))
    early_rows, late_send = lax.optimization_barrier((early_rows, late_send))
    late_rows = swap(late_send, ("dp", "seq"))
    gate_full = in_seq_order(gate_parts, BF16).reshape(width, hidden_units)
    up_full = in_seq_order(up_parts, BF16).reshape(width, hidden_units)
    down_full = in_seq_order(down_parts, BF16).reshape(hidden_units, width)
    early_rows, gate_full, up_full, down_full, early_grads, late_grads = (
        lax.optimization_barrier(
            (early_rows, gate_full, up_full, down_full, early_grads, late_grads)
        )
    )

    def run_expert(slot_rows, grads):
        blocks = slot_rows.shape[:2]
        slot_rows, grads = slot_rows.reshape(-1, width), grads.reshape(-1, width)
        gate_pre = nn(slot_rows, gate_full)
        up_pre = nn(slot_rows, up_full)
        gate_sigmoid = jax.nn.sigmoid(gate_pre)
        gate_act = gate_pre * gate_sigmoid
        gate_slope = gate_sigmoid * (1.0 + gate_pre * (1.0 - gate_sigmoid))
        hidden = (gate_act * up_pre).astype(BF16)
        hidden_grad = nt(grads, down_full)
        gate_pre_grad = (hidden_grad * up_pre * gate_slope).astype(BF16)
        up_pre_grad = (hidden_grad * gate_act).astype(BF16)
        return [x.reshape(blocks + (-1,)) for x in (hidden, gate_pre_grad, up_pre_grad)]

    def row_grads(gate_pre_grad, up_pre_grad):
        blocks = gate_pre_grad.shape[:2]
        gate_pre_grad = gate_pre_grad.reshape(-1, hidden_units)
        up_pre_grad = up_pre_grad.reshape(-1, hidden_units)
        row_grad = (nt(gate_pre_grad, gate_full) + nt(up_pre_grad, up_full)).astype(BF16)
        return row_grad.reshape(blocks + (width,))

    def both_parts(early, late):
        return jnp.concatenate([early, late], axis=1).reshape(slots, -1)

    def to_owners(grad):
        grad = grad.reshape(seq_count, -1, grad.shape[1])

        def block_for(peer):
            return lax.dynamic_index_in_dim(grad, peer, 0, keepdims=False)

        return seq_permutes(block_for)

    def owned_sum(pieces):
        whole = in_seq_order(pieces, F32)
        return jnp.sum(whole.reshape((own_experts, sharers) + whole.shape[1:]), axis=1)

    early_hidden, *early_pre_grads = run_expert(early_rows, early_grads)
    early_row_grad = row_grads(*early_pre_grads)
    late_rows, early_row_grad = lax.optimization_barrier((late_rows, early_row_grad))
    early_back = swap(early_row_grad, ("dp", "seq"))
    late_hidden, *late_pre_grads = run_expert(late_rows, late_grads)
    expert_hidden = both_parts(early_hidden, late_hidden)
    (down_grad,) = weight_grads(expert_hidden, [grad_rows.reshape(slots, width)], "down_grads")
    late_rows, late_pre_grads, down_grad = lax.optimization_barrier(
        (late_rows, late_pre_grads, down_grad)
    )
    down_grad_parts = to_owners(down_grad)
    slot_rows = both_parts(early_rows, late_rows)
    gate_pre_grad, up_pre_grad = map(both_parts, early_pre_grads, late_pre_grads)
    gate_grad, up_grad = weight_grads(slot_rows, [gate_pre_grad, up_pre_grad], "gate_up_grads")
    late_row_grad = row_grads(*late_pre_grads)
    early_back, late_row_grad, down_grad_parts, gate_grad, up_grad, expert_hidden = (
        lax.optimization_barrier(
            (early_back, late_row_grad, down_grad_parts, gate_grad, up_grad, expert_hidden)
        )
    )
    late_back = swap(late_row_grad, ("dp", "seq"))
    gate_owned, up_owned = owned_sum(to_owners(gate_grad)), owned_sum(to_owners(up_grad))
    down_owned = owned_sum(down_grad_parts)
    expert_out = nn(expert_hidden, down_full).astype(BF16)
    expert_out, late_back, gate_owned, up_owned, down_owned = lax.optimization_barrier(
        (expert_out, late_back, gate_owned, up_owned, down_owned)
    )
    returned = swap(expert_out.reshape(devices, CAP, width), ("dp", "seq")).reshape(slots, width)
    early_back, late_back = early_back.reshape(-1, width), late_back.reshape(-1, width)
    moe_input_grad = nn(early_hot, early_back) + nn(late_hot, late_back)
    middle_norm_grad, gain_two_grad = norm_back(middle, scale_two, gain_two, moe_input_grad)
    middle_grad = out_grad + middle_norm_grad
    branch_grad = middle_grad.astype(BF16)
    out_terms = tn(attended, branch_grad).astype(BF16)
    attended_grad = nt(branch_grad, out_full).astype(BF16)
    projected_grad = attention_back(
        lengths,
        query_flat,
        kv_all,
        attended_grad,
        log_total,
        attended,
        cosines,
        sines,
        4,
    )
    normed_grad = nt(projected_grad, packed_full)
    input_norm_grad, gain_one_grad = norm_back(inputs, scale_one, gain_one, normed_grad)
    input_grad = middle_grad + input_norm_grad

    lane = lax.broadcasted_iota(jnp.int32, (width, LANES), 1)
    gain_terms = jnp.where(lane == 0, gain_one_grad[:, None], gain_two_grad[:, None])
    gain_terms = jnp.where(lane < 2, gain_terms, 0.0).astype(BF16)
    query_terms = tn(normed, projected_grad).astype(BF16)
    if staged:
        out_owned, gains_owned, owned = staged_scatter(
            [out_terms, gain_terms, query_terms], [], None, 6, "scatter_attention_grads"
        )
    else:
        terms = jnp.concatenate([out_terms, gain_terms, query_terms], axis=1)
        terms = lax.psum_scatter(terms, BOTH, scatter_dimension=0, tiled=True).astype(F32)
        out_owned, gains_owned = terms[:, :width], terms[:, width : width + LANES]
        owned = terms[:, width + LANES :]
    returned, owned = lax.optimization_barrier((returned, owned))
    expert_grads = [gate_owned, up_owned, down_owned]

    gate_hot = jnp.sum(jnp.where(hits, gate_rows[:, :, None], 0.0), axis=1).astype(BF16)
    layer_out = middle + nn(gate_hot, returned)
    return (
        layer_out[None],
        input_grad[None],
        gains_owned[:, 0],
        gains_owned[:, 1],
        owned[:, :q_width],
        owned[:, q_width : q_width + kv_width],
        owned[:, q_width + kv_width : q_width + 2 * kv_width],
        out_owned,
        *expert_grads,
    )


def solution(mesh):
    part = P("dp", "seq", None)
    both = P(BOTH)
    both_rows = P(BOTH, None)
    return jax.shard_map(
        on_device,
        mesh=mesh,
        in_specs=(part, P("dp"), part, part, part, both, both)
        + (both_rows,) * 4
        + (part,) * 4,
        out_specs=(part, part, both, both) + (both_rows,) * 4 + (part,) * 3,
        check_vma=False,
    )
```

```python
import functools
import math

import jax
import jax.numpy as jnp
from jax import lax
from jax.experimental import pallas as pl
from jax.experimental.pallas import tpu as pltpu
from jax.sharding import PartitionSpec as P

HEAD_DIM = 128
EXPERTS = 32
TOP = 4
CAP = 40
EARLY = 24

EPSILON = 1e-06
ROPE_BASE = 10000.0
NEG_FILL = -1e30
LANES = 128
BOTH = ("seq", "dp")
BF16 = jnp.bfloat16
F32 = jnp.float32


def rope_angles(positions, head_size):
    half_dim = head_size // 2
    frequency = ROPE_BASE ** (-(2.0 * jnp.arange(half_dim, dtype=F32)) / head_size)
    angles = positions.astype(F32)[:, None] * frequency[None, :]
    return (jnp.cos(angles)[:, None, :], jnp.sin(angles)[:, None, :])


def dot(left, right, contract):
    return lax.dot_general(left, right, (contract, ((), ())), preferred_element_type=F32)


def nn(left, right):
    return dot(left, right, ((1,), (0,)))


def nt(left, right):
    return dot(left, right, ((1,), (1,)))


def tn(left, right):
    return dot(left, right, ((0,), (0,)))


def claim_places(routes, priority, is_valid):
    pair_routes = routes.reshape(-1)
    live = jnp.repeat(is_valid, TOP)
    key = jnp.where(live, pair_routes, -1)
    earlier = (key[None, :] == pair_routes[:, None]) & (priority[None, :] < priority[:, None])
    place = jnp.sum(earlier.astype(F32), axis=1).astype(jnp.int32)
    return pair_routes, place, live & (place < CAP)


def norm_back(values, scale_rows, gain_vec, incoming):
    weighted = incoming * gain_vec
    inner_mean = jnp.mean(weighted * values, axis=-1, keepdims=True)
    values_grad = scale_rows * weighted - values * scale_rows * scale_rows * scale_rows * inner_mean
    return (values_grad, jnp.sum(incoming * values * scale_rows, axis=0))


def swap(blocks, axes):
    return lax.all_to_all(blocks, axes, split_axis=0, concat_axis=0, tiled=True)


MESH_IDS = pl.DeviceIdType.MESH


def torus_place():
    seq, dp = lax.axis_index("seq"), lax.axis_index("dp")
    return seq // 2, seq % 2, dp // 2, dp % 2


def torus_id(a, b, z, c):
    return {"seq": 2 * a + b, "dp": 2 * z + c}


def torus_peers(line):
    a, b, z, c = torus_place()
    peers = [torus_id(a, b, z, 1 - c), torus_id(a, 1 - b, z, c), torus_id(1 - a, b, z, c)]
    peers.append(torus_id(1 - a, 1 - b, z, c))
    return peers + [torus_id(a, b, lax.rem(z + k, line), c) for k in range(1, line)]


def greet(peers):
    barrier = pltpu.get_barrier_semaphore()
    for peer in peers:
        pl.semaphore_signal(barrier, inc=1, device_id=peer, device_id_type=MESH_IDS)
    pl.semaphore_wait(barrier, len(peers))


def column_chunks(widths, parts):
    chunks = []
    for part in range(parts):
        for k, whole in enumerate(widths):
            tiles = whole // LANES
            first, end = tiles * part // parts, tiles * (part + 1) // parts
            if end > first:
                chunks.append((k, first * LANES, (end - first) * LANES))
    return chunks


def remote(src, dst, sems, i, j, device_id):
    send, recv = sems
    return pltpu.make_async_remote_copy(
        src_ref=src,
        dst_ref=dst,
        send_sem=send.at[i, j],
        recv_sem=recv.at[i, j],
        device_id=device_id,
        device_id_type=MESH_IDS,
    )


def start_exchange(count, sources, targets, block_of, sems):
    send_sems, recv_sems, local_sems = sems
    me = lax.axis_index("seq")
    copies = []
    for i, source in enumerate(sources):
        for step in range(1, count):
            peer = lax.rem(me + step, count)
            copies.append(
                pltpu.make_async_remote_copy(
                    src_ref=block_of(source, peer),
                    dst_ref=targets[i].at[me],
                    send_sem=send_sems.at[i, step - 1],
                    recv_sem=recv_sems.at[i, step - 1],
                    device_id={"seq": peer},
                    device_id_type=MESH_IDS,
                )
            )
        copies.append(
            pltpu.make_async_copy(block_of(source, me), targets[i].at[me], local_sems.at[i])
        )
    for copy in copies:
        copy.start()
    return copies


def exchange_sems(n, count):
    return [
        pltpu.SemaphoreType.DMA((n, count - 1)),
        pltpu.SemaphoreType.DMA((n, count - 1)),
        pltpu.SemaphoreType.DMA((n,)),
    ]


def in_steps(count, stages, after=None):
    for step in range((count + 1) // 2 + len(stages) - 1):
        if after is not None and step == (count + 1) // 2 + 1:
            after()
        for behind, stage in enumerate(stages):
            for i in (2 * (step - behind), 2 * (step - behind) + 1):
                if 0 <= i < count:
                    stage(i)


def gather_kernel(line, chunks, n, extras, block_of, *refs):
    sources, more_sources = refs[:n], refs[n : n + extras]
    refs = refs[n + extras :]
    targets, more_targets = refs[:n], refs[n : n + extras]
    send, recv, local, *more_sems = refs[n + extras :]
    sems = (send, recv)
    a, b, z, c = torus_place()
    greet(torus_peers(line))
    more = start_exchange(4, more_sources, more_targets, block_of, more_sems) if extras else []
    sent = []

    def start(copy):
        copy.start()
        sent.append(copy)
        return copy

    along_line, first_hop, second_hop, third_hop = {}, {}, {}, {}

    def send_line(i):
        k, first, size = chunks[i]
        cols = pl.ds(first, size)
        own = targets[k].at[a, b, z, c, :, cols]
        keep = pltpu.make_async_copy(sources[k].at[:, cols], own, local.at[i])
        keep.start()
        along_line[i] = [
            start(
                remote(
                    sources[k].at[:, cols],
                    own,
                    sems,
                    i,
                    2 + step,
                    torus_id(a, b, lax.rem(z + step, line), c),
                )
            )
            for step in range(1, line)
        ]
        along_line[i].append(keep)

    def send_first(i):
        k, first, size = chunks[i]
        *copies, keep = along_line[i]
        keep.wait()
        for copy in copies:
            copy.wait_recv()
        block = targets[k].at[a, b, :, c, :, pl.ds(first, size)]
        peer = torus_id(a, 1 - b, z, c) if i % 2 == 0 else torus_id(1 - a, b, z, c)
        first_hop[i] = start(remote(block, block, sems, i, 1, peer))

    def send_second(i):
        k, first, size = chunks[i]
        first_hop[i].wait_recv()
        cols = pl.ds(first, size)
        if i % 2 == 0:
            block, peer = targets[k].at[a, :, :, c, :, cols], torus_id(1 - a, b, z, c)
        else:
            block, peer = targets[k].at[:, b, :, c, :, cols], torus_id(a, 1 - b, z, c)
        second_hop[i] = start(remote(block, block, sems, i, 2, peer))

    def send_third(i):
        k, first, size = chunks[i]
        second_hop[i].wait_recv()
        block = targets[k].at[:, :, :, c, :, pl.ds(first, size)]
        third_hop[i] = start(remote(block, block, sems, i, 0, torus_id(a, b, z, 1 - c)))

    in_steps(len(chunks), [send_line, send_first, send_second, send_third])
    for copy in third_hop.values():
        copy.wait_recv()
    for copy in sent:
        copy.wait_send()
    for copy in more:
        copy.wait()


def staged_gather(arrays, extras, block_of, collective_id, name, parts=6):
    seq_count, line = lax.axis_size("seq"), lax.axis_size("dp") // 2
    rows, n = arrays[0].shape[0], len(arrays)
    chunks = column_chunks([x.shape[1] for x in arrays], parts)
    m = len(chunks)
    shape = (seq_count // 2, 2, line, 2, rows)
    size = sum(x.shape[1] for x in arrays) * rows * 64
    count = n + len(extras)
    outs = pl.pallas_call(
        functools.partial(gather_kernel, line, chunks, n, len(extras), block_of),
        out_shape=[jax.ShapeDtypeStruct(shape + (x.shape[1],), BF16) for x in arrays]
        + [jax.ShapeDtypeStruct((seq_count,) + x.shape[1:], BF16) for x in extras],
        in_specs=[pl.BlockSpec(memory_space=pl.ANY)] * count,
        out_specs=[pl.BlockSpec(memory_space=pl.ANY)] * count,
        scratch_shapes=[
            pltpu.SemaphoreType.DMA((m, 2 + line)),
            pltpu.SemaphoreType.DMA((m, 2 + line)),
            pltpu.SemaphoreType.DMA((m,)),
        ]
        + (exchange_sems(len(extras), seq_count) if extras else []),
        compiler_params=pltpu.CompilerParams(
            collective_id=collective_id, vmem_limit_bytes=4 << 20
        ),
        cost_estimate=pl.CostEstimate(flops=0, bytes_accessed=size, transcendentals=0),
        name=name,
    )(*arrays, *extras)
    return [o.reshape(-1, o.shape[-1]) for o in outs]


def scatter_kernel(line, chunks, n, extras, block_of, *refs):
    m = len(chunks)
    sources, more_sources = refs[:n], refs[n : n + extras]
    refs = refs[n + extras :]
    targets, more_targets = refs[:n], refs[n : n + extras]
    scratch = refs[n + extras :]
    owns, ins1, accs2, ins2, accs3, ins3, ins4 = (scratch[m * s : m * (s + 1)] for s in range(7))
    send, recv, local, *more_sems = scratch[7 * m :]
    sems = (send, recv)
    a, b, z, c = torus_place()
    greet(torus_peers(line))
    sent = []

    def start(copy):
        copy.start()
        sent.append(copy)
        return copy

    def add_lines(target, left, right):
        def one(j, carry):
            target[j] = (left[j].astype(F32) + right[j].astype(F32)).astype(BF16)
            return carry

        lax.fori_loop(0, line, one, 0)

    between_cores, first_hop, second_hop, along_line = {}, {}, {}, {}

    def send_core(i):
        k, first, size = chunks[i]
        cols = pl.ds(first, size)
        keep = pltpu.make_async_copy(sources[k].at[:, :, :, c, :, cols], owns[i], local.at[i])
        keep.start()
        swap_core = remote(
            sources[k].at[:, :, :, 1 - c, :, cols], ins1[i], sems, i, 0, torus_id(a, b, z, 1 - c)
        )
        between_cores[i] = (keep, start(swap_core))

    def send_first(i):
        keep, copy = between_cores[i]
        keep.wait()
        copy.wait_recv()
        for p in range(2):
            for q in range(2):
                add_lines(owns[i].at[p, q], owns[i].at[p, q], ins1[i].at[p, q])
        if i % 2 == 0:
            block, peer = owns[i].at[:, 1 - b], torus_id(a, 1 - b, z, c)
        else:
            block, peer = owns[i].at[1 - a], torus_id(1 - a, b, z, c)
        first_hop[i] = start(remote(block, ins2[i], sems, i, 1, peer))

    def send_second(i):
        first_hop[i].wait_recv()
        for p in range(2):
            mine = owns[i].at[p, b] if i % 2 == 0 else owns[i].at[a, p]
            add_lines(accs2[i].at[p], mine, ins2[i].at[p])
        if i % 2 == 0:
            block, peer = accs2[i].at[1 - a], torus_id(1 - a, b, z, c)
        else:
            block, peer = accs2[i].at[1 - b], torus_id(a, 1 - b, z, c)
        second_hop[i] = start(remote(block, ins3[i], sems, i, 2, peer))

    def send_line(i):
        second_hop[i].wait_recv()
        add_lines(accs3[i], accs2[i].at[a if i % 2 == 0 else b], ins3[i])
        copies = []
        for step in range(1, line):
            to = lax.rem(z + step, line)
            peer = torus_id(a, b, to, c)
            copies.append(start(remote(accs3[i].at[to], ins4[i].at[z], sems, i, 2 + step, peer)))
        along_line[i] = copies

    def finish(i):
        k, first, size = chunks[i]
        total = accs3[i][z].astype(F32)
        for step in range(1, line):
            along_line[i][step - 1].wait_recv()
            total = total + ins4[i][lax.rem(z + line - step, line)].astype(F32)
        targets[k][:, first : first + size] = total

    more = []

    def send_more():
        if extras:
            more.extend(start_exchange(4, more_sources, more_targets, block_of, more_sems))

    in_steps(m, [send_core, send_first, send_second, send_line, finish], send_more)
    for copy in sent:
        copy.wait_send()
    for copy in more:
        copy.wait()


def staged_scatter(arrays, extras, block_of, collective_id, name, parts=6):
    seq_count, line = lax.axis_size("seq"), lax.axis_size("dp") // 2
    rows, n = arrays[0].shape[0] // (2 * line * seq_count), len(arrays)
    chunks = column_chunks([x.shape[1] for x in arrays], parts)
    m = len(chunks)
    leads = [(2, 2, line), (2, 2, line), (2, line), (2, line), (line,), (line,), (line,)]
    size = sum(x.shape[1] for x in arrays) * rows * 64
    anywhere = pl.BlockSpec(memory_space=pl.ANY)
    return pl.pallas_call(
        functools.partial(scatter_kernel, line, chunks, n, len(extras), block_of),
        out_shape=[jax.ShapeDtypeStruct((rows, x.shape[1]), F32) for x in arrays]
        + [jax.ShapeDtypeStruct((seq_count,) + x.shape[1:], BF16) for x in extras],
        in_specs=[anywhere] * (n + len(extras)),
        out_specs=[pl.BlockSpec(memory_space=pltpu.VMEM)] * n + [anywhere] * len(extras),
        scratch_shapes=[
            pltpu.VMEM(lead + (rows, width), BF16) for lead in leads for _, _, width in chunks
        ]
        + [
            pltpu.SemaphoreType.DMA((m, 2 + line)),
            pltpu.SemaphoreType.DMA((m, 2 + line)),
            pltpu.SemaphoreType.DMA((m,)),
        ]
        + (exchange_sems(len(extras), seq_count) if extras else []),
        compiler_params=pltpu.CompilerParams(
            collective_id=collective_id, vmem_limit_bytes=36 << 20
        ),
        cost_estimate=pl.CostEstimate(flops=0, bytes_accessed=size, transcendentals=0),
        name=name,
    )(*[x.reshape(2, 2, line, 2, rows, x.shape[1]) for x in arrays], *extras)


def rotate(values, cosines, sines):
    return values * cosines + pltpu.roll(values, HEAD_DIM // 2, 1) * sines


def attention_kernel(count, heads, kv_heads, *refs):
    length_ref, projected_ref, cos_ref, sin_ref = refs[:4]
    attended_ref, lse_ref, q_ref, kv_ref = refs[4:8]
    max_ref, sum_ref, acc_ref, send, recv = refs[8:]
    me = lax.axis_index("seq")
    rows, kv_width = q_ref.shape[0], kv_heads * HEAD_DIM
    q_width, group, scale = heads * HEAD_DIM, heads // kv_heads, 1.0 / math.sqrt(HEAD_DIM)
    greet([{"seq": lax.rem(me + step, count)} for step in range(1, count)])
    cosines, sines = cos_ref[...], sin_ref[...]
    for g in range(kv_heads):
        cols = slice(g * HEAD_DIM, (g + 1) * HEAD_DIM)
        keys = projected_ref[:, q_width + g * HEAD_DIM : q_width + (g + 1) * HEAD_DIM]
        kv_ref[me, :, cols] = rotate(keys, cosines, sines).astype(BF16)
    kv_ref[me, :, kv_width:] = projected_ref[:, q_width + kv_width :].astype(BF16)

    def to_later(peer):
        return pltpu.make_async_remote_copy(
            src_ref=kv_ref.at[me],
            dst_ref=kv_ref.at[me],
            send_sem=send.at[peer],
            recv_sem=recv.at[me],
            device_id={"seq": peer},
            device_id_type=MESH_IDS,
        )

    def start(peer, carry):
        to_later(peer).start()
        return carry

    lax.fori_loop(me + 1, count, start, 0)

    def one_query(h, carry):
        cols = pl.ds(pl.multiple_of(h * HEAD_DIM, HEAD_DIM), HEAD_DIM)
        q_ref[:, cols] = rotate(projected_ref[:, cols], cosines, sines).astype(BF16)
        return carry

    lax.fori_loop(0, heads, one_query, 0)
    max_ref[...] = jnp.full_like(max_ref, NEG_FILL)
    sum_ref[...] = jnp.zeros_like(sum_ref)
    acc_ref[...] = jnp.zeros_like(acc_ref)
    length = length_ref[0]
    query_pos = me * rows + lax.broadcasted_iota(jnp.int32, (rows, rows), 1)
    key_local = lax.broadcasted_iota(jnp.int32, (rows, rows), 0)

    def key_block(j):
        key_pos = j * rows + key_local
        mask = (key_pos <= query_pos) & (key_pos < length)
        for g in range(kv_heads):
            key_cols = slice(g * HEAD_DIM, (g + 1) * HEAD_DIM)
            value_cols = slice(kv_width + g * HEAD_DIM, kv_width + (g + 1) * HEAD_DIM)

            def one_head(i, carry):
                h = g * group + i
                cols = pl.ds(pl.multiple_of(h * HEAD_DIM, HEAD_DIM), HEAD_DIM)
                row = pl.ds(h, 1)
                keys, values = kv_ref[j, :, key_cols], kv_ref[j, :, value_cols]
                scores = jnp.where(mask, nt(keys, q_ref[:, cols]) * scale, NEG_FILL)
                before = max_ref[row, :]
                top = jnp.maximum(before, jnp.max(scores, axis=0, keepdims=True))
                shrink = jnp.exp(before - top)
                weights = jnp.exp(scores - top)
                max_ref[row, :] = top
                sum_ref[row, :] = sum_ref[row, :] * shrink + jnp.sum(weights, axis=0, keepdims=True)
                acc_ref[h] = acc_ref[h] * shrink + tn(values, weights.astype(BF16))
                return carry

            lax.fori_loop(0, group, one_head, 0, unroll=2)

    key_block(me)

    def earlier_block(j, carry):
        pltpu.make_async_remote_copy(
            src_ref=kv_ref.at[j],
            dst_ref=kv_ref.at[j],
            send_sem=send.at[j],
            recv_sem=recv.at[j],
            device_id={"seq": j},
            device_id_type=MESH_IDS,
        ).wait_recv()
        key_block(j)
        return carry

    lax.fori_loop(0, me, earlier_block, 0)
    lse_ref[...] = max_ref[...] + jnp.log(sum_ref[...])

    def finish(h, carry):
        cols = pl.ds(pl.multiple_of(h * HEAD_DIM, HEAD_DIM), HEAD_DIM)
        attended_ref[:, cols] = (acc_ref[h] / sum_ref[pl.ds(h, 1), :]).T.astype(BF16)
        return carry

    lax.fori_loop(0, heads, finish, 0)

    def sent(peer, carry):
        to_later(peer).wait_send()
        return carry

    lax.fori_loop(me + 1, count, sent, 0)


def attention(length, projected, cosines, sines, q_width, collective_id):
    count = lax.axis_size("seq")
    rows = projected.shape[0]
    kv_width = (projected.shape[1] - q_width) // 2
    heads, kv_heads = q_width // HEAD_DIM, kv_width // HEAD_DIM
    vmem = pl.BlockSpec(memory_space=pltpu.VMEM)
    return pl.pallas_call(
        functools.partial(attention_kernel, count, heads, kv_heads),
        out_shape=[
            jax.ShapeDtypeStruct((rows, q_width), BF16),
            jax.ShapeDtypeStruct((heads, rows), F32),
            jax.ShapeDtypeStruct((rows, q_width), BF16),
            jax.ShapeDtypeStruct((count, rows, 2 * kv_width), BF16),
        ],
        in_specs=[pl.BlockSpec(memory_space=pltpu.SMEM)] + [vmem] * 3,
        out_specs=[vmem] * 4,
        scratch_shapes=[
            pltpu.VMEM((heads, rows), F32),
            pltpu.VMEM((heads, rows), F32),
            pltpu.VMEM((heads, HEAD_DIM, rows), F32),
            pltpu.SemaphoreType.DMA((count,)),
            pltpu.SemaphoreType.DMA((count,)),
        ],
        compiler_params=pltpu.CompilerParams(
            collective_id=collective_id, vmem_limit_bytes=30 << 20
        ),
        cost_estimate=pl.CostEstimate(flops=0, bytes_accessed=1 << 20, transcendentals=0),
        name="attention_forward",
    )(length, projected, cosines, sines)


def attention_back_kernel(count, heads, kv_heads, *refs):
    length_ref, q_ref, kv_ref, grad_ref, lse_ref, attended_ref, cos_ref, sin_ref = refs[:8]
    out_ref, delta_ref, dq_ref, part_ref, leaving, arriving, send, recv = refs[8:]
    me = lax.axis_index("seq")
    rows, kv_width = q_ref.shape[0], kv_heads * HEAD_DIM
    group, scale = heads // kv_heads, 1.0 / math.sqrt(HEAD_DIM)
    greet([{"seq": lax.rem(me + step, count)} for step in range(1, count)])
    length = length_ref[0]
    query_pos = me * rows + lax.broadcasted_iota(jnp.int32, (rows, rows), 1)
    key_local = lax.broadcasted_iota(jnp.int32, (rows, rows), 0)
    dq_ref[...] = jnp.zeros_like(dq_ref)
    ones = jnp.ones((8, HEAD_DIM), BF16)
    for h in range(heads):
        cols = slice(h * HEAD_DIM, (h + 1) * HEAD_DIM)
        terms = grad_ref[:, cols].astype(F32) * attended_ref[:, cols].astype(F32)
        high = terms.astype(BF16)
        low = (terms - high.astype(F32)).astype(BF16)
        delta_ref[h : h + 1, :] = (nt(ones, high) + nt(ones, low))[:1]

    def key_block(j):
        key_pos = j * rows + key_local
        mask = (key_pos <= query_pos) & (key_pos < length)
        part_ref[...] = jnp.zeros_like(part_ref)
        key_rows = pl.ds(pl.multiple_of(j * rows, rows), rows)
        for g in range(kv_heads):
            key_cols = slice(g * HEAD_DIM, (g + 1) * HEAD_DIM)
            value_cols = slice(kv_width + g * HEAD_DIM, kv_width + (g + 1) * HEAD_DIM)

            def one_head(i, carry):
                h = g * group + i
                cols = pl.ds(pl.multiple_of(h * HEAD_DIM, HEAD_DIM), HEAD_DIM)
                keys, values = kv_ref[key_rows, key_cols], kv_ref[key_rows, value_cols]
                queries, grads = q_ref[:, cols], grad_ref[:, cols]
                scores = nt(keys, queries) * scale
                probs = jnp.where(mask, jnp.exp(scores - lse_ref[pl.ds(h, 1), :]), 0.0)
                prob_grad = nt(values, grads)
                score_grad = (probs * (prob_grad - delta_ref[pl.ds(h, 1), :])).astype(BF16)
                part_ref[:, key_cols] += nn(score_grad, queries)
                part_ref[:, value_cols] += nn(probs.astype(BF16), grads)
                dq_ref[:, cols] += tn(score_grad, keys)
                return carry

            lax.fori_loop(0, group, one_head, 0, unroll=3)
        part_ref[:, :kv_width] = part_ref[:, :kv_width] * scale

    def to_owner(j):
        return pltpu.make_async_remote_copy(
            src_ref=leaving.at[j],
            dst_ref=arriving.at[me],
            send_sem=send.at[j],
            recv_sem=recv.at[me],
            device_id={"seq": j},
            device_id_type=MESH_IDS,
        )

    def other_block(j, carry):
        key_block(j)
        leaving[j] = part_ref[...].astype(BF16)
        to_owner(j).start()
        return carry

    lax.fori_loop(0, me, other_block, 0)
    key_block(me)
    part_ref[...] = part_ref[...].astype(BF16).astype(F32)
    cosines, sines = cos_ref[...], -sin_ref[...]

    def one_query(h, carry):
        cols = pl.ds(pl.multiple_of(h * HEAD_DIM, HEAD_DIM), HEAD_DIM)
        out_ref[:, cols] = rotate(dq_ref[:, cols] * scale, cosines, sines).astype(BF16)
        return carry

    lax.fori_loop(0, heads, one_query, 0)

    def add_arrived(m, carry):
        pltpu.make_async_remote_copy(
            src_ref=leaving.at[m],
            dst_ref=arriving.at[m],
            send_sem=send.at[m],
            recv_sem=recv.at[m],
            device_id={"seq": m},
            device_id_type=MESH_IDS,
        ).wait_recv()
        part_ref[...] += arriving[m].astype(F32)
        return carry

    lax.fori_loop(me + 1, count, add_arrived, 0)
    first = heads * HEAD_DIM
    for g in range(kv_heads):
        cols = slice(g * HEAD_DIM, (g + 1) * HEAD_DIM)
        out_ref[:, first + g * HEAD_DIM : first + (g + 1) * HEAD_DIM] = rotate(
            part_ref[:, cols], cosines, sines
        ).astype(BF16)
    out_ref[:, first + kv_width :] = part_ref[:, kv_width:].astype(BF16)

    def sent(j, carry):
        to_owner(j).wait_send()
        return carry

    lax.fori_loop(0, me, sent, 0)


def attention_back(length, queries, kv_all, grads, lse, attended, cosines, sines, collective_id):
    count = lax.axis_size("seq")
    rows, q_width = queries.shape
    kv_width = kv_all.shape[1] // 2
    heads, kv_heads = q_width // HEAD_DIM, kv_width // HEAD_DIM
    vmem = pl.BlockSpec(memory_space=pltpu.VMEM)
    return pl.pallas_call(
        functools.partial(attention_back_kernel, count, heads, kv_heads),
        out_shape=jax.ShapeDtypeStruct((rows, q_width + 2 * kv_width), BF16),
        in_specs=[pl.BlockSpec(memory_space=pltpu.SMEM)] + [vmem] * 7,
        out_specs=vmem,
        scratch_shapes=[
            pltpu.VMEM((heads, rows), F32),
            pltpu.VMEM((rows, q_width), F32),
            pltpu.VMEM((rows, 2 * kv_width), F32),
            pltpu.VMEM((count, rows, 2 * kv_width), BF16),
            pltpu.VMEM((count, rows, 2 * kv_width), BF16),
            pltpu.SemaphoreType.DMA((count,)),
            pltpu.SemaphoreType.DMA((count,)),
        ],
        compiler_params=pltpu.CompilerParams(
            collective_id=collective_id, vmem_limit_bytes=30 << 20
        ),
        cost_estimate=pl.CostEstimate(
            flops=10 * count * rows * rows * q_width, bytes_accessed=1 << 20, transcendentals=0
        ),
        name="attention_backward",
    )(length, queries, kv_all, grads, lse, attended, cosines, sines)


def weight_grad_kernel(n, *refs):
    lefts, rights, outs = refs[:2], refs[2 : 2 + 2 * n], refs[2 + 2 * n :]
    for k, out_ref in enumerate(outs):
        early, late = rights[2 * k : 2 * k + 2]
        total = tn(lefts[0][...], early[...]) + tn(lefts[1][...], late[...])
        out_ref[...] = total.astype(BF16)


def weight_grads(lefts, rights, name):
    columns, tile = lefts[0].shape[1], 256
    flat = [part for pair in rights for part in pair]
    return pl.pallas_call(
        functools.partial(weight_grad_kernel, len(rights)),
        grid=(columns // tile,),
        out_shape=[jax.ShapeDtypeStruct((columns, r[0].shape[1]), BF16) for r in rights],
        in_specs=[pl.BlockSpec((x.shape[0], tile), lambda i: (0, i)) for x in lefts]
        + [pl.BlockSpec(r.shape, lambda i: (0, 0), pipeline_mode=pl.Buffered(1)) for r in flat],
        out_specs=[pl.BlockSpec((tile, r[0].shape[1]), lambda i: (i, 0)) for r in rights],
        compiler_params=pltpu.CompilerParams(vmem_limit_bytes=48 << 20),
        cost_estimate=pl.CostEstimate(flops=0, bytes_accessed=1 << 20, transcendentals=0),
        name=name,
    )(*lefts, *flat)


def seq_permutes(block_for):
    count, me = lax.axis_size("seq"), lax.axis_index("seq")
    pieces = [block_for(me)]
    for step in range(1, count):
        ring = [(i, (i + step) % count) for i in range(count)]
        pieces.append(lax.ppermute(block_for(lax.rem(me + step, count)), "seq", ring))
    return pieces


def in_seq_order(pieces, dtype):
    count, me = len(pieces), lax.axis_index("seq")
    whole = jnp.zeros((count,) + pieces[0].shape, dtype)
    for step, piece in enumerate(pieces):
        place = lax.rem(me + count - step, count)
        whole = lax.dynamic_update_index_in_dim(whole, piece.astype(dtype), place, 0)
    return whole


def on_device(
    hidden_in,
    lengths,
    routes,
    gates,
    priority,
    attn_gain,
    mlp_gain,
    w_query,
    key_projection,
    value_projection,
    w_out,
    w_gate,
    w_up,
    w_down,
    cotangent,
):
    rows = hidden_in.shape[1]
    width = hidden_in.shape[2]
    dp_count = lax.axis_size("dp")
    seq_count = lax.axis_size("seq")
    devices = dp_count * seq_count
    own_experts = w_gate.shape[0]
    sharers = seq_count // own_experts
    hidden_units = w_gate.shape[2]
    my_seq = lax.axis_index("seq")
    extent = rows * seq_count
    query_pos = my_seq * rows + jnp.arange(rows, dtype=jnp.int32)
    length = lengths[0]
    is_valid = query_pos < length
    q_width = w_query.shape[1]
    kv_width = key_projection.shape[1]
    cosine_lookup, sine_lookup = rope_angles(query_pos, HEAD_DIM)

    gain_block = jnp.concatenate(
        [attn_gain[:, None], mlp_gain[:, None], jnp.zeros((attn_gain.shape[0], LANES - 2), BF16)],
        axis=1,
    )
    packed = jnp.concatenate([w_query, key_projection, value_projection], axis=1)
    staged = seq_count == 4 and w_query.shape[0] % 16 == 0

    def expert_pieces(weights):
        def block_for(peer):
            return lax.dynamic_index_in_dim(weights, peer // sharers, 0, keepdims=False)

        return seq_permutes(block_for)

    gate_parts = expert_pieces(w_gate)
    if staged:
        packed_full, gains_full, out_full = staged_gather(
            [packed, gain_block, w_out], [], None, 2, "gather_attention_weights"
        )
    else:
        packed_full = lax.all_gather(packed, BOTH, axis=0, tiled=True)
        gains_full = lax.all_gather(gain_block, BOTH, axis=0, tiled=True)
        out_full = lax.all_gather(w_out, BOTH, axis=0, tiled=True)

    pair_routes, place, kept = claim_places(routes[0], priority[0, 0], is_valid)
    holder = (pair_routes // own_experts) * seq_count + (pair_routes % own_experts) * sharers
    holder = holder + my_seq * sharers // seq_count
    slots = devices * CAP
    target = jnp.where(kept, holder * CAP + place, slots).reshape(rows, TOP)
    slot_ids = jnp.arange(slots, dtype=jnp.int32)
    hits = target[:, :, None] == slot_ids[None, None, :]
    gate_rows = gates[0]
    token_hot = jnp.any(hits, axis=1).astype(BF16)

    def hot_of(first, size):
        mine = kept & (place >= first) & (place < first + size)
        spot = jnp.where(mine, holder * size + place - first, slots).reshape(rows, TOP)
        ids = jnp.arange(devices * size, dtype=jnp.int32)
        return jnp.any(spot[:, :, None] == ids[None, None, :], axis=1).astype(BF16)

    early_hot, late_hot = hot_of(0, EARLY), hot_of(EARLY, CAP - EARLY)
    slot_gate = jnp.sum(jnp.where(hits, gate_rows[:, :, None], 0.0), axis=(0, 1))

    live_cotangent = jnp.where(is_valid[:, None], cotangent[0], jnp.zeros((), BF16))
    out_grad = live_cotangent.astype(F32)
    grad_send = (tn(token_hot, live_cotangent) * slot_gate[:, None]).astype(BF16)
    packed_full, gains_full, out_full, gate_parts, grad_send = lax.optimization_barrier(
        (packed_full, gains_full, out_full, gate_parts, grad_send)
    )
    gain_one, gain_two = gains_full[:, 0].astype(F32), gains_full[:, 1].astype(F32)
    grad_rows = swap(grad_send.reshape(devices, CAP, width), ("dp", "seq"))

    inputs = hidden_in[0].astype(F32)
    scale_one = lax.rsqrt(jnp.mean(inputs * inputs, axis=-1, keepdims=True) + EPSILON)
    normed = (inputs * scale_one * gain_one).astype(BF16)
    projected, w_up = lax.optimization_barrier((nn(normed, packed_full), w_up))
    up_parts = expert_pieces(w_up)
    cosines, sines = cosine_lookup[:, 0], sine_lookup[:, 0]
    cosines = jnp.concatenate([cosines, cosines], axis=1)
    sines = jnp.concatenate([-sines, sines], axis=1)
    attended, log_total, query_flat, kv_all = attention(
        lengths, projected, cosines, sines, q_width, 1
    )
    kv_all = kv_all.reshape(extent, 2 * kv_width)
    middle = inputs + nn(attended, out_full)
    scale_two = lax.rsqrt(jnp.mean(middle * middle, axis=-1, keepdims=True) + EPSILON)
    moe_input = (middle * scale_two * gain_two).astype(BF16)

    def to_experts(hot):
        return tn(hot, moe_input).astype(BF16).reshape(devices, -1, width)

    early_send, late_send = to_experts(early_hot), to_experts(late_hot)
    early_send, late_send, grad_rows, up_parts, w_down = lax.optimization_barrier(
        (early_send, late_send, grad_rows, up_parts, w_down)
    )
    early_grads, late_grads, w_down = lax.optimization_barrier(
        (grad_rows[:, :EARLY], grad_rows[:, EARLY:], w_down)
    )
    down_parts = expert_pieces(w_down)
    early_rows = swap(early_send, ("dp", "seq"))
    early_rows, late_send = lax.optimization_barrier((early_rows, late_send))
    late_rows = swap(late_send, ("dp", "seq"))
    gate_full = in_seq_order(gate_parts, BF16).reshape(width, hidden_units)
    up_full = in_seq_order(up_parts, BF16).reshape(width, hidden_units)
    down_full = in_seq_order(down_parts, BF16).reshape(hidden_units, width)
    early_rows, gate_full, up_full, down_full, early_grads, late_grads = (
        lax.optimization_barrier(
            (early_rows, gate_full, up_full, down_full, early_grads, late_grads)
        )
    )

    def run_expert(slot_rows, grads):
        blocks = slot_rows.shape[:2]
        slot_rows, grads = slot_rows.reshape(-1, width), grads.reshape(-1, width)
        gate_pre = nn(slot_rows, gate_full)
        up_pre = nn(slot_rows, up_full)
        gate_sigmoid = jax.nn.sigmoid(gate_pre)
        gate_act = gate_pre * gate_sigmoid
        gate_slope = gate_sigmoid * (1.0 + gate_pre * (1.0 - gate_sigmoid))
        hidden = (gate_act * up_pre).astype(BF16)
        hidden_grad = nt(grads, down_full)
        gate_pre_grad = (hidden_grad * up_pre * gate_slope).astype(BF16)
        up_pre_grad = (hidden_grad * gate_act).astype(BF16)
        return [x.reshape(blocks + (-1,)) for x in (hidden, gate_pre_grad, up_pre_grad)]

    def row_grads(gate_pre_grad, up_pre_grad):
        blocks = gate_pre_grad.shape[:2]
        gate_pre_grad = gate_pre_grad.reshape(-1, hidden_units)
        up_pre_grad = up_pre_grad.reshape(-1, hidden_units)
        row_grad = (nt(gate_pre_grad, gate_full) + nt(up_pre_grad, up_full)).astype(BF16)
        return row_grad.reshape(blocks + (width,))

    def both_parts(early, late):
        return jnp.concatenate([early, late], axis=1).reshape(slots, -1)

    def to_owners(grad):
        grad = grad.reshape(seq_count, -1, grad.shape[1])

        def block_for(peer):
            return lax.dynamic_index_in_dim(grad, peer, 0, keepdims=False)

        return seq_permutes(block_for)

    def owned_sum(pieces):
        whole = in_seq_order(pieces, F32)
        return jnp.sum(whole.reshape((own_experts, sharers) + whole.shape[1:]), axis=1)

    early_hidden, *early_pre_grads = run_expert(early_rows, early_grads)
    early_row_grad = row_grads(*early_pre_grads)
    late_rows, early_row_grad = lax.optimization_barrier((late_rows, early_row_grad))
    early_back = swap(early_row_grad, ("dp", "seq"))
    late_hidden, *late_pre_grads = run_expert(late_rows, late_grads)

    def flat(*parts):
        return [part.reshape(-1, part.shape[-1]) for part in parts]

    (down_grad,) = weight_grads(
        flat(early_hidden, late_hidden), [flat(early_grads, late_grads)], "down_grads"
    )
    late_rows, late_pre_grads, down_grad = lax.optimization_barrier(
        (late_rows, late_pre_grads, down_grad)
    )
    down_grad_parts = to_owners(down_grad)
    gate_grad, up_grad = weight_grads(
        flat(early_rows, late_rows),
        [flat(*pair) for pair in zip(early_pre_grads, late_pre_grads, strict=True)],
        "gate_up_grads",
    )
    late_row_grad = row_grads(*late_pre_grads)
    early_back, late_row_grad, down_grad_parts, gate_grad, up_grad, late_hidden = (
        lax.optimization_barrier(
            (early_back, late_row_grad, down_grad_parts, gate_grad, up_grad, late_hidden)
        )
    )
    expert_hidden = both_parts(early_hidden, late_hidden)
    late_back = swap(late_row_grad, ("dp", "seq"))
    gate_owned, up_owned = owned_sum(to_owners(gate_grad)), owned_sum(to_owners(up_grad))
    down_owned = owned_sum(down_grad_parts)
    expert_out = nn(expert_hidden, down_full).astype(BF16)
    expert_out, late_back, gate_owned, up_owned, down_owned = lax.optimization_barrier(
        (expert_out, late_back, gate_owned, up_owned, down_owned)
    )
    returned = swap(expert_out.reshape(devices, CAP, width), ("dp", "seq")).reshape(slots, width)
    early_back, late_back = early_back.reshape(-1, width), late_back.reshape(-1, width)
    moe_input_grad = nn(early_hot, early_back) + nn(late_hot, late_back)
    middle_norm_grad, gain_two_grad = norm_back(middle, scale_two, gain_two, moe_input_grad)
    middle_grad = out_grad + middle_norm_grad
    branch_grad = middle_grad.astype(BF16)
    out_terms = tn(attended, branch_grad).astype(BF16)
    attended_grad = nt(branch_grad, out_full).astype(BF16)
    projected_grad = attention_back(
        lengths,
        query_flat,
        kv_all,
        attended_grad,
        log_total,
        attended,
        cosines,
        sines,
        4,
    )
    normed_grad = nt(projected_grad, packed_full)
    input_norm_grad, gain_one_grad = norm_back(inputs, scale_one, gain_one, normed_grad)
    input_grad = middle_grad + input_norm_grad

    lane = lax.broadcasted_iota(jnp.int32, (width, LANES), 1)
    gain_terms = jnp.where(lane == 0, gain_one_grad[:, None], gain_two_grad[:, None])
    gain_terms = jnp.where(lane < 2, gain_terms, 0.0).astype(BF16)
    query_terms = tn(normed, projected_grad).astype(BF16)
    if staged:
        out_owned, gains_owned, owned = staged_scatter(
            [out_terms, gain_terms, query_terms], [], None, 6, "scatter_attention_grads"
        )
    else:
        terms = jnp.concatenate([out_terms, gain_terms, query_terms], axis=1)
        terms = lax.psum_scatter(terms, BOTH, scatter_dimension=0, tiled=True).astype(F32)
        out_owned, gains_owned = terms[:, :width], terms[:, width : width + LANES]
        owned = terms[:, width + LANES :]
    returned, owned = lax.optimization_barrier((returned, owned))
    expert_grads = [gate_owned, up_owned, down_owned]

    gate_hot = jnp.sum(jnp.where(hits, gate_rows[:, :, None], 0.0), axis=1).astype(BF16)
    layer_out = middle + nn(gate_hot, returned)
    return (
        layer_out[None],
        input_grad[None],
        gains_owned[:, 0],
        gains_owned[:, 1],
        owned[:, :q_width],
        owned[:, q_width : q_width + kv_width],
        owned[:, q_width + kv_width : q_width + 2 * kv_width],
        out_owned,
        *expert_grads,
    )


def solution(mesh):
    part = P("dp", "seq", None)
    both = P(BOTH)
    both_rows = P(BOTH, None)
    return jax.shard_map(
        on_device,
        mesh=mesh,
        in_specs=(part, P("dp"), part, part, part, both, both)
        + (both_rows,) * 4
        + (part,) * 4,
        out_specs=(part, part, both, both) + (both_rows,) * 4 + (part,) * 3,
        check_vma=False,
    )
```

```python
import functools
import math

import jax
import jax.numpy as jnp
from jax import lax
from jax.experimental import pallas as pl
from jax.experimental.pallas import tpu as pltpu
from jax.sharding import PartitionSpec as P

HEAD_DIM = 128
EXPERTS = 32
TOP = 4
CAP = 40
EARLY = 24

EPSILON = 1e-06
ROPE_BASE = 10000.0
NEG_FILL = -1e30
LANES = 128
BOTH = ("seq", "dp")
BF16 = jnp.bfloat16
F32 = jnp.float32


def rope_angles(positions, head_size):
    half_dim = head_size // 2
    frequency = ROPE_BASE ** (-(2.0 * jnp.arange(half_dim, dtype=F32)) / head_size)
    angles = positions.astype(F32)[:, None] * frequency[None, :]
    return (jnp.cos(angles)[:, None, :], jnp.sin(angles)[:, None, :])


def dot(left, right, contract):
    return lax.dot_general(left, right, (contract, ((), ())), preferred_element_type=F32)


def nn(left, right):
    return dot(left, right, ((1,), (0,)))


def nt(left, right):
    return dot(left, right, ((1,), (1,)))


def tn(left, right):
    return dot(left, right, ((0,), (0,)))


def claim_places(routes, priority, is_valid):
    pair_routes = routes.reshape(-1)
    live = jnp.repeat(is_valid, TOP)
    key = jnp.where(live, pair_routes, -1)
    earlier = (key[None, :] == pair_routes[:, None]) & (priority[None, :] < priority[:, None])
    place = jnp.sum(earlier.astype(F32), axis=1).astype(jnp.int32)
    return pair_routes, place, live & (place < CAP)


def norm_back(values, scale_rows, gain_vec, incoming):
    weighted = incoming * gain_vec
    inner_mean = jnp.mean(weighted * values, axis=-1, keepdims=True)
    values_grad = scale_rows * weighted - values * scale_rows * scale_rows * scale_rows * inner_mean
    return (values_grad, jnp.sum(incoming * values * scale_rows, axis=0))


def swap(blocks, axes):
    return lax.all_to_all(blocks, axes, split_axis=0, concat_axis=0, tiled=True)


MESH_IDS = pl.DeviceIdType.MESH


def torus_place():
    seq, dp = lax.axis_index("seq"), lax.axis_index("dp")
    return seq // 2, seq % 2, dp // 2, dp % 2


def torus_id(a, b, z, c):
    return {"seq": 2 * a + b, "dp": 2 * z + c}


def torus_peers(line):
    a, b, z, c = torus_place()
    peers = [torus_id(a, b, z, 1 - c), torus_id(a, 1 - b, z, c), torus_id(1 - a, b, z, c)]
    peers.append(torus_id(1 - a, 1 - b, z, c))
    return peers + [torus_id(a, b, lax.rem(z + k, line), c) for k in range(1, line)]


def greet(peers):
    barrier = pltpu.get_barrier_semaphore()
    for peer in peers:
        pl.semaphore_signal(barrier, inc=1, device_id=peer, device_id_type=MESH_IDS)
    pl.semaphore_wait(barrier, len(peers))


def column_chunks(widths, parts):
    chunks = []
    for part in range(parts):
        for k, whole in enumerate(widths):
            tiles = whole // LANES
            first, end = tiles * part // parts, tiles * (part + 1) // parts
            if end > first:
                chunks.append((k, first * LANES, (end - first) * LANES))
    return chunks


def remote(src, dst, sems, i, j, device_id):
    send, recv = sems
    return pltpu.make_async_remote_copy(
        src_ref=src,
        dst_ref=dst,
        send_sem=send.at[i, j],
        recv_sem=recv.at[i, j],
        device_id=device_id,
        device_id_type=MESH_IDS,
    )


def start_exchange(count, sources, targets, block_of, sems):
    send_sems, recv_sems, local_sems = sems
    me = lax.axis_index("seq")
    copies = []
    for i, source in enumerate(sources):
        for step in range(1, count):
            peer = lax.rem(me + step, count)
            copies.append(
                pltpu.make_async_remote_copy(
                    src_ref=block_of(source, peer),
                    dst_ref=targets[i].at[me],
                    send_sem=send_sems.at[i, step - 1],
                    recv_sem=recv_sems.at[i, step - 1],
                    device_id={"seq": peer},
                    device_id_type=MESH_IDS,
                )
            )
        copies.append(
            pltpu.make_async_copy(block_of(source, me), targets[i].at[me], local_sems.at[i])
        )
    for copy in copies:
        copy.start()
    return copies


def exchange_sems(n, count):
    return [
        pltpu.SemaphoreType.DMA((n, count - 1)),
        pltpu.SemaphoreType.DMA((n, count - 1)),
        pltpu.SemaphoreType.DMA((n,)),
    ]


def in_steps(count, stages, after=None):
    for step in range((count + 1) // 2 + len(stages) - 1):
        if after is not None and step == (count + 1) // 2 + 1:
            after()
        for behind, stage in enumerate(stages):
            for i in (2 * (step - behind), 2 * (step - behind) + 1):
                if 0 <= i < count:
                    stage(i)


def gather_kernel(line, chunks, n, extras, block_of, *refs):
    sources, more_sources = refs[:n], refs[n : n + extras]
    refs = refs[n + extras :]
    targets, more_targets = refs[:n], refs[n : n + extras]
    send, recv, local, *more_sems = refs[n + extras :]
    sems = (send, recv)
    a, b, z, c = torus_place()
    greet(torus_peers(line))
    more = start_exchange(4, more_sources, more_targets, block_of, more_sems) if extras else []
    sent = []

    def start(copy):
        copy.start()
        sent.append(copy)
        return copy

    along_line, first_hop, second_hop, third_hop = {}, {}, {}, {}

    def send_line(i):
        k, first, size = chunks[i]
        cols = pl.ds(first, size)
        own = targets[k].at[a, b, z, c, :, cols]
        keep = pltpu.make_async_copy(sources[k].at[:, cols], own, local.at[i])
        keep.start()
        along_line[i] = [
            start(
                remote(
                    sources[k].at[:, cols],
                    own,
                    sems,
                    i,
                    2 + step,
                    torus_id(a, b, lax.rem(z + step, line), c),
                )
            )
            for step in range(1, line)
        ]
        along_line[i].append(keep)

    def send_first(i):
        k, first, size = chunks[i]
        *copies, keep = along_line[i]
        keep.wait()
        for copy in copies:
            copy.wait_recv()
        block = targets[k].at[a, b, :, c, :, pl.ds(first, size)]
        peer = torus_id(a, 1 - b, z, c) if i % 2 == 0 else torus_id(1 - a, b, z, c)
        first_hop[i] = start(remote(block, block, sems, i, 1, peer))

    def send_second(i):
        k, first, size = chunks[i]
        first_hop[i].wait_recv()
        cols = pl.ds(first, size)
        if i % 2 == 0:
            block, peer = targets[k].at[a, :, :, c, :, cols], torus_id(1 - a, b, z, c)
        else:
            block, peer = targets[k].at[:, b, :, c, :, cols], torus_id(a, 1 - b, z, c)
        second_hop[i] = start(remote(block, block, sems, i, 2, peer))

    def send_third(i):
        k, first, size = chunks[i]
        second_hop[i].wait_recv()
        block = targets[k].at[:, :, :, c, :, pl.ds(first, size)]
        third_hop[i] = start(remote(block, block, sems, i, 0, torus_id(a, b, z, 1 - c)))

    in_steps(len(chunks), [send_line, send_first, send_second, send_third])
    for copy in third_hop.values():
        copy.wait_recv()
    for copy in sent:
        copy.wait_send()
    for copy in more:
        copy.wait()


def staged_gather(arrays, extras, block_of, collective_id, name, parts=6):
    seq_count, line = lax.axis_size("seq"), lax.axis_size("dp") // 2
    rows, n = arrays[0].shape[0], len(arrays)
    chunks = column_chunks([x.shape[1] for x in arrays], parts)
    m = len(chunks)
    shape = (seq_count // 2, 2, line, 2, rows)
    size = sum(x.shape[1] for x in arrays) * rows * 64
    count = n + len(extras)
    outs = pl.pallas_call(
        functools.partial(gather_kernel, line, chunks, n, len(extras), block_of),
        out_shape=[jax.ShapeDtypeStruct(shape + (x.shape[1],), BF16) for x in arrays]
        + [jax.ShapeDtypeStruct((seq_count,) + x.shape[1:], BF16) for x in extras],
        in_specs=[pl.BlockSpec(memory_space=pl.ANY)] * count,
        out_specs=[pl.BlockSpec(memory_space=pltpu.HBM)] * count,
        scratch_shapes=[
            pltpu.SemaphoreType.DMA((m, 2 + line)),
            pltpu.SemaphoreType.DMA((m, 2 + line)),
            pltpu.SemaphoreType.DMA((m,)),
        ]
        + (exchange_sems(len(extras), seq_count) if extras else []),
        compiler_params=pltpu.CompilerParams(
            collective_id=collective_id, vmem_limit_bytes=4 << 20
        ),
        cost_estimate=pl.CostEstimate(flops=0, bytes_accessed=size, transcendentals=0),
        name=name,
    )(*arrays, *extras)
    return [o.reshape(-1, o.shape[-1]) for o in outs]


def scatter_kernel(line, chunks, n, extras, block_of, *refs):
    m = len(chunks)
    sources, more_sources = refs[:n], refs[n : n + extras]
    refs = refs[n + extras :]
    targets, more_targets = refs[:n], refs[n : n + extras]
    scratch = refs[n + extras :]
    owns, ins1, accs2, ins2, accs3, ins3, ins4 = (scratch[m * s : m * (s + 1)] for s in range(7))
    send, recv, local, *more_sems = scratch[7 * m :]
    sems = (send, recv)
    a, b, z, c = torus_place()
    greet(torus_peers(line))
    sent = []

    def start(copy):
        copy.start()
        sent.append(copy)
        return copy

    def add_lines(target, left, right):
        def one(j, carry):
            target[j] = (left[j].astype(F32) + right[j].astype(F32)).astype(BF16)
            return carry

        lax.fori_loop(0, line, one, 0)

    between_cores, first_hop, second_hop, along_line = {}, {}, {}, {}

    def send_core(i):
        k, first, size = chunks[i]
        cols = pl.ds(first, size)
        keep = pltpu.make_async_copy(sources[k].at[:, :, :, c, :, cols], owns[i], local.at[i])
        keep.start()
        swap_core = remote(
            sources[k].at[:, :, :, 1 - c, :, cols], ins1[i], sems, i, 0, torus_id(a, b, z, 1 - c)
        )
        between_cores[i] = (keep, start(swap_core))

    def send_first(i):
        keep, copy = between_cores[i]
        keep.wait()
        copy.wait_recv()
        for p in range(2):
            for q in range(2):
                add_lines(owns[i].at[p, q], owns[i].at[p, q], ins1[i].at[p, q])
        if i % 2 == 0:
            block, peer = owns[i].at[:, 1 - b], torus_id(a, 1 - b, z, c)
        else:
            block, peer = owns[i].at[1 - a], torus_id(1 - a, b, z, c)
        first_hop[i] = start(remote(block, ins2[i], sems, i, 1, peer))

    def send_second(i):
        first_hop[i].wait_recv()
        for p in range(2):
            mine = owns[i].at[p, b] if i % 2 == 0 else owns[i].at[a, p]
            add_lines(accs2[i].at[p], mine, ins2[i].at[p])
        if i % 2 == 0:
            block, peer = accs2[i].at[1 - a], torus_id(1 - a, b, z, c)
        else:
            block, peer = accs2[i].at[1 - b], torus_id(a, 1 - b, z, c)
        second_hop[i] = start(remote(block, ins3[i], sems, i, 2, peer))

    def send_line(i):
        second_hop[i].wait_recv()
        add_lines(accs3[i], accs2[i].at[a if i % 2 == 0 else b], ins3[i])
        copies = []
        for step in range(1, line):
            to = lax.rem(z + step, line)
            peer = torus_id(a, b, to, c)
            copies.append(start(remote(accs3[i].at[to], ins4[i].at[z], sems, i, 2 + step, peer)))
        along_line[i] = copies

    def finish(i):
        k, first, size = chunks[i]
        total = accs3[i][z].astype(F32)
        for step in range(1, line):
            along_line[i][step - 1].wait_recv()
            total = total + ins4[i][lax.rem(z + line - step, line)].astype(F32)
        targets[k][:, first : first + size] = total

    more = []

    def send_more():
        if extras:
            more.extend(start_exchange(4, more_sources, more_targets, block_of, more_sems))

    in_steps(m, [send_core, send_first, send_second, send_line, finish], send_more)
    for copy in sent:
        copy.wait_send()
    for copy in more:
        copy.wait()


def staged_scatter(arrays, extras, block_of, collective_id, name, parts=6):
    seq_count, line = lax.axis_size("seq"), lax.axis_size("dp") // 2
    rows, n = arrays[0].shape[0] // (2 * line * seq_count), len(arrays)
    chunks = column_chunks([x.shape[1] for x in arrays], parts)
    m = len(chunks)
    leads = [(2, 2, line), (2, 2, line), (2, line), (2, line), (line,), (line,), (line,)]
    size = sum(x.shape[1] for x in arrays) * rows * 64
    anywhere = pl.BlockSpec(memory_space=pl.ANY)
    return pl.pallas_call(
        functools.partial(scatter_kernel, line, chunks, n, len(extras), block_of),
        out_shape=[jax.ShapeDtypeStruct((rows, x.shape[1]), F32) for x in arrays]
        + [jax.ShapeDtypeStruct((seq_count,) + x.shape[1:], BF16) for x in extras],
        in_specs=[anywhere] * (n + len(extras)),
        out_specs=[pl.BlockSpec(memory_space=pltpu.VMEM)] * n + [anywhere] * len(extras),
        scratch_shapes=[
            pltpu.VMEM(lead + (rows, width), BF16) for lead in leads for _, _, width in chunks
        ]
        + [
            pltpu.SemaphoreType.DMA((m, 2 + line)),
            pltpu.SemaphoreType.DMA((m, 2 + line)),
            pltpu.SemaphoreType.DMA((m,)),
        ]
        + (exchange_sems(len(extras), seq_count) if extras else []),
        compiler_params=pltpu.CompilerParams(
            collective_id=collective_id, vmem_limit_bytes=36 << 20
        ),
        cost_estimate=pl.CostEstimate(flops=0, bytes_accessed=size, transcendentals=0),
        name=name,
    )(*[x.reshape(2, 2, line, 2, rows, x.shape[1]) for x in arrays], *extras)


def rotate(values, cosines, sines):
    return values * cosines + pltpu.roll(values, HEAD_DIM // 2, 1) * sines


def attention_kernel(count, heads, kv_heads, *refs):
    length_ref, projected_ref, cos_ref, sin_ref = refs[:4]
    attended_ref, lse_ref, q_ref, kv_ref = refs[4:8]
    max_ref, sum_ref, acc_ref, send, recv = refs[8:]
    me = lax.axis_index("seq")
    rows, kv_width = q_ref.shape[0], kv_heads * HEAD_DIM
    q_width, group, scale = heads * HEAD_DIM, heads // kv_heads, 1.0 / math.sqrt(HEAD_DIM)
    greet([{"seq": lax.rem(me + step, count)} for step in range(1, count)])
    cosines, sines = cos_ref[...], sin_ref[...]
    for g in range(kv_heads):
        cols = slice(g * HEAD_DIM, (g + 1) * HEAD_DIM)
        keys = projected_ref[:, q_width + g * HEAD_DIM : q_width + (g + 1) * HEAD_DIM]
        kv_ref[me, :, cols] = rotate(keys, cosines, sines).astype(BF16)
    kv_ref[me, :, kv_width:] = projected_ref[:, q_width + kv_width :].astype(BF16)

    def to_later(peer):
        return pltpu.make_async_remote_copy(
            src_ref=kv_ref.at[me],
            dst_ref=kv_ref.at[me],
            send_sem=send.at[peer],
            recv_sem=recv.at[me],
            device_id={"seq": peer},
            device_id_type=MESH_IDS,
        )

    def start(peer, carry):
        to_later(peer).start()
        return carry

    lax.fori_loop(me + 1, count, start, 0)

    def one_query(h, carry):
        cols = pl.ds(pl.multiple_of(h * HEAD_DIM, HEAD_DIM), HEAD_DIM)
        q_ref[:, cols] = rotate(projected_ref[:, cols], cosines, sines).astype(BF16)
        return carry

    lax.fori_loop(0, heads, one_query, 0)
    max_ref[...] = jnp.full_like(max_ref, NEG_FILL)
    sum_ref[...] = jnp.zeros_like(sum_ref)
    acc_ref[...] = jnp.zeros_like(acc_ref)
    length = length_ref[0]
    query_pos = me * rows + lax.broadcasted_iota(jnp.int32, (rows, rows), 1)
    key_local = lax.broadcasted_iota(jnp.int32, (rows, rows), 0)

    def key_block(j):
        key_pos = j * rows + key_local
        mask = (key_pos <= query_pos) & (key_pos < length)
        for g in range(kv_heads):
            key_cols = slice(g * HEAD_DIM, (g + 1) * HEAD_DIM)
            value_cols = slice(kv_width + g * HEAD_DIM, kv_width + (g + 1) * HEAD_DIM)

            def one_head(i, carry):
                h = g * group + i
                cols = pl.ds(pl.multiple_of(h * HEAD_DIM, HEAD_DIM), HEAD_DIM)
                row = pl.ds(h, 1)
                keys, values = kv_ref[j, :, key_cols], kv_ref[j, :, value_cols]
                scores = jnp.where(mask, nt(keys, q_ref[:, cols]) * scale, NEG_FILL)
                before = max_ref[row, :]
                top = jnp.maximum(before, jnp.max(scores, axis=0, keepdims=True))
                shrink = jnp.exp(before - top)
                weights = jnp.exp(scores - top)
                max_ref[row, :] = top
                sum_ref[row, :] = sum_ref[row, :] * shrink + jnp.sum(weights, axis=0, keepdims=True)
                acc_ref[h] = acc_ref[h] * shrink + tn(values, weights.astype(BF16))
                return carry

            lax.fori_loop(0, group, one_head, 0, unroll=2)

    key_block(me)

    def earlier_block(j, carry):
        pltpu.make_async_remote_copy(
            src_ref=kv_ref.at[j],
            dst_ref=kv_ref.at[j],
            send_sem=send.at[j],
            recv_sem=recv.at[j],
            device_id={"seq": j},
            device_id_type=MESH_IDS,
        ).wait_recv()
        key_block(j)
        return carry

    lax.fori_loop(0, me, earlier_block, 0)
    lse_ref[...] = max_ref[...] + jnp.log(sum_ref[...])

    def finish(h, carry):
        cols = pl.ds(pl.multiple_of(h * HEAD_DIM, HEAD_DIM), HEAD_DIM)
        attended_ref[:, cols] = (acc_ref[h] / sum_ref[pl.ds(h, 1), :]).T.astype(BF16)
        return carry

    lax.fori_loop(0, heads, finish, 0)

    def sent(peer, carry):
        to_later(peer).wait_send()
        return carry

    lax.fori_loop(me + 1, count, sent, 0)


def attention(length, projected, cosines, sines, q_width, collective_id):
    count = lax.axis_size("seq")
    rows = projected.shape[0]
    kv_width = (projected.shape[1] - q_width) // 2
    heads, kv_heads = q_width // HEAD_DIM, kv_width // HEAD_DIM
    vmem = pl.BlockSpec(memory_space=pltpu.VMEM)
    return pl.pallas_call(
        functools.partial(attention_kernel, count, heads, kv_heads),
        out_shape=[
            jax.ShapeDtypeStruct((rows, q_width), BF16),
            jax.ShapeDtypeStruct((heads, rows), F32),
            jax.ShapeDtypeStruct((rows, q_width), BF16),
            jax.ShapeDtypeStruct((count, rows, 2 * kv_width), BF16),
        ],
        in_specs=[pl.BlockSpec(memory_space=pltpu.SMEM)] + [vmem] * 3,
        out_specs=[vmem] * 4,
        scratch_shapes=[
            pltpu.VMEM((heads, rows), F32),
            pltpu.VMEM((heads, rows), F32),
            pltpu.VMEM((heads, HEAD_DIM, rows), F32),
            pltpu.SemaphoreType.DMA((count,)),
            pltpu.SemaphoreType.DMA((count,)),
        ],
        compiler_params=pltpu.CompilerParams(
            collective_id=collective_id, vmem_limit_bytes=30 << 20
        ),
        cost_estimate=pl.CostEstimate(flops=0, bytes_accessed=1 << 20, transcendentals=0),
        name="attention_forward",
    )(length, projected, cosines, sines)


def attention_back_kernel(count, heads, kv_heads, *refs):
    length_ref, q_ref, kv_ref, grad_ref, lse_ref, attended_ref, cos_ref, sin_ref = refs[:8]
    out_ref, delta_ref, dq_ref, part_ref, leaving, arriving, send, recv = refs[8:]
    me = lax.axis_index("seq")
    rows, kv_width = q_ref.shape[0], kv_heads * HEAD_DIM
    group, scale = heads // kv_heads, 1.0 / math.sqrt(HEAD_DIM)
    greet([{"seq": lax.rem(me + step, count)} for step in range(1, count)])
    length = length_ref[0]
    query_pos = me * rows + lax.broadcasted_iota(jnp.int32, (rows, rows), 1)
    key_local = lax.broadcasted_iota(jnp.int32, (rows, rows), 0)
    dq_ref[...] = jnp.zeros_like(dq_ref)
    ones = jnp.ones((8, HEAD_DIM), BF16)
    for h in range(heads):
        cols = slice(h * HEAD_DIM, (h + 1) * HEAD_DIM)
        terms = grad_ref[:, cols].astype(F32) * attended_ref[:, cols].astype(F32)
        high = terms.astype(BF16)
        low = (terms - high.astype(F32)).astype(BF16)
        delta_ref[h : h + 1, :] = (nt(ones, high) + nt(ones, low))[:1]

    def key_block(j):
        key_pos = j * rows + key_local
        mask = (key_pos <= query_pos) & (key_pos < length)
        part_ref[...] = jnp.zeros_like(part_ref)
        key_rows = pl.ds(pl.multiple_of(j * rows, rows), rows)
        for g in range(kv_heads):
            key_cols = slice(g * HEAD_DIM, (g + 1) * HEAD_DIM)
            value_cols = slice(kv_width + g * HEAD_DIM, kv_width + (g + 1) * HEAD_DIM)

            def one_head(i, carry):
                h = g * group + i
                cols = pl.ds(pl.multiple_of(h * HEAD_DIM, HEAD_DIM), HEAD_DIM)
                keys, values = kv_ref[key_rows, key_cols], kv_ref[key_rows, value_cols]
                queries, grads = q_ref[:, cols], grad_ref[:, cols]
                scores = nt(keys, queries) * scale
                probs = jnp.where(mask, jnp.exp(scores - lse_ref[pl.ds(h, 1), :]), 0.0)
                prob_grad = nt(values, grads)
                score_grad = (probs * (prob_grad - delta_ref[pl.ds(h, 1), :])).astype(BF16)
                part_ref[:, key_cols] += nn(score_grad, queries)
                part_ref[:, value_cols] += nn(probs.astype(BF16), grads)
                dq_ref[:, cols] += tn(score_grad, keys)
                return carry

            lax.fori_loop(0, group, one_head, 0, unroll=3)
        part_ref[:, :kv_width] = part_ref[:, :kv_width] * scale

    def to_owner(j):
        return pltpu.make_async_remote_copy(
            src_ref=leaving.at[j],
            dst_ref=arriving.at[me],
            send_sem=send.at[j],
            recv_sem=recv.at[me],
            device_id={"seq": j},
            device_id_type=MESH_IDS,
        )

    def other_block(j, carry):
        key_block(j)
        leaving[j] = part_ref[...].astype(BF16)
        to_owner(j).start()
        return carry

    lax.fori_loop(0, me, other_block, 0)
    key_block(me)
    part_ref[...] = part_ref[...].astype(BF16).astype(F32)
    cosines, sines = cos_ref[...], -sin_ref[...]

    def one_query(h, carry):
        cols = pl.ds(pl.multiple_of(h * HEAD_DIM, HEAD_DIM), HEAD_DIM)
        out_ref[:, cols] = rotate(dq_ref[:, cols] * scale, cosines, sines).astype(BF16)
        return carry

    lax.fori_loop(0, heads, one_query, 0)

    def add_arrived(m, carry):
        pltpu.make_async_remote_copy(
            src_ref=leaving.at[m],
            dst_ref=arriving.at[m],
            send_sem=send.at[m],
            recv_sem=recv.at[m],
            device_id={"seq": m},
            device_id_type=MESH_IDS,
        ).wait_recv()
        part_ref[...] += arriving[m].astype(F32)
        return carry

    lax.fori_loop(me + 1, count, add_arrived, 0)
    first = heads * HEAD_DIM
    for g in range(kv_heads):
        cols = slice(g * HEAD_DIM, (g + 1) * HEAD_DIM)
        out_ref[:, first + g * HEAD_DIM : first + (g + 1) * HEAD_DIM] = rotate(
            part_ref[:, cols], cosines, sines
        ).astype(BF16)
    out_ref[:, first + kv_width :] = part_ref[:, kv_width:].astype(BF16)

    def sent(j, carry):
        to_owner(j).wait_send()
        return carry

    lax.fori_loop(0, me, sent, 0)


def attention_back(length, queries, kv_all, grads, lse, attended, cosines, sines, collective_id):
    count = lax.axis_size("seq")
    rows, q_width = queries.shape
    kv_width = kv_all.shape[1] // 2
    heads, kv_heads = q_width // HEAD_DIM, kv_width // HEAD_DIM
    vmem = pl.BlockSpec(memory_space=pltpu.VMEM)
    return pl.pallas_call(
        functools.partial(attention_back_kernel, count, heads, kv_heads),
        out_shape=jax.ShapeDtypeStruct((rows, q_width + 2 * kv_width), BF16),
        in_specs=[pl.BlockSpec(memory_space=pltpu.SMEM)] + [vmem] * 7,
        out_specs=vmem,
        scratch_shapes=[
            pltpu.VMEM((heads, rows), F32),
            pltpu.VMEM((rows, q_width), F32),
            pltpu.VMEM((rows, 2 * kv_width), F32),
            pltpu.VMEM((count, rows, 2 * kv_width), BF16),
            pltpu.VMEM((count, rows, 2 * kv_width), BF16),
            pltpu.SemaphoreType.DMA((count,)),
            pltpu.SemaphoreType.DMA((count,)),
        ],
        compiler_params=pltpu.CompilerParams(
            collective_id=collective_id, vmem_limit_bytes=30 << 20
        ),
        cost_estimate=pl.CostEstimate(
            flops=10 * count * rows * rows * q_width, bytes_accessed=1 << 20, transcendentals=0
        ),
        name="attention_backward",
    )(length, queries, kv_all, grads, lse, attended, cosines, sines)


def weight_grad_kernel(n, *refs):
    lefts, rights, outs = refs[:2], refs[2 : 2 + 2 * n], refs[2 + 2 * n :]
    for k, out_ref in enumerate(outs):
        early, late = rights[2 * k : 2 * k + 2]
        total = tn(lefts[0][...], early[...]) + tn(lefts[1][...], late[...])
        out_ref[...] = total.astype(BF16)


def weight_grads(lefts, rights, name):
    columns, tile = lefts[0].shape[1], 256
    flat = [part for pair in rights for part in pair]
    return pl.pallas_call(
        functools.partial(weight_grad_kernel, len(rights)),
        grid=(columns // tile,),
        out_shape=[jax.ShapeDtypeStruct((columns, r[0].shape[1]), BF16) for r in rights],
        in_specs=[pl.BlockSpec((x.shape[0], tile), lambda i: (0, i)) for x in lefts]
        + [pl.BlockSpec(r.shape, lambda i: (0, 0), pipeline_mode=pl.Buffered(1)) for r in flat],
        out_specs=[pl.BlockSpec((tile, r[0].shape[1]), lambda i: (i, 0)) for r in rights],
        compiler_params=pltpu.CompilerParams(vmem_limit_bytes=48 << 20),
        cost_estimate=pl.CostEstimate(flops=0, bytes_accessed=1 << 20, transcendentals=0),
        name=name,
    )(*lefts, *flat)


def seq_permutes(block_for):
    count, me = lax.axis_size("seq"), lax.axis_index("seq")
    pieces = [block_for(me)]
    for step in range(1, count):
        ring = [(i, (i + step) % count) for i in range(count)]
        pieces.append(lax.ppermute(block_for(lax.rem(me + step, count)), "seq", ring))
    return pieces


def in_seq_order(pieces, dtype):
    count, me = len(pieces), lax.axis_index("seq")
    whole = jnp.zeros((count,) + pieces[0].shape, dtype)
    for step, piece in enumerate(pieces):
        place = lax.rem(me + count - step, count)
        whole = lax.dynamic_update_index_in_dim(whole, piece.astype(dtype), place, 0)
    return whole


def on_device(
    hidden_in,
    lengths,
    routes,
    gates,
    priority,
    attn_gain,
    mlp_gain,
    w_query,
    key_projection,
    value_projection,
    w_out,
    w_gate,
    w_up,
    w_down,
    cotangent,
):
    rows = hidden_in.shape[1]
    width = hidden_in.shape[2]
    dp_count = lax.axis_size("dp")
    seq_count = lax.axis_size("seq")
    devices = dp_count * seq_count
    own_experts = w_gate.shape[0]
    sharers = seq_count // own_experts
    hidden_units = w_gate.shape[2]
    my_seq = lax.axis_index("seq")
    extent = rows * seq_count
    query_pos = my_seq * rows + jnp.arange(rows, dtype=jnp.int32)
    length = lengths[0]
    is_valid = query_pos < length
    q_width = w_query.shape[1]
    kv_width = key_projection.shape[1]
    cosine_lookup, sine_lookup = rope_angles(query_pos, HEAD_DIM)

    gain_block = jnp.concatenate(
        [attn_gain[:, None], mlp_gain[:, None], jnp.zeros((attn_gain.shape[0], LANES - 2), BF16)],
        axis=1,
    )
    packed = jnp.concatenate([w_query, key_projection, value_projection], axis=1)
    staged = seq_count == 4 and w_query.shape[0] % 16 == 0

    def expert_pieces(weights):
        def block_for(peer):
            return lax.dynamic_index_in_dim(weights, peer // sharers, 0, keepdims=False)

        return seq_permutes(block_for)

    gate_parts = expert_pieces(w_gate)
    if staged:
        packed_full, gains_full, out_full = staged_gather(
            [packed, gain_block, w_out], [], None, 2, "gather_attention_weights"
        )
    else:
        packed_full = lax.all_gather(packed, BOTH, axis=0, tiled=True)
        gains_full = lax.all_gather(gain_block, BOTH, axis=0, tiled=True)
        out_full = lax.all_gather(w_out, BOTH, axis=0, tiled=True)

    pair_routes, place, kept = claim_places(routes[0], priority[0, 0], is_valid)
    holder = (pair_routes // own_experts) * seq_count + (pair_routes % own_experts) * sharers
    holder = holder + my_seq * sharers // seq_count
    slots = devices * CAP
    target = jnp.where(kept, holder * CAP + place, slots).reshape(rows, TOP)
    slot_ids = jnp.arange(slots, dtype=jnp.int32)
    hits = target[:, :, None] == slot_ids[None, None, :]
    gate_rows = gates[0]
    token_hot = jnp.any(hits, axis=1).astype(BF16)

    def hot_of(first, size):
        mine = kept & (place >= first) & (place < first + size)
        spot = jnp.where(mine, holder * size + place - first, slots).reshape(rows, TOP)
        ids = jnp.arange(devices * size, dtype=jnp.int32)
        return jnp.any(spot[:, :, None] == ids[None, None, :], axis=1).astype(BF16)

    early_hot, late_hot = hot_of(0, EARLY), hot_of(EARLY, CAP - EARLY)
    slot_gate = jnp.sum(jnp.where(hits, gate_rows[:, :, None], 0.0), axis=(0, 1))

    live_cotangent = jnp.where(is_valid[:, None], cotangent[0], jnp.zeros((), BF16))
    out_grad = live_cotangent.astype(F32)
    grad_send = (tn(token_hot, live_cotangent) * slot_gate[:, None]).astype(BF16)
    packed_full, gains_full, out_full, gate_parts, grad_send = lax.optimization_barrier(
        (packed_full, gains_full, out_full, gate_parts, grad_send)
    )
    gain_one, gain_two = gains_full[:, 0].astype(F32), gains_full[:, 1].astype(F32)
    grad_rows = swap(grad_send.reshape(devices, CAP, width), ("dp", "seq"))

    inputs = hidden_in[0].astype(F32)
    scale_one = lax.rsqrt(jnp.mean(inputs * inputs, axis=-1, keepdims=True) + EPSILON)
    normed = (inputs * scale_one * gain_one).astype(BF16)
    projected = nn(normed, packed_full)
    cosines, sines = cosine_lookup[:, 0], sine_lookup[:, 0]
    cosines = jnp.concatenate([cosines, cosines], axis=1)
    sines = jnp.concatenate([-sines, sines], axis=1)
    attended, log_total, query_flat, kv_all = attention(
        lengths, projected, cosines, sines, q_width, 1
    )
    kv_all = kv_all.reshape(extent, 2 * kv_width)
    attended, w_up = lax.optimization_barrier((attended, w_up))
    up_parts = expert_pieces(w_up)
    middle = inputs + nn(attended, out_full)
    scale_two = lax.rsqrt(jnp.mean(middle * middle, axis=-1, keepdims=True) + EPSILON)
    moe_input = (middle * scale_two * gain_two).astype(BF16)

    def to_experts(hot):
        return tn(hot, moe_input).astype(BF16).reshape(devices, -1, width)

    early_send, late_send = to_experts(early_hot), to_experts(late_hot)
    early_send, late_send, grad_rows, up_parts, w_down = lax.optimization_barrier(
        (early_send, late_send, grad_rows, up_parts, w_down)
    )
    early_grads, late_grads, w_down = lax.optimization_barrier(
        (grad_rows[:, :EARLY], grad_rows[:, EARLY:], w_down)
    )
    down_parts = expert_pieces(w_down)
    early_rows = swap(early_send, ("dp", "seq"))
    early_rows, late_send = lax.optimization_barrier((early_rows, late_send))
    late_rows = swap(late_send, ("dp", "seq"))
    gate_full = in_seq_order(gate_parts, BF16).reshape(width, hidden_units)
    up_full = in_seq_order(up_parts, BF16).reshape(width, hidden_units)
    down_full = in_seq_order(down_parts, BF16).reshape(hidden_units, width)
    early_rows, gate_full, up_full, down_full, early_grads, late_grads = (
        lax.optimization_barrier(
            (early_rows, gate_full, up_full, down_full, early_grads, late_grads)
        )
    )

    def run_expert(slot_rows, grads):
        blocks = slot_rows.shape[:2]
        slot_rows, grads = slot_rows.reshape(-1, width), grads.reshape(-1, width)
        gate_pre = nn(slot_rows, gate_full)
        up_pre = nn(slot_rows, up_full)
        gate_sigmoid = jax.nn.sigmoid(gate_pre)
        gate_act = gate_pre * gate_sigmoid
        gate_slope = gate_sigmoid * (1.0 + gate_pre * (1.0 - gate_sigmoid))
        hidden = (gate_act * up_pre).astype(BF16)
        hidden_grad = nt(grads, down_full)
        gate_pre_grad = (hidden_grad * up_pre * gate_slope).astype(BF16)
        up_pre_grad = (hidden_grad * gate_act).astype(BF16)
        return [x.reshape(blocks + (-1,)) for x in (hidden, gate_pre_grad, up_pre_grad)]

    def row_grads(gate_pre_grad, up_pre_grad):
        blocks = gate_pre_grad.shape[:2]
        gate_pre_grad = gate_pre_grad.reshape(-1, hidden_units)
        up_pre_grad = up_pre_grad.reshape(-1, hidden_units)
        row_grad = (nt(gate_pre_grad, gate_full) + nt(up_pre_grad, up_full)).astype(BF16)
        return row_grad.reshape(blocks + (width,))

    def both_parts(early, late):
        return jnp.concatenate([early, late], axis=1).reshape(slots, -1)

    def to_owners(grad):
        grad = grad.reshape(seq_count, -1, grad.shape[1])

        def block_for(peer):
            return lax.dynamic_index_in_dim(grad, peer, 0, keepdims=False)

        return seq_permutes(block_for)

    def owned_sum(pieces):
        whole = in_seq_order(pieces, F32)
        return jnp.sum(whole.reshape((own_experts, sharers) + whole.shape[1:]), axis=1)

    early_hidden, *early_pre_grads = run_expert(early_rows, early_grads)
    early_row_grad = row_grads(*early_pre_grads)
    late_rows, early_row_grad = lax.optimization_barrier((late_rows, early_row_grad))
    early_back = swap(early_row_grad, ("dp", "seq"))
    late_hidden, *late_pre_grads = run_expert(late_rows, late_grads)

    def flat(*parts):
        return [part.reshape(-1, part.shape[-1]) for part in parts]

    gate_grad, up_grad = weight_grads(
        flat(early_rows, late_rows),
        [flat(*pair) for pair in zip(early_pre_grads, late_pre_grads, strict=True)],
        "gate_up_grads",
    )
    late_pre_grads, late_hidden, gate_grad, up_grad = lax.optimization_barrier(
        (late_pre_grads, late_hidden, gate_grad, up_grad)
    )
    gate_grad_parts, up_grad_parts = to_owners(gate_grad), to_owners(up_grad)
    late_row_grad = row_grads(*late_pre_grads)
    (down_grad,) = weight_grads(
        flat(early_hidden, late_hidden), [flat(early_grads, late_grads)], "down_grads"
    )
    early_back, late_row_grad, gate_grad_parts, up_grad_parts, down_grad, late_hidden = (
        lax.optimization_barrier(
            (early_back, late_row_grad, gate_grad_parts, up_grad_parts, down_grad, late_hidden)
        )
    )
    expert_hidden = both_parts(early_hidden, late_hidden)
    late_back = swap(late_row_grad, ("dp", "seq"))
    down_owned = owned_sum(to_owners(down_grad))
    gate_owned, up_owned = owned_sum(gate_grad_parts), owned_sum(up_grad_parts)
    expert_out = nn(expert_hidden, down_full).astype(BF16)
    expert_out, late_back, gate_owned, up_owned, down_owned = lax.optimization_barrier(
        (expert_out, late_back, gate_owned, up_owned, down_owned)
    )
    returned = swap(expert_out.reshape(devices, CAP, width), ("dp", "seq")).reshape(slots, width)
    early_back, late_back = early_back.reshape(-1, width), late_back.reshape(-1, width)
    moe_input_grad = nn(early_hot, early_back) + nn(late_hot, late_back)
    middle_norm_grad, gain_two_grad = norm_back(middle, scale_two, gain_two, moe_input_grad)
    middle_grad = out_grad + middle_norm_grad
    branch_grad = middle_grad.astype(BF16)
    out_terms = tn(attended, branch_grad).astype(BF16)
    attended_grad = nt(branch_grad, out_full).astype(BF16)
    projected_grad = attention_back(
        lengths,
        query_flat,
        kv_all,
        attended_grad,
        log_total,
        attended,
        cosines,
        sines,
        4,
    )
    normed_grad = nt(projected_grad, packed_full)
    input_norm_grad, gain_one_grad = norm_back(inputs, scale_one, gain_one, normed_grad)
    input_grad = middle_grad + input_norm_grad

    lane = lax.broadcasted_iota(jnp.int32, (width, LANES), 1)
    gain_terms = jnp.where(lane == 0, gain_one_grad[:, None], gain_two_grad[:, None])
    gain_terms = jnp.where(lane < 2, gain_terms, 0.0).astype(BF16)
    query_terms = tn(normed, projected_grad).astype(BF16)
    if staged:
        out_owned, gains_owned, owned = staged_scatter(
            [out_terms, gain_terms, query_terms], [], None, 6, "scatter_attention_grads"
        )
    else:
        terms = jnp.concatenate([out_terms, gain_terms, query_terms], axis=1)
        terms = lax.psum_scatter(terms, BOTH, scatter_dimension=0, tiled=True).astype(F32)
        out_owned, gains_owned = terms[:, :width], terms[:, width : width + LANES]
        owned = terms[:, width + LANES :]
    returned, owned = lax.optimization_barrier((returned, owned))
    expert_grads = [gate_owned, up_owned, down_owned]

    gate_hot = jnp.sum(jnp.where(hits, gate_rows[:, :, None], 0.0), axis=1).astype(BF16)
    layer_out = middle + nn(gate_hot, returned)
    return (
        layer_out[None],
        input_grad[None],
        gains_owned[:, 0],
        gains_owned[:, 1],
        owned[:, :q_width],
        owned[:, q_width : q_width + kv_width],
        owned[:, q_width + kv_width : q_width + 2 * kv_width],
        out_owned,
        *expert_grads,
    )


def solution(mesh):
    part = P("dp", "seq", None)
    both = P(BOTH)
    both_rows = P(BOTH, None)
    return jax.shard_map(
        on_device,
        mesh=mesh,
        in_specs=(part, P("dp"), part, part, part, both, both)
        + (both_rows,) * 4
        + (part,) * 4,
        out_specs=(part, part, both, both) + (both_rows,) * 4 + (part,) * 3,
        check_vma=False,
    )
```

```python
import functools
import math

import jax
import jax.numpy as jnp
from jax import lax
from jax.experimental import pallas as pl
from jax.experimental.pallas import tpu as pltpu
from jax.sharding import PartitionSpec as P

HEAD_DIM = 128
EXPERTS = 32
TOP = 4
CAP = 40
EARLY = 24

EPSILON = 1e-06
ROPE_BASE = 10000.0
NEG_FILL = -1e30
LANES = 128
BOTH = ("seq", "dp")
BF16 = jnp.bfloat16
F32 = jnp.float32


def rope_angles(positions, head_size):
    half_dim = head_size // 2
    frequency = ROPE_BASE ** (-(2.0 * jnp.arange(half_dim, dtype=F32)) / head_size)
    angles = positions.astype(F32)[:, None] * frequency[None, :]
    return (jnp.cos(angles)[:, None, :], jnp.sin(angles)[:, None, :])


def dot(left, right, contract):
    return lax.dot_general(left, right, (contract, ((), ())), preferred_element_type=F32)


def nn(left, right):
    return dot(left, right, ((1,), (0,)))


def nt(left, right):
    return dot(left, right, ((1,), (1,)))


def tn(left, right):
    return dot(left, right, ((0,), (0,)))


def claim_places(routes, priority, is_valid):
    pair_routes = routes.reshape(-1)
    live = jnp.repeat(is_valid, TOP)
    key = jnp.where(live, pair_routes, -1)
    earlier = (key[None, :] == pair_routes[:, None]) & (priority[None, :] < priority[:, None])
    place = jnp.sum(earlier.astype(F32), axis=1).astype(jnp.int32)
    return pair_routes, place, live & (place < CAP)


def norm_back(values, scale_rows, gain_vec, incoming):
    weighted = incoming * gain_vec
    inner_mean = jnp.mean(weighted * values, axis=-1, keepdims=True)
    values_grad = scale_rows * weighted - values * scale_rows * scale_rows * scale_rows * inner_mean
    return (values_grad, jnp.sum(incoming * values * scale_rows, axis=0))


def swap(blocks, axes):
    return lax.all_to_all(blocks, axes, split_axis=0, concat_axis=0, tiled=True)


MESH_IDS = pl.DeviceIdType.MESH


def torus_place():
    seq, dp = lax.axis_index("seq"), lax.axis_index("dp")
    return seq // 2, seq % 2, dp // 2, dp % 2


def torus_id(a, b, z, c):
    return {"seq": 2 * a + b, "dp": 2 * z + c}


def torus_peers(line):
    a, b, z, c = torus_place()
    peers = [torus_id(a, b, z, 1 - c), torus_id(a, 1 - b, z, c), torus_id(1 - a, b, z, c)]
    peers.append(torus_id(1 - a, 1 - b, z, c))
    return peers + [torus_id(a, b, lax.rem(z + k, line), c) for k in range(1, line)]


def greet(peers):
    barrier = pltpu.get_barrier_semaphore()
    for peer in peers:
        pl.semaphore_signal(barrier, inc=1, device_id=peer, device_id_type=MESH_IDS)
    pl.semaphore_wait(barrier, len(peers))


def column_chunks(widths, parts):
    chunks = []
    for part in range(parts):
        for k, whole in enumerate(widths):
            tiles = whole // LANES
            first, end = tiles * part // parts, tiles * (part + 1) // parts
            if end > first:
                chunks.append((k, first * LANES, (end - first) * LANES))
    return chunks


def remote(src, dst, sems, i, j, device_id):
    send, recv = sems
    return pltpu.make_async_remote_copy(
        src_ref=src,
        dst_ref=dst,
        send_sem=send.at[i, j],
        recv_sem=recv.at[i, j],
        device_id=device_id,
        device_id_type=MESH_IDS,
    )


def start_exchange(count, sources, targets, block_of, sems):
    send_sems, recv_sems, local_sems = sems
    me = lax.axis_index("seq")
    copies = []
    for i, source in enumerate(sources):
        for step in range(1, count):
            peer = lax.rem(me + step, count)
            copies.append(
                pltpu.make_async_remote_copy(
                    src_ref=block_of(source, peer),
                    dst_ref=targets[i].at[me],
                    send_sem=send_sems.at[i, step - 1],
                    recv_sem=recv_sems.at[i, step - 1],
                    device_id={"seq": peer},
                    device_id_type=MESH_IDS,
                )
            )
        copies.append(
            pltpu.make_async_copy(block_of(source, me), targets[i].at[me], local_sems.at[i])
        )
    for copy in copies:
        copy.start()
    return copies


def exchange_sems(n, count):
    return [
        pltpu.SemaphoreType.DMA((n, count - 1)),
        pltpu.SemaphoreType.DMA((n, count - 1)),
        pltpu.SemaphoreType.DMA((n,)),
    ]


def in_steps(count, stages, after=None):
    for step in range((count + 1) // 2 + len(stages) - 1):
        if after is not None and step == (count + 1) // 2 + 1:
            after()
        for behind, stage in enumerate(stages):
            for i in (2 * (step - behind), 2 * (step - behind) + 1):
                if 0 <= i < count:
                    stage(i)


def gather_kernel(line, chunks, n, extras, block_of, *refs):
    sources, more_sources = refs[:n], refs[n : n + extras]
    refs = refs[n + extras :]
    targets, more_targets = refs[:n], refs[n : n + extras]
    send, recv, local, *more_sems = refs[n + extras :]
    sems = (send, recv)
    a, b, z, c = torus_place()
    greet(torus_peers(line))
    more = start_exchange(4, more_sources, more_targets, block_of, more_sems) if extras else []
    sent = []

    def start(copy):
        copy.start()
        sent.append(copy)
        return copy

    along_line, first_hop, second_hop, third_hop = {}, {}, {}, {}

    def send_line(i):
        k, first, size = chunks[i]
        cols = pl.ds(first, size)
        own = targets[k].at[a, b, z, c, :, cols]
        keep = pltpu.make_async_copy(sources[k].at[:, cols], own, local.at[i])
        keep.start()
        along_line[i] = [
            start(
                remote(
                    sources[k].at[:, cols],
                    own,
                    sems,
                    i,
                    2 + step,
                    torus_id(a, b, lax.rem(z + step, line), c),
                )
            )
            for step in range(1, line)
        ]
        along_line[i].append(keep)

    def send_first(i):
        k, first, size = chunks[i]
        *copies, keep = along_line[i]
        keep.wait()
        for copy in copies:
            copy.wait_recv()
        block = targets[k].at[a, b, :, c, :, pl.ds(first, size)]
        peer = torus_id(a, 1 - b, z, c) if i % 2 == 0 else torus_id(1 - a, b, z, c)
        first_hop[i] = start(remote(block, block, sems, i, 1, peer))

    def send_second(i):
        k, first, size = chunks[i]
        first_hop[i].wait_recv()
        cols = pl.ds(first, size)
        if i % 2 == 0:
            block, peer = targets[k].at[a, :, :, c, :, cols], torus_id(1 - a, b, z, c)
        else:
            block, peer = targets[k].at[:, b, :, c, :, cols], torus_id(a, 1 - b, z, c)
        second_hop[i] = start(remote(block, block, sems, i, 2, peer))

    def send_third(i):
        k, first, size = chunks[i]
        second_hop[i].wait_recv()
        block = targets[k].at[:, :, :, c, :, pl.ds(first, size)]
        third_hop[i] = start(remote(block, block, sems, i, 0, torus_id(a, b, z, 1 - c)))

    in_steps(len(chunks), [send_line, send_first, send_second, send_third])
    for copy in third_hop.values():
        copy.wait_recv()
    for copy in sent:
        copy.wait_send()
    for copy in more:
        copy.wait()


def staged_gather(arrays, extras, block_of, collective_id, name, parts=6):
    seq_count, line = lax.axis_size("seq"), lax.axis_size("dp") // 2
    rows, n = arrays[0].shape[0], len(arrays)
    chunks = column_chunks([x.shape[1] for x in arrays], parts)
    m = len(chunks)
    shape = (seq_count // 2, 2, line, 2, rows)
    size = sum(x.shape[1] for x in arrays) * rows * 64
    count = n + len(extras)
    outs = pl.pallas_call(
        functools.partial(gather_kernel, line, chunks, n, len(extras), block_of),
        out_shape=[jax.ShapeDtypeStruct(shape + (x.shape[1],), BF16) for x in arrays]
        + [jax.ShapeDtypeStruct((seq_count,) + x.shape[1:], BF16) for x in extras],
        in_specs=[pl.BlockSpec(memory_space=pl.ANY)] * count,
        out_specs=[pl.BlockSpec(memory_space=pl.ANY)] * count,
        scratch_shapes=[
            pltpu.SemaphoreType.DMA((m, 2 + line)),
            pltpu.SemaphoreType.DMA((m, 2 + line)),
            pltpu.SemaphoreType.DMA((m,)),
        ]
        + (exchange_sems(len(extras), seq_count) if extras else []),
        compiler_params=pltpu.CompilerParams(
            collective_id=collective_id, vmem_limit_bytes=56 << 20
        ),
        cost_estimate=pl.CostEstimate(flops=0, bytes_accessed=size, transcendentals=0),
        name=name,
    )(*arrays, *extras)
    return [o.reshape(-1, o.shape[-1]) for o in outs]


def scatter_kernel(line, chunks, n, extras, block_of, *refs):
    m = len(chunks)
    sources, more_sources = refs[:n], refs[n : n + extras]
    refs = refs[n + extras :]
    targets, more_targets = refs[:n], refs[n : n + extras]
    scratch = refs[n + extras :]
    owns, ins1, accs2, ins2, accs3, ins3, ins4 = (scratch[m * s : m * (s + 1)] for s in range(7))
    send, recv, local, *more_sems = scratch[7 * m :]
    sems = (send, recv)
    a, b, z, c = torus_place()
    greet(torus_peers(line))
    sent = []

    def start(copy):
        copy.start()
        sent.append(copy)
        return copy

    def add_lines(target, left, right):
        def one(j, carry):
            target[j] = (left[j].astype(F32) + right[j].astype(F32)).astype(BF16)
            return carry

        lax.fori_loop(0, line, one, 0)

    between_cores, first_hop, second_hop, along_line = {}, {}, {}, {}

    def send_core(i):
        k, first, size = chunks[i]
        cols = pl.ds(first, size)
        keep = pltpu.make_async_copy(sources[k].at[:, :, :, c, :, cols], owns[i], local.at[i])
        keep.start()
        swap_core = remote(
            sources[k].at[:, :, :, 1 - c, :, cols], ins1[i], sems, i, 0, torus_id(a, b, z, 1 - c)
        )
        between_cores[i] = (keep, start(swap_core))

    def send_first(i):
        keep, copy = between_cores[i]
        keep.wait()
        copy.wait_recv()
        for p in range(2):
            for q in range(2):
                add_lines(owns[i].at[p, q], owns[i].at[p, q], ins1[i].at[p, q])
        if i % 2 == 0:
            block, peer = owns[i].at[:, 1 - b], torus_id(a, 1 - b, z, c)
        else:
            block, peer = owns[i].at[1 - a], torus_id(1 - a, b, z, c)
        first_hop[i] = start(remote(block, ins2[i], sems, i, 1, peer))

    def send_second(i):
        first_hop[i].wait_recv()
        for p in range(2):
            mine = owns[i].at[p, b] if i % 2 == 0 else owns[i].at[a, p]
            add_lines(accs2[i].at[p], mine, ins2[i].at[p])
        if i % 2 == 0:
            block, peer = accs2[i].at[1 - a], torus_id(1 - a, b, z, c)
        else:
            block, peer = accs2[i].at[1 - b], torus_id(a, 1 - b, z, c)
        second_hop[i] = start(remote(block, ins3[i], sems, i, 2, peer))

    def send_line(i):
        second_hop[i].wait_recv()
        add_lines(accs3[i], accs2[i].at[a if i % 2 == 0 else b], ins3[i])
        copies = []
        for step in range(1, line):
            to = lax.rem(z + step, line)
            peer = torus_id(a, b, to, c)
            copies.append(start(remote(accs3[i].at[to], ins4[i].at[z], sems, i, 2 + step, peer)))
        along_line[i] = copies

    def finish(i):
        k, first, size = chunks[i]
        total = accs3[i][z].astype(F32)
        for step in range(1, line):
            along_line[i][step - 1].wait_recv()
            total = total + ins4[i][lax.rem(z + line - step, line)].astype(F32)
        targets[k][:, first : first + size] = total

    more = []

    def send_more():
        if extras:
            more.extend(start_exchange(4, more_sources, more_targets, block_of, more_sems))

    in_steps(m, [send_core, send_first, send_second, send_line, finish], send_more)
    for copy in sent:
        copy.wait_send()
    for copy in more:
        copy.wait()


def staged_scatter(arrays, extras, block_of, collective_id, name, parts=6):
    seq_count, line = lax.axis_size("seq"), lax.axis_size("dp") // 2
    rows, n = arrays[0].shape[0] // (2 * line * seq_count), len(arrays)
    chunks = column_chunks([x.shape[1] for x in arrays], parts)
    m = len(chunks)
    leads = [(2, 2, line), (2, 2, line), (2, line), (2, line), (line,), (line,), (line,)]
    size = sum(x.shape[1] for x in arrays) * rows * 64
    anywhere = pl.BlockSpec(memory_space=pl.ANY)
    return pl.pallas_call(
        functools.partial(scatter_kernel, line, chunks, n, len(extras), block_of),
        out_shape=[jax.ShapeDtypeStruct((rows, x.shape[1]), F32) for x in arrays]
        + [jax.ShapeDtypeStruct((seq_count,) + x.shape[1:], BF16) for x in extras],
        in_specs=[anywhere] * (n + len(extras)),
        out_specs=[pl.BlockSpec(memory_space=pltpu.VMEM)] * n + [anywhere] * len(extras),
        scratch_shapes=[
            pltpu.VMEM(lead + (rows, width), BF16) for lead in leads for _, _, width in chunks
        ]
        + [
            pltpu.SemaphoreType.DMA((m, 2 + line)),
            pltpu.SemaphoreType.DMA((m, 2 + line)),
            pltpu.SemaphoreType.DMA((m,)),
        ]
        + (exchange_sems(len(extras), seq_count) if extras else []),
        compiler_params=pltpu.CompilerParams(
            collective_id=collective_id, vmem_limit_bytes=36 << 20
        ),
        cost_estimate=pl.CostEstimate(flops=0, bytes_accessed=size, transcendentals=0),
        name=name,
    )(*[x.reshape(2, 2, line, 2, rows, x.shape[1]) for x in arrays], *extras)


def rotate(values, cosines, sines):
    return values * cosines + pltpu.roll(values, HEAD_DIM // 2, 1) * sines


def attention_kernel(count, heads, kv_heads, *refs):
    length_ref, projected_ref, cos_ref, sin_ref = refs[:4]
    attended_ref, lse_ref, q_ref, kv_ref = refs[4:8]
    max_ref, sum_ref, acc_ref, send, recv = refs[8:]
    me = lax.axis_index("seq")
    rows, kv_width = q_ref.shape[0], kv_heads * HEAD_DIM
    q_width, group, scale = heads * HEAD_DIM, heads // kv_heads, 1.0 / math.sqrt(HEAD_DIM)
    greet([{"seq": lax.rem(me + step, count)} for step in range(1, count)])
    cosines, sines = cos_ref[...], sin_ref[...]
    for g in range(kv_heads):
        cols = slice(g * HEAD_DIM, (g + 1) * HEAD_DIM)
        keys = projected_ref[:, q_width + g * HEAD_DIM : q_width + (g + 1) * HEAD_DIM]
        kv_ref[me, :, cols] = rotate(keys, cosines, sines).astype(BF16)
    kv_ref[me, :, kv_width:] = projected_ref[:, q_width + kv_width :].astype(BF16)

    def to_later(peer):
        return pltpu.make_async_remote_copy(
            src_ref=kv_ref.at[me],
            dst_ref=kv_ref.at[me],
            send_sem=send.at[peer],
            recv_sem=recv.at[me],
            device_id={"seq": peer},
            device_id_type=MESH_IDS,
        )

    def start(peer, carry):
        to_later(peer).start()
        return carry

    lax.fori_loop(me + 1, count, start, 0)

    def one_query(h, carry):
        cols = pl.ds(pl.multiple_of(h * HEAD_DIM, HEAD_DIM), HEAD_DIM)
        q_ref[:, cols] = rotate(projected_ref[:, cols], cosines, sines).astype(BF16)
        return carry

    lax.fori_loop(0, heads, one_query, 0)
    max_ref[...] = jnp.full_like(max_ref, NEG_FILL)
    sum_ref[...] = jnp.zeros_like(sum_ref)
    acc_ref[...] = jnp.zeros_like(acc_ref)
    length = length_ref[0]
    query_pos = me * rows + lax.broadcasted_iota(jnp.int32, (rows, rows), 1)
    key_local = lax.broadcasted_iota(jnp.int32, (rows, rows), 0)

    def key_block(j):
        key_pos = j * rows + key_local
        mask = (key_pos <= query_pos) & (key_pos < length)
        for g in range(kv_heads):
            key_cols = slice(g * HEAD_DIM, (g + 1) * HEAD_DIM)
            value_cols = slice(kv_width + g * HEAD_DIM, kv_width + (g + 1) * HEAD_DIM)

            def one_head(i, carry):
                h = g * group + i
                cols = pl.ds(pl.multiple_of(h * HEAD_DIM, HEAD_DIM), HEAD_DIM)
                row = pl.ds(h, 1)
                keys, values = kv_ref[j, :, key_cols], kv_ref[j, :, value_cols]
                scores = jnp.where(mask, nt(keys, q_ref[:, cols]) * scale, NEG_FILL)
                before = max_ref[row, :]
                top = jnp.maximum(before, jnp.max(scores, axis=0, keepdims=True))
                shrink = jnp.exp(before - top)
                weights = jnp.exp(scores - top)
                max_ref[row, :] = top
                sum_ref[row, :] = sum_ref[row, :] * shrink + jnp.sum(weights, axis=0, keepdims=True)
                acc_ref[h] = acc_ref[h] * shrink + tn(values, weights.astype(BF16))
                return carry

            lax.fori_loop(0, group, one_head, 0, unroll=2)

    key_block(me)

    def earlier_block(j, carry):
        pltpu.make_async_remote_copy(
            src_ref=kv_ref.at[j],
            dst_ref=kv_ref.at[j],
            send_sem=send.at[j],
            recv_sem=recv.at[j],
            device_id={"seq": j},
            device_id_type=MESH_IDS,
        ).wait_recv()
        key_block(j)
        return carry

    lax.fori_loop(0, me, earlier_block, 0)
    lse_ref[...] = max_ref[...] + jnp.log(sum_ref[...])

    def finish(h, carry):
        cols = pl.ds(pl.multiple_of(h * HEAD_DIM, HEAD_DIM), HEAD_DIM)
        attended_ref[:, cols] = (acc_ref[h] / sum_ref[pl.ds(h, 1), :]).T.astype(BF16)
        return carry

    lax.fori_loop(0, heads, finish, 0)

    def sent(peer, carry):
        to_later(peer).wait_send()
        return carry

    lax.fori_loop(me + 1, count, sent, 0)


def attention(length, projected, cosines, sines, q_width, collective_id):
    count = lax.axis_size("seq")
    rows = projected.shape[0]
    kv_width = (projected.shape[1] - q_width) // 2
    heads, kv_heads = q_width // HEAD_DIM, kv_width // HEAD_DIM
    vmem = pl.BlockSpec(memory_space=pltpu.VMEM)
    return pl.pallas_call(
        functools.partial(attention_kernel, count, heads, kv_heads),
        out_shape=[
            jax.ShapeDtypeStruct((rows, q_width), BF16),
            jax.ShapeDtypeStruct((heads, rows), F32),
            jax.ShapeDtypeStruct((rows, q_width), BF16),
            jax.ShapeDtypeStruct((count, rows, 2 * kv_width), BF16),
        ],
        in_specs=[pl.BlockSpec(memory_space=pltpu.SMEM)] + [vmem] * 3,
        out_specs=[vmem] * 4,
        scratch_shapes=[
            pltpu.VMEM((heads, rows), F32),
            pltpu.VMEM((heads, rows), F32),
            pltpu.VMEM((heads, HEAD_DIM, rows), F32),
            pltpu.SemaphoreType.DMA((count,)),
            pltpu.SemaphoreType.DMA((count,)),
        ],
        compiler_params=pltpu.CompilerParams(
            collective_id=collective_id, vmem_limit_bytes=30 << 20
        ),
        cost_estimate=pl.CostEstimate(flops=0, bytes_accessed=1 << 20, transcendentals=0),
        name="attention_forward",
    )(length, projected, cosines, sines)


def attention_back_kernel(count, heads, kv_heads, *refs):
    length_ref, q_ref, kv_ref, grad_ref, lse_ref, attended_ref, cos_ref, sin_ref = refs[:8]
    out_ref, delta_ref, dq_ref, part_ref, leaving, arriving, send, recv = refs[8:]
    me = lax.axis_index("seq")
    rows, kv_width = q_ref.shape[0], kv_heads * HEAD_DIM
    group, scale = heads // kv_heads, 1.0 / math.sqrt(HEAD_DIM)
    greet([{"seq": lax.rem(me + step, count)} for step in range(1, count)])
    length = length_ref[0]
    query_pos = me * rows + lax.broadcasted_iota(jnp.int32, (rows, rows), 1)
    key_local = lax.broadcasted_iota(jnp.int32, (rows, rows), 0)
    dq_ref[...] = jnp.zeros_like(dq_ref)
    ones = jnp.ones((8, HEAD_DIM), BF16)
    for h in range(heads):
        cols = slice(h * HEAD_DIM, (h + 1) * HEAD_DIM)
        terms = grad_ref[:, cols].astype(F32) * attended_ref[:, cols].astype(F32)
        high = terms.astype(BF16)
        low = (terms - high.astype(F32)).astype(BF16)
        delta_ref[h : h + 1, :] = (nt(ones, high) + nt(ones, low))[:1]

    def key_block(j):
        key_pos = j * rows + key_local
        mask = (key_pos <= query_pos) & (key_pos < length)
        part_ref[...] = jnp.zeros_like(part_ref)
        key_rows = pl.ds(pl.multiple_of(j * rows, rows), rows)
        for g in range(kv_heads):
            key_cols = slice(g * HEAD_DIM, (g + 1) * HEAD_DIM)
            value_cols = slice(kv_width + g * HEAD_DIM, kv_width + (g + 1) * HEAD_DIM)

            def one_head(i, carry):
                h = g * group + i
                cols = pl.ds(pl.multiple_of(h * HEAD_DIM, HEAD_DIM), HEAD_DIM)
                keys, values = kv_ref[key_rows, key_cols], kv_ref[key_rows, value_cols]
                queries, grads = q_ref[:, cols], grad_ref[:, cols]
                scores = nt(keys, queries) * scale
                probs = jnp.where(mask, jnp.exp(scores - lse_ref[pl.ds(h, 1), :]), 0.0)
                prob_grad = nt(values, grads)
                score_grad = (probs * (prob_grad - delta_ref[pl.ds(h, 1), :])).astype(BF16)
                part_ref[:, key_cols] += nn(score_grad, queries)
                part_ref[:, value_cols] += nn(probs.astype(BF16), grads)
                dq_ref[:, cols] += tn(score_grad, keys)
                return carry

            lax.fori_loop(0, group, one_head, 0, unroll=3)
        part_ref[:, :kv_width] = part_ref[:, :kv_width] * scale

    def to_owner(j):
        return pltpu.make_async_remote_copy(
            src_ref=leaving.at[j],
            dst_ref=arriving.at[me],
            send_sem=send.at[j],
            recv_sem=recv.at[me],
            device_id={"seq": j},
            device_id_type=MESH_IDS,
        )

    def other_block(j, carry):
        key_block(j)
        leaving[j] = part_ref[...].astype(BF16)
        to_owner(j).start()
        return carry

    lax.fori_loop(0, me, other_block, 0)
    key_block(me)
    part_ref[...] = part_ref[...].astype(BF16).astype(F32)
    cosines, sines = cos_ref[...], -sin_ref[...]

    def one_query(h, carry):
        cols = pl.ds(pl.multiple_of(h * HEAD_DIM, HEAD_DIM), HEAD_DIM)
        out_ref[:, cols] = rotate(dq_ref[:, cols] * scale, cosines, sines).astype(BF16)
        return carry

    lax.fori_loop(0, heads, one_query, 0)

    def add_arrived(m, carry):
        pltpu.make_async_remote_copy(
            src_ref=leaving.at[m],
            dst_ref=arriving.at[m],
            send_sem=send.at[m],
            recv_sem=recv.at[m],
            device_id={"seq": m},
            device_id_type=MESH_IDS,
        ).wait_recv()
        part_ref[...] += arriving[m].astype(F32)
        return carry

    lax.fori_loop(me + 1, count, add_arrived, 0)
    first = heads * HEAD_DIM
    for g in range(kv_heads):
        cols = slice(g * HEAD_DIM, (g + 1) * HEAD_DIM)
        out_ref[:, first + g * HEAD_DIM : first + (g + 1) * HEAD_DIM] = rotate(
            part_ref[:, cols], cosines, sines
        ).astype(BF16)
    out_ref[:, first + kv_width :] = part_ref[:, kv_width:].astype(BF16)

    def sent(j, carry):
        to_owner(j).wait_send()
        return carry

    lax.fori_loop(0, me, sent, 0)


def attention_back(length, queries, kv_all, grads, lse, attended, cosines, sines, collective_id):
    count = lax.axis_size("seq")
    rows, q_width = queries.shape
    kv_width = kv_all.shape[1] // 2
    heads, kv_heads = q_width // HEAD_DIM, kv_width // HEAD_DIM
    vmem = pl.BlockSpec(memory_space=pltpu.VMEM)
    return pl.pallas_call(
        functools.partial(attention_back_kernel, count, heads, kv_heads),
        out_shape=jax.ShapeDtypeStruct((rows, q_width + 2 * kv_width), BF16),
        in_specs=[pl.BlockSpec(memory_space=pltpu.SMEM)] + [vmem] * 7,
        out_specs=vmem,
        scratch_shapes=[
            pltpu.VMEM((heads, rows), F32),
            pltpu.VMEM((rows, q_width), F32),
            pltpu.VMEM((rows, 2 * kv_width), F32),
            pltpu.VMEM((count, rows, 2 * kv_width), BF16),
            pltpu.VMEM((count, rows, 2 * kv_width), BF16),
            pltpu.SemaphoreType.DMA((count,)),
            pltpu.SemaphoreType.DMA((count,)),
        ],
        compiler_params=pltpu.CompilerParams(
            collective_id=collective_id, vmem_limit_bytes=30 << 20
        ),
        cost_estimate=pl.CostEstimate(
            flops=10 * count * rows * rows * q_width, bytes_accessed=1 << 20, transcendentals=0
        ),
        name="attention_backward",
    )(length, queries, kv_all, grads, lse, attended, cosines, sines)


def weight_grad_kernel(n, *refs):
    lefts, rights, outs = refs[:2], refs[2 : 2 + 2 * n], refs[2 + 2 * n :]
    for k, out_ref in enumerate(outs):
        early, late = rights[2 * k : 2 * k + 2]
        total = tn(lefts[0][...], early[...]) + tn(lefts[1][...], late[...])
        out_ref[...] = total.astype(BF16)


def weight_grads(lefts, rights, name):
    columns, tile = lefts[0].shape[1], 256
    flat = [part for pair in rights for part in pair]
    return pl.pallas_call(
        functools.partial(weight_grad_kernel, len(rights)),
        grid=(columns // tile,),
        out_shape=[jax.ShapeDtypeStruct((columns, r[0].shape[1]), BF16) for r in rights],
        in_specs=[pl.BlockSpec((x.shape[0], tile), lambda i: (0, i)) for x in lefts]
        + [pl.BlockSpec(r.shape, lambda i: (0, 0), pipeline_mode=pl.Buffered(1)) for r in flat],
        out_specs=[pl.BlockSpec((tile, r[0].shape[1]), lambda i: (i, 0)) for r in rights],
        compiler_params=pltpu.CompilerParams(vmem_limit_bytes=48 << 20),
        cost_estimate=pl.CostEstimate(flops=0, bytes_accessed=1 << 20, transcendentals=0),
        name=name,
    )(*lefts, *flat)


def seq_permutes(block_for):
    count, me = lax.axis_size("seq"), lax.axis_index("seq")
    pieces = [block_for(me)]
    for step in range(1, count):
        ring = [(i, (i + step) % count) for i in range(count)]
        pieces.append(lax.ppermute(block_for(lax.rem(me + step, count)), "seq", ring))
    return pieces


def in_seq_order(pieces, dtype):
    count, me = len(pieces), lax.axis_index("seq")
    whole = jnp.zeros((count,) + pieces[0].shape, dtype)
    for step, piece in enumerate(pieces):
        place = lax.rem(me + count - step, count)
        whole = lax.dynamic_update_index_in_dim(whole, piece.astype(dtype), place, 0)
    return whole


def on_device(
    hidden_in,
    lengths,
    routes,
    gates,
    priority,
    attn_gain,
    mlp_gain,
    w_query,
    key_projection,
    value_projection,
    w_out,
    w_gate,
    w_up,
    w_down,
    cotangent,
):
    rows = hidden_in.shape[1]
    width = hidden_in.shape[2]
    dp_count = lax.axis_size("dp")
    seq_count = lax.axis_size("seq")
    devices = dp_count * seq_count
    own_experts = w_gate.shape[0]
    sharers = seq_count // own_experts
    hidden_units = w_gate.shape[2]
    my_seq = lax.axis_index("seq")
    extent = rows * seq_count
    query_pos = my_seq * rows + jnp.arange(rows, dtype=jnp.int32)
    length = lengths[0]
    is_valid = query_pos < length
    q_width = w_query.shape[1]
    kv_width = key_projection.shape[1]
    cosine_lookup, sine_lookup = rope_angles(query_pos, HEAD_DIM)

    gain_block = jnp.concatenate(
        [attn_gain[:, None], mlp_gain[:, None], jnp.zeros((attn_gain.shape[0], LANES - 2), BF16)],
        axis=1,
    )
    packed = jnp.concatenate([w_query, key_projection, value_projection], axis=1)
    staged = seq_count == 4 and w_query.shape[0] % 16 == 0

    def expert_pieces(weights):
        def block_for(peer):
            return lax.dynamic_index_in_dim(weights, peer // sharers, 0, keepdims=False)

        return seq_permutes(block_for)

    gate_parts = expert_pieces(w_gate)
    if staged:
        packed_full, gains_full, out_full = staged_gather(
            [packed, gain_block, w_out], [], None, 2, "gather_attention_weights"
        )
    else:
        packed_full = lax.all_gather(packed, BOTH, axis=0, tiled=True)
        gains_full = lax.all_gather(gain_block, BOTH, axis=0, tiled=True)
        out_full = lax.all_gather(w_out, BOTH, axis=0, tiled=True)

    pair_routes, place, kept = claim_places(routes[0], priority[0, 0], is_valid)
    holder = (pair_routes // own_experts) * seq_count + (pair_routes % own_experts) * sharers
    holder = holder + my_seq * sharers // seq_count
    slots = devices * CAP
    target = jnp.where(kept, holder * CAP + place, slots).reshape(rows, TOP)
    slot_ids = jnp.arange(slots, dtype=jnp.int32)
    hits = target[:, :, None] == slot_ids[None, None, :]
    gate_rows = gates[0]
    token_hot = jnp.any(hits, axis=1).astype(BF16)

    def hot_of(first, size):
        mine = kept & (place >= first) & (place < first + size)
        spot = jnp.where(mine, holder * size + place - first, slots).reshape(rows, TOP)
        ids = jnp.arange(devices * size, dtype=jnp.int32)
        return jnp.any(spot[:, :, None] == ids[None, None, :], axis=1).astype(BF16)

    early_hot, late_hot = hot_of(0, EARLY), hot_of(EARLY, CAP - EARLY)
    slot_gate = jnp.sum(jnp.where(hits, gate_rows[:, :, None], 0.0), axis=(0, 1))

    live_cotangent = jnp.where(is_valid[:, None], cotangent[0], jnp.zeros((), BF16))
    out_grad = live_cotangent.astype(F32)
    grad_send = (tn(token_hot, live_cotangent) * slot_gate[:, None]).astype(BF16)
    packed_full, gains_full, out_full, gate_parts, grad_send = lax.optimization_barrier(
        (packed_full, gains_full, out_full, gate_parts, grad_send)
    )
    gain_one, gain_two = gains_full[:, 0].astype(F32), gains_full[:, 1].astype(F32)
    grad_rows = swap(grad_send.reshape(devices, CAP, width), ("dp", "seq"))

    inputs = hidden_in[0].astype(F32)
    scale_one = lax.rsqrt(jnp.mean(inputs * inputs, axis=-1, keepdims=True) + EPSILON)
    normed = (inputs * scale_one * gain_one).astype(BF16)
    projected = nn(normed, packed_full)
    cosines, sines = cosine_lookup[:, 0], sine_lookup[:, 0]
    cosines = jnp.concatenate([cosines, cosines], axis=1)
    sines = jnp.concatenate([-sines, sines], axis=1)
    attended, log_total, query_flat, kv_all = attention(
        lengths, projected, cosines, sines, q_width, 1
    )
    kv_all = kv_all.reshape(extent, 2 * kv_width)
    attended, w_up = lax.optimization_barrier((attended, w_up))
    up_parts = expert_pieces(w_up)
    middle = inputs + nn(attended, out_full)
    scale_two = lax.rsqrt(jnp.mean(middle * middle, axis=-1, keepdims=True) + EPSILON)
    moe_input = (middle * scale_two * gain_two).astype(BF16)

    def to_experts(hot):
        return tn(hot, moe_input).astype(BF16).reshape(devices, -1, width)

    early_send, late_send = to_experts(early_hot), to_experts(late_hot)
    early_send, late_send, grad_rows, up_parts, w_down = lax.optimization_barrier(
        (early_send, late_send, grad_rows, up_parts, w_down)
    )
    early_grads, late_grads, w_down = lax.optimization_barrier(
        (grad_rows[:, :EARLY], grad_rows[:, EARLY:], w_down)
    )
    down_parts = expert_pieces(w_down)
    early_rows = swap(early_send, ("dp", "seq"))
    early_rows, late_send = lax.optimization_barrier((early_rows, late_send))
    late_rows = swap(late_send, ("dp", "seq"))
    gate_full = in_seq_order(gate_parts, BF16).reshape(width, hidden_units)
    up_full = in_seq_order(up_parts, BF16).reshape(width, hidden_units)
    down_full = in_seq_order(down_parts, BF16).reshape(hidden_units, width)
    early_rows, gate_full, up_full, down_full, early_grads, late_grads = (
        lax.optimization_barrier(
            (early_rows, gate_full, up_full, down_full, early_grads, late_grads)
        )
    )

    def run_expert(slot_rows, grads):
        blocks = slot_rows.shape[:2]
        slot_rows, grads = slot_rows.reshape(-1, width), grads.reshape(-1, width)
        gate_pre = nn(slot_rows, gate_full)
        up_pre = nn(slot_rows, up_full)
        gate_sigmoid = jax.nn.sigmoid(gate_pre)
        gate_act = gate_pre * gate_sigmoid
        gate_slope = gate_sigmoid * (1.0 + gate_pre * (1.0 - gate_sigmoid))
        hidden = (gate_act * up_pre).astype(BF16)
        hidden_grad = nt(grads, down_full)
        gate_pre_grad = (hidden_grad * up_pre * gate_slope).astype(BF16)
        up_pre_grad = (hidden_grad * gate_act).astype(BF16)
        return [x.reshape(blocks + (-1,)) for x in (hidden, gate_pre_grad, up_pre_grad)]

    def row_grads(gate_pre_grad, up_pre_grad):
        blocks = gate_pre_grad.shape[:2]
        gate_pre_grad = gate_pre_grad.reshape(-1, hidden_units)
        up_pre_grad = up_pre_grad.reshape(-1, hidden_units)
        row_grad = (nt(gate_pre_grad, gate_full) + nt(up_pre_grad, up_full)).astype(BF16)
        return row_grad.reshape(blocks + (width,))

    def both_parts(early, late):
        return jnp.concatenate([early, late], axis=1).reshape(slots, -1)

    def to_owners(grad):
        grad = grad.reshape(seq_count, -1, grad.shape[1])

        def block_for(peer):
            return lax.dynamic_index_in_dim(grad, peer, 0, keepdims=False)

        return seq_permutes(block_for)

    def owned_sum(pieces):
        whole = in_seq_order(pieces, F32)
        return jnp.sum(whole.reshape((own_experts, sharers) + whole.shape[1:]), axis=1)

    early_hidden, *early_pre_grads = run_expert(early_rows, early_grads)
    early_row_grad = row_grads(*early_pre_grads)
    late_rows, early_row_grad = lax.optimization_barrier((late_rows, early_row_grad))
    early_back = swap(early_row_grad, ("dp", "seq"))
    late_hidden, *late_pre_grads = run_expert(late_rows, late_grads)

    def flat(*parts):
        return [part.reshape(-1, part.shape[-1]) for part in parts]

    gate_grad, up_grad = weight_grads(
        flat(early_rows, late_rows),
        [flat(*pair) for pair in zip(early_pre_grads, late_pre_grads, strict=True)],
        "gate_up_grads",
    )
    late_pre_grads, late_hidden, gate_grad, up_grad = lax.optimization_barrier(
        (late_pre_grads, late_hidden, gate_grad, up_grad)
    )
    gate_grad_parts = to_owners(gate_grad)
    late_row_grad = row_grads(*late_pre_grads)
    early_back, late_row_grad, gate_grad_parts, up_grad, late_hidden = lax.optimization_barrier(
        (early_back, late_row_grad, gate_grad_parts, up_grad, late_hidden)
    )
    expert_hidden = both_parts(early_hidden, late_hidden)
    late_back = swap(late_row_grad, ("dp", "seq"))
    gate_owned, up_owned = owned_sum(gate_grad_parts), owned_sum(to_owners(up_grad))
    (down_grad,) = weight_grads(
        flat(early_hidden, late_hidden), [flat(early_grads, late_grads)], "down_grads"
    )
    expert_out = nn(expert_hidden, down_full).astype(BF16)
    expert_out, late_back, gate_owned, up_owned, down_grad = lax.optimization_barrier(
        (expert_out, late_back, gate_owned, up_owned, down_grad)
    )
    returned = swap(expert_out.reshape(devices, CAP, width), ("dp", "seq")).reshape(slots, width)
    early_back, late_back = early_back.reshape(-1, width), late_back.reshape(-1, width)
    moe_input_grad = nn(early_hot, early_back) + nn(late_hot, late_back)
    middle_norm_grad, gain_two_grad = norm_back(middle, scale_two, gain_two, moe_input_grad)
    middle_grad = out_grad + middle_norm_grad
    branch_grad = middle_grad.astype(BF16)
    out_terms = tn(attended, branch_grad).astype(BF16)
    attended_grad = nt(branch_grad, out_full).astype(BF16)
    projected_grad = attention_back(
        lengths,
        query_flat,
        kv_all,
        attended_grad,
        log_total,
        attended,
        cosines,
        sines,
        4,
    )
    normed_grad = nt(projected_grad, packed_full)
    input_norm_grad, gain_one_grad = norm_back(inputs, scale_one, gain_one, normed_grad)
    input_grad = middle_grad + input_norm_grad

    lane = lax.broadcasted_iota(jnp.int32, (width, LANES), 1)
    gain_terms = jnp.where(lane == 0, gain_one_grad[:, None], gain_two_grad[:, None])
    gain_terms = jnp.where(lane < 2, gain_terms, 0.0).astype(BF16)
    query_terms = tn(normed, projected_grad).astype(BF16)
    if staged:
        out_owned, gains_owned, owned, down_owned = staged_scatter(
            [out_terms, gain_terms, query_terms],
            [down_grad.reshape(seq_count, -1, width)],
            lambda ref, peer: ref.at[peer],
            6,
            "scatter_attention_grads",
        )
        down_owned = down_owned.reshape((own_experts, sharers) + down_owned.shape[1:])
        down_owned = jnp.sum(down_owned.astype(F32), axis=1)
    else:
        terms = jnp.concatenate([out_terms, gain_terms, query_terms], axis=1)
        terms = lax.psum_scatter(terms, BOTH, scatter_dimension=0, tiled=True).astype(F32)
        out_owned, gains_owned = terms[:, :width], terms[:, width : width + LANES]
        owned = terms[:, width + LANES :]
        down_owned = owned_sum(to_owners(down_grad))
    returned, owned = lax.optimization_barrier((returned, owned))
    expert_grads = [gate_owned, up_owned, down_owned]

    gate_hot = jnp.sum(jnp.where(hits, gate_rows[:, :, None], 0.0), axis=1).astype(BF16)
    layer_out = middle + nn(gate_hot, returned)
    return (
        layer_out[None],
        input_grad[None],
        gains_owned[:, 0],
        gains_owned[:, 1],
        owned[:, :q_width],
        owned[:, q_width : q_width + kv_width],
        owned[:, q_width + kv_width : q_width + 2 * kv_width],
        out_owned,
        *expert_grads,
    )


def solution(mesh):
    part = P("dp", "seq", None)
    both = P(BOTH)
    both_rows = P(BOTH, None)
    return jax.shard_map(
        on_device,
        mesh=mesh,
        in_specs=(part, P("dp"), part, part, part, both, both)
        + (both_rows,) * 4
        + (part,) * 4,
        out_specs=(part, part, both, both) + (both_rows,) * 4 + (part,) * 3,
        check_vma=False,
    )
```

```python
import functools
import math

import jax
import jax.numpy as jnp
from jax import lax
from jax.experimental import pallas as pl
from jax.experimental.pallas import tpu as pltpu
from jax.sharding import PartitionSpec as P

HEAD_DIM = 128
EXPERTS = 32
TOP = 4
CAP = 40
EARLY = 16

EPSILON = 1e-06
ROPE_BASE = 10000.0
NEG_FILL = -1e30
LANES = 128
BOTH = ("seq", "dp")
BF16 = jnp.bfloat16
F32 = jnp.float32


def rope_angles(positions, head_size):
    half_dim = head_size // 2
    frequency = ROPE_BASE ** (-(2.0 * jnp.arange(half_dim, dtype=F32)) / head_size)
    angles = positions.astype(F32)[:, None] * frequency[None, :]
    return (jnp.cos(angles)[:, None, :], jnp.sin(angles)[:, None, :])


def dot(left, right, contract):
    return lax.dot_general(left, right, (contract, ((), ())), preferred_element_type=F32)


def nn(left, right):
    return dot(left, right, ((1,), (0,)))


def nt(left, right):
    return dot(left, right, ((1,), (1,)))


def tn(left, right):
    return dot(left, right, ((0,), (0,)))


def claim_places(routes, priority, is_valid):
    pair_routes = routes.reshape(-1)
    live = jnp.repeat(is_valid, TOP)
    key = jnp.where(live, pair_routes, -1)
    earlier = (key[None, :] == pair_routes[:, None]) & (priority[None, :] < priority[:, None])
    place = jnp.sum(earlier.astype(F32), axis=1).astype(jnp.int32)
    return pair_routes, place, live & (place < CAP)


def norm_back(values, scale_rows, gain_vec, incoming):
    weighted = incoming * gain_vec
    inner_mean = jnp.mean(weighted * values, axis=-1, keepdims=True)
    values_grad = scale_rows * weighted - values * scale_rows * scale_rows * scale_rows * inner_mean
    return (values_grad, jnp.sum(incoming * values * scale_rows, axis=0))


def swap(blocks, axes):
    return lax.all_to_all(blocks, axes, split_axis=0, concat_axis=0, tiled=True)


MESH_IDS = pl.DeviceIdType.MESH


def torus_place():
    seq, dp = lax.axis_index("seq"), lax.axis_index("dp")
    return seq // 2, seq % 2, dp // 2, dp % 2


def torus_id(a, b, z, c):
    return {"seq": 2 * a + b, "dp": 2 * z + c}


def torus_peers(line):
    a, b, z, c = torus_place()
    peers = [torus_id(a, b, z, 1 - c), torus_id(a, 1 - b, z, c), torus_id(1 - a, b, z, c)]
    peers.append(torus_id(1 - a, 1 - b, z, c))
    return peers + [torus_id(a, b, lax.rem(z + k, line), c) for k in range(1, line)]


def greet(peers):
    barrier = pltpu.get_barrier_semaphore()
    for peer in peers:
        pl.semaphore_signal(barrier, inc=1, device_id=peer, device_id_type=MESH_IDS)
    pl.semaphore_wait(barrier, len(peers))


def column_chunks(widths, parts):
    chunks = []
    for part in range(parts):
        for k, whole in enumerate(widths):
            tiles = whole // LANES
            first, end = tiles * part // parts, tiles * (part + 1) // parts
            if end > first:
                chunks.append((k, first * LANES, (end - first) * LANES))
    return chunks


def remote(src, dst, sems, i, j, device_id):
    send, recv = sems
    return pltpu.make_async_remote_copy(
        src_ref=src,
        dst_ref=dst,
        send_sem=send.at[i, j],
        recv_sem=recv.at[i, j],
        device_id=device_id,
        device_id_type=MESH_IDS,
    )


def start_exchange(count, sources, targets, block_of, sems):
    send_sems, recv_sems, local_sems = sems
    me = lax.axis_index("seq")
    copies = []
    for i, source in enumerate(sources):
        for step in range(1, count):
            peer = lax.rem(me + step, count)
            copies.append(
                pltpu.make_async_remote_copy(
                    src_ref=block_of(source, peer),
                    dst_ref=targets[i].at[me],
                    send_sem=send_sems.at[i, step - 1],
                    recv_sem=recv_sems.at[i, step - 1],
                    device_id={"seq": peer},
                    device_id_type=MESH_IDS,
                )
            )
        copies.append(
            pltpu.make_async_copy(block_of(source, me), targets[i].at[me], local_sems.at[i])
        )
    for copy in copies:
        copy.start()
    return copies


def exchange_sems(n, count):
    return [
        pltpu.SemaphoreType.DMA((n, count - 1)),
        pltpu.SemaphoreType.DMA((n, count - 1)),
        pltpu.SemaphoreType.DMA((n,)),
    ]


def in_steps(count, stages, after=None):
    for step in range((count + 1) // 2 + len(stages) - 1):
        if after is not None and step == (count + 1) // 2 + 1:
            after()
        for behind, stage in enumerate(stages):
            for i in (2 * (step - behind), 2 * (step - behind) + 1):
                if 0 <= i < count:
                    stage(i)


def gather_kernel(line, chunks, n, extras, block_of, *refs):
    sources, more_sources = refs[:n], refs[n : n + extras]
    refs = refs[n + extras :]
    targets, more_targets = refs[:n], refs[n : n + extras]
    send, recv, local, *more_sems = refs[n + extras :]
    sems = (send, recv)
    a, b, z, c = torus_place()
    greet(torus_peers(line))
    more = start_exchange(4, more_sources, more_targets, block_of, more_sems) if extras else []
    sent = []

    def start(copy):
        copy.start()
        sent.append(copy)
        return copy

    along_line, first_hop, second_hop, third_hop = {}, {}, {}, {}

    def send_line(i):
        k, first, size = chunks[i]
        cols = pl.ds(first, size)
        own = targets[k].at[a, b, z, c, :, cols]
        keep = pltpu.make_async_copy(sources[k].at[:, cols], own, local.at[i])
        keep.start()
        along_line[i] = [
            start(
                remote(
                    sources[k].at[:, cols],
                    own,
                    sems,
                    i,
                    2 + step,
                    torus_id(a, b, lax.rem(z + step, line), c),
                )
            )
            for step in range(1, line)
        ]
        along_line[i].append(keep)

    def send_first(i):
        k, first, size = chunks[i]
        *copies, keep = along_line[i]
        keep.wait()
        for copy in copies:
            copy.wait_recv()
        block = targets[k].at[a, b, :, c, :, pl.ds(first, size)]
        peer = torus_id(a, 1 - b, z, c) if i % 2 == 0 else torus_id(1 - a, b, z, c)
        first_hop[i] = start(remote(block, block, sems, i, 1, peer))

    def send_second(i):
        k, first, size = chunks[i]
        first_hop[i].wait_recv()
        cols = pl.ds(first, size)
        if i % 2 == 0:
            block, peer = targets[k].at[a, :, :, c, :, cols], torus_id(1 - a, b, z, c)
        else:
            block, peer = targets[k].at[:, b, :, c, :, cols], torus_id(a, 1 - b, z, c)
        second_hop[i] = start(remote(block, block, sems, i, 2, peer))

    def send_third(i):
        k, first, size = chunks[i]
        second_hop[i].wait_recv()
        block = targets[k].at[:, :, :, c, :, pl.ds(first, size)]
        third_hop[i] = start(remote(block, block, sems, i, 0, torus_id(a, b, z, 1 - c)))

    in_steps(len(chunks), [send_line, send_first, send_second, send_third])
    for copy in third_hop.values():
        copy.wait_recv()
    for copy in sent:
        copy.wait_send()
    for copy in more:
        copy.wait()


def staged_gather(arrays, extras, block_of, collective_id, name, parts=8):
    seq_count, line = lax.axis_size("seq"), lax.axis_size("dp") // 2
    rows, n = arrays[0].shape[0], len(arrays)
    chunks = column_chunks([x.shape[1] for x in arrays], parts)
    m = len(chunks)
    shape = (seq_count // 2, 2, line, 2, rows)
    size = sum(x.shape[1] for x in arrays) * rows * 64
    count = n + len(extras)
    outs = pl.pallas_call(
        functools.partial(gather_kernel, line, chunks, n, len(extras), block_of),
        out_shape=[jax.ShapeDtypeStruct(shape + (x.shape[1],), BF16) for x in arrays]
        + [jax.ShapeDtypeStruct((seq_count,) + x.shape[1:], BF16) for x in extras],
        in_specs=[pl.BlockSpec(memory_space=pl.ANY)] * count,
        out_specs=[pl.BlockSpec(memory_space=pl.ANY)] * count,
        scratch_shapes=[
            pltpu.SemaphoreType.DMA((m, 2 + line)),
            pltpu.SemaphoreType.DMA((m, 2 + line)),
            pltpu.SemaphoreType.DMA((m,)),
        ]
        + (exchange_sems(len(extras), seq_count) if extras else []),
        compiler_params=pltpu.CompilerParams(
            collective_id=collective_id, vmem_limit_bytes=56 << 20
        ),
        cost_estimate=pl.CostEstimate(flops=0, bytes_accessed=size, transcendentals=0),
        name=name,
    )(*arrays, *extras)
    return [o.reshape(-1, o.shape[-1]) for o in outs]


def scatter_kernel(line, chunks, n, extras, block_of, *refs):
    m = len(chunks)
    sources, more_sources = refs[:n], refs[n : n + extras]
    refs = refs[n + extras :]
    targets, more_targets = refs[:n], refs[n : n + extras]
    scratch = refs[n + extras :]
    owns, ins1, accs2, ins2, accs3, ins3, ins4 = (scratch[m * s : m * (s + 1)] for s in range(7))
    send, recv, local, *more_sems = scratch[7 * m :]
    sems = (send, recv)
    a, b, z, c = torus_place()
    greet(torus_peers(line))
    sent = []

    def start(copy):
        copy.start()
        sent.append(copy)
        return copy

    def add_lines(target, left, right):
        def one(j, carry):
            target[j] = (left[j].astype(F32) + right[j].astype(F32)).astype(BF16)
            return carry

        lax.fori_loop(0, line, one, 0)

    between_cores, first_hop, second_hop, along_line = {}, {}, {}, {}

    def send_core(i):
        k, first, size = chunks[i]
        cols = pl.ds(first, size)
        keep = pltpu.make_async_copy(sources[k].at[:, :, :, c, :, cols], owns[i], local.at[i])
        keep.start()
        swap_core = remote(
            sources[k].at[:, :, :, 1 - c, :, cols], ins1[i], sems, i, 0, torus_id(a, b, z, 1 - c)
        )
        between_cores[i] = (keep, start(swap_core))

    def send_first(i):
        keep, copy = between_cores[i]
        keep.wait()
        copy.wait_recv()
        for p in range(2):
            for q in range(2):
                add_lines(owns[i].at[p, q], owns[i].at[p, q], ins1[i].at[p, q])
        if i % 2 == 0:
            block, peer = owns[i].at[:, 1 - b], torus_id(a, 1 - b, z, c)
        else:
            block, peer = owns[i].at[1 - a], torus_id(1 - a, b, z, c)
        first_hop[i] = start(remote(block, ins2[i], sems, i, 1, peer))

    def send_second(i):
        first_hop[i].wait_recv()
        for p in range(2):
            mine = owns[i].at[p, b] if i % 2 == 0 else owns[i].at[a, p]
            add_lines(accs2[i].at[p], mine, ins2[i].at[p])
        if i % 2 == 0:
            block, peer = accs2[i].at[1 - a], torus_id(1 - a, b, z, c)
        else:
            block, peer = accs2[i].at[1 - b], torus_id(a, 1 - b, z, c)
        second_hop[i] = start(remote(block, ins3[i], sems, i, 2, peer))

    def send_line(i):
        second_hop[i].wait_recv()
        add_lines(accs3[i], accs2[i].at[a if i % 2 == 0 else b], ins3[i])
        copies = []
        for step in range(1, line):
            to = lax.rem(z + step, line)
            peer = torus_id(a, b, to, c)
            copies.append(start(remote(accs3[i].at[to], ins4[i].at[z], sems, i, 2 + step, peer)))
        along_line[i] = copies

    def finish(i):
        k, first, size = chunks[i]
        total = accs3[i][z].astype(F32)
        for step in range(1, line):
            along_line[i][step - 1].wait_recv()
            total = total + ins4[i][lax.rem(z + line - step, line)].astype(F32)
        targets[k][:, first : first + size] = total

    more = []

    def send_more():
        if extras:
            more.extend(start_exchange(4, more_sources, more_targets, block_of, more_sems))

    in_steps(m, [send_core, send_first, send_second, send_line, finish], send_more)
    for copy in sent:
        copy.wait_send()
    for copy in more:
        copy.wait()


def staged_scatter(arrays, extras, block_of, collective_id, name, parts=8):
    seq_count, line = lax.axis_size("seq"), lax.axis_size("dp") // 2
    rows, n = arrays[0].shape[0] // (2 * line * seq_count), len(arrays)
    chunks = column_chunks([x.shape[1] for x in arrays], parts)
    m = len(chunks)
    leads = [(2, 2, line), (2, 2, line), (2, line), (2, line), (line,), (line,), (line,)]
    size = sum(x.shape[1] for x in arrays) * rows * 64
    anywhere = pl.BlockSpec(memory_space=pl.ANY)
    return pl.pallas_call(
        functools.partial(scatter_kernel, line, chunks, n, len(extras), block_of),
        out_shape=[jax.ShapeDtypeStruct((rows, x.shape[1]), F32) for x in arrays]
        + [jax.ShapeDtypeStruct((seq_count,) + x.shape[1:], BF16) for x in extras],
        in_specs=[anywhere] * (n + len(extras)),
        out_specs=[pl.BlockSpec(memory_space=pltpu.VMEM)] * n + [anywhere] * len(extras),
        scratch_shapes=[
            pltpu.VMEM(lead + (rows, width), BF16) for lead in leads for _, _, width in chunks
        ]
        + [
            pltpu.SemaphoreType.DMA((m, 2 + line)),
            pltpu.SemaphoreType.DMA((m, 2 + line)),
            pltpu.SemaphoreType.DMA((m,)),
        ]
        + (exchange_sems(len(extras), seq_count) if extras else []),
        compiler_params=pltpu.CompilerParams(
            collective_id=collective_id, vmem_limit_bytes=36 << 20
        ),
        cost_estimate=pl.CostEstimate(flops=0, bytes_accessed=size, transcendentals=0),
        name=name,
    )(*[x.reshape(2, 2, line, 2, rows, x.shape[1]) for x in arrays], *extras)


def rotate(values, cosines, sines):
    return values * cosines + pltpu.roll(values, HEAD_DIM // 2, 1) * sines


def attention_kernel(count, heads, kv_heads, *refs):
    length_ref, projected_ref, cos_ref, sin_ref = refs[:4]
    attended_ref, lse_ref, q_ref, kv_ref = refs[4:8]
    max_ref, sum_ref, acc_ref, send, recv = refs[8:]
    me = lax.axis_index("seq")
    rows, kv_width = q_ref.shape[0], kv_heads * HEAD_DIM
    q_width, group, scale = heads * HEAD_DIM, heads // kv_heads, 1.0 / math.sqrt(HEAD_DIM)
    greet([{"seq": lax.rem(me + step, count)} for step in range(1, count)])
    cosines, sines = cos_ref[...], sin_ref[...]
    for g in range(kv_heads):
        cols = slice(g * HEAD_DIM, (g + 1) * HEAD_DIM)
        keys = projected_ref[:, q_width + g * HEAD_DIM : q_width + (g + 1) * HEAD_DIM]
        kv_ref[me, :, cols] = rotate(keys, cosines, sines).astype(BF16)
    kv_ref[me, :, kv_width:] = projected_ref[:, q_width + kv_width :].astype(BF16)

    def to_later(peer):
        return pltpu.make_async_remote_copy(
            src_ref=kv_ref.at[me],
            dst_ref=kv_ref.at[me],
            send_sem=send.at[peer],
            recv_sem=recv.at[me],
            device_id={"seq": peer},
            device_id_type=MESH_IDS,
        )

    def start(peer, carry):
        to_later(peer).start()
        return carry

    lax.fori_loop(me + 1, count, start, 0)

    def one_query(h, carry):
        cols = pl.ds(pl.multiple_of(h * HEAD_DIM, HEAD_DIM), HEAD_DIM)
        q_ref[:, cols] = rotate(projected_ref[:, cols], cosines, sines).astype(BF16)
        return carry

    lax.fori_loop(0, heads, one_query, 0)
    max_ref[...] = jnp.full_like(max_ref, NEG_FILL)
    sum_ref[...] = jnp.zeros_like(sum_ref)
    acc_ref[...] = jnp.zeros_like(acc_ref)
    length = length_ref[0]
    query_pos = me * rows + lax.broadcasted_iota(jnp.int32, (rows, rows), 1)
    key_local = lax.broadcasted_iota(jnp.int32, (rows, rows), 0)

    def key_block(j):
        key_pos = j * rows + key_local
        mask = (key_pos <= query_pos) & (key_pos < length)
        for g in range(kv_heads):
            key_cols = slice(g * HEAD_DIM, (g + 1) * HEAD_DIM)
            value_cols = slice(kv_width + g * HEAD_DIM, kv_width + (g + 1) * HEAD_DIM)

            def one_head(i, carry):
                h = g * group + i
                cols = pl.ds(pl.multiple_of(h * HEAD_DIM, HEAD_DIM), HEAD_DIM)
                row = pl.ds(h, 1)
                keys, values = kv_ref[j, :, key_cols], kv_ref[j, :, value_cols]
                scores = jnp.where(mask, nt(keys, q_ref[:, cols]) * scale, NEG_FILL)
                before = max_ref[row, :]
                top = jnp.maximum(before, jnp.max(scores, axis=0, keepdims=True))
                shrink = jnp.exp(before - top)
                weights = jnp.exp(scores - top)
                max_ref[row, :] = top
                sum_ref[row, :] = sum_ref[row, :] * shrink + jnp.sum(weights, axis=0, keepdims=True)
                acc_ref[h] = acc_ref[h] * shrink + tn(values, weights.astype(BF16))
                return carry

            lax.fori_loop(0, group, one_head, 0, unroll=2)

    key_block(me)

    def earlier_block(j, carry):
        pltpu.make_async_remote_copy(
            src_ref=kv_ref.at[j],
            dst_ref=kv_ref.at[j],
            send_sem=send.at[j],
            recv_sem=recv.at[j],
            device_id={"seq": j},
            device_id_type=MESH_IDS,
        ).wait_recv()
        key_block(j)
        return carry

    lax.fori_loop(0, me, earlier_block, 0)
    lse_ref[...] = max_ref[...] + jnp.log(sum_ref[...])

    def finish(h, carry):
        cols = pl.ds(pl.multiple_of(h * HEAD_DIM, HEAD_DIM), HEAD_DIM)
        attended_ref[:, cols] = (acc_ref[h] / sum_ref[pl.ds(h, 1), :]).T.astype(BF16)
        return carry

    lax.fori_loop(0, heads, finish, 0)

    def sent(peer, carry):
        to_later(peer).wait_send()
        return carry

    lax.fori_loop(me + 1, count, sent, 0)


def attention(length, projected, cosines, sines, q_width, collective_id):
    count = lax.axis_size("seq")
    rows = projected.shape[0]
    kv_width = (projected.shape[1] - q_width) // 2
    heads, kv_heads = q_width // HEAD_DIM, kv_width // HEAD_DIM
    vmem = pl.BlockSpec(memory_space=pltpu.VMEM)
    return pl.pallas_call(
        functools.partial(attention_kernel, count, heads, kv_heads),
        out_shape=[
            jax.ShapeDtypeStruct((rows, q_width), BF16),
            jax.ShapeDtypeStruct((heads, rows), F32),
            jax.ShapeDtypeStruct((rows, q_width), BF16),
            jax.ShapeDtypeStruct((count, rows, 2 * kv_width), BF16),
        ],
        in_specs=[pl.BlockSpec(memory_space=pltpu.SMEM)] + [vmem] * 3,
        out_specs=[vmem] * 4,
        scratch_shapes=[
            pltpu.VMEM((heads, rows), F32),
            pltpu.VMEM((heads, rows), F32),
            pltpu.VMEM((heads, HEAD_DIM, rows), F32),
            pltpu.SemaphoreType.DMA((count,)),
            pltpu.SemaphoreType.DMA((count,)),
        ],
        compiler_params=pltpu.CompilerParams(
            collective_id=collective_id, vmem_limit_bytes=30 << 20
        ),
        cost_estimate=pl.CostEstimate(flops=0, bytes_accessed=1 << 20, transcendentals=0),
        name="attention_forward",
    )(length, projected, cosines, sines)


def attention_back_kernel(count, heads, kv_heads, *refs):
    length_ref, q_ref, kv_ref, grad_ref, lse_ref, attended_ref, cos_ref, sin_ref = refs[:8]
    out_ref, delta_ref, dq_ref, part_ref, leaving, arriving, send, recv = refs[8:]
    me = lax.axis_index("seq")
    rows, kv_width = q_ref.shape[0], kv_heads * HEAD_DIM
    group, scale = heads // kv_heads, 1.0 / math.sqrt(HEAD_DIM)
    greet([{"seq": lax.rem(me + step, count)} for step in range(1, count)])
    length = length_ref[0]
    query_pos = me * rows + lax.broadcasted_iota(jnp.int32, (rows, rows), 1)
    key_local = lax.broadcasted_iota(jnp.int32, (rows, rows), 0)
    dq_ref[...] = jnp.zeros_like(dq_ref)
    ones = jnp.ones((8, HEAD_DIM), BF16)
    for h in range(heads):
        cols = slice(h * HEAD_DIM, (h + 1) * HEAD_DIM)
        terms = grad_ref[:, cols].astype(F32) * attended_ref[:, cols].astype(F32)
        high = terms.astype(BF16)
        low = (terms - high.astype(F32)).astype(BF16)
        delta_ref[h : h + 1, :] = (nt(ones, high) + nt(ones, low))[:1]

    def key_block(j):
        key_pos = j * rows + key_local
        mask = (key_pos <= query_pos) & (key_pos < length)
        part_ref[...] = jnp.zeros_like(part_ref)
        key_rows = pl.ds(pl.multiple_of(j * rows, rows), rows)
        for g in range(kv_heads):
            key_cols = slice(g * HEAD_DIM, (g + 1) * HEAD_DIM)
            value_cols = slice(kv_width + g * HEAD_DIM, kv_width + (g + 1) * HEAD_DIM)

            def one_head(i, carry):
                h = g * group + i
                cols = pl.ds(pl.multiple_of(h * HEAD_DIM, HEAD_DIM), HEAD_DIM)
                keys, values = kv_ref[key_rows, key_cols], kv_ref[key_rows, value_cols]
                queries, grads = q_ref[:, cols], grad_ref[:, cols]
                scores = nt(keys, queries) * scale
                probs = jnp.where(mask, jnp.exp(scores - lse_ref[pl.ds(h, 1), :]), 0.0)
                prob_grad = nt(values, grads)
                score_grad = (probs * (prob_grad - delta_ref[pl.ds(h, 1), :])).astype(BF16)
                part_ref[:, key_cols] += nn(score_grad, queries)
                part_ref[:, value_cols] += nn(probs.astype(BF16), grads)
                dq_ref[:, cols] += tn(score_grad, keys)
                return carry

            lax.fori_loop(0, group, one_head, 0, unroll=3)
        part_ref[:, :kv_width] = part_ref[:, :kv_width] * scale

    def to_owner(j):
        return pltpu.make_async_remote_copy(
            src_ref=leaving.at[j],
            dst_ref=arriving.at[me],
            send_sem=send.at[j],
            recv_sem=recv.at[me],
            device_id={"seq": j},
            device_id_type=MESH_IDS,
        )

    def other_block(j, carry):
        key_block(j)
        leaving[j] = part_ref[...].astype(BF16)
        to_owner(j).start()
        return carry

    lax.fori_loop(0, me, other_block, 0)
    key_block(me)
    part_ref[...] = part_ref[...].astype(BF16).astype(F32)
    cosines, sines = cos_ref[...], -sin_ref[...]

    def one_query(h, carry):
        cols = pl.ds(pl.multiple_of(h * HEAD_DIM, HEAD_DIM), HEAD_DIM)
        out_ref[:, cols] = rotate(dq_ref[:, cols] * scale, cosines, sines).astype(BF16)
        return carry

    lax.fori_loop(0, heads, one_query, 0)

    def add_arrived(m, carry):
        pltpu.make_async_remote_copy(
            src_ref=leaving.at[m],
            dst_ref=arriving.at[m],
            send_sem=send.at[m],
            recv_sem=recv.at[m],
            device_id={"seq": m},
            device_id_type=MESH_IDS,
        ).wait_recv()
        part_ref[...] += arriving[m].astype(F32)
        return carry

    lax.fori_loop(me + 1, count, add_arrived, 0)
    first = heads * HEAD_DIM
    for g in range(kv_heads):
        cols = slice(g * HEAD_DIM, (g + 1) * HEAD_DIM)
        out_ref[:, first + g * HEAD_DIM : first + (g + 1) * HEAD_DIM] = rotate(
            part_ref[:, cols], cosines, sines
        ).astype(BF16)
    out_ref[:, first + kv_width :] = part_ref[:, kv_width:].astype(BF16)

    def sent(j, carry):
        to_owner(j).wait_send()
        return carry

    lax.fori_loop(0, me, sent, 0)


def attention_back(length, queries, kv_all, grads, lse, attended, cosines, sines, collective_id):
    count = lax.axis_size("seq")
    rows, q_width = queries.shape
    kv_width = kv_all.shape[1] // 2
    heads, kv_heads = q_width // HEAD_DIM, kv_width // HEAD_DIM
    vmem = pl.BlockSpec(memory_space=pltpu.VMEM)
    return pl.pallas_call(
        functools.partial(attention_back_kernel, count, heads, kv_heads),
        out_shape=jax.ShapeDtypeStruct((rows, q_width + 2 * kv_width), BF16),
        in_specs=[pl.BlockSpec(memory_space=pltpu.SMEM)] + [vmem] * 7,
        out_specs=vmem,
        scratch_shapes=[
            pltpu.VMEM((heads, rows), F32),
            pltpu.VMEM((rows, q_width), F32),
            pltpu.VMEM((rows, 2 * kv_width), F32),
            pltpu.VMEM((count, rows, 2 * kv_width), BF16),
            pltpu.VMEM((count, rows, 2 * kv_width), BF16),
            pltpu.SemaphoreType.DMA((count,)),
            pltpu.SemaphoreType.DMA((count,)),
        ],
        compiler_params=pltpu.CompilerParams(
            collective_id=collective_id, vmem_limit_bytes=30 << 20
        ),
        cost_estimate=pl.CostEstimate(
            flops=10 * count * rows * rows * q_width, bytes_accessed=1 << 20, transcendentals=0
        ),
        name="attention_backward",
    )(length, queries, kv_all, grads, lse, attended, cosines, sines)


def weight_grad_kernel(n, *refs):
    lefts, rights, outs = refs[:2], refs[2 : 2 + 2 * n], refs[2 + 2 * n :]
    for k, out_ref in enumerate(outs):
        early, late = rights[2 * k : 2 * k + 2]
        total = tn(lefts[0][...], early[...]) + tn(lefts[1][...], late[...])
        out_ref[...] = total.astype(BF16)


def weight_grads(lefts, rights, name):
    columns, tile = lefts[0].shape[1], 256
    flat = [part for pair in rights for part in pair]
    return pl.pallas_call(
        functools.partial(weight_grad_kernel, len(rights)),
        grid=(columns // tile,),
        out_shape=[jax.ShapeDtypeStruct((columns, r[0].shape[1]), BF16) for r in rights],
        in_specs=[pl.BlockSpec((x.shape[0], tile), lambda i: (0, i)) for x in lefts]
        + [pl.BlockSpec(r.shape, lambda i: (0, 0), pipeline_mode=pl.Buffered(1)) for r in flat],
        out_specs=[pl.BlockSpec((tile, r[0].shape[1]), lambda i: (i, 0)) for r in rights],
        compiler_params=pltpu.CompilerParams(vmem_limit_bytes=48 << 20),
        cost_estimate=pl.CostEstimate(flops=0, bytes_accessed=1 << 20, transcendentals=0),
        name=name,
    )(*lefts, *flat)


def seq_permutes(block_for):
    count, me = lax.axis_size("seq"), lax.axis_index("seq")
    pieces = [block_for(me)]
    for step in range(1, count):
        ring = [(i, (i + step) % count) for i in range(count)]
        pieces.append(lax.ppermute(block_for(lax.rem(me + step, count)), "seq", ring))
    return pieces


def in_seq_order(pieces, dtype):
    count, me = len(pieces), lax.axis_index("seq")
    whole = jnp.zeros((count,) + pieces[0].shape, dtype)
    for step, piece in enumerate(pieces):
        place = lax.rem(me + count - step, count)
        whole = lax.dynamic_update_index_in_dim(whole, piece.astype(dtype), place, 0)
    return whole


def on_device(
    hidden_in,
    lengths,
    routes,
    gates,
    priority,
    attn_gain,
    mlp_gain,
    w_query,
    key_projection,
    value_projection,
    w_out,
    w_gate,
    w_up,
    w_down,
    cotangent,
):
    rows = hidden_in.shape[1]
    width = hidden_in.shape[2]
    dp_count = lax.axis_size("dp")
    seq_count = lax.axis_size("seq")
    devices = dp_count * seq_count
    own_experts = w_gate.shape[0]
    sharers = seq_count // own_experts
    hidden_units = w_gate.shape[2]
    my_seq = lax.axis_index("seq")
    extent = rows * seq_count
    query_pos = my_seq * rows + jnp.arange(rows, dtype=jnp.int32)
    length = lengths[0]
    is_valid = query_pos < length
    q_width = w_query.shape[1]
    kv_width = key_projection.shape[1]
    cosine_lookup, sine_lookup = rope_angles(query_pos, HEAD_DIM)

    gain_block = jnp.concatenate(
        [attn_gain[:, None], mlp_gain[:, None], jnp.zeros((attn_gain.shape[0], LANES - 2), BF16)],
        axis=1,
    )
    packed = jnp.concatenate([w_query, key_projection, value_projection], axis=1)
    staged = seq_count == 4 and w_query.shape[0] % 16 == 0

    def expert_pieces(weights):
        def block_for(peer):
            return lax.dynamic_index_in_dim(weights, peer // sharers, 0, keepdims=False)

        return seq_permutes(block_for)

    gate_parts = expert_pieces(w_gate)
    if staged:
        packed_full, gains_full, out_full = staged_gather(
            [packed, gain_block, w_out], [], None, 2, "gather_attention_weights"
        )
    else:
        packed_full = lax.all_gather(packed, BOTH, axis=0, tiled=True)
        gains_full = lax.all_gather(gain_block, BOTH, axis=0, tiled=True)
        out_full = lax.all_gather(w_out, BOTH, axis=0, tiled=True)

    pair_routes, place, kept = claim_places(routes[0], priority[0, 0], is_valid)
    holder = (pair_routes // own_experts) * seq_count + (pair_routes % own_experts) * sharers
    holder = holder + my_seq * sharers // seq_count
    slots = devices * CAP
    target = jnp.where(kept, holder * CAP + place, slots).reshape(rows, TOP)
    slot_ids = jnp.arange(slots, dtype=jnp.int32)
    hits = target[:, :, None] == slot_ids[None, None, :]
    gate_rows = gates[0]
    token_hot = jnp.any(hits, axis=1).astype(BF16)

    def hot_of(first, size):
        mine = kept & (place >= first) & (place < first + size)
        spot = jnp.where(mine, holder * size + place - first, slots).reshape(rows, TOP)
        ids = jnp.arange(devices * size, dtype=jnp.int32)
        return jnp.any(spot[:, :, None] == ids[None, None, :], axis=1).astype(BF16)

    early_hot, late_hot = hot_of(0, EARLY), hot_of(EARLY, CAP - EARLY)
    slot_gate = jnp.sum(jnp.where(hits, gate_rows[:, :, None], 0.0), axis=(0, 1))

    live_cotangent = jnp.where(is_valid[:, None], cotangent[0], jnp.zeros((), BF16))
    out_grad = live_cotangent.astype(F32)
    grad_send = (tn(token_hot, live_cotangent) * slot_gate[:, None]).astype(BF16)
    packed_full, gains_full, out_full, gate_parts, grad_send = lax.optimization_barrier(
        (packed_full, gains_full, out_full, gate_parts, grad_send)
    )
    gain_one, gain_two = gains_full[:, 0].astype(F32), gains_full[:, 1].astype(F32)
    grad_rows = swap(grad_send.reshape(devices, CAP, width), ("dp", "seq"))

    inputs = hidden_in[0].astype(F32)
    scale_one = lax.rsqrt(jnp.mean(inputs * inputs, axis=-1, keepdims=True) + EPSILON)
    normed = (inputs * scale_one * gain_one).astype(BF16)
    projected = nn(normed, packed_full)
    cosines, sines = cosine_lookup[:, 0], sine_lookup[:, 0]
    cosines = jnp.concatenate([cosines, cosines], axis=1)
    sines = jnp.concatenate([-sines, sines], axis=1)
    attended, log_total, query_flat, kv_all = attention(
        lengths, projected, cosines, sines, q_width, 1
    )
    kv_all = kv_all.reshape(extent, 2 * kv_width)
    attended, w_up = lax.optimization_barrier((attended, w_up))
    up_parts = expert_pieces(w_up)
    middle = inputs + nn(attended, out_full)
    scale_two = lax.rsqrt(jnp.mean(middle * middle, axis=-1, keepdims=True) + EPSILON)
    moe_input = (middle * scale_two * gain_two).astype(BF16)

    def to_experts(hot):
        return tn(hot, moe_input).astype(BF16).reshape(devices, -1, width)

    early_send, late_send = to_experts(early_hot), to_experts(late_hot)
    early_send, late_send, grad_rows, up_parts, w_down = lax.optimization_barrier(
        (early_send, late_send, grad_rows, up_parts, w_down)
    )
    early_grads, late_grads, w_down = lax.optimization_barrier(
        (grad_rows[:, :EARLY], grad_rows[:, EARLY:], w_down)
    )
    down_parts = expert_pieces(w_down)
    early_rows = swap(early_send, ("dp", "seq"))
    early_rows, late_send = lax.optimization_barrier((early_rows, late_send))
    late_rows = swap(late_send, ("dp", "seq"))
    gate_full = in_seq_order(gate_parts, BF16).reshape(width, hidden_units)
    up_full = in_seq_order(up_parts, BF16).reshape(width, hidden_units)
    down_full = in_seq_order(down_parts, BF16).reshape(hidden_units, width)
    early_rows, gate_full, up_full, down_full, early_grads, late_grads = (
        lax.optimization_barrier(
            (early_rows, gate_full, up_full, down_full, early_grads, late_grads)
        )
    )

    def run_expert(slot_rows, grads):
        blocks = slot_rows.shape[:2]
        slot_rows, grads = slot_rows.reshape(-1, width), grads.reshape(-1, width)
        gate_pre = nn(slot_rows, gate_full)
        up_pre = nn(slot_rows, up_full)
        gate_sigmoid = jax.nn.sigmoid(gate_pre)
        gate_act = gate_pre * gate_sigmoid
        gate_slope = gate_sigmoid * (1.0 + gate_pre * (1.0 - gate_sigmoid))
        hidden = (gate_act * up_pre).astype(BF16)
        hidden_grad = nt(grads, down_full)
        gate_pre_grad = (hidden_grad * up_pre * gate_slope).astype(BF16)
        up_pre_grad = (hidden_grad * gate_act).astype(BF16)
        return [x.reshape(blocks + (-1,)) for x in (hidden, gate_pre_grad, up_pre_grad)]

    def row_grads(gate_pre_grad, up_pre_grad):
        blocks = gate_pre_grad.shape[:2]
        gate_pre_grad = gate_pre_grad.reshape(-1, hidden_units)
        up_pre_grad = up_pre_grad.reshape(-1, hidden_units)
        row_grad = (nt(gate_pre_grad, gate_full) + nt(up_pre_grad, up_full)).astype(BF16)
        return row_grad.reshape(blocks + (width,))

    def both_parts(early, late):
        return jnp.concatenate([early, late], axis=1).reshape(slots, -1)

    def to_owners(grad):
        grad = grad.reshape(seq_count, -1, grad.shape[1])

        def block_for(peer):
            return lax.dynamic_index_in_dim(grad, peer, 0, keepdims=False)

        return seq_permutes(block_for)

    def owned_sum(pieces):
        whole = in_seq_order(pieces, F32)
        return jnp.sum(whole.reshape((own_experts, sharers) + whole.shape[1:]), axis=1)

    early_hidden, *early_pre_grads = run_expert(early_rows, early_grads)
    early_row_grad = row_grads(*early_pre_grads)
    late_rows, early_row_grad = lax.optimization_barrier((late_rows, early_row_grad))
    early_back = swap(early_row_grad, ("dp", "seq"))
    late_hidden, *late_pre_grads = run_expert(late_rows, late_grads)

    def flat(*parts):
        return [part.reshape(-1, part.shape[-1]) for part in parts]

    gate_grad, up_grad = weight_grads(
        flat(early_rows, late_rows),
        [flat(*pair) for pair in zip(early_pre_grads, late_pre_grads, strict=True)],
        "gate_up_grads",
    )
    late_pre_grads, late_hidden, gate_grad, up_grad = lax.optimization_barrier(
        (late_pre_grads, late_hidden, gate_grad, up_grad)
    )
    gate_grad_parts = to_owners(gate_grad)
    late_row_grad = row_grads(*late_pre_grads)
    early_back, late_row_grad, gate_grad_parts, up_grad, late_hidden = lax.optimization_barrier(
        (early_back, late_row_grad, gate_grad_parts, up_grad, late_hidden)
    )
    expert_hidden = both_parts(early_hidden, late_hidden)
    late_back = swap(late_row_grad, ("dp", "seq"))
    gate_owned, up_owned = owned_sum(gate_grad_parts), owned_sum(to_owners(up_grad))
    (down_grad,) = weight_grads(
        flat(early_hidden, late_hidden), [flat(early_grads, late_grads)], "down_grads"
    )
    expert_out = nn(expert_hidden, down_full).astype(BF16)
    expert_out, late_back, gate_owned, up_owned, down_grad = lax.optimization_barrier(
        (expert_out, late_back, gate_owned, up_owned, down_grad)
    )
    returned = swap(expert_out.reshape(devices, CAP, width), ("dp", "seq")).reshape(slots, width)
    early_back, late_back = early_back.reshape(-1, width), late_back.reshape(-1, width)
    moe_input_grad = nn(early_hot, early_back) + nn(late_hot, late_back)
    middle_norm_grad, gain_two_grad = norm_back(middle, scale_two, gain_two, moe_input_grad)
    middle_grad = out_grad + middle_norm_grad
    branch_grad = middle_grad.astype(BF16)
    out_terms = tn(attended, branch_grad).astype(BF16)
    attended_grad = nt(branch_grad, out_full).astype(BF16)
    projected_grad = attention_back(
        lengths,
        query_flat,
        kv_all,
        attended_grad,
        log_total,
        attended,
        cosines,
        sines,
        4,
    )
    normed_grad = nt(projected_grad, packed_full)
    input_norm_grad, gain_one_grad = norm_back(inputs, scale_one, gain_one, normed_grad)
    input_grad = middle_grad + input_norm_grad

    lane = lax.broadcasted_iota(jnp.int32, (width, LANES), 1)
    gain_terms = jnp.where(lane == 0, gain_one_grad[:, None], gain_two_grad[:, None])
    gain_terms = jnp.where(lane < 2, gain_terms, 0.0).astype(BF16)
    query_terms = tn(normed, projected_grad).astype(BF16)
    if staged:
        out_owned, gains_owned, owned, down_owned = staged_scatter(
            [out_terms, gain_terms, query_terms],
            [down_grad.reshape(seq_count, -1, width)],
            lambda ref, peer: ref.at[peer],
            6,
            "scatter_attention_grads",
        )
        down_owned = down_owned.reshape((own_experts, sharers) + down_owned.shape[1:])
        down_owned = jnp.sum(down_owned.astype(F32), axis=1)
    else:
        terms = jnp.concatenate([out_terms, gain_terms, query_terms], axis=1)
        terms = lax.psum_scatter(terms, BOTH, scatter_dimension=0, tiled=True).astype(F32)
        out_owned, gains_owned = terms[:, :width], terms[:, width : width + LANES]
        owned = terms[:, width + LANES :]
        down_owned = owned_sum(to_owners(down_grad))
    returned, owned = lax.optimization_barrier((returned, owned))
    expert_grads = [gate_owned, up_owned, down_owned]

    gate_hot = jnp.sum(jnp.where(hits, gate_rows[:, :, None], 0.0), axis=1).astype(BF16)
    layer_out = middle + nn(gate_hot, returned)
    return (
        layer_out[None],
        input_grad[None],
        gains_owned[:, 0],
        gains_owned[:, 1],
        owned[:, :q_width],
        owned[:, q_width : q_width + kv_width],
        owned[:, q_width + kv_width : q_width + 2 * kv_width],
        out_owned,
        *expert_grads,
    )


def solution(mesh):
    part = P("dp", "seq", None)
    both = P(BOTH)
    both_rows = P(BOTH, None)
    return jax.shard_map(
        on_device,
        mesh=mesh,
        in_specs=(part, P("dp"), part, part, part, both, both)
        + (both_rows,) * 4
        + (part,) * 4,
        out_specs=(part, part, both, both) + (both_rows,) * 4 + (part,) * 3,
        check_vma=False,
    )
```

```python
import functools
import math

import jax
import jax.numpy as jnp
from jax import lax
from jax.experimental import pallas as pl
from jax.experimental.pallas import tpu as pltpu
from jax.sharding import PartitionSpec as P

HEAD_DIM = 128
EXPERTS = 32
TOP = 4
CAP = 40
EARLY = 24

EPSILON = 1e-06
ROPE_BASE = 10000.0
NEG_FILL = -1e30
LANES = 128
BOTH = ("seq", "dp")
BF16 = jnp.bfloat16
F32 = jnp.float32


def rope_angles(positions, head_size):
    half_dim = head_size // 2
    frequency = ROPE_BASE ** (-(2.0 * jnp.arange(half_dim, dtype=F32)) / head_size)
    angles = positions.astype(F32)[:, None] * frequency[None, :]
    return (jnp.cos(angles)[:, None, :], jnp.sin(angles)[:, None, :])


def dot(left, right, contract):
    return lax.dot_general(left, right, (contract, ((), ())), preferred_element_type=F32)


def nn(left, right):
    return dot(left, right, ((1,), (0,)))


def nt(left, right):
    return dot(left, right, ((1,), (1,)))


def tn(left, right):
    return dot(left, right, ((0,), (0,)))


def claim_places(routes, priority, is_valid):
    pair_routes = routes.reshape(-1)
    live = jnp.repeat(is_valid, TOP)
    key = jnp.where(live, pair_routes, -1)
    earlier = (key[None, :] == pair_routes[:, None]) & (priority[None, :] < priority[:, None])
    place = jnp.sum(earlier.astype(F32), axis=1).astype(jnp.int32)
    return pair_routes, place, live & (place < CAP)


def norm_back(values, scale_rows, gain_vec, incoming):
    weighted = incoming * gain_vec
    inner_mean = jnp.mean(weighted * values, axis=-1, keepdims=True)
    values_grad = scale_rows * weighted - values * scale_rows * scale_rows * scale_rows * inner_mean
    return (values_grad, jnp.sum(incoming * values * scale_rows, axis=0))


def swap(blocks, axes):
    return lax.all_to_all(blocks, axes, split_axis=0, concat_axis=0, tiled=True)


MESH_IDS = pl.DeviceIdType.MESH


def torus_place():
    seq, dp = lax.axis_index("seq"), lax.axis_index("dp")
    return seq // 2, seq % 2, dp // 2, dp % 2


def torus_id(a, b, z, c):
    return {"seq": 2 * a + b, "dp": 2 * z + c}


def torus_peers(line):
    a, b, z, c = torus_place()
    peers = [torus_id(a, b, z, 1 - c), torus_id(a, 1 - b, z, c), torus_id(1 - a, b, z, c)]
    peers.append(torus_id(1 - a, 1 - b, z, c))
    return peers + [torus_id(a, b, lax.rem(z + k, line), c) for k in range(1, line)]


def greet(peers):
    barrier = pltpu.get_barrier_semaphore()
    for peer in peers:
        pl.semaphore_signal(barrier, inc=1, device_id=peer, device_id_type=MESH_IDS)
    pl.semaphore_wait(barrier, len(peers))


def column_chunks(widths, parts):
    chunks = []
    for part in range(parts):
        for k, whole in enumerate(widths):
            tiles = whole // LANES
            first, end = tiles * part // parts, tiles * (part + 1) // parts
            if end > first:
                chunks.append((k, first * LANES, (end - first) * LANES))
    return chunks


def remote(src, dst, sems, i, j, device_id):
    send, recv = sems
    return pltpu.make_async_remote_copy(
        src_ref=src,
        dst_ref=dst,
        send_sem=send.at[i, j],
        recv_sem=recv.at[i, j],
        device_id=device_id,
        device_id_type=MESH_IDS,
    )


def start_exchange(count, sources, targets, block_of, sems):
    send_sems, recv_sems, local_sems = sems
    me = lax.axis_index("seq")
    copies = []
    for i, source in enumerate(sources):
        for step in range(1, count):
            peer = lax.rem(me + step, count)
            copies.append(
                pltpu.make_async_remote_copy(
                    src_ref=block_of(source, peer),
                    dst_ref=targets[i].at[me],
                    send_sem=send_sems.at[i, step - 1],
                    recv_sem=recv_sems.at[i, step - 1],
                    device_id={"seq": peer},
                    device_id_type=MESH_IDS,
                )
            )
        copies.append(
            pltpu.make_async_copy(block_of(source, me), targets[i].at[me], local_sems.at[i])
        )
    for copy in copies:
        copy.start()
    return copies


def exchange_sems(n, count):
    return [
        pltpu.SemaphoreType.DMA((n, count - 1)),
        pltpu.SemaphoreType.DMA((n, count - 1)),
        pltpu.SemaphoreType.DMA((n,)),
    ]


def in_steps(count, stages, after=None):
    for step in range((count + 1) // 2 + len(stages) - 1):
        if after is not None and step == (count + 1) // 2 + 1:
            after()
        for behind, stage in enumerate(stages):
            for i in (2 * (step - behind), 2 * (step - behind) + 1):
                if 0 <= i < count:
                    stage(i)


def gather_kernel(line, chunks, n, extras, block_of, *refs):
    sources, more_sources = refs[:n], refs[n : n + extras]
    refs = refs[n + extras :]
    targets, more_targets = refs[:n], refs[n : n + extras]
    send, recv, local, *more_sems = refs[n + extras :]
    sems = (send, recv)
    a, b, z, c = torus_place()
    greet(torus_peers(line))
    more = start_exchange(4, more_sources, more_targets, block_of, more_sems) if extras else []
    sent = []

    def start(copy):
        copy.start()
        sent.append(copy)
        return copy

    along_line, first_hop, second_hop, third_hop = {}, {}, {}, {}

    def send_line(i):
        k, first, size = chunks[i]
        cols = pl.ds(first, size)
        own = targets[k].at[a, b, z, c, :, cols]
        keep = pltpu.make_async_copy(sources[k].at[:, cols], own, local.at[i])
        keep.start()
        along_line[i] = [
            start(
                remote(
                    sources[k].at[:, cols],
                    own,
                    sems,
                    i,
                    2 + step,
                    torus_id(a, b, lax.rem(z + step, line), c),
                )
            )
            for step in range(1, line)
        ]
        along_line[i].append(keep)

    def send_first(i):
        k, first, size = chunks[i]
        *copies, keep = along_line[i]
        keep.wait()
        for copy in copies:
            copy.wait_recv()
        block = targets[k].at[a, b, :, c, :, pl.ds(first, size)]
        peer = torus_id(a, 1 - b, z, c) if i % 2 == 0 else torus_id(1 - a, b, z, c)
        first_hop[i] = start(remote(block, block, sems, i, 1, peer))

    def send_second(i):
        k, first, size = chunks[i]
        first_hop[i].wait_recv()
        cols = pl.ds(first, size)
        if i % 2 == 0:
            block, peer = targets[k].at[a, :, :, c, :, cols], torus_id(1 - a, b, z, c)
        else:
            block, peer = targets[k].at[:, b, :, c, :, cols], torus_id(a, 1 - b, z, c)
        second_hop[i] = start(remote(block, block, sems, i, 2, peer))

    def send_third(i):
        k, first, size = chunks[i]
        second_hop[i].wait_recv()
        block = targets[k].at[:, :, :, c, :, pl.ds(first, size)]
        third_hop[i] = start(remote(block, block, sems, i, 0, torus_id(a, b, z, 1 - c)))

    in_steps(len(chunks), [send_line, send_first, send_second, send_third])
    for copy in third_hop.values():
        copy.wait_recv()
    for copy in sent:
        copy.wait_send()
    for copy in more:
        copy.wait()


def staged_gather(arrays, extras, block_of, collective_id, name, parts=6):
    seq_count, line = lax.axis_size("seq"), lax.axis_size("dp") // 2
    rows, n = arrays[0].shape[0], len(arrays)
    chunks = column_chunks([x.shape[1] for x in arrays], parts)
    m = len(chunks)
    shape = (seq_count // 2, 2, line, 2, rows)
    size = sum(x.shape[1] for x in arrays) * rows * 64
    count = n + len(extras)
    outs = pl.pallas_call(
        functools.partial(gather_kernel, line, chunks, n, len(extras), block_of),
        out_shape=[jax.ShapeDtypeStruct(shape + (x.shape[1],), BF16) for x in arrays]
        + [jax.ShapeDtypeStruct((seq_count,) + x.shape[1:], BF16) for x in extras],
        in_specs=[pl.BlockSpec(memory_space=pl.ANY)] * count,
        out_specs=[pl.BlockSpec(memory_space=pl.ANY)] * count,
        scratch_shapes=[
            pltpu.SemaphoreType.DMA((m, 2 + line)),
            pltpu.SemaphoreType.DMA((m, 2 + line)),
            pltpu.SemaphoreType.DMA((m,)),
        ]
        + (exchange_sems(len(extras), seq_count) if extras else []),
        compiler_params=pltpu.CompilerParams(
            collective_id=collective_id, vmem_limit_bytes=56 << 20
        ),
        cost_estimate=pl.CostEstimate(flops=0, bytes_accessed=size, transcendentals=0),
        name=name,
    )(*arrays, *extras)
    return [o.reshape(-1, o.shape[-1]) for o in outs]


def scatter_kernel(line, chunks, n, extras, block_of, *refs):
    m = len(chunks)
    lefts, rights, more_sources = refs[:n], refs[n : 2 * n], refs[2 * n : 2 * n + extras]
    refs = refs[2 * n + extras :]
    targets, more_targets = refs[:n], refs[n : n + extras]
    scratch = refs[n + extras :]
    terms, owns, ins1, accs2, ins2, accs3, ins3, ins4 = (
        scratch[m * s : m * (s + 1)] for s in range(8)
    )
    send, recv, *more_sems = scratch[8 * m :]
    sems = (send, recv)
    a, b, z, c = torus_place()
    greet(torus_peers(line))
    sent = []

    def start(copy):
        copy.start()
        sent.append(copy)
        return copy

    def add_lines(target, left, right):
        def one(j, carry):
            target[j] = (left[j].astype(F32) + right[j].astype(F32)).astype(BF16)
            return carry

        lax.fori_loop(0, line, one, 0)

    between_cores, first_hop, second_hop, along_line = {}, {}, {}, {}

    def send_core(i):
        k, first, size = chunks[i]
        right = rights[k][:, first : first + size]
        rows = terms[i].shape[4]
        for p in range(2):
            for q in range(2):
                start_row = (2 * p + q) * 2 * line * rows
                left = lefts[k][:, start_row : start_row + 2 * line * rows]
                product = tn(left, right).astype(BF16)
                for block in range(2 * line):
                    terms[i][p, q, block // 2, block % 2] = product[block * rows : (block + 1) * rows]
        swap_core = remote(
            terms[i].at[:, :, :, 1 - c], ins1[i], sems, i, 0, torus_id(a, b, z, 1 - c)
        )
        between_cores[i] = start(swap_core)

    def send_first(i):
        between_cores[i].wait_recv()
        for p in range(2):
            for q in range(2):
                add_lines(owns[i].at[p, q], terms[i].at[p, q, :, c], ins1[i].at[p, q])
        if i % 2 == 0:
            block, peer = owns[i].at[:, 1 - b], torus_id(a, 1 - b, z, c)
        else:
            block, peer = owns[i].at[1 - a], torus_id(1 - a, b, z, c)
        first_hop[i] = start(remote(block, ins2[i], sems, i, 1, peer))

    def send_second(i):
        first_hop[i].wait_recv()
        for p in range(2):
            mine = owns[i].at[p, b] if i % 2 == 0 else owns[i].at[a, p]
            add_lines(accs2[i].at[p], mine, ins2[i].at[p])
        if i % 2 == 0:
            block, peer = accs2[i].at[1 - a], torus_id(1 - a, b, z, c)
        else:
            block, peer = accs2[i].at[1 - b], torus_id(a, 1 - b, z, c)
        second_hop[i] = start(remote(block, ins3[i], sems, i, 2, peer))

    def send_line(i):
        second_hop[i].wait_recv()
        add_lines(accs3[i], accs2[i].at[a if i % 2 == 0 else b], ins3[i])
        copies = []
        for step in range(1, line):
            to = lax.rem(z + step, line)
            peer = torus_id(a, b, to, c)
            copies.append(start(remote(accs3[i].at[to], ins4[i].at[z], sems, i, 2 + step, peer)))
        along_line[i] = copies

    def finish(i):
        k, first, size = chunks[i]
        total = accs3[i][z].astype(F32)
        for step in range(1, line):
            along_line[i][step - 1].wait_recv()
            total = total + ins4[i][lax.rem(z + line - step, line)].astype(F32)
        targets[k][:, first : first + size] = total

    more = []

    def send_more():
        if extras:
            more.extend(start_exchange(4, more_sources, more_targets, block_of, more_sems))

    in_steps(m, [send_core, send_first, send_second, send_line, finish], send_more)
    for copy in sent:
        copy.wait_send()
    for copy in more:
        copy.wait()


def staged_scatter(products, extras, block_of, collective_id, name, parts=6):
    seq_count, line = lax.axis_size("seq"), lax.axis_size("dp") // 2
    lefts, rights = zip(*products, strict=True)
    rows, n = lefts[0].shape[1] // (2 * line * seq_count), len(products)
    widths = [x.shape[1] for x in rights]
    chunks = column_chunks(widths, parts)
    m = len(chunks)
    leads = [(2, 2, line, 2), (2, 2, line), (2, 2, line), (2, line), (2, line)] + [(line,)] * 3
    size = sum(widths) * rows * 64
    anywhere, vmem = pl.BlockSpec(memory_space=pl.ANY), pl.BlockSpec(memory_space=pltpu.VMEM)
    return pl.pallas_call(
        functools.partial(scatter_kernel, line, chunks, n, len(extras), block_of),
        out_shape=[jax.ShapeDtypeStruct((rows, w), F32) for w in widths]
        + [jax.ShapeDtypeStruct((seq_count,) + x.shape[1:], BF16) for x in extras],
        in_specs=[vmem] * (2 * n) + [anywhere] * len(extras),
        out_specs=[vmem] * n + [anywhere] * len(extras),
        scratch_shapes=[
            pltpu.VMEM(lead + (rows, width), BF16) for lead in leads for _, _, width in chunks
        ]
        + [
            pltpu.SemaphoreType.DMA((m, 2 + line)),
            pltpu.SemaphoreType.DMA((m, 2 + line)),
        ]
        + (exchange_sems(len(extras), seq_count) if extras else []),
        compiler_params=pltpu.CompilerParams(
            collective_id=collective_id, vmem_limit_bytes=56 << 20
        ),
        cost_estimate=pl.CostEstimate(flops=0, bytes_accessed=size, transcendentals=0),
        name=name,
    )(*lefts, *rights, *extras)


def rotate(values, cosines, sines):
    return values * cosines + pltpu.roll(values, HEAD_DIM // 2, 1) * sines


def attention_kernel(count, heads, kv_heads, *refs):
    length_ref, projected_ref, cos_ref, sin_ref = refs[:4]
    attended_ref, lse_ref, q_ref, kv_ref = refs[4:8]
    max_ref, sum_ref, acc_ref, send, recv = refs[8:]
    me = lax.axis_index("seq")
    rows, kv_width = q_ref.shape[0], kv_heads * HEAD_DIM
    q_width, group, scale = heads * HEAD_DIM, heads // kv_heads, 1.0 / math.sqrt(HEAD_DIM)
    greet([{"seq": lax.rem(me + step, count)} for step in range(1, count)])
    cosines, sines = cos_ref[...], sin_ref[...]
    for g in range(kv_heads):
        cols = slice(g * HEAD_DIM, (g + 1) * HEAD_DIM)
        keys = projected_ref[:, q_width + g * HEAD_DIM : q_width + (g + 1) * HEAD_DIM]
        kv_ref[me, :, cols] = rotate(keys, cosines, sines).astype(BF16)
    kv_ref[me, :, kv_width:] = projected_ref[:, q_width + kv_width :].astype(BF16)

    def to_later(peer):
        return pltpu.make_async_remote_copy(
            src_ref=kv_ref.at[me],
            dst_ref=kv_ref.at[me],
            send_sem=send.at[peer],
            recv_sem=recv.at[me],
            device_id={"seq": peer},
            device_id_type=MESH_IDS,
        )

    def start(peer, carry):
        to_later(peer).start()
        return carry

    lax.fori_loop(me + 1, count, start, 0)

    def one_query(h, carry):
        cols = pl.ds(pl.multiple_of(h * HEAD_DIM, HEAD_DIM), HEAD_DIM)
        q_ref[:, cols] = rotate(projected_ref[:, cols], cosines, sines).astype(BF16)
        return carry

    lax.fori_loop(0, heads, one_query, 0)
    max_ref[...] = jnp.full_like(max_ref, NEG_FILL)
    sum_ref[...] = jnp.zeros_like(sum_ref)
    acc_ref[...] = jnp.zeros_like(acc_ref)
    length = length_ref[0]
    query_pos = me * rows + lax.broadcasted_iota(jnp.int32, (rows, rows), 1)
    key_local = lax.broadcasted_iota(jnp.int32, (rows, rows), 0)

    def key_block(j):
        key_pos = j * rows + key_local
        mask = (key_pos <= query_pos) & (key_pos < length)
        for g in range(kv_heads):
            key_cols = slice(g * HEAD_DIM, (g + 1) * HEAD_DIM)
            value_cols = slice(kv_width + g * HEAD_DIM, kv_width + (g + 1) * HEAD_DIM)

            def one_head(i, carry):
                h = g * group + i
                cols = pl.ds(pl.multiple_of(h * HEAD_DIM, HEAD_DIM), HEAD_DIM)
                row = pl.ds(h, 1)
                keys, values = kv_ref[j, :, key_cols], kv_ref[j, :, value_cols]
                scores = jnp.where(mask, nt(keys, q_ref[:, cols]) * scale, NEG_FILL)
                before = max_ref[row, :]
                top = jnp.maximum(before, jnp.max(scores, axis=0, keepdims=True))
                shrink = jnp.exp(before - top)
                weights = jnp.exp(scores - top)
                max_ref[row, :] = top
                sum_ref[row, :] = sum_ref[row, :] * shrink + jnp.sum(weights, axis=0, keepdims=True)
                acc_ref[h] = acc_ref[h] * shrink + tn(values, weights.astype(BF16))
                return carry

            lax.fori_loop(0, group, one_head, 0, unroll=2)

    key_block(me)

    def earlier_block(j, carry):
        pltpu.make_async_remote_copy(
            src_ref=kv_ref.at[j],
            dst_ref=kv_ref.at[j],
            send_sem=send.at[j],
            recv_sem=recv.at[j],
            device_id={"seq": j},
            device_id_type=MESH_IDS,
        ).wait_recv()
        key_block(j)
        return carry

    lax.fori_loop(0, me, earlier_block, 0)
    lse_ref[...] = max_ref[...] + jnp.log(sum_ref[...])

    def finish(h, carry):
        cols = pl.ds(pl.multiple_of(h * HEAD_DIM, HEAD_DIM), HEAD_DIM)
        attended_ref[:, cols] = (acc_ref[h] / sum_ref[pl.ds(h, 1), :]).T.astype(BF16)
        return carry

    lax.fori_loop(0, heads, finish, 0)

    def sent(peer, carry):
        to_later(peer).wait_send()
        return carry

    lax.fori_loop(me + 1, count, sent, 0)


def attention(length, projected, cosines, sines, q_width, collective_id):
    count = lax.axis_size("seq")
    rows = projected.shape[0]
    kv_width = (projected.shape[1] - q_width) // 2
    heads, kv_heads = q_width // HEAD_DIM, kv_width // HEAD_DIM
    vmem = pl.BlockSpec(memory_space=pltpu.VMEM)
    return pl.pallas_call(
        functools.partial(attention_kernel, count, heads, kv_heads),
        out_shape=[
            jax.ShapeDtypeStruct((rows, q_width), BF16),
            jax.ShapeDtypeStruct((heads, rows), F32),
            jax.ShapeDtypeStruct((rows, q_width), BF16),
            jax.ShapeDtypeStruct((count, rows, 2 * kv_width), BF16),
        ],
        in_specs=[pl.BlockSpec(memory_space=pltpu.SMEM)] + [vmem] * 3,
        out_specs=[vmem] * 4,
        scratch_shapes=[
            pltpu.VMEM((heads, rows), F32),
            pltpu.VMEM((heads, rows), F32),
            pltpu.VMEM((heads, HEAD_DIM, rows), F32),
            pltpu.SemaphoreType.DMA((count,)),
            pltpu.SemaphoreType.DMA((count,)),
        ],
        compiler_params=pltpu.CompilerParams(
            collective_id=collective_id, vmem_limit_bytes=30 << 20
        ),
        cost_estimate=pl.CostEstimate(flops=0, bytes_accessed=1 << 20, transcendentals=0),
        name="attention_forward",
    )(length, projected, cosines, sines)


def attention_back_kernel(count, heads, kv_heads, *refs):
    length_ref, q_ref, kv_ref, grad_ref, lse_ref, attended_ref, cos_ref, sin_ref = refs[:8]
    out_ref, delta_ref, dq_ref, part_ref, leaving, arriving, send, recv = refs[8:]
    me = lax.axis_index("seq")
    rows, kv_width = q_ref.shape[0], kv_heads * HEAD_DIM
    group, scale = heads // kv_heads, 1.0 / math.sqrt(HEAD_DIM)
    greet([{"seq": lax.rem(me + step, count)} for step in range(1, count)])
    length = length_ref[0]
    query_pos = me * rows + lax.broadcasted_iota(jnp.int32, (rows, rows), 1)
    key_local = lax.broadcasted_iota(jnp.int32, (rows, rows), 0)
    dq_ref[...] = jnp.zeros_like(dq_ref)
    ones = jnp.ones((8, HEAD_DIM), BF16)
    for h in range(heads):
        cols = slice(h * HEAD_DIM, (h + 1) * HEAD_DIM)
        terms = grad_ref[:, cols].astype(F32) * attended_ref[:, cols].astype(F32)
        high = terms.astype(BF16)
        low = (terms - high.astype(F32)).astype(BF16)
        delta_ref[h : h + 1, :] = (nt(ones, high) + nt(ones, low))[:1]

    def key_block(j):
        key_pos = j * rows + key_local
        mask = (key_pos <= query_pos) & (key_pos < length)
        part_ref[...] = jnp.zeros_like(part_ref)
        key_rows = pl.ds(pl.multiple_of(j * rows, rows), rows)
        for g in range(kv_heads):
            key_cols = slice(g * HEAD_DIM, (g + 1) * HEAD_DIM)
            value_cols = slice(kv_width + g * HEAD_DIM, kv_width + (g + 1) * HEAD_DIM)

            def one_head(i, carry):
                h = g * group + i
                cols = pl.ds(pl.multiple_of(h * HEAD_DIM, HEAD_DIM), HEAD_DIM)
                keys, values = kv_ref[key_rows, key_cols], kv_ref[key_rows, value_cols]
                queries, grads = q_ref[:, cols], grad_ref[:, cols]
                scores = nt(keys, queries) * scale
                probs = jnp.where(mask, jnp.exp(scores - lse_ref[pl.ds(h, 1), :]), 0.0)
                prob_grad = nt(values, grads)
                score_grad = (probs * (prob_grad - delta_ref[pl.ds(h, 1), :])).astype(BF16)
                part_ref[:, key_cols] += nn(score_grad, queries)
                part_ref[:, value_cols] += nn(probs.astype(BF16), grads)
                dq_ref[:, cols] += tn(score_grad, keys)
                return carry

            lax.fori_loop(0, group, one_head, 0, unroll=3)
        part_ref[:, :kv_width] = part_ref[:, :kv_width] * scale

    def to_owner(j):
        return pltpu.make_async_remote_copy(
            src_ref=leaving.at[j],
            dst_ref=arriving.at[me],
            send_sem=send.at[j],
            recv_sem=recv.at[me],
            device_id={"seq": j},
            device_id_type=MESH_IDS,
        )

    def other_block(j, carry):
        key_block(j)
        leaving[j] = part_ref[...].astype(BF16)
        to_owner(j).start()
        return carry

    lax.fori_loop(0, me, other_block, 0)
    key_block(me)
    part_ref[...] = part_ref[...].astype(BF16).astype(F32)
    cosines, sines = cos_ref[...], -sin_ref[...]

    def one_query(h, carry):
        cols = pl.ds(pl.multiple_of(h * HEAD_DIM, HEAD_DIM), HEAD_DIM)
        out_ref[:, cols] = rotate(dq_ref[:, cols] * scale, cosines, sines).astype(BF16)
        return carry

    lax.fori_loop(0, heads, one_query, 0)

    def add_arrived(m, carry):
        pltpu.make_async_remote_copy(
            src_ref=leaving.at[m],
            dst_ref=arriving.at[m],
            send_sem=send.at[m],
            recv_sem=recv.at[m],
            device_id={"seq": m},
            device_id_type=MESH_IDS,
        ).wait_recv()
        part_ref[...] += arriving[m].astype(F32)
        return carry

    lax.fori_loop(me + 1, count, add_arrived, 0)
    first = heads * HEAD_DIM
    for g in range(kv_heads):
        cols = slice(g * HEAD_DIM, (g + 1) * HEAD_DIM)
        out_ref[:, first + g * HEAD_DIM : first + (g + 1) * HEAD_DIM] = rotate(
            part_ref[:, cols], cosines, sines
        ).astype(BF16)
    out_ref[:, first + kv_width :] = part_ref[:, kv_width:].astype(BF16)

    def sent(j, carry):
        to_owner(j).wait_send()
        return carry

    lax.fori_loop(0, me, sent, 0)


def attention_back(length, queries, kv_all, grads, lse, attended, cosines, sines, collective_id):
    count = lax.axis_size("seq")
    rows, q_width = queries.shape
    kv_width = kv_all.shape[1] // 2
    heads, kv_heads = q_width // HEAD_DIM, kv_width // HEAD_DIM
    vmem = pl.BlockSpec(memory_space=pltpu.VMEM)
    return pl.pallas_call(
        functools.partial(attention_back_kernel, count, heads, kv_heads),
        out_shape=jax.ShapeDtypeStruct((rows, q_width + 2 * kv_width), BF16),
        in_specs=[pl.BlockSpec(memory_space=pltpu.SMEM)] + [vmem] * 7,
        out_specs=vmem,
        scratch_shapes=[
            pltpu.VMEM((heads, rows), F32),
            pltpu.VMEM((rows, q_width), F32),
            pltpu.VMEM((rows, 2 * kv_width), F32),
            pltpu.VMEM((count, rows, 2 * kv_width), BF16),
            pltpu.VMEM((count, rows, 2 * kv_width), BF16),
            pltpu.SemaphoreType.DMA((count,)),
            pltpu.SemaphoreType.DMA((count,)),
        ],
        compiler_params=pltpu.CompilerParams(
            collective_id=collective_id, vmem_limit_bytes=30 << 20
        ),
        cost_estimate=pl.CostEstimate(
            flops=10 * count * rows * rows * q_width, bytes_accessed=1 << 20, transcendentals=0
        ),
        name="attention_backward",
    )(length, queries, kv_all, grads, lse, attended, cosines, sines)


def weight_grad_kernel(n, *refs):
    lefts, rights, outs = refs[:2], refs[2 : 2 + 2 * n], refs[2 + 2 * n :]
    for k, out_ref in enumerate(outs):
        early, late = rights[2 * k : 2 * k + 2]
        total = tn(lefts[0][...], early[...]) + tn(lefts[1][...], late[...])
        out_ref[...] = total.astype(BF16)


def weight_grads(lefts, rights, name):
    columns, tile = lefts[0].shape[1], 256
    flat = [part for pair in rights for part in pair]
    return pl.pallas_call(
        functools.partial(weight_grad_kernel, len(rights)),
        grid=(columns // tile,),
        out_shape=[jax.ShapeDtypeStruct((columns, r[0].shape[1]), BF16) for r in rights],
        in_specs=[pl.BlockSpec((x.shape[0], tile), lambda i: (0, i)) for x in lefts]
        + [pl.BlockSpec(r.shape, lambda i: (0, 0), pipeline_mode=pl.Buffered(1)) for r in flat],
        out_specs=[pl.BlockSpec((tile, r[0].shape[1]), lambda i: (i, 0)) for r in rights],
        compiler_params=pltpu.CompilerParams(vmem_limit_bytes=48 << 20),
        cost_estimate=pl.CostEstimate(flops=0, bytes_accessed=1 << 20, transcendentals=0),
        name=name,
    )(*lefts, *flat)


def seq_permutes(block_for):
    count, me = lax.axis_size("seq"), lax.axis_index("seq")
    pieces = [block_for(me)]
    for step in range(1, count):
        ring = [(i, (i + step) % count) for i in range(count)]
        pieces.append(lax.ppermute(block_for(lax.rem(me + step, count)), "seq", ring))
    return pieces


def in_seq_order(pieces, dtype):
    count, me = len(pieces), lax.axis_index("seq")
    whole = jnp.zeros((count,) + pieces[0].shape, dtype)
    for step, piece in enumerate(pieces):
        place = lax.rem(me + count - step, count)
        whole = lax.dynamic_update_index_in_dim(whole, piece.astype(dtype), place, 0)
    return whole


def on_device(
    hidden_in,
    lengths,
    routes,
    gates,
    priority,
    attn_gain,
    mlp_gain,
    w_query,
    key_projection,
    value_projection,
    w_out,
    w_gate,
    w_up,
    w_down,
    cotangent,
):
    rows = hidden_in.shape[1]
    width = hidden_in.shape[2]
    dp_count = lax.axis_size("dp")
    seq_count = lax.axis_size("seq")
    devices = dp_count * seq_count
    own_experts = w_gate.shape[0]
    sharers = seq_count // own_experts
    hidden_units = w_gate.shape[2]
    my_seq = lax.axis_index("seq")
    extent = rows * seq_count
    query_pos = my_seq * rows + jnp.arange(rows, dtype=jnp.int32)
    length = lengths[0]
    is_valid = query_pos < length
    q_width = w_query.shape[1]
    kv_width = key_projection.shape[1]
    cosine_lookup, sine_lookup = rope_angles(query_pos, HEAD_DIM)

    gain_block = jnp.concatenate(
        [attn_gain[:, None], mlp_gain[:, None], jnp.zeros((attn_gain.shape[0], LANES - 2), BF16)],
        axis=1,
    )
    packed = jnp.concatenate([w_query, key_projection, value_projection], axis=1)
    staged = seq_count == 4 and w_query.shape[0] % 16 == 0

    def expert_pieces(weights):
        def block_for(peer):
            return lax.dynamic_index_in_dim(weights, peer // sharers, 0, keepdims=False)

        return seq_permutes(block_for)

    gate_parts = expert_pieces(w_gate)
    if staged:
        packed_full, gains_full, out_full = staged_gather(
            [packed, gain_block, w_out], [], None, 2, "gather_attention_weights"
        )
    else:
        packed_full = lax.all_gather(packed, BOTH, axis=0, tiled=True)
        gains_full = lax.all_gather(gain_block, BOTH, axis=0, tiled=True)
        out_full = lax.all_gather(w_out, BOTH, axis=0, tiled=True)

    pair_routes, place, kept = claim_places(routes[0], priority[0, 0], is_valid)
    holder = (pair_routes // own_experts) * seq_count + (pair_routes % own_experts) * sharers
    holder = holder + my_seq * sharers // seq_count
    slots = devices * CAP
    target = jnp.where(kept, holder * CAP + place, slots).reshape(rows, TOP)
    slot_ids = jnp.arange(slots, dtype=jnp.int32)
    hits = target[:, :, None] == slot_ids[None, None, :]
    gate_rows = gates[0]
    token_hot = jnp.any(hits, axis=1).astype(BF16)

    def hot_of(first, size):
        mine = kept & (place >= first) & (place < first + size)
        spot = jnp.where(mine, holder * size + place - first, slots).reshape(rows, TOP)
        ids = jnp.arange(devices * size, dtype=jnp.int32)
        return jnp.any(spot[:, :, None] == ids[None, None, :], axis=1).astype(BF16)

    early_hot, late_hot = hot_of(0, EARLY), hot_of(EARLY, CAP - EARLY)
    slot_gate = jnp.sum(jnp.where(hits, gate_rows[:, :, None], 0.0), axis=(0, 1))

    live_cotangent = jnp.where(is_valid[:, None], cotangent[0], jnp.zeros((), BF16))
    out_grad = live_cotangent.astype(F32)
    grad_send = (tn(token_hot, live_cotangent) * slot_gate[:, None]).astype(BF16)
    packed_full, gains_full, out_full, gate_parts, grad_send = lax.optimization_barrier(
        (packed_full, gains_full, out_full, gate_parts, grad_send)
    )
    gain_one, gain_two = gains_full[:, 0].astype(F32), gains_full[:, 1].astype(F32)
    grad_rows = swap(grad_send.reshape(devices, CAP, width), ("dp", "seq"))

    inputs = hidden_in[0].astype(F32)
    scale_one = lax.rsqrt(jnp.mean(inputs * inputs, axis=-1, keepdims=True) + EPSILON)
    normed = (inputs * scale_one * gain_one).astype(BF16)
    projected = nn(normed, packed_full)
    cosines, sines = cosine_lookup[:, 0], sine_lookup[:, 0]
    cosines = jnp.concatenate([cosines, cosines], axis=1)
    sines = jnp.concatenate([-sines, sines], axis=1)
    attended, log_total, query_flat, kv_all = attention(
        lengths, projected, cosines, sines, q_width, 1
    )
    kv_all = kv_all.reshape(extent, 2 * kv_width)
    attended, w_up = lax.optimization_barrier((attended, w_up))
    up_parts = expert_pieces(w_up)
    middle = inputs + nn(attended, out_full)
    scale_two = lax.rsqrt(jnp.mean(middle * middle, axis=-1, keepdims=True) + EPSILON)
    moe_input = (middle * scale_two * gain_two).astype(BF16)

    def to_experts(hot):
        return tn(hot, moe_input).astype(BF16).reshape(devices, -1, width)

    early_send, late_send = to_experts(early_hot), to_experts(late_hot)
    early_send, late_send, grad_rows, up_parts, w_down = lax.optimization_barrier(
        (early_send, late_send, grad_rows, up_parts, w_down)
    )
    early_grads, late_grads, w_down = lax.optimization_barrier(
        (grad_rows[:, :EARLY], grad_rows[:, EARLY:], w_down)
    )
    down_parts = expert_pieces(w_down)
    early_rows = swap(early_send, ("dp", "seq"))
    early_rows, late_send = lax.optimization_barrier((early_rows, late_send))
    late_rows = swap(late_send, ("dp", "seq"))
    gate_full = in_seq_order(gate_parts, BF16).reshape(width, hidden_units)
    up_full = in_seq_order(up_parts, BF16).reshape(width, hidden_units)
    down_full = in_seq_order(down_parts, BF16).reshape(hidden_units, width)
    early_rows, gate_full, up_full, down_full, early_grads, late_grads = (
        lax.optimization_barrier(
            (early_rows, gate_full, up_full, down_full, early_grads, late_grads)
        )
    )

    def run_expert(slot_rows, grads):
        blocks = slot_rows.shape[:2]
        slot_rows, grads = slot_rows.reshape(-1, width), grads.reshape(-1, width)
        gate_pre = nn(slot_rows, gate_full)
        up_pre = nn(slot_rows, up_full)
        gate_sigmoid = jax.nn.sigmoid(gate_pre)
        gate_act = gate_pre * gate_sigmoid
        gate_slope = gate_sigmoid * (1.0 + gate_pre * (1.0 - gate_sigmoid))
        hidden = (gate_act * up_pre).astype(BF16)
        hidden_grad = nt(grads, down_full)
        gate_pre_grad = (hidden_grad * up_pre * gate_slope).astype(BF16)
        up_pre_grad = (hidden_grad * gate_act).astype(BF16)
        return [x.reshape(blocks + (-1,)) for x in (hidden, gate_pre_grad, up_pre_grad)]

    def row_grads(gate_pre_grad, up_pre_grad):
        blocks = gate_pre_grad.shape[:2]
        gate_pre_grad = gate_pre_grad.reshape(-1, hidden_units)
        up_pre_grad = up_pre_grad.reshape(-1, hidden_units)
        row_grad = (nt(gate_pre_grad, gate_full) + nt(up_pre_grad, up_full)).astype(BF16)
        return row_grad.reshape(blocks + (width,))

    def both_parts(early, late):
        return jnp.concatenate([early, late], axis=1).reshape(slots, -1)

    def to_owners(grad):
        grad = grad.reshape(seq_count, -1, grad.shape[1])

        def block_for(peer):
            return lax.dynamic_index_in_dim(grad, peer, 0, keepdims=False)

        return seq_permutes(block_for)

    def owned_sum(pieces):
        whole = in_seq_order(pieces, F32)
        return jnp.sum(whole.reshape((own_experts, sharers) + whole.shape[1:]), axis=1)

    early_hidden, *early_pre_grads = run_expert(early_rows, early_grads)
    early_row_grad = row_grads(*early_pre_grads)
    late_rows, early_row_grad = lax.optimization_barrier((late_rows, early_row_grad))
    early_back = swap(early_row_grad, ("dp", "seq"))
    late_hidden, *late_pre_grads = run_expert(late_rows, late_grads)

    def flat(*parts):
        return [part.reshape(-1, part.shape[-1]) for part in parts]

    gate_grad, up_grad = weight_grads(
        flat(early_rows, late_rows),
        [flat(*pair) for pair in zip(early_pre_grads, late_pre_grads, strict=True)],
        "gate_up_grads",
    )
    late_pre_grads, late_hidden, gate_grad, up_grad = lax.optimization_barrier(
        (late_pre_grads, late_hidden, gate_grad, up_grad)
    )
    gate_grad_parts = to_owners(gate_grad)
    late_row_grad = row_grads(*late_pre_grads)
    early_back, late_row_grad, gate_grad_parts, up_grad, late_hidden = lax.optimization_barrier(
        (early_back, late_row_grad, gate_grad_parts, up_grad, late_hidden)
    )
    expert_hidden = both_parts(early_hidden, late_hidden)
    late_back = swap(late_row_grad, ("dp", "seq"))
    gate_owned, up_owned = owned_sum(gate_grad_parts), owned_sum(to_owners(up_grad))
    (down_grad,) = weight_grads(
        flat(early_hidden, late_hidden), [flat(early_grads, late_grads)], "down_grads"
    )
    expert_out = nn(expert_hidden, down_full).astype(BF16)
    expert_out, late_back, gate_owned, up_owned, down_grad = lax.optimization_barrier(
        (expert_out, late_back, gate_owned, up_owned, down_grad)
    )
    returned = swap(expert_out.reshape(devices, CAP, width), ("dp", "seq")).reshape(slots, width)
    early_back, late_back = early_back.reshape(-1, width), late_back.reshape(-1, width)
    moe_input_grad = nn(early_hot, early_back) + nn(late_hot, late_back)
    middle_norm_grad, gain_two_grad = norm_back(middle, scale_two, gain_two, moe_input_grad)
    middle_grad = out_grad + middle_norm_grad
    branch_grad = middle_grad.astype(BF16)
    attended_grad = nt(branch_grad, out_full).astype(BF16)
    projected_grad = attention_back(
        lengths,
        query_flat,
        kv_all,
        attended_grad,
        log_total,
        attended,
        cosines,
        sines,
        4,
    )
    normed_grad = nt(projected_grad, packed_full)
    input_norm_grad, gain_one_grad = norm_back(inputs, scale_one, gain_one, normed_grad)
    input_grad = middle_grad + input_norm_grad

    gain_rows = jnp.pad(
        jnp.stack([gain_one_grad, gain_two_grad]).astype(BF16), ((0, 14), (0, 0))
    )
    gain_places = jnp.eye(16, LANES, dtype=BF16)
    products = [(attended, branch_grad), (gain_rows, gain_places), (normed, projected_grad)]
    if staged:
        out_owned, gains_owned, owned, down_owned = staged_scatter(
            products,
            [down_grad.reshape(seq_count, -1, width)],
            lambda ref, peer: ref.at[peer],
            6,
            "scatter_attention_grads",
        )
        down_owned = down_owned.reshape((own_experts, sharers) + down_owned.shape[1:])
        down_owned = jnp.sum(down_owned.astype(F32), axis=1)
    else:
        terms = jnp.concatenate([tn(*pair).astype(BF16) for pair in products], axis=1)
        terms = lax.psum_scatter(terms, BOTH, scatter_dimension=0, tiled=True).astype(F32)
        out_owned, gains_owned = terms[:, :width], terms[:, width : width + LANES]
        owned = terms[:, width + LANES :]
        down_owned = owned_sum(to_owners(down_grad))
    returned, owned = lax.optimization_barrier((returned, owned))
    expert_grads = [gate_owned, up_owned, down_owned]

    gate_hot = jnp.sum(jnp.where(hits, gate_rows[:, :, None], 0.0), axis=1).astype(BF16)
    layer_out = middle + nn(gate_hot, returned)
    return (
        layer_out[None],
        input_grad[None],
        gains_owned[:, 0],
        gains_owned[:, 1],
        owned[:, :q_width],
        owned[:, q_width : q_width + kv_width],
        owned[:, q_width + kv_width : q_width + 2 * kv_width],
        out_owned,
        *expert_grads,
    )


def solution(mesh):
    part = P("dp", "seq", None)
    both = P(BOTH)
    both_rows = P(BOTH, None)
    return jax.shard_map(
        on_device,
        mesh=mesh,
        in_specs=(part, P("dp"), part, part, part, both, both)
        + (both_rows,) * 4
        + (part,) * 4,
        out_specs=(part, part, both, both) + (both_rows,) * 4 + (part,) * 3,
        check_vma=False,
    )
```

```python
import functools
import math

import jax
import jax.numpy as jnp
from jax import lax
from jax.experimental import pallas as pl
from jax.experimental.pallas import tpu as pltpu
from jax.sharding import PartitionSpec as P

HEAD_DIM = 128
EXPERTS = 32
TOP = 4
CAP = 40
EARLY = 24

EPSILON = 1e-06
ROPE_BASE = 10000.0
NEG_FILL = -1e30
LANES = 128
BOTH = ("seq", "dp")
BF16 = jnp.bfloat16
F32 = jnp.float32


def rope_angles(positions, head_size):
    half_dim = head_size // 2
    frequency = ROPE_BASE ** (-(2.0 * jnp.arange(half_dim, dtype=F32)) / head_size)
    angles = positions.astype(F32)[:, None] * frequency[None, :]
    return (jnp.cos(angles)[:, None, :], jnp.sin(angles)[:, None, :])


def dot(left, right, contract):
    return lax.dot_general(left, right, (contract, ((), ())), preferred_element_type=F32)


def nn(left, right):
    return dot(left, right, ((1,), (0,)))


def nt(left, right):
    return dot(left, right, ((1,), (1,)))


def tn(left, right):
    return dot(left, right, ((0,), (0,)))


def claim_places(routes, priority, is_valid):
    pair_routes = routes.reshape(-1)
    live = jnp.repeat(is_valid, TOP)
    key = jnp.where(live, pair_routes, -1)
    earlier = (key[None, :] == pair_routes[:, None]) & (priority[None, :] < priority[:, None])
    place = jnp.sum(earlier.astype(F32), axis=1).astype(jnp.int32)
    return pair_routes, place, live & (place < CAP)


def norm_back(values, scale_rows, gain_vec, incoming):
    weighted = incoming * gain_vec
    inner_mean = jnp.mean(weighted * values, axis=-1, keepdims=True)
    values_grad = scale_rows * weighted - values * scale_rows * scale_rows * scale_rows * inner_mean
    return (values_grad, jnp.sum(incoming * values * scale_rows, axis=0))


def swap(blocks, axes):
    return lax.all_to_all(blocks, axes, split_axis=0, concat_axis=0, tiled=True)


MESH_IDS = pl.DeviceIdType.MESH


def torus_place():
    seq, dp = lax.axis_index("seq"), lax.axis_index("dp")
    return seq // 2, seq % 2, dp // 2, dp % 2


def torus_id(a, b, z, c):
    return {"seq": 2 * a + b, "dp": 2 * z + c}


def torus_peers(line):
    a, b, z, c = torus_place()
    peers = [torus_id(a, b, z, 1 - c), torus_id(a, 1 - b, z, c), torus_id(1 - a, b, z, c)]
    peers.append(torus_id(1 - a, 1 - b, z, c))
    return peers + [torus_id(a, b, lax.rem(z + k, line), c) for k in range(1, line)]


def greet(peers):
    barrier = pltpu.get_barrier_semaphore()
    for peer in peers:
        pl.semaphore_signal(barrier, inc=1, device_id=peer, device_id_type=MESH_IDS)
    pl.semaphore_wait(barrier, len(peers))


def column_chunks(widths, parts):
    chunks = []
    for part in range(parts):
        for k, whole in enumerate(widths):
            tiles = whole // LANES
            first, end = tiles * part // parts, tiles * (part + 1) // parts
            if end > first:
                chunks.append((k, first * LANES, (end - first) * LANES))
    return chunks


def remote(src, dst, sems, i, j, device_id):
    send, recv = sems
    return pltpu.make_async_remote_copy(
        src_ref=src,
        dst_ref=dst,
        send_sem=send.at[i, j],
        recv_sem=recv.at[i, j],
        device_id=device_id,
        device_id_type=MESH_IDS,
    )


def start_exchange(count, sources, targets, block_of, sems):
    send_sems, recv_sems, local_sems = sems
    me = lax.axis_index("seq")
    copies = []
    for i, source in enumerate(sources):
        for step in range(1, count):
            peer = lax.rem(me + step, count)
            copies.append(
                pltpu.make_async_remote_copy(
                    src_ref=block_of(source, peer),
                    dst_ref=targets[i].at[me],
                    send_sem=send_sems.at[i, step - 1],
                    recv_sem=recv_sems.at[i, step - 1],
                    device_id={"seq": peer},
                    device_id_type=MESH_IDS,
                )
            )
        copies.append(
            pltpu.make_async_copy(block_of(source, me), targets[i].at[me], local_sems.at[i])
        )
    for copy in copies:
        copy.start()
    return copies


def exchange_sems(n, count):
    return [
        pltpu.SemaphoreType.DMA((n, count - 1)),
        pltpu.SemaphoreType.DMA((n, count - 1)),
        pltpu.SemaphoreType.DMA((n,)),
    ]


def in_steps(count, stages, after=None):
    for step in range((count + 1) // 2 + len(stages) - 1):
        if after is not None and step == (count + 1) // 2 + 1:
            after()
        for behind, stage in enumerate(stages):
            for i in (2 * (step - behind), 2 * (step - behind) + 1):
                if 0 <= i < count:
                    stage(i)


def gather_kernel(line, chunks, n, extras, block_of, *refs):
    sources, more_sources = refs[:n], refs[n : n + extras]
    refs = refs[n + extras :]
    targets, more_targets = refs[:n], refs[n : n + extras]
    send, recv, local, *more_sems = refs[n + extras :]
    sems = (send, recv)
    a, b, z, c = torus_place()
    greet(torus_peers(line))
    more = start_exchange(4, more_sources, more_targets, block_of, more_sems) if extras else []
    sent = []

    def start(copy):
        copy.start()
        sent.append(copy)
        return copy

    along_line, first_hop, second_hop, third_hop = {}, {}, {}, {}

    def send_line(i):
        k, first, size = chunks[i]
        cols = pl.ds(first, size)
        own = targets[k].at[a, b, z, c, :, cols]
        keep = pltpu.make_async_copy(sources[k].at[:, cols], own, local.at[i])
        keep.start()
        along_line[i] = [
            start(
                remote(
                    sources[k].at[:, cols],
                    own,
                    sems,
                    i,
                    2 + step,
                    torus_id(a, b, lax.rem(z + step, line), c),
                )
            )
            for step in range(1, line)
        ]
        along_line[i].append(keep)

    def send_first(i):
        k, first, size = chunks[i]
        *copies, keep = along_line[i]
        keep.wait()
        for copy in copies:
            copy.wait_recv()
        block = targets[k].at[a, b, :, c, :, pl.ds(first, size)]
        peer = torus_id(a, 1 - b, z, c) if i % 2 == 0 else torus_id(1 - a, b, z, c)
        first_hop[i] = start(remote(block, block, sems, i, 1, peer))

    def send_second(i):
        k, first, size = chunks[i]
        first_hop[i].wait_recv()
        cols = pl.ds(first, size)
        if i % 2 == 0:
            block, peer = targets[k].at[a, :, :, c, :, cols], torus_id(1 - a, b, z, c)
        else:
            block, peer = targets[k].at[:, b, :, c, :, cols], torus_id(a, 1 - b, z, c)
        second_hop[i] = start(remote(block, block, sems, i, 2, peer))

    def send_third(i):
        k, first, size = chunks[i]
        second_hop[i].wait_recv()
        block = targets[k].at[:, :, :, c, :, pl.ds(first, size)]
        third_hop[i] = start(remote(block, block, sems, i, 0, torus_id(a, b, z, 1 - c)))

    in_steps(len(chunks), [send_line, send_first, send_second, send_third])
    for copy in third_hop.values():
        copy.wait_recv()
    for copy in sent:
        copy.wait_send()
    for copy in more:
        copy.wait()


def staged_gather(arrays, extras, block_of, collective_id, name, parts=6):
    seq_count, line = lax.axis_size("seq"), lax.axis_size("dp") // 2
    rows, n = arrays[0].shape[0], len(arrays)
    chunks = column_chunks([x.shape[1] for x in arrays], parts)
    m = len(chunks)
    shape = (seq_count // 2, 2, line, 2, rows)
    size = sum(x.shape[1] for x in arrays) * rows * 64
    count = n + len(extras)
    outs = pl.pallas_call(
        functools.partial(gather_kernel, line, chunks, n, len(extras), block_of),
        out_shape=[jax.ShapeDtypeStruct(shape + (x.shape[1],), BF16) for x in arrays]
        + [jax.ShapeDtypeStruct((seq_count,) + x.shape[1:], BF16) for x in extras],
        in_specs=[pl.BlockSpec(memory_space=pl.ANY)] * count,
        out_specs=[pl.BlockSpec(memory_space=pl.ANY)] * count,
        scratch_shapes=[
            pltpu.SemaphoreType.DMA((m, 2 + line)),
            pltpu.SemaphoreType.DMA((m, 2 + line)),
            pltpu.SemaphoreType.DMA((m,)),
        ]
        + (exchange_sems(len(extras), seq_count) if extras else []),
        compiler_params=pltpu.CompilerParams(
            collective_id=collective_id, vmem_limit_bytes=56 << 20
        ),
        cost_estimate=pl.CostEstimate(flops=0, bytes_accessed=size, transcendentals=0),
        name=name,
    )(*arrays, *extras)
    return [o.reshape(-1, o.shape[-1]) for o in outs]


def scatter_kernel(line, chunks, n, extras, block_of, *refs):
    m = len(chunks)
    sources, more_sources = refs[:n], refs[n : n + extras]
    refs = refs[n + extras :]
    targets, more_targets = refs[:n], refs[n : n + extras]
    scratch = refs[n + extras :]
    owns, ins1, accs2, ins2, accs3, ins3, ins4 = (scratch[m * s : m * (s + 1)] for s in range(7))
    send, recv, local, *more_sems = scratch[7 * m :]
    sems = (send, recv)
    a, b, z, c = torus_place()
    greet(torus_peers(line))
    sent = []

    def start(copy):
        copy.start()
        sent.append(copy)
        return copy

    def add_lines(target, left, right):
        def one(j, carry):
            target[j] = (left[j].astype(F32) + right[j].astype(F32)).astype(BF16)
            return carry

        lax.fori_loop(0, line, one, 0)

    between_cores, first_hop, second_hop, along_line = {}, {}, {}, {}

    def send_core(i):
        k, first, size = chunks[i]
        cols = pl.ds(first, size)
        keep = pltpu.make_async_copy(sources[k].at[:, :, :, c, :, cols], owns[i], local.at[i])
        keep.start()
        swap_core = remote(
            sources[k].at[:, :, :, 1 - c, :, cols], ins1[i], sems, i, 0, torus_id(a, b, z, 1 - c)
        )
        between_cores[i] = (keep, start(swap_core))

    def send_first(i):
        keep, copy = between_cores[i]
        keep.wait()
        copy.wait_recv()
        for p in range(2):
            for q in range(2):
                add_lines(owns[i].at[p, q], owns[i].at[p, q], ins1[i].at[p, q])
        if i % 2 == 0:
            block, peer = owns[i].at[:, 1 - b], torus_id(a, 1 - b, z, c)
        else:
            block, peer = owns[i].at[1 - a], torus_id(1 - a, b, z, c)
        first_hop[i] = start(remote(block, ins2[i], sems, i, 1, peer))

    def send_second(i):
        first_hop[i].wait_recv()
        for p in range(2):
            mine = owns[i].at[p, b] if i % 2 == 0 else owns[i].at[a, p]
            add_lines(accs2[i].at[p], mine, ins2[i].at[p])
        if i % 2 == 0:
            block, peer = accs2[i].at[1 - a], torus_id(1 - a, b, z, c)
        else:
            block, peer = accs2[i].at[1 - b], torus_id(a, 1 - b, z, c)
        second_hop[i] = start(remote(block, ins3[i], sems, i, 2, peer))

    def send_line(i):
        second_hop[i].wait_recv()
        add_lines(accs3[i], accs2[i].at[a if i % 2 == 0 else b], ins3[i])
        copies = []
        for step in range(1, line):
            to = lax.rem(z + step, line)
            peer = torus_id(a, b, to, c)
            copies.append(start(remote(accs3[i].at[to], ins4[i].at[z], sems, i, 2 + step, peer)))
        along_line[i] = copies

    def finish(i):
        k, first, size = chunks[i]
        total = accs3[i][z].astype(F32)
        for step in range(1, line):
            along_line[i][step - 1].wait_recv()
            total = total + ins4[i][lax.rem(z + line - step, line)].astype(F32)
        targets[k][:, first : first + size] = total

    more = []

    def send_more():
        if extras:
            more.extend(start_exchange(4, more_sources, more_targets, block_of, more_sems))

    in_steps(m, [send_core, send_first, send_second, send_line, finish], send_more)
    for copy in sent:
        copy.wait_send()
    for copy in more:
        copy.wait()


def staged_scatter(arrays, extras, block_of, collective_id, name, parts=6):
    seq_count, line = lax.axis_size("seq"), lax.axis_size("dp") // 2
    rows, n = arrays[0].shape[0] // (2 * line * seq_count), len(arrays)
    chunks = column_chunks([x.shape[1] for x in arrays], parts)
    m = len(chunks)
    leads = [(2, 2, line), (2, 2, line), (2, line), (2, line), (line,), (line,), (line,)]
    size = sum(x.shape[1] for x in arrays) * rows * 64
    anywhere = pl.BlockSpec(memory_space=pl.ANY)
    return pl.pallas_call(
        functools.partial(scatter_kernel, line, chunks, n, len(extras), block_of),
        out_shape=[jax.ShapeDtypeStruct((rows, x.shape[1]), F32) for x in arrays]
        + [jax.ShapeDtypeStruct((seq_count,) + x.shape[1:], BF16) for x in extras],
        in_specs=[anywhere] * (n + len(extras)),
        out_specs=[pl.BlockSpec(memory_space=pltpu.VMEM)] * n + [anywhere] * len(extras),
        scratch_shapes=[
            pltpu.VMEM(lead + (rows, width), BF16) for lead in leads for _, _, width in chunks
        ]
        + [
            pltpu.SemaphoreType.DMA((m, 2 + line)),
            pltpu.SemaphoreType.DMA((m, 2 + line)),
            pltpu.SemaphoreType.DMA((m,)),
        ]
        + (exchange_sems(len(extras), seq_count) if extras else []),
        compiler_params=pltpu.CompilerParams(
            collective_id=collective_id, vmem_limit_bytes=36 << 20
        ),
        cost_estimate=pl.CostEstimate(flops=0, bytes_accessed=size, transcendentals=0),
        name=name,
    )(*[x.reshape(2, 2, line, 2, rows, x.shape[1]) for x in arrays], *extras)


def rotate(values, cosines, sines):
    return values * cosines + pltpu.roll(values, HEAD_DIM // 2, 1) * sines


def attention_kernel(count, heads, kv_heads, *refs):
    length_ref, projected_ref, cos_ref, sin_ref = refs[:4]
    attended_ref, lse_ref, q_ref, kv_ref = refs[4:8]
    max_ref, sum_ref, acc_ref, send, recv = refs[8:]
    me = lax.axis_index("seq")
    rows, kv_width = q_ref.shape[0], kv_heads * HEAD_DIM
    q_width, group, scale = heads * HEAD_DIM, heads // kv_heads, 1.0 / math.sqrt(HEAD_DIM)
    greet([{"seq": lax.rem(me + step, count)} for step in range(1, count)])
    cosines, sines = cos_ref[...], sin_ref[...]
    for g in range(kv_heads):
        cols = slice(g * HEAD_DIM, (g + 1) * HEAD_DIM)
        keys = projected_ref[:, q_width + g * HEAD_DIM : q_width + (g + 1) * HEAD_DIM]
        kv_ref[me, :, cols] = rotate(keys, cosines, sines).astype(BF16)
    kv_ref[me, :, kv_width:] = projected_ref[:, q_width + kv_width :].astype(BF16)

    def to_later(peer):
        return pltpu.make_async_remote_copy(
            src_ref=kv_ref.at[me],
            dst_ref=kv_ref.at[me],
            send_sem=send.at[peer],
            recv_sem=recv.at[me],
            device_id={"seq": peer},
            device_id_type=MESH_IDS,
        )

    def start(peer, carry):
        to_later(peer).start()
        return carry

    lax.fori_loop(me + 1, count, start, 0)

    def one_query(h, carry):
        cols = pl.ds(pl.multiple_of(h * HEAD_DIM, HEAD_DIM), HEAD_DIM)
        q_ref[:, cols] = rotate(projected_ref[:, cols], cosines, sines).astype(BF16)
        return carry

    lax.fori_loop(0, heads, one_query, 0)
    max_ref[...] = jnp.full_like(max_ref, NEG_FILL)
    sum_ref[...] = jnp.zeros_like(sum_ref)
    acc_ref[...] = jnp.zeros_like(acc_ref)
    length = length_ref[0]
    query_pos = me * rows + lax.broadcasted_iota(jnp.int32, (rows, rows), 1)
    key_local = lax.broadcasted_iota(jnp.int32, (rows, rows), 0)

    def key_block(j):
        key_pos = j * rows + key_local
        mask = (key_pos <= query_pos) & (key_pos < length)
        for g in range(kv_heads):
            key_cols = slice(g * HEAD_DIM, (g + 1) * HEAD_DIM)
            value_cols = slice(kv_width + g * HEAD_DIM, kv_width + (g + 1) * HEAD_DIM)

            def one_head(i, carry):
                h = g * group + i
                cols = pl.ds(pl.multiple_of(h * HEAD_DIM, HEAD_DIM), HEAD_DIM)
                row = pl.ds(h, 1)
                keys, values = kv_ref[j, :, key_cols], kv_ref[j, :, value_cols]
                scores = jnp.where(mask, nt(keys, q_ref[:, cols]) * scale, NEG_FILL)
                before = max_ref[row, :]
                top = jnp.maximum(before, jnp.max(scores, axis=0, keepdims=True))
                shrink = jnp.exp(before - top)
                weights = jnp.exp(scores - top)
                max_ref[row, :] = top
                sum_ref[row, :] = sum_ref[row, :] * shrink + jnp.sum(weights, axis=0, keepdims=True)
                acc_ref[h] = acc_ref[h] * shrink + tn(values, weights.astype(BF16))
                return carry

            lax.fori_loop(0, group, one_head, 0, unroll=2)

    key_block(me)

    def earlier_block(j, carry):
        pltpu.make_async_remote_copy(
            src_ref=kv_ref.at[j],
            dst_ref=kv_ref.at[j],
            send_sem=send.at[j],
            recv_sem=recv.at[j],
            device_id={"seq": j},
            device_id_type=MESH_IDS,
        ).wait_recv()
        key_block(j)
        return carry

    lax.fori_loop(0, me, earlier_block, 0)
    lse_ref[...] = max_ref[...] + jnp.log(sum_ref[...])

    def finish(h, carry):
        cols = pl.ds(pl.multiple_of(h * HEAD_DIM, HEAD_DIM), HEAD_DIM)
        attended_ref[:, cols] = (acc_ref[h] / sum_ref[pl.ds(h, 1), :]).T.astype(BF16)
        return carry

    lax.fori_loop(0, heads, finish, 0)

    def sent(peer, carry):
        to_later(peer).wait_send()
        return carry

    lax.fori_loop(me + 1, count, sent, 0)


def attention(length, projected, cosines, sines, q_width, collective_id):
    count = lax.axis_size("seq")
    rows = projected.shape[0]
    kv_width = (projected.shape[1] - q_width) // 2
    heads, kv_heads = q_width // HEAD_DIM, kv_width // HEAD_DIM
    vmem = pl.BlockSpec(memory_space=pltpu.VMEM)
    return pl.pallas_call(
        functools.partial(attention_kernel, count, heads, kv_heads),
        out_shape=[
            jax.ShapeDtypeStruct((rows, q_width), BF16),
            jax.ShapeDtypeStruct((heads, rows), F32),
            jax.ShapeDtypeStruct((rows, q_width), BF16),
            jax.ShapeDtypeStruct((count, rows, 2 * kv_width), BF16),
        ],
        in_specs=[pl.BlockSpec(memory_space=pltpu.SMEM)] + [vmem] * 3,
        out_specs=[vmem] * 4,
        scratch_shapes=[
            pltpu.VMEM((heads, rows), F32),
            pltpu.VMEM((heads, rows), F32),
            pltpu.VMEM((heads, HEAD_DIM, rows), F32),
            pltpu.SemaphoreType.DMA((count,)),
            pltpu.SemaphoreType.DMA((count,)),
        ],
        compiler_params=pltpu.CompilerParams(
            collective_id=collective_id, vmem_limit_bytes=30 << 20
        ),
        cost_estimate=pl.CostEstimate(flops=0, bytes_accessed=1 << 20, transcendentals=0),
        name="attention_forward",
    )(length, projected, cosines, sines)


def attention_back_kernel(count, heads, kv_heads, *refs):
    length_ref, q_ref, kv_ref, grad_ref, lse_ref, attended_ref, cos_ref, sin_ref = refs[:8]
    out_ref, delta_ref, dq_ref, part_ref, leaving, arriving, send, recv = refs[8:]
    me = lax.axis_index("seq")
    rows, kv_width = q_ref.shape[0], kv_heads * HEAD_DIM
    group, scale = heads // kv_heads, 1.0 / math.sqrt(HEAD_DIM)
    greet([{"seq": lax.rem(me + step, count)} for step in range(1, count)])
    length = length_ref[0]
    query_pos = me * rows + lax.broadcasted_iota(jnp.int32, (rows, rows), 1)
    key_local = lax.broadcasted_iota(jnp.int32, (rows, rows), 0)
    dq_ref[...] = jnp.zeros_like(dq_ref)
    ones = jnp.ones((8, HEAD_DIM), BF16)
    for h in range(heads):
        cols = slice(h * HEAD_DIM, (h + 1) * HEAD_DIM)
        terms = grad_ref[:, cols].astype(F32) * attended_ref[:, cols].astype(F32)
        high = terms.astype(BF16)
        low = (terms - high.astype(F32)).astype(BF16)
        delta_ref[h : h + 1, :] = (nt(ones, high) + nt(ones, low))[:1]

    def key_block(j):
        key_pos = j * rows + key_local
        mask = (key_pos <= query_pos) & (key_pos < length)
        part_ref[...] = jnp.zeros_like(part_ref)
        key_rows = pl.ds(pl.multiple_of(j * rows, rows), rows)
        for g in range(kv_heads):
            key_cols = slice(g * HEAD_DIM, (g + 1) * HEAD_DIM)
            value_cols = slice(kv_width + g * HEAD_DIM, kv_width + (g + 1) * HEAD_DIM)

            def one_head(i, carry):
                h = g * group + i
                cols = pl.ds(pl.multiple_of(h * HEAD_DIM, HEAD_DIM), HEAD_DIM)
                keys, values = kv_ref[key_rows, key_cols], kv_ref[key_rows, value_cols]
                queries, grads = q_ref[:, cols], grad_ref[:, cols]
                scores = nt(keys, queries) * scale
                probs = jnp.where(mask, jnp.exp(scores - lse_ref[pl.ds(h, 1), :]), 0.0)
                prob_grad = nt(values, grads)
                score_grad = (probs * (prob_grad - delta_ref[pl.ds(h, 1), :])).astype(BF16)
                part_ref[:, key_cols] += nn(score_grad, queries)
                part_ref[:, value_cols] += nn(probs.astype(BF16), grads)
                dq_ref[:, cols] += tn(score_grad, keys)
                return carry

            lax.fori_loop(0, group, one_head, 0, unroll=3)
        part_ref[:, :kv_width] = part_ref[:, :kv_width] * scale

    def to_owner(j):
        return pltpu.make_async_remote_copy(
            src_ref=leaving.at[j],
            dst_ref=arriving.at[me],
            send_sem=send.at[j],
            recv_sem=recv.at[me],
            device_id={"seq": j},
            device_id_type=MESH_IDS,
        )

    def other_block(j, carry):
        key_block(j)
        leaving[j] = part_ref[...].astype(BF16)
        to_owner(j).start()
        return carry

    lax.fori_loop(0, me, other_block, 0)
    key_block(me)
    part_ref[...] = part_ref[...].astype(BF16).astype(F32)
    cosines, sines = cos_ref[...], -sin_ref[...]

    def one_query(h, carry):
        cols = pl.ds(pl.multiple_of(h * HEAD_DIM, HEAD_DIM), HEAD_DIM)
        out_ref[:, cols] = rotate(dq_ref[:, cols] * scale, cosines, sines).astype(BF16)
        return carry

    lax.fori_loop(0, heads, one_query, 0)

    def add_arrived(m, carry):
        pltpu.make_async_remote_copy(
            src_ref=leaving.at[m],
            dst_ref=arriving.at[m],
            send_sem=send.at[m],
            recv_sem=recv.at[m],
            device_id={"seq": m},
            device_id_type=MESH_IDS,
        ).wait_recv()
        part_ref[...] += arriving[m].astype(F32)
        return carry

    lax.fori_loop(me + 1, count, add_arrived, 0)
    first = heads * HEAD_DIM
    for g in range(kv_heads):
        cols = slice(g * HEAD_DIM, (g + 1) * HEAD_DIM)
        out_ref[:, first + g * HEAD_DIM : first + (g + 1) * HEAD_DIM] = rotate(
            part_ref[:, cols], cosines, sines
        ).astype(BF16)
    out_ref[:, first + kv_width :] = part_ref[:, kv_width:].astype(BF16)

    def sent(j, carry):
        to_owner(j).wait_send()
        return carry

    lax.fori_loop(0, me, sent, 0)


def attention_back(length, queries, kv_all, grads, lse, attended, cosines, sines, collective_id):
    count = lax.axis_size("seq")
    rows, q_width = queries.shape
    kv_width = kv_all.shape[1] // 2
    heads, kv_heads = q_width // HEAD_DIM, kv_width // HEAD_DIM
    vmem = pl.BlockSpec(memory_space=pltpu.VMEM)
    return pl.pallas_call(
        functools.partial(attention_back_kernel, count, heads, kv_heads),
        out_shape=jax.ShapeDtypeStruct((rows, q_width + 2 * kv_width), BF16),
        in_specs=[pl.BlockSpec(memory_space=pltpu.SMEM)] + [vmem] * 7,
        out_specs=vmem,
        scratch_shapes=[
            pltpu.VMEM((heads, rows), F32),
            pltpu.VMEM((rows, q_width), F32),
            pltpu.VMEM((rows, 2 * kv_width), F32),
            pltpu.VMEM((count, rows, 2 * kv_width), BF16),
            pltpu.VMEM((count, rows, 2 * kv_width), BF16),
            pltpu.SemaphoreType.DMA((count,)),
            pltpu.SemaphoreType.DMA((count,)),
        ],
        compiler_params=pltpu.CompilerParams(
            collective_id=collective_id, vmem_limit_bytes=30 << 20
        ),
        cost_estimate=pl.CostEstimate(
            flops=10 * count * rows * rows * q_width, bytes_accessed=1 << 20, transcendentals=0
        ),
        name="attention_backward",
    )(length, queries, kv_all, grads, lse, attended, cosines, sines)


def weight_grad_kernel(n, *refs):
    lefts, rights, outs = refs[:2], refs[2 : 2 + 2 * n], refs[2 + 2 * n :]
    for k, out_ref in enumerate(outs):
        early, late = rights[2 * k : 2 * k + 2]
        total = tn(lefts[0][...], early[...]) + tn(lefts[1][...], late[...])
        out_ref[...] = total.astype(BF16)


def weight_grads(lefts, rights, name):
    columns, tile = lefts[0].shape[1], 256
    flat = [part for pair in rights for part in pair]
    return pl.pallas_call(
        functools.partial(weight_grad_kernel, len(rights)),
        grid=(columns // tile,),
        out_shape=[jax.ShapeDtypeStruct((columns, r[0].shape[1]), BF16) for r in rights],
        in_specs=[pl.BlockSpec((x.shape[0], tile), lambda i: (0, i)) for x in lefts]
        + [pl.BlockSpec(r.shape, lambda i: (0, 0), pipeline_mode=pl.Buffered(1)) for r in flat],
        out_specs=[pl.BlockSpec((tile, r[0].shape[1]), lambda i: (i, 0)) for r in rights],
        compiler_params=pltpu.CompilerParams(vmem_limit_bytes=48 << 20),
        cost_estimate=pl.CostEstimate(flops=0, bytes_accessed=1 << 20, transcendentals=0),
        name=name,
    )(*lefts, *flat)


def seq_permutes(block_for):
    count, me = lax.axis_size("seq"), lax.axis_index("seq")
    pieces = [block_for(me)]
    for step in range(1, count):
        ring = [(i, (i + step) % count) for i in range(count)]
        pieces.append(lax.ppermute(block_for(lax.rem(me + step, count)), "seq", ring))
    return pieces


def in_seq_order(pieces, dtype):
    count, me = len(pieces), lax.axis_index("seq")
    whole = jnp.zeros((count,) + pieces[0].shape, dtype)
    for step, piece in enumerate(pieces):
        place = lax.rem(me + count - step, count)
        whole = lax.dynamic_update_index_in_dim(whole, piece.astype(dtype), place, 0)
    return whole


def on_device(
    hidden_in,
    lengths,
    routes,
    gates,
    priority,
    attn_gain,
    mlp_gain,
    w_query,
    key_projection,
    value_projection,
    w_out,
    w_gate,
    w_up,
    w_down,
    cotangent,
):
    rows = hidden_in.shape[1]
    width = hidden_in.shape[2]
    dp_count = lax.axis_size("dp")
    seq_count = lax.axis_size("seq")
    devices = dp_count * seq_count
    own_experts = w_gate.shape[0]
    sharers = seq_count // own_experts
    hidden_units = w_gate.shape[2]
    my_seq = lax.axis_index("seq")
    extent = rows * seq_count
    query_pos = my_seq * rows + jnp.arange(rows, dtype=jnp.int32)
    length = lengths[0]
    is_valid = query_pos < length
    q_width = w_query.shape[1]
    kv_width = key_projection.shape[1]
    cosine_lookup, sine_lookup = rope_angles(query_pos, HEAD_DIM)

    gain_block = jnp.concatenate(
        [attn_gain[:, None], mlp_gain[:, None], jnp.zeros((attn_gain.shape[0], LANES - 2), BF16)],
        axis=1,
    )
    packed = jnp.concatenate([w_query, key_projection, value_projection], axis=1)
    staged = seq_count == 4 and w_query.shape[0] % 16 == 0

    def expert_pieces(weights):
        def block_for(peer):
            return lax.dynamic_index_in_dim(weights, peer // sharers, 0, keepdims=False)

        return seq_permutes(block_for)

    gate_parts = expert_pieces(w_gate)
    if staged:
        packed_full, gains_full, out_full = staged_gather(
            [packed, gain_block, w_out], [], None, 2, "gather_attention_weights"
        )
    else:
        packed_full = lax.all_gather(packed, BOTH, axis=0, tiled=True)
        gains_full = lax.all_gather(gain_block, BOTH, axis=0, tiled=True)
        out_full = lax.all_gather(w_out, BOTH, axis=0, tiled=True)

    pair_routes, place, kept = claim_places(routes[0], priority[0, 0], is_valid)
    holder = (pair_routes // own_experts) * seq_count + (pair_routes % own_experts) * sharers
    holder = holder + my_seq * sharers // seq_count
    slots = devices * CAP
    target = jnp.where(kept, holder * CAP + place, slots).reshape(rows, TOP)
    slot_ids = jnp.arange(slots, dtype=jnp.int32)
    hits = target[:, :, None] == slot_ids[None, None, :]
    gate_rows = gates[0]
    token_hot = jnp.any(hits, axis=1).astype(BF16)

    def hot_of(first, size):
        mine = kept & (place >= first) & (place < first + size)
        spot = jnp.where(mine, holder * size + place - first, slots).reshape(rows, TOP)
        ids = jnp.arange(devices * size, dtype=jnp.int32)
        return jnp.any(spot[:, :, None] == ids[None, None, :], axis=1).astype(BF16)

    early_hot, late_hot = hot_of(0, EARLY), hot_of(EARLY, CAP - EARLY)
    slot_gate = jnp.sum(jnp.where(hits, gate_rows[:, :, None], 0.0), axis=(0, 1))

    live_cotangent = jnp.where(is_valid[:, None], cotangent[0], jnp.zeros((), BF16))
    out_grad = live_cotangent.astype(F32)
    grad_send = (tn(token_hot, live_cotangent) * slot_gate[:, None]).astype(BF16)
    packed_full, gains_full, out_full, gate_parts, grad_send = lax.optimization_barrier(
        (packed_full, gains_full, out_full, gate_parts, grad_send)
    )
    gain_one, gain_two = gains_full[:, 0].astype(F32), gains_full[:, 1].astype(F32)
    grad_rows = swap(grad_send.reshape(devices, CAP, width), ("dp", "seq"))

    inputs = hidden_in[0].astype(F32)
    scale_one = lax.rsqrt(jnp.mean(inputs * inputs, axis=-1, keepdims=True) + EPSILON)
    normed = (inputs * scale_one * gain_one).astype(BF16)
    projected = nn(normed, packed_full)
    cosines, sines = cosine_lookup[:, 0], sine_lookup[:, 0]
    cosines = jnp.concatenate([cosines, cosines], axis=1)
    sines = jnp.concatenate([-sines, sines], axis=1)
    attended, log_total, query_flat, kv_all = attention(
        lengths, projected, cosines, sines, q_width, 1
    )
    kv_all = kv_all.reshape(extent, 2 * kv_width)
    attended, w_up = lax.optimization_barrier((attended, w_up))
    up_parts = expert_pieces(w_up)
    middle = inputs + nn(attended, out_full)
    scale_two = lax.rsqrt(jnp.mean(middle * middle, axis=-1, keepdims=True) + EPSILON)
    moe_input = (middle * scale_two * gain_two).astype(BF16)

    def to_experts(hot):
        return tn(hot, moe_input).astype(BF16).reshape(devices, -1, width)

    early_send, late_send = to_experts(early_hot), to_experts(late_hot)
    *up_parts, last_up = up_parts
    early_send, late_send, grad_rows, up_parts, w_down = lax.optimization_barrier(
        (early_send, late_send, grad_rows, up_parts, w_down)
    )
    up_parts = [*up_parts, last_up]
    early_grads, late_grads, w_down = lax.optimization_barrier(
        (grad_rows[:, :EARLY], grad_rows[:, EARLY:], w_down)
    )
    down_parts = expert_pieces(w_down)
    early_rows = swap(early_send, ("dp", "seq"))
    early_rows, late_send = lax.optimization_barrier((early_rows, late_send))
    late_rows = swap(late_send, ("dp", "seq"))
    gate_full = in_seq_order(gate_parts, BF16).reshape(width, hidden_units)
    up_full = in_seq_order(up_parts, BF16).reshape(width, hidden_units)
    down_full = in_seq_order(down_parts, BF16).reshape(hidden_units, width)
    early_rows, gate_full, up_full, down_full, early_grads, late_grads = (
        lax.optimization_barrier(
            (early_rows, gate_full, up_full, down_full, early_grads, late_grads)
        )
    )

    def run_expert(slot_rows, grads):
        blocks = slot_rows.shape[:2]
        slot_rows, grads = slot_rows.reshape(-1, width), grads.reshape(-1, width)
        gate_pre = nn(slot_rows, gate_full)
        up_pre = nn(slot_rows, up_full)
        gate_sigmoid = jax.nn.sigmoid(gate_pre)
        gate_act = gate_pre * gate_sigmoid
        gate_slope = gate_sigmoid * (1.0 + gate_pre * (1.0 - gate_sigmoid))
        hidden = (gate_act * up_pre).astype(BF16)
        hidden_grad = nt(grads, down_full)
        gate_pre_grad = (hidden_grad * up_pre * gate_slope).astype(BF16)
        up_pre_grad = (hidden_grad * gate_act).astype(BF16)
        return [x.reshape(blocks + (-1,)) for x in (hidden, gate_pre_grad, up_pre_grad)]

    def row_grads(gate_pre_grad, up_pre_grad):
        blocks = gate_pre_grad.shape[:2]
        gate_pre_grad = gate_pre_grad.reshape(-1, hidden_units)
        up_pre_grad = up_pre_grad.reshape(-1, hidden_units)
        row_grad = (nt(gate_pre_grad, gate_full) + nt(up_pre_grad, up_full)).astype(BF16)
        return row_grad.reshape(blocks + (width,))

    def both_parts(early, late):
        return jnp.concatenate([early, late], axis=1).reshape(slots, -1)

    def to_owners(grad):
        grad = grad.reshape(seq_count, -1, grad.shape[1])

        def block_for(peer):
            return lax.dynamic_index_in_dim(grad, peer, 0, keepdims=False)

        return seq_permutes(block_for)

    def owned_sum(pieces):
        whole = in_seq_order(pieces, F32)
        return jnp.sum(whole.reshape((own_experts, sharers) + whole.shape[1:]), axis=1)

    early_hidden, *early_pre_grads = run_expert(early_rows, early_grads)
    early_row_grad = row_grads(*early_pre_grads)
    late_rows, early_row_grad = lax.optimization_barrier((late_rows, early_row_grad))
    early_back = swap(early_row_grad, ("dp", "seq"))
    late_hidden, *late_pre_grads = run_expert(late_rows, late_grads)

    def flat(*parts):
        return [part.reshape(-1, part.shape[-1]) for part in parts]

    gate_grad, up_grad = weight_grads(
        flat(early_rows, late_rows),
        [flat(*pair) for pair in zip(early_pre_grads, late_pre_grads, strict=True)],
        "gate_up_grads",
    )
    late_pre_grads, late_hidden, gate_grad, up_grad = lax.optimization_barrier(
        (late_pre_grads, late_hidden, gate_grad, up_grad)
    )
    gate_grad_parts = to_owners(gate_grad)
    late_row_grad = row_grads(*late_pre_grads)
    *gate_grad_parts, last_gate = gate_grad_parts
    early_back, late_row_grad, gate_grad_parts, up_grad, late_hidden = lax.optimization_barrier(
        (early_back, late_row_grad, gate_grad_parts, up_grad, late_hidden)
    )
    gate_grad_parts = [*gate_grad_parts, last_gate]
    expert_hidden = both_parts(early_hidden, late_hidden)
    late_back = swap(late_row_grad, ("dp", "seq"))
    gate_owned, up_owned = owned_sum(gate_grad_parts), owned_sum(to_owners(up_grad))
    (down_grad,) = weight_grads(
        flat(early_hidden, late_hidden), [flat(early_grads, late_grads)], "down_grads"
    )
    expert_out = nn(expert_hidden, down_full).astype(BF16)
    expert_out, late_back, gate_owned, up_owned, down_grad = lax.optimization_barrier(
        (expert_out, late_back, gate_owned, up_owned, down_grad)
    )
    returned = swap(expert_out.reshape(devices, CAP, width), ("dp", "seq")).reshape(slots, width)
    early_back, late_back = early_back.reshape(-1, width), late_back.reshape(-1, width)
    moe_input_grad = nn(early_hot, early_back) + nn(late_hot, late_back)
    middle_norm_grad, gain_two_grad = norm_back(middle, scale_two, gain_two, moe_input_grad)
    middle_grad = out_grad + middle_norm_grad
    branch_grad = middle_grad.astype(BF16)
    out_terms = tn(attended, branch_grad).astype(BF16)
    attended_grad = nt(branch_grad, out_full).astype(BF16)
    projected_grad = attention_back(
        lengths,
        query_flat,
        kv_all,
        attended_grad,
        log_total,
        attended,
        cosines,
        sines,
        4,
    )
    normed_grad = nt(projected_grad, packed_full)
    input_norm_grad, gain_one_grad = norm_back(inputs, scale_one, gain_one, normed_grad)
    input_grad = middle_grad + input_norm_grad

    lane = lax.broadcasted_iota(jnp.int32, (width, LANES), 1)
    gain_terms = jnp.where(lane == 0, gain_one_grad[:, None], gain_two_grad[:, None])
    gain_terms = jnp.where(lane < 2, gain_terms, 0.0).astype(BF16)
    query_terms = tn(normed, projected_grad).astype(BF16)
    if staged:
        out_owned, gains_owned, owned, down_owned = staged_scatter(
            [out_terms, gain_terms, query_terms],
            [down_grad.reshape(seq_count, -1, width)],
            lambda ref, peer: ref.at[peer],
            6,
            "scatter_attention_grads",
        )
        down_owned = down_owned.reshape((own_experts, sharers) + down_owned.shape[1:])
        down_owned = jnp.sum(down_owned.astype(F32), axis=1)
    else:
        terms = jnp.concatenate([out_terms, gain_terms, query_terms], axis=1)
        terms = lax.psum_scatter(terms, BOTH, scatter_dimension=0, tiled=True).astype(F32)
        out_owned, gains_owned = terms[:, :width], terms[:, width : width + LANES]
        owned = terms[:, width + LANES :]
        down_owned = owned_sum(to_owners(down_grad))
    returned, owned = lax.optimization_barrier((returned, owned))
    expert_grads = [gate_owned, up_owned, down_owned]

    gate_hot = jnp.sum(jnp.where(hits, gate_rows[:, :, None], 0.0), axis=1).astype(BF16)
    layer_out = middle + nn(gate_hot, returned)
    return (
        layer_out[None],
        input_grad[None],
        gains_owned[:, 0],
        gains_owned[:, 1],
        owned[:, :q_width],
        owned[:, q_width : q_width + kv_width],
        owned[:, q_width + kv_width : q_width + 2 * kv_width],
        out_owned,
        *expert_grads,
    )


def solution(mesh):
    part = P("dp", "seq", None)
    both = P(BOTH)
    both_rows = P(BOTH, None)
    return jax.shard_map(
        on_device,
        mesh=mesh,
        in_specs=(part, P("dp"), part, part, part, both, both)
        + (both_rows,) * 4
        + (part,) * 4,
        out_specs=(part, part, both, both) + (both_rows,) * 4 + (part,) * 3,
        check_vma=False,
    )
```

```python
import functools
import math

import jax
import jax.numpy as jnp
from jax import lax
from jax.experimental import pallas as pl
from jax.experimental.pallas import tpu as pltpu
from jax.sharding import PartitionSpec as P

HEAD_DIM = 128
EXPERTS = 32
TOP = 4
CAP = 40
EARLY = 24

EPSILON = 1e-06
ROPE_BASE = 10000.0
NEG_FILL = -1e30
LANES = 128
BOTH = ("seq", "dp")
BF16 = jnp.bfloat16
F32 = jnp.float32


def rope_angles(positions, head_size):
    half_dim = head_size // 2
    frequency = ROPE_BASE ** (-(2.0 * jnp.arange(half_dim, dtype=F32)) / head_size)
    angles = positions.astype(F32)[:, None] * frequency[None, :]
    return (jnp.cos(angles)[:, None, :], jnp.sin(angles)[:, None, :])


def dot(left, right, contract):
    return lax.dot_general(left, right, (contract, ((), ())), preferred_element_type=F32)


def nn(left, right):
    return dot(left, right, ((1,), (0,)))


def nt(left, right):
    return dot(left, right, ((1,), (1,)))


def tn(left, right):
    return dot(left, right, ((0,), (0,)))


def claim_places(routes, priority, is_valid):
    pair_routes = routes.reshape(-1)
    live = jnp.repeat(is_valid, TOP)
    key = jnp.where(live, pair_routes, -1)
    earlier = (key[None, :] == pair_routes[:, None]) & (priority[None, :] < priority[:, None])
    place = jnp.sum(earlier.astype(F32), axis=1).astype(jnp.int32)
    return pair_routes, place, live & (place < CAP)


def norm_back(values, scale_rows, gain_vec, incoming):
    weighted = incoming * gain_vec
    inner_mean = jnp.mean(weighted * values, axis=-1, keepdims=True)
    values_grad = scale_rows * weighted - values * scale_rows * scale_rows * scale_rows * inner_mean
    return (values_grad, jnp.sum(incoming * values * scale_rows, axis=0))


def swap(blocks, axes):
    return lax.all_to_all(blocks, axes, split_axis=0, concat_axis=0, tiled=True)


MESH_IDS = pl.DeviceIdType.MESH


def torus_place():
    seq, dp = lax.axis_index("seq"), lax.axis_index("dp")
    return seq // 2, seq % 2, dp // 2, dp % 2


def torus_id(a, b, z, c):
    return {"seq": 2 * a + b, "dp": 2 * z + c}


def torus_peers(line):
    a, b, z, c = torus_place()
    peers = [torus_id(a, b, z, 1 - c), torus_id(a, 1 - b, z, c), torus_id(1 - a, b, z, c)]
    peers.append(torus_id(1 - a, 1 - b, z, c))
    return peers + [torus_id(a, b, lax.rem(z + k, line), c) for k in range(1, line)]


def greet(peers):
    barrier = pltpu.get_barrier_semaphore()
    for peer in peers:
        pl.semaphore_signal(barrier, inc=1, device_id=peer, device_id_type=MESH_IDS)
    pl.semaphore_wait(barrier, len(peers))


def column_chunks(widths, parts):
    chunks = []
    for part in range(parts):
        for k, whole in enumerate(widths):
            tiles = whole // LANES
            first, end = tiles * part // parts, tiles * (part + 1) // parts
            if end > first:
                chunks.append((k, first * LANES, (end - first) * LANES))
    return chunks


def first_links(chunks):
    loads, choices = [0, 0], []
    for _, _, size in chunks:
        link = int(loads[0] > loads[1])
        loads[link] += 2 * size
        loads[1 - link] += size
        choices.append(link == 0)
    return choices


def remote(src, dst, sems, i, j, device_id):
    send, recv = sems
    return pltpu.make_async_remote_copy(
        src_ref=src,
        dst_ref=dst,
        send_sem=send.at[i, j],
        recv_sem=recv.at[i, j],
        device_id=device_id,
        device_id_type=MESH_IDS,
    )


def start_exchange(count, sources, targets, block_of, sems):
    send_sems, recv_sems, local_sems = sems
    me = lax.axis_index("seq")
    copies = []
    for i, source in enumerate(sources):
        for step in range(1, count):
            peer = lax.rem(me + step, count)
            copies.append(
                pltpu.make_async_remote_copy(
                    src_ref=block_of(source, peer),
                    dst_ref=targets[i].at[me],
                    send_sem=send_sems.at[i, step - 1],
                    recv_sem=recv_sems.at[i, step - 1],
                    device_id={"seq": peer},
                    device_id_type=MESH_IDS,
                )
            )
        copies.append(
            pltpu.make_async_copy(block_of(source, me), targets[i].at[me], local_sems.at[i])
        )
    for copy in copies:
        copy.start()
    return copies


def exchange_sems(n, count):
    return [
        pltpu.SemaphoreType.DMA((n, count - 1)),
        pltpu.SemaphoreType.DMA((n, count - 1)),
        pltpu.SemaphoreType.DMA((n,)),
    ]


def in_steps(count, stages, after=None):
    for step in range((count + 1) // 2 + len(stages) - 1):
        if after is not None and step == (count + 1) // 2 + 1:
            after()
        for behind, stage in enumerate(stages):
            for i in (2 * (step - behind), 2 * (step - behind) + 1):
                if 0 <= i < count:
                    stage(i)


def gather_kernel(line, chunks, n, extras, block_of, *refs):
    sources, more_sources = refs[:n], refs[n : n + extras]
    refs = refs[n + extras :]
    targets, more_targets = refs[:n], refs[n : n + extras]
    send, recv, local, *more_sems = refs[n + extras :]
    sems = (send, recv)
    a, b, z, c = torus_place()
    over_b = first_links(chunks)
    greet(torus_peers(line))
    more = start_exchange(4, more_sources, more_targets, block_of, more_sems) if extras else []
    sent = []

    def start(copy):
        copy.start()
        sent.append(copy)
        return copy

    along_line, first_hop, second_hop, third_hop = {}, {}, {}, {}

    def send_line(i):
        k, first, size = chunks[i]
        cols = pl.ds(first, size)
        own = targets[k].at[a, b, z, c, :, cols]
        keep = pltpu.make_async_copy(sources[k].at[:, cols], own, local.at[i])
        keep.start()
        along_line[i] = [
            start(
                remote(
                    sources[k].at[:, cols],
                    own,
                    sems,
                    i,
                    2 + step,
                    torus_id(a, b, lax.rem(z + step, line), c),
                )
            )
            for step in range(1, line)
        ]
        along_line[i].append(keep)

    def send_first(i):
        k, first, size = chunks[i]
        *copies, keep = along_line[i]
        keep.wait()
        for copy in copies:
            copy.wait_recv()
        block = targets[k].at[a, b, :, c, :, pl.ds(first, size)]
        peer = torus_id(a, 1 - b, z, c) if over_b[i] else torus_id(1 - a, b, z, c)
        first_hop[i] = start(remote(block, block, sems, i, 1, peer))

    def send_second(i):
        k, first, size = chunks[i]
        first_hop[i].wait_recv()
        cols = pl.ds(first, size)
        if over_b[i]:
            block, peer = targets[k].at[a, :, :, c, :, cols], torus_id(1 - a, b, z, c)
        else:
            block, peer = targets[k].at[:, b, :, c, :, cols], torus_id(a, 1 - b, z, c)
        second_hop[i] = start(remote(block, block, sems, i, 2, peer))

    def send_third(i):
        k, first, size = chunks[i]
        second_hop[i].wait_recv()
        block = targets[k].at[:, :, :, c, :, pl.ds(first, size)]
        third_hop[i] = start(remote(block, block, sems, i, 0, torus_id(a, b, z, 1 - c)))

    in_steps(len(chunks), [send_line, send_first, send_second, send_third])
    for copy in third_hop.values():
        copy.wait_recv()
    for copy in sent:
        copy.wait_send()
    for copy in more:
        copy.wait()


def staged_gather(arrays, extras, block_of, collective_id, name, parts=6):
    seq_count, line = lax.axis_size("seq"), lax.axis_size("dp") // 2
    rows, n = arrays[0].shape[0], len(arrays)
    chunks = column_chunks([x.shape[1] for x in arrays], parts)
    m = len(chunks)
    shape = (seq_count // 2, 2, line, 2, rows)
    size = sum(x.shape[1] for x in arrays) * rows * 64
    count = n + len(extras)
    outs = pl.pallas_call(
        functools.partial(gather_kernel, line, chunks, n, len(extras), block_of),
        out_shape=[jax.ShapeDtypeStruct(shape + (x.shape[1],), BF16) for x in arrays]
        + [jax.ShapeDtypeStruct((seq_count,) + x.shape[1:], BF16) for x in extras],
        in_specs=[pl.BlockSpec(memory_space=pl.ANY)] * count,
        out_specs=[pl.BlockSpec(memory_space=pl.ANY)] * count,
        scratch_shapes=[
            pltpu.SemaphoreType.DMA((m, 2 + line)),
            pltpu.SemaphoreType.DMA((m, 2 + line)),
            pltpu.SemaphoreType.DMA((m,)),
        ]
        + (exchange_sems(len(extras), seq_count) if extras else []),
        compiler_params=pltpu.CompilerParams(
            collective_id=collective_id, vmem_limit_bytes=56 << 20
        ),
        cost_estimate=pl.CostEstimate(flops=0, bytes_accessed=size, transcendentals=0),
        name=name,
    )(*arrays, *extras)
    return [o.reshape(-1, o.shape[-1]) for o in outs]


def scatter_kernel(line, chunks, n, extras, block_of, *refs):
    m = len(chunks)
    sources, more_sources = refs[:n], refs[n : n + extras]
    refs = refs[n + extras :]
    targets, more_targets = refs[:n], refs[n : n + extras]
    scratch = refs[n + extras :]
    owns, ins1, accs2, ins2, accs3, ins3, ins4 = (scratch[m * s : m * (s + 1)] for s in range(7))
    send, recv, local, *more_sems = scratch[7 * m :]
    sems = (send, recv)
    a, b, z, c = torus_place()
    over_b = first_links(chunks)
    greet(torus_peers(line))
    sent = []

    def start(copy):
        copy.start()
        sent.append(copy)
        return copy

    def add_lines(target, left, right):
        def one(j, carry):
            target[j] = (left[j].astype(F32) + right[j].astype(F32)).astype(BF16)
            return carry

        lax.fori_loop(0, line, one, 0)

    between_cores, first_hop, second_hop, along_line = {}, {}, {}, {}

    def send_core(i):
        k, first, size = chunks[i]
        cols = pl.ds(first, size)
        keep = pltpu.make_async_copy(sources[k].at[:, :, :, c, :, cols], owns[i], local.at[i])
        keep.start()
        swap_core = remote(
            sources[k].at[:, :, :, 1 - c, :, cols], ins1[i], sems, i, 0, torus_id(a, b, z, 1 - c)
        )
        between_cores[i] = (keep, start(swap_core))

    def send_first(i):
        keep, copy = between_cores[i]
        keep.wait()
        copy.wait_recv()
        for p in range(2):
            for q in range(2):
                add_lines(owns[i].at[p, q], owns[i].at[p, q], ins1[i].at[p, q])
        if over_b[i]:
            block, peer = owns[i].at[:, 1 - b], torus_id(a, 1 - b, z, c)
        else:
            block, peer = owns[i].at[1 - a], torus_id(1 - a, b, z, c)
        first_hop[i] = start(remote(block, ins2[i], sems, i, 1, peer))

    def send_second(i):
        first_hop[i].wait_recv()
        for p in range(2):
            mine = owns[i].at[p, b] if over_b[i] else owns[i].at[a, p]
            add_lines(accs2[i].at[p], mine, ins2[i].at[p])
        if over_b[i]:
            block, peer = accs2[i].at[1 - a], torus_id(1 - a, b, z, c)
        else:
            block, peer = accs2[i].at[1 - b], torus_id(a, 1 - b, z, c)
        second_hop[i] = start(remote(block, ins3[i], sems, i, 2, peer))

    def send_line(i):
        second_hop[i].wait_recv()
        add_lines(accs3[i], accs2[i].at[a if over_b[i] else b], ins3[i])
        copies = []
        for step in range(1, line):
            to = lax.rem(z + step, line)
            peer = torus_id(a, b, to, c)
            copies.append(start(remote(accs3[i].at[to], ins4[i].at[z], sems, i, 2 + step, peer)))
        along_line[i] = copies

    def finish(i):
        k, first, size = chunks[i]
        total = accs3[i][z].astype(F32)
        for step in range(1, line):
            along_line[i][step - 1].wait_recv()
            total = total + ins4[i][lax.rem(z + line - step, line)].astype(F32)
        targets[k][:, first : first + size] = total

    more = []

    def send_more():
        if extras:
            more.extend(start_exchange(4, more_sources, more_targets, block_of, more_sems))

    in_steps(m, [send_core, send_first, send_second, send_line, finish], send_more)
    for copy in sent:
        copy.wait_send()
    for copy in more:
        copy.wait()


def staged_scatter(arrays, extras, block_of, collective_id, name, parts=6):
    seq_count, line = lax.axis_size("seq"), lax.axis_size("dp") // 2
    rows, n = arrays[0].shape[0] // (2 * line * seq_count), len(arrays)
    chunks = column_chunks([x.shape[1] for x in arrays], parts)
    m = len(chunks)
    leads = [(2, 2, line), (2, 2, line), (2, line), (2, line), (line,), (line,), (line,)]
    size = sum(x.shape[1] for x in arrays) * rows * 64
    anywhere = pl.BlockSpec(memory_space=pl.ANY)
    return pl.pallas_call(
        functools.partial(scatter_kernel, line, chunks, n, len(extras), block_of),
        out_shape=[jax.ShapeDtypeStruct((rows, x.shape[1]), F32) for x in arrays]
        + [jax.ShapeDtypeStruct((seq_count,) + x.shape[1:], BF16) for x in extras],
        in_specs=[anywhere] * (n + len(extras)),
        out_specs=[pl.BlockSpec(memory_space=pltpu.VMEM)] * n + [anywhere] * len(extras),
        scratch_shapes=[
            pltpu.VMEM(lead + (rows, width), BF16) for lead in leads for _, _, width in chunks
        ]
        + [
            pltpu.SemaphoreType.DMA((m, 2 + line)),
            pltpu.SemaphoreType.DMA((m, 2 + line)),
            pltpu.SemaphoreType.DMA((m,)),
        ]
        + (exchange_sems(len(extras), seq_count) if extras else []),
        compiler_params=pltpu.CompilerParams(
            collective_id=collective_id, vmem_limit_bytes=36 << 20
        ),
        cost_estimate=pl.CostEstimate(flops=0, bytes_accessed=size, transcendentals=0),
        name=name,
    )(*[x.reshape(2, 2, line, 2, rows, x.shape[1]) for x in arrays], *extras)


def rotate(values, cosines, sines):
    return values * cosines + pltpu.roll(values, HEAD_DIM // 2, 1) * sines


def attention_kernel(count, heads, kv_heads, *refs):
    length_ref, projected_ref, cos_ref, sin_ref = refs[:4]
    attended_ref, lse_ref, q_ref, kv_ref = refs[4:8]
    max_ref, sum_ref, acc_ref, send, recv = refs[8:]
    me = lax.axis_index("seq")
    rows, kv_width = q_ref.shape[0], kv_heads * HEAD_DIM
    q_width, group, scale = heads * HEAD_DIM, heads // kv_heads, 1.0 / math.sqrt(HEAD_DIM)
    greet([{"seq": lax.rem(me + step, count)} for step in range(1, count)])
    cosines, sines = cos_ref[...], sin_ref[...]
    for g in range(kv_heads):
        cols = slice(g * HEAD_DIM, (g + 1) * HEAD_DIM)
        keys = projected_ref[:, q_width + g * HEAD_DIM : q_width + (g + 1) * HEAD_DIM]
        kv_ref[me, :, cols] = rotate(keys, cosines, sines).astype(BF16)
    kv_ref[me, :, kv_width:] = projected_ref[:, q_width + kv_width :].astype(BF16)

    def to_later(peer):
        return pltpu.make_async_remote_copy(
            src_ref=kv_ref.at[me],
            dst_ref=kv_ref.at[me],
            send_sem=send.at[peer],
            recv_sem=recv.at[me],
            device_id={"seq": peer},
            device_id_type=MESH_IDS,
        )

    def start(peer, carry):
        to_later(peer).start()
        return carry

    lax.fori_loop(me + 1, count, start, 0)

    def one_query(h, carry):
        cols = pl.ds(pl.multiple_of(h * HEAD_DIM, HEAD_DIM), HEAD_DIM)
        q_ref[:, cols] = rotate(projected_ref[:, cols], cosines, sines).astype(BF16)
        return carry

    lax.fori_loop(0, heads, one_query, 0)
    max_ref[...] = jnp.full_like(max_ref, NEG_FILL)
    sum_ref[...] = jnp.zeros_like(sum_ref)
    acc_ref[...] = jnp.zeros_like(acc_ref)
    length = length_ref[0]
    query_pos = me * rows + lax.broadcasted_iota(jnp.int32, (rows, rows), 1)
    key_local = lax.broadcasted_iota(jnp.int32, (rows, rows), 0)

    def key_block(j):
        key_pos = j * rows + key_local
        mask = (key_pos <= query_pos) & (key_pos < length)
        for g in range(kv_heads):
            key_cols = slice(g * HEAD_DIM, (g + 1) * HEAD_DIM)
            value_cols = slice(kv_width + g * HEAD_DIM, kv_width + (g + 1) * HEAD_DIM)

            def one_head(i, carry):
                h = g * group + i
                cols = pl.ds(pl.multiple_of(h * HEAD_DIM, HEAD_DIM), HEAD_DIM)
                row = pl.ds(h, 1)
                keys, values = kv_ref[j, :, key_cols], kv_ref[j, :, value_cols]
                scores = jnp.where(mask, nt(keys, q_ref[:, cols]) * scale, NEG_FILL)
                before = max_ref[row, :]
                top = jnp.maximum(before, jnp.max(scores, axis=0, keepdims=True))
                shrink = jnp.exp(before - top)
                weights = jnp.exp(scores - top)
                max_ref[row, :] = top
                sum_ref[row, :] = sum_ref[row, :] * shrink + jnp.sum(weights, axis=0, keepdims=True)
                acc_ref[h] = acc_ref[h] * shrink + tn(values, weights.astype(BF16))
                return carry

            lax.fori_loop(0, group, one_head, 0, unroll=2)

    key_block(me)

    def earlier_block(j, carry):
        pltpu.make_async_remote_copy(
            src_ref=kv_ref.at[j],
            dst_ref=kv_ref.at[j],
            send_sem=send.at[j],
            recv_sem=recv.at[j],
            device_id={"seq": j},
            device_id_type=MESH_IDS,
        ).wait_recv()
        key_block(j)
        return carry

    lax.fori_loop(0, me, earlier_block, 0)
    lse_ref[...] = max_ref[...] + jnp.log(sum_ref[...])

    def finish(h, carry):
        cols = pl.ds(pl.multiple_of(h * HEAD_DIM, HEAD_DIM), HEAD_DIM)
        attended_ref[:, cols] = (acc_ref[h] / sum_ref[pl.ds(h, 1), :]).T.astype(BF16)
        return carry

    lax.fori_loop(0, heads, finish, 0)

    def sent(peer, carry):
        to_later(peer).wait_send()
        return carry

    lax.fori_loop(me + 1, count, sent, 0)


def attention(length, projected, cosines, sines, q_width, collective_id):
    count = lax.axis_size("seq")
    rows = projected.shape[0]
    kv_width = (projected.shape[1] - q_width) // 2
    heads, kv_heads = q_width // HEAD_DIM, kv_width // HEAD_DIM
    vmem = pl.BlockSpec(memory_space=pltpu.VMEM)
    return pl.pallas_call(
        functools.partial(attention_kernel, count, heads, kv_heads),
        out_shape=[
            jax.ShapeDtypeStruct((rows, q_width), BF16),
            jax.ShapeDtypeStruct((heads, rows), F32),
            jax.ShapeDtypeStruct((rows, q_width), BF16),
            jax.ShapeDtypeStruct((count, rows, 2 * kv_width), BF16),
        ],
        in_specs=[pl.BlockSpec(memory_space=pltpu.SMEM)] + [vmem] * 3,
        out_specs=[vmem] * 4,
        scratch_shapes=[
            pltpu.VMEM((heads, rows), F32),
            pltpu.VMEM((heads, rows), F32),
            pltpu.VMEM((heads, HEAD_DIM, rows), F32),
            pltpu.SemaphoreType.DMA((count,)),
            pltpu.SemaphoreType.DMA((count,)),
        ],
        compiler_params=pltpu.CompilerParams(
            collective_id=collective_id, vmem_limit_bytes=30 << 20
        ),
        cost_estimate=pl.CostEstimate(flops=0, bytes_accessed=1 << 20, transcendentals=0),
        name="attention_forward",
    )(length, projected, cosines, sines)


def attention_back_kernel(count, heads, kv_heads, *refs):
    length_ref, q_ref, kv_ref, grad_ref, lse_ref, attended_ref, cos_ref, sin_ref = refs[:8]
    out_ref, delta_ref, dq_ref, part_ref, leaving, arriving, send, recv = refs[8:]
    me = lax.axis_index("seq")
    rows, kv_width = q_ref.shape[0], kv_heads * HEAD_DIM
    group, scale = heads // kv_heads, 1.0 / math.sqrt(HEAD_DIM)
    greet([{"seq": lax.rem(me + step, count)} for step in range(1, count)])
    length = length_ref[0]
    query_pos = me * rows + lax.broadcasted_iota(jnp.int32, (rows, rows), 1)
    key_local = lax.broadcasted_iota(jnp.int32, (rows, rows), 0)
    dq_ref[...] = jnp.zeros_like(dq_ref)
    ones = jnp.ones((8, HEAD_DIM), BF16)
    for h in range(heads):
        cols = slice(h * HEAD_DIM, (h + 1) * HEAD_DIM)
        terms = grad_ref[:, cols].astype(F32) * attended_ref[:, cols].astype(F32)
        high = terms.astype(BF16)
        low = (terms - high.astype(F32)).astype(BF16)
        delta_ref[h : h + 1, :] = (nt(ones, high) + nt(ones, low))[:1]

    def key_block(j):
        key_pos = j * rows + key_local
        mask = (key_pos <= query_pos) & (key_pos < length)
        part_ref[...] = jnp.zeros_like(part_ref)
        key_rows = pl.ds(pl.multiple_of(j * rows, rows), rows)
        for g in range(kv_heads):
            key_cols = slice(g * HEAD_DIM, (g + 1) * HEAD_DIM)
            value_cols = slice(kv_width + g * HEAD_DIM, kv_width + (g + 1) * HEAD_DIM)

            def one_head(i, carry):
                h = g * group + i
                cols = pl.ds(pl.multiple_of(h * HEAD_DIM, HEAD_DIM), HEAD_DIM)
                keys, values = kv_ref[key_rows, key_cols], kv_ref[key_rows, value_cols]
                queries, grads = q_ref[:, cols], grad_ref[:, cols]
                scores = nt(keys, queries) * scale
                probs = jnp.where(mask, jnp.exp(scores - lse_ref[pl.ds(h, 1), :]), 0.0)
                prob_grad = nt(values, grads)
                score_grad = (probs * (prob_grad - delta_ref[pl.ds(h, 1), :])).astype(BF16)
                part_ref[:, key_cols] += nn(score_grad, queries)
                part_ref[:, value_cols] += nn(probs.astype(BF16), grads)
                dq_ref[:, cols] += tn(score_grad, keys)
                return carry

            lax.fori_loop(0, group, one_head, 0, unroll=3)
        part_ref[:, :kv_width] = part_ref[:, :kv_width] * scale

    def to_owner(j):
        return pltpu.make_async_remote_copy(
            src_ref=leaving.at[j],
            dst_ref=arriving.at[me],
            send_sem=send.at[j],
            recv_sem=recv.at[me],
            device_id={"seq": j},
            device_id_type=MESH_IDS,
        )

    def other_block(j, carry):
        key_block(j)
        leaving[j] = part_ref[...].astype(BF16)
        to_owner(j).start()
        return carry

    lax.fori_loop(0, me, other_block, 0)
    key_block(me)
    part_ref[...] = part_ref[...].astype(BF16).astype(F32)
    cosines, sines = cos_ref[...], -sin_ref[...]

    def one_query(h, carry):
        cols = pl.ds(pl.multiple_of(h * HEAD_DIM, HEAD_DIM), HEAD_DIM)
        out_ref[:, cols] = rotate(dq_ref[:, cols] * scale, cosines, sines).astype(BF16)
        return carry

    lax.fori_loop(0, heads, one_query, 0)

    def add_arrived(m, carry):
        pltpu.make_async_remote_copy(
            src_ref=leaving.at[m],
            dst_ref=arriving.at[m],
            send_sem=send.at[m],
            recv_sem=recv.at[m],
            device_id={"seq": m},
            device_id_type=MESH_IDS,
        ).wait_recv()
        part_ref[...] += arriving[m].astype(F32)
        return carry

    lax.fori_loop(me + 1, count, add_arrived, 0)
    first = heads * HEAD_DIM
    for g in range(kv_heads):
        cols = slice(g * HEAD_DIM, (g + 1) * HEAD_DIM)
        out_ref[:, first + g * HEAD_DIM : first + (g + 1) * HEAD_DIM] = rotate(
            part_ref[:, cols], cosines, sines
        ).astype(BF16)
    out_ref[:, first + kv_width :] = part_ref[:, kv_width:].astype(BF16)

    def sent(j, carry):
        to_owner(j).wait_send()
        return carry

    lax.fori_loop(0, me, sent, 0)


def attention_back(length, queries, kv_all, grads, lse, attended, cosines, sines, collective_id):
    count = lax.axis_size("seq")
    rows, q_width = queries.shape
    kv_width = kv_all.shape[1] // 2
    heads, kv_heads = q_width // HEAD_DIM, kv_width // HEAD_DIM
    vmem = pl.BlockSpec(memory_space=pltpu.VMEM)
    return pl.pallas_call(
        functools.partial(attention_back_kernel, count, heads, kv_heads),
        out_shape=jax.ShapeDtypeStruct((rows, q_width + 2 * kv_width), BF16),
        in_specs=[pl.BlockSpec(memory_space=pltpu.SMEM)] + [vmem] * 7,
        out_specs=vmem,
        scratch_shapes=[
            pltpu.VMEM((heads, rows), F32),
            pltpu.VMEM((rows, q_width), F32),
            pltpu.VMEM((rows, 2 * kv_width), F32),
            pltpu.VMEM((count, rows, 2 * kv_width), BF16),
            pltpu.VMEM((count, rows, 2 * kv_width), BF16),
            pltpu.SemaphoreType.DMA((count,)),
            pltpu.SemaphoreType.DMA((count,)),
        ],
        compiler_params=pltpu.CompilerParams(
            collective_id=collective_id, vmem_limit_bytes=30 << 20
        ),
        cost_estimate=pl.CostEstimate(
            flops=10 * count * rows * rows * q_width, bytes_accessed=1 << 20, transcendentals=0
        ),
        name="attention_backward",
    )(length, queries, kv_all, grads, lse, attended, cosines, sines)


def weight_grad_kernel(n, *refs):
    lefts, rights, outs = refs[:2], refs[2 : 2 + 2 * n], refs[2 + 2 * n :]
    for k, out_ref in enumerate(outs):
        early, late = rights[2 * k : 2 * k + 2]
        total = tn(lefts[0][...], early[...]) + tn(lefts[1][...], late[...])
        out_ref[...] = total.astype(BF16)


def weight_grads(lefts, rights, name):
    columns, tile = lefts[0].shape[1], 256
    flat = [part for pair in rights for part in pair]
    return pl.pallas_call(
        functools.partial(weight_grad_kernel, len(rights)),
        grid=(columns // tile,),
        out_shape=[jax.ShapeDtypeStruct((columns, r[0].shape[1]), BF16) for r in rights],
        in_specs=[pl.BlockSpec((x.shape[0], tile), lambda i: (0, i)) for x in lefts]
        + [pl.BlockSpec(r.shape, lambda i: (0, 0), pipeline_mode=pl.Buffered(1)) for r in flat],
        out_specs=[pl.BlockSpec((tile, r[0].shape[1]), lambda i: (i, 0)) for r in rights],
        compiler_params=pltpu.CompilerParams(vmem_limit_bytes=48 << 20),
        cost_estimate=pl.CostEstimate(flops=0, bytes_accessed=1 << 20, transcendentals=0),
        name=name,
    )(*lefts, *flat)


def seq_permutes(block_for):
    count, me = lax.axis_size("seq"), lax.axis_index("seq")
    pieces = [block_for(me)]
    for step in range(1, count):
        ring = [(i, (i + step) % count) for i in range(count)]
        pieces.append(lax.ppermute(block_for(lax.rem(me + step, count)), "seq", ring))
    return pieces


def in_seq_order(pieces, dtype):
    count, me = len(pieces), lax.axis_index("seq")
    whole = jnp.zeros((count,) + pieces[0].shape, dtype)
    for step, piece in enumerate(pieces):
        place = lax.rem(me + count - step, count)
        whole = lax.dynamic_update_index_in_dim(whole, piece.astype(dtype), place, 0)
    return whole


def on_device(
    hidden_in,
    lengths,
    routes,
    gates,
    priority,
    attn_gain,
    mlp_gain,
    w_query,
    key_projection,
    value_projection,
    w_out,
    w_gate,
    w_up,
    w_down,
    cotangent,
):
    rows = hidden_in.shape[1]
    width = hidden_in.shape[2]
    dp_count = lax.axis_size("dp")
    seq_count = lax.axis_size("seq")
    devices = dp_count * seq_count
    own_experts = w_gate.shape[0]
    sharers = seq_count // own_experts
    hidden_units = w_gate.shape[2]
    my_seq = lax.axis_index("seq")
    extent = rows * seq_count
    query_pos = my_seq * rows + jnp.arange(rows, dtype=jnp.int32)
    length = lengths[0]
    is_valid = query_pos < length
    q_width = w_query.shape[1]
    kv_width = key_projection.shape[1]
    cosine_lookup, sine_lookup = rope_angles(query_pos, HEAD_DIM)

    gain_block = jnp.concatenate(
        [attn_gain[:, None], mlp_gain[:, None], jnp.zeros((attn_gain.shape[0], LANES - 2), BF16)],
        axis=1,
    )
    packed = jnp.concatenate([w_query, key_projection, value_projection], axis=1)
    staged = seq_count == 4 and w_query.shape[0] % 16 == 0

    def expert_pieces(weights):
        def block_for(peer):
            return lax.dynamic_index_in_dim(weights, peer // sharers, 0, keepdims=False)

        return seq_permutes(block_for)

    gate_parts = expert_pieces(w_gate)
    if staged:
        packed_full, gains_full, out_full = staged_gather(
            [packed, gain_block, w_out], [], None, 2, "gather_attention_weights"
        )
    else:
        packed_full = lax.all_gather(packed, BOTH, axis=0, tiled=True)
        gains_full = lax.all_gather(gain_block, BOTH, axis=0, tiled=True)
        out_full = lax.all_gather(w_out, BOTH, axis=0, tiled=True)

    pair_routes, place, kept = claim_places(routes[0], priority[0, 0], is_valid)
    holder = (pair_routes // own_experts) * seq_count + (pair_routes % own_experts) * sharers
    holder = holder + my_seq * sharers // seq_count
    slots = devices * CAP
    target = jnp.where(kept, holder * CAP + place, slots).reshape(rows, TOP)
    slot_ids = jnp.arange(slots, dtype=jnp.int32)
    hits = target[:, :, None] == slot_ids[None, None, :]
    gate_rows = gates[0]
    token_hot = jnp.any(hits, axis=1).astype(BF16)

    def hot_of(first, size):
        mine = kept & (place >= first) & (place < first + size)
        spot = jnp.where(mine, holder * size + place - first, slots).reshape(rows, TOP)
        ids = jnp.arange(devices * size, dtype=jnp.int32)
        return jnp.any(spot[:, :, None] == ids[None, None, :], axis=1).astype(BF16)

    early_hot, late_hot = hot_of(0, EARLY), hot_of(EARLY, CAP - EARLY)
    slot_gate = jnp.sum(jnp.where(hits, gate_rows[:, :, None], 0.0), axis=(0, 1))

    live_cotangent = jnp.where(is_valid[:, None], cotangent[0], jnp.zeros((), BF16))
    out_grad = live_cotangent.astype(F32)
    grad_send = (tn(token_hot, live_cotangent) * slot_gate[:, None]).astype(BF16)
    packed_full, gains_full, out_full, gate_parts, grad_send = lax.optimization_barrier(
        (packed_full, gains_full, out_full, gate_parts, grad_send)
    )
    gain_one, gain_two = gains_full[:, 0].astype(F32), gains_full[:, 1].astype(F32)
    grad_rows = swap(grad_send.reshape(devices, CAP, width), ("dp", "seq"))

    inputs = hidden_in[0].astype(F32)
    scale_one = lax.rsqrt(jnp.mean(inputs * inputs, axis=-1, keepdims=True) + EPSILON)
    normed = (inputs * scale_one * gain_one).astype(BF16)
    projected = nn(normed, packed_full)
    cosines, sines = cosine_lookup[:, 0], sine_lookup[:, 0]
    cosines = jnp.concatenate([cosines, cosines], axis=1)
    sines = jnp.concatenate([-sines, sines], axis=1)
    attended, log_total, query_flat, kv_all = attention(
        lengths, projected, cosines, sines, q_width, 1
    )
    kv_all = kv_all.reshape(extent, 2 * kv_width)
    attended, w_up = lax.optimization_barrier((attended, w_up))
    up_parts = expert_pieces(w_up)
    middle = inputs + nn(attended, out_full)
    scale_two = lax.rsqrt(jnp.mean(middle * middle, axis=-1, keepdims=True) + EPSILON)
    moe_input = (middle * scale_two * gain_two).astype(BF16)

    def to_experts(hot):
        return tn(hot, moe_input).astype(BF16).reshape(devices, -1, width)

    early_send, late_send = to_experts(early_hot), to_experts(late_hot)
    early_send, late_send, grad_rows, up_parts, w_down = lax.optimization_barrier(
        (early_send, late_send, grad_rows, up_parts, w_down)
    )
    early_grads, late_grads, w_down = lax.optimization_barrier(
        (grad_rows[:, :EARLY], grad_rows[:, EARLY:], w_down)
    )
    down_parts = expert_pieces(w_down)
    early_rows = swap(early_send, ("dp", "seq"))
    early_rows, late_send = lax.optimization_barrier((early_rows, late_send))
    late_rows = swap(late_send, ("dp", "seq"))
    gate_full = in_seq_order(gate_parts, BF16).reshape(width, hidden_units)
    up_full = in_seq_order(up_parts, BF16).reshape(width, hidden_units)
    down_full = in_seq_order(down_parts, BF16).reshape(hidden_units, width)
    early_rows, gate_full, up_full, down_full, early_grads, late_grads = (
        lax.optimization_barrier(
            (early_rows, gate_full, up_full, down_full, early_grads, late_grads)
        )
    )

    def run_expert(slot_rows, grads):
        blocks = slot_rows.shape[:2]
        slot_rows, grads = slot_rows.reshape(-1, width), grads.reshape(-1, width)
        gate_pre = nn(slot_rows, gate_full)
        up_pre = nn(slot_rows, up_full)
        gate_sigmoid = jax.nn.sigmoid(gate_pre)
        gate_act = gate_pre * gate_sigmoid
        gate_slope = gate_sigmoid * (1.0 + gate_pre * (1.0 - gate_sigmoid))
        hidden = (gate_act * up_pre).astype(BF16)
        hidden_grad = nt(grads, down_full)
        gate_pre_grad = (hidden_grad * up_pre * gate_slope).astype(BF16)
        up_pre_grad = (hidden_grad * gate_act).astype(BF16)
        return [x.reshape(blocks + (-1,)) for x in (hidden, gate_pre_grad, up_pre_grad)]

    def row_grads(gate_pre_grad, up_pre_grad):
        blocks = gate_pre_grad.shape[:2]
        gate_pre_grad = gate_pre_grad.reshape(-1, hidden_units)
        up_pre_grad = up_pre_grad.reshape(-1, hidden_units)
        row_grad = (nt(gate_pre_grad, gate_full) + nt(up_pre_grad, up_full)).astype(BF16)
        return row_grad.reshape(blocks + (width,))

    def both_parts(early, late):
        return jnp.concatenate([early, late], axis=1).reshape(slots, -1)

    def to_owners(grad):
        grad = grad.reshape(seq_count, -1, grad.shape[1])

        def block_for(peer):
            return lax.dynamic_index_in_dim(grad, peer, 0, keepdims=False)

        return seq_permutes(block_for)

    def owned_sum(pieces):
        whole = in_seq_order(pieces, F32)
        return jnp.sum(whole.reshape((own_experts, sharers) + whole.shape[1:]), axis=1)

    early_hidden, *early_pre_grads = run_expert(early_rows, early_grads)
    early_row_grad = row_grads(*early_pre_grads)
    late_rows, early_row_grad = lax.optimization_barrier((late_rows, early_row_grad))
    early_back = swap(early_row_grad, ("dp", "seq"))
    late_hidden, *late_pre_grads = run_expert(late_rows, late_grads)

    def flat(*parts):
        return [part.reshape(-1, part.shape[-1]) for part in parts]

    gate_grad, up_grad = weight_grads(
        flat(early_rows, late_rows),
        [flat(*pair) for pair in zip(early_pre_grads, late_pre_grads, strict=True)],
        "gate_up_grads",
    )
    late_pre_grads, late_hidden, gate_grad, up_grad = lax.optimization_barrier(
        (late_pre_grads, late_hidden, gate_grad, up_grad)
    )
    gate_grad_parts = to_owners(gate_grad)
    late_row_grad = row_grads(*late_pre_grads)
    early_back, late_row_grad, gate_grad_parts, up_grad, late_hidden = lax.optimization_barrier(
        (early_back, late_row_grad, gate_grad_parts, up_grad, late_hidden)
    )
    expert_hidden = both_parts(early_hidden, late_hidden)
    late_back = swap(late_row_grad, ("dp", "seq"))
    gate_owned, up_owned = owned_sum(gate_grad_parts), owned_sum(to_owners(up_grad))
    (down_grad,) = weight_grads(
        flat(early_hidden, late_hidden), [flat(early_grads, late_grads)], "down_grads"
    )
    expert_out = nn(expert_hidden, down_full).astype(BF16)
    expert_out, late_back, gate_owned, up_owned, down_grad = lax.optimization_barrier(
        (expert_out, late_back, gate_owned, up_owned, down_grad)
    )
    returned = swap(expert_out.reshape(devices, CAP, width), ("dp", "seq")).reshape(slots, width)
    early_back, late_back = early_back.reshape(-1, width), late_back.reshape(-1, width)
    moe_input_grad = nn(early_hot, early_back) + nn(late_hot, late_back)
    middle_norm_grad, gain_two_grad = norm_back(middle, scale_two, gain_two, moe_input_grad)
    middle_grad = out_grad + middle_norm_grad
    branch_grad = middle_grad.astype(BF16)
    out_terms = tn(attended, branch_grad).astype(BF16)
    attended_grad = nt(branch_grad, out_full).astype(BF16)
    projected_grad = attention_back(
        lengths,
        query_flat,
        kv_all,
        attended_grad,
        log_total,
        attended,
        cosines,
        sines,
        4,
    )
    normed_grad = nt(projected_grad, packed_full)
    input_norm_grad, gain_one_grad = norm_back(inputs, scale_one, gain_one, normed_grad)
    input_grad = middle_grad + input_norm_grad

    lane = lax.broadcasted_iota(jnp.int32, (width, LANES), 1)
    gain_terms = jnp.where(lane == 0, gain_one_grad[:, None], gain_two_grad[:, None])
    gain_terms = jnp.where(lane < 2, gain_terms, 0.0).astype(BF16)
    query_terms = tn(normed, projected_grad).astype(BF16)
    if staged:
        out_owned, gains_owned, owned, down_owned = staged_scatter(
            [out_terms, gain_terms, query_terms],
            [down_grad.reshape(seq_count, -1, width)],
            lambda ref, peer: ref.at[peer],
            6,
            "scatter_attention_grads",
        )
        down_owned = down_owned.reshape((own_experts, sharers) + down_owned.shape[1:])
        down_owned = jnp.sum(down_owned.astype(F32), axis=1)
    else:
        terms = jnp.concatenate([out_terms, gain_terms, query_terms], axis=1)
        terms = lax.psum_scatter(terms, BOTH, scatter_dimension=0, tiled=True).astype(F32)
        out_owned, gains_owned = terms[:, :width], terms[:, width : width + LANES]
        owned = terms[:, width + LANES :]
        down_owned = owned_sum(to_owners(down_grad))
    returned, owned = lax.optimization_barrier((returned, owned))
    expert_grads = [gate_owned, up_owned, down_owned]

    gate_hot = jnp.sum(jnp.where(hits, gate_rows[:, :, None], 0.0), axis=1).astype(BF16)
    layer_out = middle + nn(gate_hot, returned)
    return (
        layer_out[None],
        input_grad[None],
        gains_owned[:, 0],
        gains_owned[:, 1],
        owned[:, :q_width],
        owned[:, q_width : q_width + kv_width],
        owned[:, q_width + kv_width : q_width + 2 * kv_width],
        out_owned,
        *expert_grads,
    )


def solution(mesh):
    part = P("dp", "seq", None)
    both = P(BOTH)
    both_rows = P(BOTH, None)
    return jax.shard_map(
        on_device,
        mesh=mesh,
        in_specs=(part, P("dp"), part, part, part, both, both)
        + (both_rows,) * 4
        + (part,) * 4,
        out_specs=(part, part, both, both) + (both_rows,) * 4 + (part,) * 3,
        check_vma=False,
    )
```

```python
import functools
import math

import jax
import jax.numpy as jnp
from jax import lax
from jax.experimental import pallas as pl
from jax.experimental.pallas import tpu as pltpu
from jax.sharding import PartitionSpec as P

HEAD_DIM = 128
EXPERTS = 32
TOP = 4
CAP = 40
EARLY = 24

EPSILON = 1e-06
ROPE_BASE = 10000.0
NEG_FILL = -1e30
LANES = 128
BOTH = ("seq", "dp")
BF16 = jnp.bfloat16
F32 = jnp.float32


def rope_angles(positions, head_size):
    half_dim = head_size // 2
    frequency = ROPE_BASE ** (-(2.0 * jnp.arange(half_dim, dtype=F32)) / head_size)
    angles = positions.astype(F32)[:, None] * frequency[None, :]
    return (jnp.cos(angles)[:, None, :], jnp.sin(angles)[:, None, :])


def dot(left, right, contract):
    return lax.dot_general(left, right, (contract, ((), ())), preferred_element_type=F32)


def nn(left, right):
    return dot(left, right, ((1,), (0,)))


def nt(left, right):
    return dot(left, right, ((1,), (1,)))


def tn(left, right):
    return dot(left, right, ((0,), (0,)))


def claim_places(routes, priority, is_valid):
    pair_routes = routes.reshape(-1)
    live = jnp.repeat(is_valid, TOP)
    key = jnp.where(live, pair_routes, -1)
    earlier = (key[None, :] == pair_routes[:, None]) & (priority[None, :] < priority[:, None])
    place = jnp.sum(earlier.astype(F32), axis=1).astype(jnp.int32)
    return pair_routes, place, live & (place < CAP)


def norm_back(values, scale_rows, gain_vec, incoming):
    weighted = incoming * gain_vec
    inner_mean = jnp.mean(weighted * values, axis=-1, keepdims=True)
    values_grad = scale_rows * weighted - values * scale_rows * scale_rows * scale_rows * inner_mean
    return (values_grad, jnp.sum(incoming * values * scale_rows, axis=0))


def swap(blocks, axes):
    return lax.all_to_all(blocks, axes, split_axis=0, concat_axis=0, tiled=True)


MESH_IDS = pl.DeviceIdType.MESH


def torus_place():
    seq, dp = lax.axis_index("seq"), lax.axis_index("dp")
    return seq // 2, seq % 2, dp // 2, dp % 2


def torus_id(a, b, z, c):
    return {"seq": 2 * a + b, "dp": 2 * z + c}


def torus_peers(line):
    a, b, z, c = torus_place()
    peers = [torus_id(a, b, z, 1 - c), torus_id(a, 1 - b, z, c), torus_id(1 - a, b, z, c)]
    peers.append(torus_id(1 - a, 1 - b, z, c))
    return peers + [torus_id(a, b, lax.rem(z + k, line), c) for k in range(1, line)]


def greet(peers):
    barrier = pltpu.get_barrier_semaphore()
    for peer in peers:
        pl.semaphore_signal(barrier, inc=1, device_id=peer, device_id_type=MESH_IDS)
    pl.semaphore_wait(barrier, len(peers))


def column_chunks(widths, parts):
    chunks = []
    for part in range(parts):
        for k, whole in enumerate(widths):
            tiles = whole // LANES
            first, end = tiles * part // parts, tiles * (part + 1) // parts
            if end > first:
                chunks.append((k, first * LANES, (end - first) * LANES))
    return chunks


def first_links(chunks):
    loads, choices = [0, 0], []
    for _, _, size in chunks:
        link = int(loads[0] > loads[1])
        loads[link] += 2 * size
        loads[1 - link] += size
        choices.append(link == 0)
    return choices


def remote(src, dst, sems, i, j, device_id):
    send, recv = sems
    return pltpu.make_async_remote_copy(
        src_ref=src,
        dst_ref=dst,
        send_sem=send.at[i, j],
        recv_sem=recv.at[i, j],
        device_id=device_id,
        device_id_type=MESH_IDS,
    )


def start_exchange(count, sources, targets, block_of, sems):
    send_sems, recv_sems, local_sems = sems
    me = lax.axis_index("seq")
    copies = []
    for i, source in enumerate(sources):
        for step in range(1, count):
            peer = lax.rem(me + step, count)
            copies.append(
                pltpu.make_async_remote_copy(
                    src_ref=block_of(source, peer),
                    dst_ref=targets[i].at[me],
                    send_sem=send_sems.at[i, step - 1],
                    recv_sem=recv_sems.at[i, step - 1],
                    device_id={"seq": peer},
                    device_id_type=MESH_IDS,
                )
            )
        copies.append(
            pltpu.make_async_copy(block_of(source, me), targets[i].at[me], local_sems.at[i])
        )
    for copy in copies:
        copy.start()
    return copies


def exchange_sems(n, count):
    return [
        pltpu.SemaphoreType.DMA((n, count - 1)),
        pltpu.SemaphoreType.DMA((n, count - 1)),
        pltpu.SemaphoreType.DMA((n,)),
    ]


def in_steps(count, stages, after=None):
    for step in range((count + 1) // 2 + len(stages) - 1):
        if after is not None and step == 1:
            after()
        for behind, stage in enumerate(stages):
            for i in (2 * (step - behind), 2 * (step - behind) + 1):
                if 0 <= i < count:
                    stage(i)


def gather_kernel(line, chunks, n, extras, block_of, *refs):
    sources, more_sources = refs[:n], refs[n : n + extras]
    refs = refs[n + extras :]
    targets, more_targets = refs[:n], refs[n : n + extras]
    send, recv, local, *more_sems = refs[n + extras :]
    sems = (send, recv)
    a, b, z, c = torus_place()
    over_b = first_links(chunks)
    greet(torus_peers(line))
    more = start_exchange(4, more_sources, more_targets, block_of, more_sems) if extras else []
    sent = []

    def start(copy):
        copy.start()
        sent.append(copy)
        return copy

    along_line, first_hop, second_hop, third_hop = {}, {}, {}, {}

    def send_line(i):
        k, first, size = chunks[i]
        cols = pl.ds(first, size)
        own = targets[k].at[a, b, z, c, :, cols]
        keep = pltpu.make_async_copy(sources[k].at[:, cols], own, local.at[i])
        keep.start()
        along_line[i] = [
            start(
                remote(
                    sources[k].at[:, cols],
                    own,
                    sems,
                    i,
                    2 + step,
                    torus_id(a, b, lax.rem(z + step, line), c),
                )
            )
            for step in range(1, line)
        ]
        along_line[i].append(keep)

    def send_first(i):
        k, first, size = chunks[i]
        *copies, keep = along_line[i]
        keep.wait()
        for copy in copies:
            copy.wait_recv()
        block = targets[k].at[a, b, :, c, :, pl.ds(first, size)]
        peer = torus_id(a, 1 - b, z, c) if over_b[i] else torus_id(1 - a, b, z, c)
        first_hop[i] = start(remote(block, block, sems, i, 1, peer))

    def send_second(i):
        k, first, size = chunks[i]
        first_hop[i].wait_recv()
        cols = pl.ds(first, size)
        if over_b[i]:
            block, peer = targets[k].at[a, :, :, c, :, cols], torus_id(1 - a, b, z, c)
        else:
            block, peer = targets[k].at[:, b, :, c, :, cols], torus_id(a, 1 - b, z, c)
        second_hop[i] = start(remote(block, block, sems, i, 2, peer))

    def send_third(i):
        k, first, size = chunks[i]
        second_hop[i].wait_recv()
        block = targets[k].at[:, :, :, c, :, pl.ds(first, size)]
        third_hop[i] = start(remote(block, block, sems, i, 0, torus_id(a, b, z, 1 - c)))

    in_steps(len(chunks), [send_line, send_first, send_second, send_third])
    for copy in third_hop.values():
        copy.wait_recv()
    for copy in sent:
        copy.wait_send()
    for copy in more:
        copy.wait()


def staged_gather(arrays, extras, block_of, collective_id, name, parts=6):
    seq_count, line = lax.axis_size("seq"), lax.axis_size("dp") // 2
    rows, n = arrays[0].shape[0], len(arrays)
    chunks = column_chunks([x.shape[1] for x in arrays], parts)
    m = len(chunks)
    shape = (seq_count // 2, 2, line, 2, rows)
    size = sum(x.shape[1] for x in arrays) * rows * 64
    count = n + len(extras)
    outs = pl.pallas_call(
        functools.partial(gather_kernel, line, chunks, n, len(extras), block_of),
        out_shape=[jax.ShapeDtypeStruct(shape + (x.shape[1],), BF16) for x in arrays]
        + [jax.ShapeDtypeStruct((seq_count,) + x.shape[1:], BF16) for x in extras],
        in_specs=[pl.BlockSpec(memory_space=pl.ANY)] * count,
        out_specs=[pl.BlockSpec(memory_space=pl.ANY)] * count,
        scratch_shapes=[
            pltpu.SemaphoreType.DMA((m, 2 + line)),
            pltpu.SemaphoreType.DMA((m, 2 + line)),
            pltpu.SemaphoreType.DMA((m,)),
        ]
        + (exchange_sems(len(extras), seq_count) if extras else []),
        compiler_params=pltpu.CompilerParams(
            collective_id=collective_id, vmem_limit_bytes=56 << 20
        ),
        cost_estimate=pl.CostEstimate(flops=0, bytes_accessed=size, transcendentals=0),
        name=name,
    )(*arrays, *extras)
    return [o.reshape(-1, o.shape[-1]) for o in outs]


def scatter_kernel(line, chunks, n, extras, block_of, *refs):
    m = len(chunks)
    sources, more_sources = refs[:n], refs[n : n + extras]
    refs = refs[n + extras :]
    targets, more_targets = refs[:n], refs[n : n + extras]
    scratch = refs[n + extras :]
    owns, ins1, accs2, ins2, accs3, ins3, ins4 = (scratch[m * s : m * (s + 1)] for s in range(7))
    send, recv, local, *more_sems = scratch[7 * m :]
    sems = (send, recv)
    a, b, z, c = torus_place()
    over_b = first_links(chunks)
    greet(torus_peers(line))
    sent = []

    def start(copy):
        copy.start()
        sent.append(copy)
        return copy

    def add_lines(target, left, right):
        def one(j, carry):
            target[j] = (left[j].astype(F32) + right[j].astype(F32)).astype(BF16)
            return carry

        lax.fori_loop(0, line, one, 0)

    between_cores, first_hop, second_hop, along_line = {}, {}, {}, {}

    def send_core(i):
        k, first, size = chunks[i]
        cols = pl.ds(first, size)
        keep = pltpu.make_async_copy(sources[k].at[:, :, :, c, :, cols], owns[i], local.at[i])
        keep.start()
        swap_core = remote(
            sources[k].at[:, :, :, 1 - c, :, cols], ins1[i], sems, i, 0, torus_id(a, b, z, 1 - c)
        )
        between_cores[i] = (keep, start(swap_core))

    def send_first(i):
        keep, copy = between_cores[i]
        keep.wait()
        copy.wait_recv()
        for p in range(2):
            for q in range(2):
                add_lines(owns[i].at[p, q], owns[i].at[p, q], ins1[i].at[p, q])
        if over_b[i]:
            block, peer = owns[i].at[:, 1 - b], torus_id(a, 1 - b, z, c)
        else:
            block, peer = owns[i].at[1 - a], torus_id(1 - a, b, z, c)
        first_hop[i] = start(remote(block, ins2[i], sems, i, 1, peer))

    def send_second(i):
        first_hop[i].wait_recv()
        for p in range(2):
            mine = owns[i].at[p, b] if over_b[i] else owns[i].at[a, p]
            add_lines(accs2[i].at[p], mine, ins2[i].at[p])
        if over_b[i]:
            block, peer = accs2[i].at[1 - a], torus_id(1 - a, b, z, c)
        else:
            block, peer = accs2[i].at[1 - b], torus_id(a, 1 - b, z, c)
        second_hop[i] = start(remote(block, ins3[i], sems, i, 2, peer))

    def send_line(i):
        second_hop[i].wait_recv()
        add_lines(accs3[i], accs2[i].at[a if over_b[i] else b], ins3[i])
        copies = []
        for step in range(1, line):
            to = lax.rem(z + step, line)
            peer = torus_id(a, b, to, c)
            copies.append(start(remote(accs3[i].at[to], ins4[i].at[z], sems, i, 2 + step, peer)))
        along_line[i] = copies

    def finish(i):
        k, first, size = chunks[i]
        total = accs3[i][z].astype(F32)
        for step in range(1, line):
            along_line[i][step - 1].wait_recv()
            total = total + ins4[i][lax.rem(z + line - step, line)].astype(F32)
        targets[k][:, first : first + size] = total

    more = []

    def send_more():
        if extras:
            more.extend(start_exchange(4, more_sources, more_targets, block_of, more_sems))

    in_steps(m, [send_core, send_first, send_second, send_line, finish], send_more)
    for copy in sent:
        copy.wait_send()
    for copy in more:
        copy.wait()


def staged_scatter(arrays, extras, block_of, collective_id, name, parts=6):
    seq_count, line = lax.axis_size("seq"), lax.axis_size("dp") // 2
    rows, n = arrays[0].shape[0] // (2 * line * seq_count), len(arrays)
    chunks = column_chunks([x.shape[1] for x in arrays], parts)
    m = len(chunks)
    leads = [(2, 2, line), (2, 2, line), (2, line), (2, line), (line,), (line,), (line,)]
    size = sum(x.shape[1] for x in arrays) * rows * 64
    anywhere = pl.BlockSpec(memory_space=pl.ANY)
    return pl.pallas_call(
        functools.partial(scatter_kernel, line, chunks, n, len(extras), block_of),
        out_shape=[jax.ShapeDtypeStruct((rows, x.shape[1]), F32) for x in arrays]
        + [jax.ShapeDtypeStruct((seq_count,) + x.shape[1:], BF16) for x in extras],
        in_specs=[anywhere] * (n + len(extras)),
        out_specs=[pl.BlockSpec(memory_space=pltpu.VMEM)] * n + [anywhere] * len(extras),
        scratch_shapes=[
            pltpu.VMEM(lead + (rows, width), BF16) for lead in leads for _, _, width in chunks
        ]
        + [
            pltpu.SemaphoreType.DMA((m, 2 + line)),
            pltpu.SemaphoreType.DMA((m, 2 + line)),
            pltpu.SemaphoreType.DMA((m,)),
        ]
        + (exchange_sems(len(extras), seq_count) if extras else []),
        compiler_params=pltpu.CompilerParams(
            collective_id=collective_id, vmem_limit_bytes=36 << 20
        ),
        cost_estimate=pl.CostEstimate(flops=0, bytes_accessed=size, transcendentals=0),
        name=name,
    )(*[x.reshape(2, 2, line, 2, rows, x.shape[1]) for x in arrays], *extras)


def rotate(values, cosines, sines):
    return values * cosines + pltpu.roll(values, HEAD_DIM // 2, 1) * sines


def attention_kernel(count, heads, kv_heads, *refs):
    length_ref, projected_ref, cos_ref, sin_ref = refs[:4]
    attended_ref, lse_ref, q_ref, kv_ref = refs[4:8]
    max_ref, sum_ref, acc_ref, send, recv = refs[8:]
    me = lax.axis_index("seq")
    rows, kv_width = q_ref.shape[0], kv_heads * HEAD_DIM
    q_width, group, scale = heads * HEAD_DIM, heads // kv_heads, 1.0 / math.sqrt(HEAD_DIM)
    greet([{"seq": lax.rem(me + step, count)} for step in range(1, count)])
    cosines, sines = cos_ref[...], sin_ref[...]
    for g in range(kv_heads):
        cols = slice(g * HEAD_DIM, (g + 1) * HEAD_DIM)
        keys = projected_ref[:, q_width + g * HEAD_DIM : q_width + (g + 1) * HEAD_DIM]
        kv_ref[me, :, cols] = rotate(keys, cosines, sines).astype(BF16)
    kv_ref[me, :, kv_width:] = projected_ref[:, q_width + kv_width :].astype(BF16)

    def to_later(peer):
        return pltpu.make_async_remote_copy(
            src_ref=kv_ref.at[me],
            dst_ref=kv_ref.at[me],
            send_sem=send.at[peer],
            recv_sem=recv.at[me],
            device_id={"seq": peer},
            device_id_type=MESH_IDS,
        )

    def start(peer, carry):
        to_later(peer).start()
        return carry

    lax.fori_loop(me + 1, count, start, 0)

    def one_query(h, carry):
        cols = pl.ds(pl.multiple_of(h * HEAD_DIM, HEAD_DIM), HEAD_DIM)
        q_ref[:, cols] = rotate(projected_ref[:, cols], cosines, sines).astype(BF16)
        return carry

    lax.fori_loop(0, heads, one_query, 0)
    max_ref[...] = jnp.full_like(max_ref, NEG_FILL)
    sum_ref[...] = jnp.zeros_like(sum_ref)
    acc_ref[...] = jnp.zeros_like(acc_ref)
    length = length_ref[0]
    query_pos = me * rows + lax.broadcasted_iota(jnp.int32, (rows, rows), 1)
    key_local = lax.broadcasted_iota(jnp.int32, (rows, rows), 0)

    def key_block(j):
        key_pos = j * rows + key_local
        mask = (key_pos <= query_pos) & (key_pos < length)
        for g in range(kv_heads):
            key_cols = slice(g * HEAD_DIM, (g + 1) * HEAD_DIM)
            value_cols = slice(kv_width + g * HEAD_DIM, kv_width + (g + 1) * HEAD_DIM)

            def one_head(i, carry):
                h = g * group + i
                cols = pl.ds(pl.multiple_of(h * HEAD_DIM, HEAD_DIM), HEAD_DIM)
                row = pl.ds(h, 1)
                keys, values = kv_ref[j, :, key_cols], kv_ref[j, :, value_cols]
                scores = jnp.where(mask, nt(keys, q_ref[:, cols]) * scale, NEG_FILL)
                before = max_ref[row, :]
                top = jnp.maximum(before, jnp.max(scores, axis=0, keepdims=True))
                shrink = jnp.exp(before - top)
                weights = jnp.exp(scores - top)
                max_ref[row, :] = top
                sum_ref[row, :] = sum_ref[row, :] * shrink + jnp.sum(weights, axis=0, keepdims=True)
                acc_ref[h] = acc_ref[h] * shrink + tn(values, weights.astype(BF16))
                return carry

            lax.fori_loop(0, group, one_head, 0, unroll=3)

    key_block(me)

    def earlier_block(j, carry):
        pltpu.make_async_remote_copy(
            src_ref=kv_ref.at[j],
            dst_ref=kv_ref.at[j],
            send_sem=send.at[j],
            recv_sem=recv.at[j],
            device_id={"seq": j},
            device_id_type=MESH_IDS,
        ).wait_recv()
        key_block(j)
        return carry

    lax.fori_loop(0, me, earlier_block, 0)
    lse_ref[...] = max_ref[...] + jnp.log(sum_ref[...])

    def finish(h, carry):
        cols = pl.ds(pl.multiple_of(h * HEAD_DIM, HEAD_DIM), HEAD_DIM)
        attended_ref[:, cols] = (acc_ref[h] / sum_ref[pl.ds(h, 1), :]).T.astype(BF16)
        return carry

    lax.fori_loop(0, heads, finish, 0)

    def sent(peer, carry):
        to_later(peer).wait_send()
        return carry

    lax.fori_loop(me + 1, count, sent, 0)


def attention(length, projected, cosines, sines, q_width, collective_id):
    count = lax.axis_size("seq")
    rows = projected.shape[0]
    kv_width = (projected.shape[1] - q_width) // 2
    heads, kv_heads = q_width // HEAD_DIM, kv_width // HEAD_DIM
    vmem = pl.BlockSpec(memory_space=pltpu.VMEM)
    return pl.pallas_call(
        functools.partial(attention_kernel, count, heads, kv_heads),
        out_shape=[
            jax.ShapeDtypeStruct((rows, q_width), BF16),
            jax.ShapeDtypeStruct((heads, rows), F32),
            jax.ShapeDtypeStruct((rows, q_width), BF16),
            jax.ShapeDtypeStruct((count, rows, 2 * kv_width), BF16),
        ],
        in_specs=[pl.BlockSpec(memory_space=pltpu.SMEM)] + [vmem] * 3,
        out_specs=[vmem] * 4,
        scratch_shapes=[
            pltpu.VMEM((heads, rows), F32),
            pltpu.VMEM((heads, rows), F32),
            pltpu.VMEM((heads, HEAD_DIM, rows), F32),
            pltpu.SemaphoreType.DMA((count,)),
            pltpu.SemaphoreType.DMA((count,)),
        ],
        compiler_params=pltpu.CompilerParams(
            collective_id=collective_id, vmem_limit_bytes=30 << 20
        ),
        cost_estimate=pl.CostEstimate(flops=0, bytes_accessed=1 << 20, transcendentals=0),
        name="attention_forward",
    )(length, projected, cosines, sines)


def attention_back_kernel(count, heads, kv_heads, *refs):
    length_ref, q_ref, kv_ref, grad_ref, lse_ref, attended_ref, cos_ref, sin_ref = refs[:8]
    out_ref, delta_ref, dq_ref, part_ref, leaving, arriving, send, recv = refs[8:]
    me = lax.axis_index("seq")
    rows, kv_width = q_ref.shape[0], kv_heads * HEAD_DIM
    group, scale = heads // kv_heads, 1.0 / math.sqrt(HEAD_DIM)
    greet([{"seq": lax.rem(me + step, count)} for step in range(1, count)])
    length = length_ref[0]
    query_pos = me * rows + lax.broadcasted_iota(jnp.int32, (rows, rows), 1)
    key_local = lax.broadcasted_iota(jnp.int32, (rows, rows), 0)
    dq_ref[...] = jnp.zeros_like(dq_ref)
    ones = jnp.ones((8, HEAD_DIM), BF16)
    for h in range(heads):
        cols = slice(h * HEAD_DIM, (h + 1) * HEAD_DIM)
        terms = grad_ref[:, cols].astype(F32) * attended_ref[:, cols].astype(F32)
        high = terms.astype(BF16)
        low = (terms - high.astype(F32)).astype(BF16)
        delta_ref[h : h + 1, :] = (nt(ones, high) + nt(ones, low))[:1]

    def key_block(j):
        key_pos = j * rows + key_local
        mask = (key_pos <= query_pos) & (key_pos < length)
        part_ref[...] = jnp.zeros_like(part_ref)
        key_rows = pl.ds(pl.multiple_of(j * rows, rows), rows)
        for g in range(kv_heads):
            key_cols = slice(g * HEAD_DIM, (g + 1) * HEAD_DIM)
            value_cols = slice(kv_width + g * HEAD_DIM, kv_width + (g + 1) * HEAD_DIM)

            def one_head(i, carry):
                h = g * group + i
                cols = pl.ds(pl.multiple_of(h * HEAD_DIM, HEAD_DIM), HEAD_DIM)
                keys, values = kv_ref[key_rows, key_cols], kv_ref[key_rows, value_cols]
                queries, grads = q_ref[:, cols], grad_ref[:, cols]
                scores = nt(keys, queries) * scale
                probs = jnp.where(mask, jnp.exp(scores - lse_ref[pl.ds(h, 1), :]), 0.0)
                prob_grad = nt(values, grads)
                score_grad = (probs * (prob_grad - delta_ref[pl.ds(h, 1), :])).astype(BF16)
                part_ref[:, key_cols] += nn(score_grad, queries)
                part_ref[:, value_cols] += nn(probs.astype(BF16), grads)
                dq_ref[:, cols] += tn(score_grad, keys)
                return carry

            lax.fori_loop(0, group, one_head, 0, unroll=6)
        part_ref[:, :kv_width] = part_ref[:, :kv_width] * scale

    def to_owner(j):
        return pltpu.make_async_remote_copy(
            src_ref=leaving.at[j],
            dst_ref=arriving.at[me],
            send_sem=send.at[j],
            recv_sem=recv.at[me],
            device_id={"seq": j},
            device_id_type=MESH_IDS,
        )

    def other_block(j, carry):
        key_block(j)
        leaving[j] = part_ref[...].astype(BF16)
        to_owner(j).start()
        return carry

    lax.fori_loop(0, me, other_block, 0)
    key_block(me)
    part_ref[...] = part_ref[...].astype(BF16).astype(F32)
    cosines, sines = cos_ref[...], -sin_ref[...]

    def one_query(h, carry):
        cols = pl.ds(pl.multiple_of(h * HEAD_DIM, HEAD_DIM), HEAD_DIM)
        out_ref[:, cols] = rotate(dq_ref[:, cols] * scale, cosines, sines).astype(BF16)
        return carry

    lax.fori_loop(0, heads, one_query, 0)

    def add_arrived(m, carry):
        pltpu.make_async_remote_copy(
            src_ref=leaving.at[m],
            dst_ref=arriving.at[m],
            send_sem=send.at[m],
            recv_sem=recv.at[m],
            device_id={"seq": m},
            device_id_type=MESH_IDS,
        ).wait_recv()
        part_ref[...] += arriving[m].astype(F32)
        return carry

    lax.fori_loop(me + 1, count, add_arrived, 0)
    first = heads * HEAD_DIM
    for g in range(kv_heads):
        cols = slice(g * HEAD_DIM, (g + 1) * HEAD_DIM)
        out_ref[:, first + g * HEAD_DIM : first + (g + 1) * HEAD_DIM] = rotate(
            part_ref[:, cols], cosines, sines
        ).astype(BF16)
    out_ref[:, first + kv_width :] = part_ref[:, kv_width:].astype(BF16)

    def sent(j, carry):
        to_owner(j).wait_send()
        return carry

    lax.fori_loop(0, me, sent, 0)


def attention_back(length, queries, kv_all, grads, lse, attended, cosines, sines, collective_id):
    count = lax.axis_size("seq")
    rows, q_width = queries.shape
    kv_width = kv_all.shape[1] // 2
    heads, kv_heads = q_width // HEAD_DIM, kv_width // HEAD_DIM
    vmem = pl.BlockSpec(memory_space=pltpu.VMEM)
    return pl.pallas_call(
        functools.partial(attention_back_kernel, count, heads, kv_heads),
        out_shape=jax.ShapeDtypeStruct((rows, q_width + 2 * kv_width), BF16),
        in_specs=[pl.BlockSpec(memory_space=pltpu.SMEM)] + [vmem] * 7,
        out_specs=vmem,
        scratch_shapes=[
            pltpu.VMEM((heads, rows), F32),
            pltpu.VMEM((rows, q_width), F32),
            pltpu.VMEM((rows, 2 * kv_width), F32),
            pltpu.VMEM((count, rows, 2 * kv_width), BF16),
            pltpu.VMEM((count, rows, 2 * kv_width), BF16),
            pltpu.SemaphoreType.DMA((count,)),
            pltpu.SemaphoreType.DMA((count,)),
        ],
        compiler_params=pltpu.CompilerParams(
            collective_id=collective_id, vmem_limit_bytes=30 << 20
        ),
        cost_estimate=pl.CostEstimate(
            flops=10 * count * rows * rows * q_width, bytes_accessed=1 << 20, transcendentals=0
        ),
        name="attention_backward",
    )(length, queries, kv_all, grads, lse, attended, cosines, sines)


def weight_grad_kernel(n, *refs):
    lefts, rights, outs = refs[:2], refs[2 : 2 + 2 * n], refs[2 + 2 * n :]
    for k, out_ref in enumerate(outs):
        early, late = rights[2 * k : 2 * k + 2]
        total = tn(lefts[0][...], early[...]) + tn(lefts[1][...], late[...])
        out_ref[...] = total.astype(BF16)


def weight_grads(lefts, rights, name):
    columns, tile = lefts[0].shape[1], 256
    flat = [part for pair in rights for part in pair]
    return pl.pallas_call(
        functools.partial(weight_grad_kernel, len(rights)),
        grid=(columns // tile,),
        out_shape=[jax.ShapeDtypeStruct((columns, r[0].shape[1]), BF16) for r in rights],
        in_specs=[pl.BlockSpec((x.shape[0], tile), lambda i: (0, i)) for x in lefts]
        + [pl.BlockSpec(r.shape, lambda i: (0, 0), pipeline_mode=pl.Buffered(1)) for r in flat],
        out_specs=[pl.BlockSpec((tile, r[0].shape[1]), lambda i: (i, 0)) for r in rights],
        compiler_params=pltpu.CompilerParams(vmem_limit_bytes=48 << 20),
        cost_estimate=pl.CostEstimate(flops=0, bytes_accessed=1 << 20, transcendentals=0),
        name=name,
    )(*lefts, *flat)


def seq_permutes(block_for):
    count, me = lax.axis_size("seq"), lax.axis_index("seq")
    pieces = [block_for(me)]
    for step in range(1, count):
        ring = [(i, (i + step) % count) for i in range(count)]
        pieces.append(lax.ppermute(block_for(lax.rem(me + step, count)), "seq", ring))
    return pieces


def in_seq_order(pieces, dtype):
    count, me = len(pieces), lax.axis_index("seq")
    whole = jnp.zeros((count,) + pieces[0].shape, dtype)
    for step, piece in enumerate(pieces):
        place = lax.rem(me + count - step, count)
        whole = lax.dynamic_update_index_in_dim(whole, piece.astype(dtype), place, 0)
    return whole


def on_device(
    hidden_in,
    lengths,
    routes,
    gates,
    priority,
    attn_gain,
    mlp_gain,
    w_query,
    key_projection,
    value_projection,
    w_out,
    w_gate,
    w_up,
    w_down,
    cotangent,
):
    rows = hidden_in.shape[1]
    width = hidden_in.shape[2]
    dp_count = lax.axis_size("dp")
    seq_count = lax.axis_size("seq")
    devices = dp_count * seq_count
    own_experts = w_gate.shape[0]
    sharers = seq_count // own_experts
    hidden_units = w_gate.shape[2]
    my_seq = lax.axis_index("seq")
    extent = rows * seq_count
    query_pos = my_seq * rows + jnp.arange(rows, dtype=jnp.int32)
    length = lengths[0]
    is_valid = query_pos < length
    q_width = w_query.shape[1]
    kv_width = key_projection.shape[1]
    cosine_lookup, sine_lookup = rope_angles(query_pos, HEAD_DIM)

    gain_block = jnp.concatenate(
        [attn_gain[:, None], mlp_gain[:, None], jnp.zeros((attn_gain.shape[0], LANES - 2), BF16)],
        axis=1,
    )
    packed = jnp.concatenate([w_query, key_projection, value_projection], axis=1)
    staged = seq_count == 4 and w_query.shape[0] % 16 == 0

    def expert_pieces(weights):
        def block_for(peer):
            return lax.dynamic_index_in_dim(weights, peer // sharers, 0, keepdims=False)

        return seq_permutes(block_for)

    gate_parts = expert_pieces(w_gate)
    if staged:
        packed_full, gains_full, out_full = staged_gather(
            [packed, gain_block, w_out], [], None, 2, "gather_attention_weights"
        )
    else:
        packed_full = lax.all_gather(packed, BOTH, axis=0, tiled=True)
        gains_full = lax.all_gather(gain_block, BOTH, axis=0, tiled=True)
        out_full = lax.all_gather(w_out, BOTH, axis=0, tiled=True)

    pair_routes, place, kept = claim_places(routes[0], priority[0, 0], is_valid)
    holder = (pair_routes // own_experts) * seq_count + (pair_routes % own_experts) * sharers
    holder = holder + my_seq * sharers // seq_count
    slots = devices * CAP
    target = jnp.where(kept, holder * CAP + place, slots).reshape(rows, TOP)
    slot_ids = jnp.arange(slots, dtype=jnp.int32)
    hits = target[:, :, None] == slot_ids[None, None, :]
    gate_rows = gates[0]
    token_hot = jnp.any(hits, axis=1).astype(BF16)

    def hot_of(first, size):
        mine = kept & (place >= first) & (place < first + size)
        spot = jnp.where(mine, holder * size + place - first, slots).reshape(rows, TOP)
        ids = jnp.arange(devices * size, dtype=jnp.int32)
        return jnp.any(spot[:, :, None] == ids[None, None, :], axis=1).astype(BF16)

    early_hot, late_hot = hot_of(0, EARLY), hot_of(EARLY, CAP - EARLY)
    slot_gate = jnp.sum(jnp.where(hits, gate_rows[:, :, None], 0.0), axis=(0, 1))

    live_cotangent = jnp.where(is_valid[:, None], cotangent[0], jnp.zeros((), BF16))
    out_grad = live_cotangent.astype(F32)
    grad_send = (tn(token_hot, live_cotangent) * slot_gate[:, None]).astype(BF16)
    packed_full, gains_full, out_full, gate_parts, grad_send = lax.optimization_barrier(
        (packed_full, gains_full, out_full, gate_parts, grad_send)
    )
    gain_one, gain_two = gains_full[:, 0].astype(F32), gains_full[:, 1].astype(F32)
    grad_rows = swap(grad_send.reshape(devices, CAP, width), ("dp", "seq"))

    inputs = hidden_in[0].astype(F32)
    scale_one = lax.rsqrt(jnp.mean(inputs * inputs, axis=-1, keepdims=True) + EPSILON)
    normed = (inputs * scale_one * gain_one).astype(BF16)
    projected = nn(normed, packed_full)
    cosines, sines = cosine_lookup[:, 0], sine_lookup[:, 0]
    cosines = jnp.concatenate([cosines, cosines], axis=1)
    sines = jnp.concatenate([-sines, sines], axis=1)
    attended, log_total, query_flat, kv_all = attention(
        lengths, projected, cosines, sines, q_width, 1
    )
    kv_all = kv_all.reshape(extent, 2 * kv_width)
    attended, w_up = lax.optimization_barrier((attended, w_up))
    up_parts = expert_pieces(w_up)
    middle = inputs + nn(attended, out_full)
    scale_two = lax.rsqrt(jnp.mean(middle * middle, axis=-1, keepdims=True) + EPSILON)
    moe_input = (middle * scale_two * gain_two).astype(BF16)

    def to_experts(hot):
        return tn(hot, moe_input).astype(BF16).reshape(devices, -1, width)

    early_send, late_send = to_experts(early_hot), to_experts(late_hot)
    early_send, late_send, grad_rows, up_parts, w_down = lax.optimization_barrier(
        (early_send, late_send, grad_rows, up_parts, w_down)
    )
    early_grads, late_grads, w_down = lax.optimization_barrier(
        (grad_rows[:, :EARLY], grad_rows[:, EARLY:], w_down)
    )
    down_parts = expert_pieces(w_down)
    early_rows = swap(early_send, ("dp", "seq"))
    early_rows, late_send = lax.optimization_barrier((early_rows, late_send))
    late_rows = swap(late_send, ("dp", "seq"))
    gate_full = in_seq_order(gate_parts, BF16).reshape(width, hidden_units)
    up_full = in_seq_order(up_parts, BF16).reshape(width, hidden_units)
    down_full = in_seq_order(down_parts, BF16).reshape(hidden_units, width)
    early_rows, gate_full, up_full, down_full, early_grads, late_grads = (
        lax.optimization_barrier(
            (early_rows, gate_full, up_full, down_full, early_grads, late_grads)
        )
    )

    def run_expert(slot_rows, grads):
        blocks = slot_rows.shape[:2]
        slot_rows, grads = slot_rows.reshape(-1, width), grads.reshape(-1, width)
        gate_pre = nn(slot_rows, gate_full)
        up_pre = nn(slot_rows, up_full)
        gate_sigmoid = jax.nn.sigmoid(gate_pre)
        gate_act = gate_pre * gate_sigmoid
        gate_slope = gate_sigmoid * (1.0 + gate_pre * (1.0 - gate_sigmoid))
        hidden = (gate_act * up_pre).astype(BF16)
        hidden_grad = nt(grads, down_full)
        gate_pre_grad = (hidden_grad * up_pre * gate_slope).astype(BF16)
        up_pre_grad = (hidden_grad * gate_act).astype(BF16)
        return [x.reshape(blocks + (-1,)) for x in (hidden, gate_pre_grad, up_pre_grad)]

    def row_grads(gate_pre_grad, up_pre_grad):
        blocks = gate_pre_grad.shape[:2]
        gate_pre_grad = gate_pre_grad.reshape(-1, hidden_units)
        up_pre_grad = up_pre_grad.reshape(-1, hidden_units)
        row_grad = (nt(gate_pre_grad, gate_full) + nt(up_pre_grad, up_full)).astype(BF16)
        return row_grad.reshape(blocks + (width,))

    def both_parts(early, late):
        return jnp.concatenate([early, late], axis=1).reshape(slots, -1)

    def to_owners(grad):
        grad = grad.reshape(seq_count, -1, grad.shape[1])

        def block_for(peer):
            return lax.dynamic_index_in_dim(grad, peer, 0, keepdims=False)

        return seq_permutes(block_for)

    def owned_sum(pieces):
        whole = in_seq_order(pieces, F32)
        return jnp.sum(whole.reshape((own_experts, sharers) + whole.shape[1:]), axis=1)

    early_hidden, *early_pre_grads = run_expert(early_rows, early_grads)
    early_row_grad = row_grads(*early_pre_grads)
    late_rows, early_row_grad = lax.optimization_barrier((late_rows, early_row_grad))
    early_back = swap(early_row_grad, ("dp", "seq"))
    late_hidden, *late_pre_grads = run_expert(late_rows, late_grads)

    def flat(*parts):
        return [part.reshape(-1, part.shape[-1]) for part in parts]

    gate_grad, up_grad = weight_grads(
        flat(early_rows, late_rows),
        [flat(*pair) for pair in zip(early_pre_grads, late_pre_grads, strict=True)],
        "gate_up_grads",
    )
    late_pre_grads, late_hidden, gate_grad, up_grad = lax.optimization_barrier(
        (late_pre_grads, late_hidden, gate_grad, up_grad)
    )
    gate_grad_parts = to_owners(gate_grad)
    late_row_grad = row_grads(*late_pre_grads)
    early_back, late_row_grad, gate_grad_parts, up_grad, late_hidden = lax.optimization_barrier(
        (early_back, late_row_grad, gate_grad_parts, up_grad, late_hidden)
    )
    expert_hidden = both_parts(early_hidden, late_hidden)
    late_back = swap(late_row_grad, ("dp", "seq"))
    gate_owned, up_owned = owned_sum(gate_grad_parts), owned_sum(to_owners(up_grad))
    (down_grad,) = weight_grads(
        flat(early_hidden, late_hidden), [flat(early_grads, late_grads)], "down_grads"
    )
    expert_out = nn(expert_hidden, down_full).astype(BF16)
    expert_out, late_back, gate_owned, up_owned, down_grad = lax.optimization_barrier(
        (expert_out, late_back, gate_owned, up_owned, down_grad)
    )
    returned = swap(expert_out.reshape(devices, CAP, width), ("dp", "seq")).reshape(slots, width)
    early_back, late_back = early_back.reshape(-1, width), late_back.reshape(-1, width)
    moe_input_grad = nn(early_hot, early_back) + nn(late_hot, late_back)
    middle_norm_grad, gain_two_grad = norm_back(middle, scale_two, gain_two, moe_input_grad)
    middle_grad = out_grad + middle_norm_grad
    branch_grad = middle_grad.astype(BF16)
    out_terms = tn(attended, branch_grad).astype(BF16)
    attended_grad = nt(branch_grad, out_full).astype(BF16)
    projected_grad = attention_back(
        lengths,
        query_flat,
        kv_all,
        attended_grad,
        log_total,
        attended,
        cosines,
        sines,
        4,
    )
    normed_grad = nt(projected_grad, packed_full)
    input_norm_grad, gain_one_grad = norm_back(inputs, scale_one, gain_one, normed_grad)
    input_grad = middle_grad + input_norm_grad

    lane = lax.broadcasted_iota(jnp.int32, (width, LANES), 1)
    gain_terms = jnp.where(lane == 0, gain_one_grad[:, None], gain_two_grad[:, None])
    gain_terms = jnp.where(lane < 2, gain_terms, 0.0).astype(BF16)
    query_terms = tn(normed, projected_grad).astype(BF16)
    if staged:
        out_owned, gains_owned, owned, down_owned = staged_scatter(
            [out_terms, gain_terms, query_terms],
            [down_grad.reshape(seq_count, -1, width)],
            lambda ref, peer: ref.at[peer],
            6,
            "scatter_attention_grads",
        )
        down_owned = down_owned.reshape((own_experts, sharers) + down_owned.shape[1:])
        down_owned = jnp.sum(down_owned.astype(F32), axis=1)
    else:
        terms = jnp.concatenate([out_terms, gain_terms, query_terms], axis=1)
        terms = lax.psum_scatter(terms, BOTH, scatter_dimension=0, tiled=True).astype(F32)
        out_owned, gains_owned = terms[:, :width], terms[:, width : width + LANES]
        owned = terms[:, width + LANES :]
        down_owned = owned_sum(to_owners(down_grad))
    returned, owned = lax.optimization_barrier((returned, owned))
    expert_grads = [gate_owned, up_owned, down_owned]

    gate_hot = jnp.sum(jnp.where(hits, gate_rows[:, :, None], 0.0), axis=1).astype(BF16)
    layer_out = middle + nn(gate_hot, returned)
    return (
        layer_out[None],
        input_grad[None],
        gains_owned[:, 0],
        gains_owned[:, 1],
        owned[:, :q_width],
        owned[:, q_width : q_width + kv_width],
        owned[:, q_width + kv_width : q_width + 2 * kv_width],
        out_owned,
        *expert_grads,
    )


def solution(mesh):
    part = P("dp", "seq", None)
    both = P(BOTH)
    both_rows = P(BOTH, None)
    return jax.shard_map(
        on_device,
        mesh=mesh,
        in_specs=(part, P("dp"), part, part, part, both, both)
        + (both_rows,) * 4
        + (part,) * 4,
        out_specs=(part, part, both, both) + (both_rows,) * 4 + (part,) * 3,
        check_vma=False,
    )
```
